32 devices in a mesh: dp: 8 (over z, x), seq: 4 (over y, core).
Axes of the slice: x: 2, y: 2, z: 4, core: 2. Of those that a mesh axis runs over, the one named last changes fastest.
Arguments:
- hidden: bfloat16 [8, 1024, 1536], P('dp', 'seq'), may hold values from -6 to 6
- segments: int32 [8, 1024], P('dp', 'seq'), may hold values from 0 to 3, never falling along the last dimension, each value on 1 to 768 neighbouring positions
- cotangent: bfloat16 [8, 1024, 1536], P('dp', 'seq'), may hold values from -6 to 6
- norm_gain: float32 [1536], replicated, may hold values from 0.5 to 1.5
- in_weight: float32 [1536, 6448], P(('dp', 'seq')), may hold values from -0.15625 to 0.15625
- conv_weight: float32 [4, 3328], replicated, may hold values from -3 to 3
- conv_bias: float32 [3328], replicated, may hold values from -3 to 3
- step_bias: float32 [48], replicated, may hold values from -4 to -1
- log_rate: float32 [48], replicated, may hold values from -5 to 0.5
- skip_gain: float32 [48], replicated, may hold values from 0.5 to 1.5
- gate_gain: float32 [3072], replicated, may hold values from 0.5 to 1.5
- out_weight: float32 [3072, 1536], P(('dp', 'seq')), may hold values from -0.109375 to 0.109375
Outputs:
- result: bfloat16 [8, 1024, 1536], P('dp', 'seq')
- d_hidden: float32 [8, 1024, 1536], P('dp', 'seq')
- d_norm_gain: float32 [1536], replicated
- d_in_weight: float32 [1536, 6448], P(('dp', 'seq'))
- d_conv_weight: float32 [4, 3328], replicated
- d_conv_bias: float32 [3328], replicated
- d_step_bias: float32 [48], replicated
- d_log_rate: float32 [48], replicated
- d_skip_gain: float32 [48], replicated
- d_gate_gain: float32 [3072], replicated
- d_out_weight: float32 [3072, 1536], P(('dp', 'seq'))
The draws below stay inside these ranges and needn't reach their ends.
Inputs may be any that keep to these rules, and one draw needn't show every extreme that they name: `segments`: along each sequence the numbers never fall; a document is a run of equal numbers of 1 to 768 tokens, and one run holds exactly 768.
All inputs are finite; a program needn't handle non-finite values.
Results may differ from the reference program's by a relative error of at most 0.0096.
Values may be sent and summed in bfloat16 or wider, within the bound.
No kernel may reach another device: no remote copies, remote signals or barrier semaphores. Data moves between devices by JAX's collectives and lax.ppermute only.
A program may use at most 256 MiB of HBM per device.

```python
import math
import jax
import jax.numpy as jnp
import numpy as np
from jax import lax

D = 1536
DI = 3072
H = 48
P_SIZE = 64
N = 128
CONV = 4
SPAN = 256
SEGS = 4
LEN = 1024
MOST_DOC = 768
SEQUENCES = 8
XBC = 3328
PROJ = 6448


def levels(key, dims, cuts, smallest, high):
    level = 1.0
    for axis_at, parts in cuts:
        steps = jax.random.uniform(jax.random.fold_in(jax.random.fold_in(key, 6), axis_at), (parts,), jnp.float32, smallest / len(cuts), high / len(cuts))
        level = level * jnp.repeat(jnp.exp(steps), dims[axis_at] // parts).reshape((-1,) + (1,) * (len(dims) - 1 - axis_at))
    return level


def split_up(amount, total, bound, lean):
    portions = [(1 << 20) // math.isqrt(standing ** lean) + 1 for standing in range(2, amount + 1)]
    spare, holding = total - bound - (amount - 1), [1] * (amount - 1)
    while spare > 0:
        free = [i for i in range(amount - 1) if holding[i] < bound]
        mass, left = sum([portions[i] for i in free]), spare
        for i in free:
            more = min(bound - holding[i], max(1, left * portions[i] // mass), spare)
            holding[i] = holding[i] + more
            spare = spare - more
    return np.array([bound] + holding)


def ragged_sizes(key, count, total, limit, slope):
    if count == 2:
        one = jax.random.randint(key, (), max(1, total - limit), min(limit, total - 1) + 1)
        return jnp.stack([one, total - one])
    lengths = jnp.asarray(split_up(count, total, limit, slope), jnp.int32)
    pairs = (count - 1) // 2
    giver, receiver = lengths[1:1 + 2 * pairs:2], lengths[2:2 + 2 * pairs:2]
    room = jnp.minimum(giver - 1, limit - receiver)
    moved = jax.random.randint(jax.random.fold_in(key, 1), (pairs,), 0, 1 << 20) % (room + 1)
    lengths = lengths.at[1:1 + 2 * pairs:2].set(giver - moved).at[2:2 + 2 * pairs:2].set(receiver + moved)
    return lengths[jax.random.permutation(jax.random.fold_in(key, 2), count)]


def gaussian(rng, dims, width, most, shards=(), dtype=jnp.bfloat16):
    array = jax.random.normal(rng, dims, jnp.float32) * width
    if len(shards) > 0:
        array = levels(rng, dims, shards, -0.22, 0.18) * array
    return jnp.clip(array, min=-most, max=most).astype(dtype)


def setup_inputs(seed: int = 0) -> dict:
    arg_keys = jax.random.split(jax.random.key(seed), 13)
    return {
        "hidden": gaussian(arg_keys[0], (SEQUENCES, LEN, D), 1.0, 6.0, ((0, 8), (1, 4))),
        "segments": jax.vmap(lambda own: jnp.searchsorted(jnp.cumsum(ragged_sizes(own, SEGS, LEN, MOST_DOC, 0)), jnp.arange(LEN), side="right"))(jax.random.split(arg_keys[1], SEQUENCES)).reshape((SEQUENCES, LEN)).astype(jnp.int32),
        "cotangent": gaussian(arg_keys[2], (SEQUENCES, LEN, D), 1.0, 6.0, ((0, 8), (1, 4))),
        "norm_gain": jnp.clip(1.0 + 0.1 * jax.random.normal(arg_keys[3], (D,), jnp.float32), 0.5, 1.5),
        "in_weight": gaussian(arg_keys[4], (D, PROJ), D ** -0.5, 0.15625, ((0, 32),), jnp.float32),
        "conv_weight": gaussian(arg_keys[5], (CONV, XBC), CONV ** -0.5, 3.0, (), jnp.float32),
        "conv_bias": gaussian(arg_keys[6], (XBC,), 0.5, 3.0, (), jnp.float32),
        "step_bias": jnp.clip(jax.random.uniform(arg_keys[7], (H,), jnp.float32, -4.0, -1.0), -4.0, -1.0),
        "log_rate": jnp.clip(jax.random.uniform(arg_keys[8], (H,), jnp.float32, -5.0, 0.5), -5.0, 0.5),
        "skip_gain": jnp.clip(jax.random.uniform(arg_keys[9], (H,), jnp.float32, 0.5, 1.5), 0.5, 1.5),
        "gate_gain": jnp.clip(1.0 + 0.1 * jax.random.normal(arg_keys[10], (DI,), jnp.float32), 0.5, 1.5),
        "out_weight": gaussian(arg_keys[11], (DI, D), DI ** -0.5, 0.109375, ((0, 32),), jnp.float32),
    }


epsilon = 1e-05
highest = lax.Precision.HIGHEST

@jax.custom_vjp
def low(v):
    return lax.optimization_barrier(v.astype(jnp.bfloat16)).astype(jnp.float32)

@jax.custom_vjp
def low_back(v):
    return v

def low_keep(v):
    return (low(v), None)

def low_pass(kept, grad):
    return (grad,)

def back_keep(v):
    return (v, None)

def back_low(kept, grad):
    return (low(grad),)
low.defvjp(low_keep, low_pass)
low_back.defvjp(back_keep, back_low)

def rms_scale(values, scaling):
    mean_sq = lax.optimization_barrier(jnp.mean(values * values, axis=-1, keepdims=True))
    return values * lax.rsqrt(mean_sq + epsilon) * scaling

def add_skip(ssd_out, x_part, skip_gain):
    dims_of = ssd_out.shape
    n_heads = skip_gain.shape[0]
    grouped = ssd_out.reshape(dims_of[:-1] + (n_heads, -1)) + skip_gain[:, None] * x_part.reshape(dims_of[:-1] + (n_heads, -1))
    return grouped.reshape(dims_of)

def conv_mixer(extended, doc_ext, conv_weight, conv_bias, step_raw, step_bias, log_rate):
    n_taps = conv_weight.shape[0]
    block = extended.shape[1] - (n_taps - 1)
    own_ids = doc_ext[:, n_taps - 1:]
    running = conv_bias + conv_weight[0] * extended[:, n_taps - 1:, :]
    for offset in range(1, n_taps):
        begin_at = n_taps - 1 - offset
        same_doc = jnp.where(doc_ext[:, begin_at:begin_at + block] == own_ids, 1.0, 0.0)
        running = running + conv_weight[offset] * extended[:, begin_at:begin_at + block, :] * same_doc[:, :, None]
    activated = jax.nn.silu(running)
    step_size = jax.nn.softplus(step_raw + step_bias)
    log_decay = -step_size * jnp.exp(log_rate)
    return (activated, step_size, log_decay)

def block_inner(x_part, b_part, c_part, step_size, log_decay, doc_ids):
    block, n_heads = step_size.shape
    x_heads = x_part.reshape(block, n_heads, -1)
    cumulative = jnp.cumsum(log_decay, axis=0)
    cum_heads = cumulative.T
    position = jnp.arange(block)
    causal = jnp.logical_and(position[:, None] >= position[None, :], doc_ids[:, None] == doc_ids[None, :])
    log_gap = jnp.where(causal[None], cum_heads[:, :, None] - cum_heads[:, None, :], 0.0)
    scores = jnp.dot(c_part, b_part.T, precision=highest)
    weights = jnp.where(causal[None], jnp.exp(log_gap), 0.0) * scores[None] * step_size.T[:, None, :]
    output = jnp.einsum('hts,shp->thp', weights, x_heads, precision=highest)
    to_end = jnp.where(doc_ids == doc_ids[-1], 1.0, 0.0)[:, None] * jnp.exp(cumulative[-1][None, :] - cumulative) * step_size
    carried = jnp.einsum('sh,shp,sn->hpn', to_end, x_heads, b_part, precision=highest)
    return (output.reshape(block, -1), carried, jnp.exp(cumulative[-1]))

def block_enter(c_part, log_decay, doc_ids, state_in, id_in):
    cumulative = jnp.cumsum(log_decay, axis=0)
    entering = jnp.where(doc_ids == id_in, 1.0, 0.0)[:, None] * jnp.exp(cumulative)
    output = jnp.einsum('tn,hpn->thp', c_part, state_in, precision=highest) * entering[:, :, None]
    return output.reshape(c_part.shape[0], -1)

def sequence_scan(x_part, b_part, c_part, step_size, log_decay, doc_ids):
    spans = LEN // SPAN

    def advance(carried, pieces):
        state_in, id_in = carried
        inner_out, local_state, retained = block_inner(*pieces)
        enter_out = block_enter(pieces[2], pieces[4], pieces[5], state_in, id_in)
        linked = jnp.where(pieces[5][-1] == id_in, 1.0, 0.0)
        state_out = local_state + (linked * retained)[:, None, None] * state_in
        return ((state_out, pieces[5][-1]), inner_out + enter_out)
    pieces = tuple((v.reshape((spans, SPAN) + v.shape[1:]) for v in (x_part, b_part, c_part, step_size, log_decay, doc_ids)))
    initial = (jnp.zeros((H, P_SIZE, N), jnp.float32), -jnp.ones((), jnp.float32))
    carried, outputs = lax.scan(jax.checkpoint(advance), initial, pieces)
    return outputs.reshape(LEN, DI)

def mamba_layer(hidden, doc_ids, params):
    norm_gain, in_weight, conv_weight, conv_bias, step_bias, log_rate, skip_gain, gate_gain, out_weight = params
    normed = low(rms_scale(hidden, norm_gain))
    projected = low_back(jnp.dot(normed, low(in_weight), precision=highest))
    gate_z = projected[:, :DI]
    conv_input = low(projected[:, DI:DI + XBC])
    step_raw = projected[:, DI + XBC:]
    extended = jnp.concatenate([jnp.zeros((1, CONV - 1, XBC), jnp.float32), conv_input[None]], axis=1)
    doc_ext = jnp.concatenate([-jnp.ones((1, CONV - 1), jnp.float32), doc_ids[None]], axis=1)
    activated, step_size, log_decay = conv_mixer(extended, doc_ext, conv_weight, conv_bias, step_raw[None], step_bias, log_rate)
    activated = activated[0]
    x_part = activated[:, :DI]
    b_part = activated[:, DI:DI + N]
    c_part = activated[:, DI + N:]
    ssd_out = sequence_scan(x_part, b_part, c_part, step_size[0], log_decay[0], doc_ids)
    gated = add_skip(ssd_out, x_part, skip_gain) * jax.nn.silu(gate_z)
    gate_normed = low(rms_scale(gated, gate_gain))
    return hidden + jnp.dot(gate_normed, low(out_weight), precision=highest)

def reference(hidden, segments, cotangent, norm_gain, in_weight, conv_weight, conv_bias, step_bias, log_rate, skip_gain, gate_gain, out_weight):
    params = (norm_gain, in_weight, conv_weight, conv_bias, step_bias, log_rate, skip_gain, gate_gain, out_weight)
    zero_grads = tuple((jnp.zeros_like(v) for v in params))

    def accumulate(totals, sample):
        sequence, doc_ids, cot_seq = sample

        def apply_layer(values, *weights):
            return mamba_layer(values, doc_ids, weights)
        output, pullback = jax.vjp(apply_layer, sequence.astype(jnp.float32), *params)
        gradients = pullback(cot_seq.astype(jnp.float32))
        summed = tuple((t + g for t, g in zip(totals, gradients[1:])))
        return (summed, (output.astype(jnp.bfloat16), gradients[0]))
    totals, (outputs, d_hidden) = lax.scan(accumulate, zero_grads, (hidden, segments.astype(jnp.float32), cotangent))
    return (outputs, d_hidden, totals[0], totals[1], totals[2], totals[3], totals[4], totals[5], totals[6], totals[7], totals[8])
```

```python
import functools

import jax
import jax.numpy as jnp
from jax import lax
from jax.experimental import pallas as pl
from jax.experimental.pallas import tpu as pltpu
from jax.sharding import PartitionSpec as P

epsilon = 1e-05
highest = lax.Precision.HIGHEST
f32 = jnp.float32
bf16 = jnp.bfloat16
LANES = 128
HALO = 16
NEG = -1e30


def mm(a, b, dims, out=f32):
    return lax.dot_general(a, b, (dims, ((), ())), preferred_element_type=out)


NN = ((1,), (0,))
NT = ((1,), (1,))
TN = ((0,), (0,))


def exact(a, b, dims):
    return lax.dot_general(a, b, (dims, ((), ())), precision=highest, preferred_element_type=f32)


def softplus(v):
    return jnp.maximum(v, 0.0) + jnp.log1p(jnp.exp(-jnp.abs(v)))


def sigmoid(v):
    return 1.0 / (1.0 + jnp.exp(-v))


def lane_iota(shape):
    return lax.broadcasted_iota(jnp.int32, shape, len(shape) - 1)


def spread(columns, first, second, wide):
    rows = columns.shape[0]
    left = jnp.broadcast_to(columns[:, first : first + 1], (rows, LANES))
    right = jnp.broadcast_to(columns[:, second : second + 1], (rows, LANES))
    return jnp.where(wide, left, right)


def step_parts(raw, rate, q):
    row = lax.broadcasted_iota(jnp.int32, (q, q), 0)
    col = lax.broadcasted_iota(jnp.int32, (q, q), 1)
    tri = jnp.where(row >= col, 1.0, 0.0).astype(f32)
    step = softplus(raw)
    decay = -step * rate
    total = exact(tri, decay, NN)
    return step, decay, total, tri, row >= col


def convolve(ext, docs_ext, own, weights, bias, lanes, q, taps):
    running = bias + weights[0:1, lanes] * ext[pl.ds(HALO, q), lanes]
    for lag in range(1, taps):
        same = jnp.where(docs_ext[pl.ds(HALO - lag, q), :] == own, 1.0, 0.0)
        running = running + weights[lag : lag + 1, lanes] * ext[pl.ds(HALO - lag, q), lanes] * same
    return running


def scan_forward(
    q, taps, pairs, head,
    x_ref, small_ref, bct_ref, dcol_ref, drow_ref, w_ref, b_ref, sb_ref, rate_ref, skip_ref,
    y_ref, states_ref,
    state, ext, docs_ext, xs, xt, last_doc,
):
    c = pl.program_id(0)
    n = bct_ref.shape[0] // 2

    @pl.when(c == 0)
    def _():
        state[...] = jnp.zeros_like(state)
        ext[pl.ds(0, HALO), :] = jnp.zeros((HALO, ext.shape[1]), f32)
        docs_ext[pl.ds(0, HALO), :] = jnp.full((HALO, LANES), -1.0, f32)
        last_doc[...] = jnp.full(last_doc.shape, -1.0, f32)

    own = dcol_ref[...]
    ext[pl.ds(HALO, q), :] = x_ref[...].astype(f32)
    docs_ext[pl.ds(HALO, q), :] = own
    step, _, cum, _, causal = step_parts(small_ref[...] + sb_ref[...], rate_ref[...], q)
    step_t = step.T
    cum_t = cum.T
    end = cum[q - 1 : q, :]
    id_in = last_doc[0:1, :]
    final = own[q - 1 : q, :]
    linked = jnp.where(final == id_in, 1.0, 0.0)
    fade = linked * jnp.exp(end)
    entering = jnp.where(own == id_in, 1.0, 0.0) * jnp.exp(cum)
    to_end = jnp.where(own == final, 1.0, 0.0) * jnp.exp(end - cum) * step
    same_doc = jnp.broadcast_to(own[:, 0:1], (q, q)) == jnp.broadcast_to(drow_ref[0:1, :], (q, q))
    hide = jnp.where(jnp.logical_and(causal, same_doc), 0.0, NEG)
    bt = bct_ref[0:n, :]
    ct = bct_ref[n : 2 * n, :]
    scores = mm(ct, bt, TN)
    states_ref[0] = state[...]
    old = state[...].astype(bf16)
    wide = lane_iota((q, LANES)) < head
    wide_row = lane_iota((1, LANES)) < head
    for k in range(pairs):
        lanes = slice(k * LANES, (k + 1) * LANES)
        h0, h1 = 2 * k, 2 * k + 1
        conv = convolve(ext, docs_ext, own, w_ref, b_ref[:, lanes], lanes, q, taps)
        x = conv * sigmoid(conv)
        xd = x * spread(step, h0, h1, wide)
        xt[:, lanes] = (x * spread(to_end, h0, h1, wide)).astype(bf16)
        mats = []
        for h in (h0, h1):
            gap = cum[:, h : h + 1] - cum_t[h : h + 1, :] + hide
            mats.append((jnp.exp(gap) * scores).astype(bf16))
        out = mm(mats[0], jnp.where(wide, xd, 0.0).astype(bf16), NN)
        out = out + mm(mats[1], jnp.where(wide, 0.0, xd).astype(bf16), NN)
        out = out + mm(ct, old[:, lanes], TN) * spread(entering, h0, h1, wide)
        y_ref[:, lanes] = out + skip_ref[:, lanes] * x
    update = mm(bt, xt[...], NN)
    for k in range(pairs):
        lanes = slice(k * LANES, (k + 1) * LANES)
        state[:, lanes] = state[:, lanes] * spread(fade, 2 * k, 2 * k + 1, wide_row) + update[:, lanes]
    ext[pl.ds(0, HALO), :] = ext[pl.ds(q, HALO), :]
    docs_ext[pl.ds(0, HALO), :] = docs_ext[pl.ds(q, HALO), :]
    last_doc[...] = jnp.broadcast_to(final, last_doc.shape)


def scan_backward(
    q, taps, pairs, head, chunks,
    x_ref, xp_ref, small_ref, bct_ref, dcol_ref, dcolp_ref, drow_ref, w_ref, b_ref, sb_ref, rate_ref,
    skip_ref, dy_ref, states_ref,
    dx_ref, dsmall_ref, dbct_ref, dconv_ref, dhead_ref,
    dstate, ext, docs_ext, dcv, docs_after, dye, xt, col_t,
):
    step_at = pl.program_id(0)
    c = chunks - 1 - step_at
    n = bct_ref.shape[0] // 2
    width = x_ref.shape[1]

    @pl.when(step_at == 0)
    def _():
        dstate[...] = jnp.zeros_like(dstate)
        dcv[pl.ds(q, HALO), :] = jnp.zeros((HALO, width), f32)
        docs_after[pl.ds(q, HALO), :] = jnp.full((HALO, LANES), -1.0, f32)
        dconv_ref[...] = jnp.zeros_like(dconv_ref)
        dhead_ref[...] = jnp.zeros_like(dhead_ref)
        col_t[...] = jnp.zeros_like(col_t)

    first = c == 0
    own = dcol_ref[...]
    before = jnp.where(first, -1.0, dcolp_ref[...])
    ext[pl.ds(0, HALO), :] = xp_ref[...].astype(f32)
    ext[pl.ds(HALO, q), :] = x_ref[...].astype(f32)
    docs_ext[pl.ds(0, HALO), :] = before
    docs_ext[pl.ds(HALO, q), :] = own
    docs_after[pl.ds(0, q), :] = own
    raw = small_ref[...] + sb_ref[...]
    rate = rate_ref[...]
    step, decay, cum, tri, causal = step_parts(raw, rate, q)
    step_t = step.T
    cum_t = cum.T
    end = cum[q - 1 : q, :]
    id_in = before[HALO - 1 : HALO, :]
    final = own[q - 1 : q, :]
    linked = jnp.where(final == id_in, 1.0, 0.0)
    fade = linked * jnp.exp(end)
    entering = jnp.where(own == id_in, 1.0, 0.0) * jnp.exp(cum)
    tail = jnp.where(own == final, 1.0, 0.0) * jnp.exp(end - cum)
    to_end = tail * step
    same_doc = jnp.broadcast_to(own[:, 0:1], (q, q)) == jnp.broadcast_to(drow_ref[0:1, :], (q, q))
    hide = jnp.where(jnp.logical_and(causal, same_doc), 0.0, NEG)
    bt = bct_ref[0:n, :]
    ct = bct_ref[n : 2 * n, :]
    scores = mm(ct, bt, TN)
    old = states_ref[0].astype(bf16)
    after = dstate[...].astype(bf16)
    wide = lane_iota((q, LANES)) < head
    wide_row = lane_iota((1, LANES)) < head
    lane = lane_iota((q, LANES))
    d_scores = jnp.zeros((q, q), f32)
    rows = jnp.zeros((q, LANES), f32)
    d_enter = jnp.zeros((q, LANES), f32)
    d_toend = jnp.zeros((q, LANES), f32)
    d_fade = jnp.zeros((8, LANES), f32)
    part = lax.broadcasted_iota(jnp.int32, (LANES, LANES), 0) // head
    to = lane_iota((LANES, LANES))
    for k in range(pairs):
        lanes = slice(k * LANES, (k + 1) * LANES)
        h0, h1 = 2 * k, 2 * k + 1
        pick = jnp.where(part + 2 * k == to, 1.0, 0.0)
        conv = convolve(ext, docs_ext, own, w_ref, b_ref[:, lanes], lanes, q, taps)
        sig = sigmoid(conv)
        x = conv * sig
        xb = x.astype(bf16)
        dy = dy_ref[:, lanes]
        halves = (jnp.where(wide, dy, 0.0).astype(bf16), jnp.where(wide, 0.0, dy).astype(bf16))
        dxd = jnp.zeros((q, LANES), f32)
        for h, half in ((h0, halves[0]), (h1, halves[1])):
            inner = mm(half, xb, NT)
            keep = jnp.exp(cum[:, h : h + 1] - cum_t[h : h + 1, :] + hide)
            grown = keep * inner
            mat = keep * scores
            dt = step_t[h : h + 1, :]
            g = grown * scores
            d_scores = d_scores + grown * dt
            rows = jnp.where(lane == h, jnp.sum(g * dt, axis=1, keepdims=True), rows)
            col_t[h : h + 1, :] = jnp.sum(g, axis=0, keepdims=True)
            dxd = dxd + mm(mat.astype(bf16), half, TN)
        v = mm(bt, after[:, lanes], TN)
        u = mm(ct, old[:, lanes], TN)
        enter_k = spread(entering, h0, h1, wide)
        end_k = spread(to_end, h0, h1, wide)
        d_enter = d_enter + exact(dy * u, pick, NN)
        d_toend = d_toend + exact(x * v, pick, NN)
        hh = jnp.sum(dstate[:, lanes] * states_ref[0, :, lanes], axis=0, keepdims=True)
        d_fade = d_fade + exact(jnp.broadcast_to(hh, (8, LANES)), pick, NN)
        dye[:, lanes] = (dy * enter_k).astype(bf16)
        xt[:, lanes] = (x * end_k).astype(bf16)
        dx = dxd * spread(step, h0, h1, wide) + end_k * v + skip_ref[:, lanes] * dy
        dconv = dx * (sig * (1.0 + conv * (1.0 - sig)))
        dcv[pl.ds(0, q), lanes] = dconv
        sums = [jnp.sum(dconv * ext[pl.ds(HALO, q), lanes], axis=0, keepdims=True)]
        dxin = w_ref[0:1, lanes] * dconv
        for lag in range(1, taps):
            same = jnp.where(docs_ext[pl.ds(HALO - lag, q), :] == own, 1.0, 0.0)
            sums.append(jnp.sum(dconv * same * ext[pl.ds(HALO - lag, q), lanes], axis=0, keepdims=True))
            follow = jnp.where(docs_after[pl.ds(lag, q), :] == own, 1.0, 0.0)
            dxin = dxin + w_ref[lag : lag + 1, lanes] * dcv[pl.ds(lag, q), lanes] * follow
        sums.append(jnp.sum(dconv, axis=0, keepdims=True))
        sums.append(jnp.sum(dy * x, axis=0, keepdims=True))
        dx_ref[:, lanes] = dxin.astype(bf16)
        for i, s in enumerate(sums):
            dconv_ref[i : i + 1, lanes] = dconv_ref[i : i + 1, lanes] + s
    dsb = d_scores.astype(bf16)
    dbct_ref[0:n, :] = mm(ct, dsb, NN) + mm(after, xt[...], NT)
    dbct_ref[n : 2 * n, :] = mm(bt, dsb, NT) + mm(old, dye[...], NT)
    new = mm(ct, dye[...], NN)
    for k in range(pairs):
        lanes = slice(k * LANES, (k + 1) * LANES)
        dstate[:, lanes] = dstate[:, lanes] * spread(fade, 2 * k, 2 * k + 1, wide_row) + new[:, lanes]
    cols = col_t[...].T
    pulled = d_toend * to_end
    at_end = jnp.sum(pulled, axis=0, keepdims=True) + fade * d_fade[0:1, :]
    d_cum = rows - step * cols + d_enter * entering - pulled
    last_row = lax.broadcasted_iota(jnp.int32, (q, LANES), 0) == q - 1
    d_cum = d_cum + jnp.where(last_row, at_end, 0.0)
    d_decay = exact(tri, d_cum, TN)
    d_step = cols + d_toend * tail - rate * d_decay
    d_raw = d_step * sigmoid(raw)
    dsmall_ref[...] = d_raw
    dhead_ref[0:1, :] = dhead_ref[0:1, :] + jnp.sum(d_raw, axis=0, keepdims=True)
    dhead_ref[1:2, :] = dhead_ref[1:2, :] + jnp.sum(d_decay * decay, axis=0, keepdims=True)
    dcv[pl.ds(q, HALO), :] = dcv[pl.ds(0, HALO), :]
    docs_after[pl.ds(q, HALO), :] = docs_after[pl.ds(0, HALO), :]


def whole(array):
    return pl.BlockSpec(array.shape, lambda c: (0,) * array.ndim)


def run_forward(q, x_in, small, bct, dcol, drow, conv_w, conv_b, sb, rate, skip, head):
    tokens, width = x_in.shape
    n = bct.shape[0] // 2
    chunks = tokens // q
    pairs = width // LANES
    taps = conv_w.shape[0]
    return pl.pallas_call(
        functools.partial(scan_forward, q, taps, pairs, head),
        grid=(chunks,),
        in_specs=[
            pl.BlockSpec((q, width), lambda c: (c, 0)),
            pl.BlockSpec((q, LANES), lambda c: (c, 0)),
            pl.BlockSpec((2 * n, q), lambda c: (0, c)),
            pl.BlockSpec((q, LANES), lambda c: (c, 0)),
            pl.BlockSpec((8, q), lambda c: (0, c)),
            whole(conv_w), whole(conv_b), whole(sb), whole(rate), whole(skip),
        ],
        out_specs=[
            pl.BlockSpec((q, width), lambda c: (c, 0)),
            pl.BlockSpec((1, n, width), lambda c: (c, 0, 0)),
        ],
        out_shape=[
            jax.ShapeDtypeStruct((tokens, width), f32),
            jax.ShapeDtypeStruct((chunks, n, width), f32),
        ],
        scratch_shapes=[
            pltpu.VMEM((n, width), f32),
            pltpu.VMEM((HALO + q, width), f32),
            pltpu.VMEM((HALO + q, LANES), f32),
            pltpu.VMEM((8, LANES), f32),
            pltpu.VMEM((q, width), bf16),
            pltpu.VMEM((8, LANES), f32),
        ],
        name="scan_forward",
    )(x_in, small, bct, dcol, drow, conv_w, conv_b, sb, rate, skip)


def run_backward(q, x_in, small, bct, dcol, drow, conv_w, conv_b, sb, rate, skip, dy, states, head):
    tokens, width = x_in.shape
    n = bct.shape[0] // 2
    chunks = tokens // q
    pairs = width // LANES
    taps = conv_w.shape[0]
    per = q // HALO

    def at(c):
        return chunks - 1 - c

    def prior(c):
        return jnp.maximum((chunks - 1 - c) * per - 1, 0)

    return pl.pallas_call(
        functools.partial(scan_backward, q, taps, pairs, head, chunks),
        grid=(chunks,),
        in_specs=[
            pl.BlockSpec((q, width), lambda c: (at(c), 0)),
            pl.BlockSpec((HALO, width), lambda c: (prior(c), 0)),
            pl.BlockSpec((q, LANES), lambda c: (at(c), 0)),
            pl.BlockSpec((2 * n, q), lambda c: (0, at(c))),
            pl.BlockSpec((q, LANES), lambda c: (at(c), 0)),
            pl.BlockSpec((HALO, LANES), lambda c: (prior(c), 0)),
            pl.BlockSpec((8, q), lambda c: (0, at(c))),
            whole(conv_w), whole(conv_b), whole(sb), whole(rate), whole(skip),
            pl.BlockSpec((q, width), lambda c: (at(c), 0)),
            pl.BlockSpec((1, n, width), lambda c: (at(c), 0, 0)),
        ],
        out_specs=[
            pl.BlockSpec((q, width), lambda c: (at(c), 0)),
            pl.BlockSpec((q, LANES), lambda c: (at(c), 0)),
            pl.BlockSpec((2 * n, q), lambda c: (0, at(c))),
            pl.BlockSpec((8, width), lambda c: (0, 0)),
            pl.BlockSpec((8, LANES), lambda c: (0, 0)),
        ],
        out_shape=[
            jax.ShapeDtypeStruct((tokens, width), bf16),
            jax.ShapeDtypeStruct((tokens, LANES), f32),
            jax.ShapeDtypeStruct((2 * n, tokens), f32),
            jax.ShapeDtypeStruct((8, width), f32),
            jax.ShapeDtypeStruct((8, LANES), f32),
        ],
        scratch_shapes=[
            pltpu.VMEM((n, width), f32),
            pltpu.VMEM((HALO + q, width), f32),
            pltpu.VMEM((HALO + q, LANES), f32),
            pltpu.VMEM((q + HALO, width), f32),
            pltpu.VMEM((q + HALO, LANES), f32),
            pltpu.VMEM((q, width), bf16),
            pltpu.VMEM((q, width), bf16),
            pltpu.VMEM((LANES, q), f32),
        ],
        name="scan_backward",
    )(x_in, x_in, small, bct, dcol, dcol, drow, conv_w, conv_b, sb, rate, skip, dy, states)


def swapped(block, bit):
    size = lax.axis_size("seq")
    return lax.ppermute(block, "seq", [(i, i ^ bit) for i in range(size)])


def bits_of(size):
    bits, bit = [], 1
    while bit < size:
        bits.append(bit)
        bit *= 2
    return bits


def gathered(block):
    index = lax.axis_index("seq")
    for bit in bits_of(lax.axis_size("seq")):
        other = swapped(block, bit)
        upper = (index & bit) != 0
        block = jnp.where(
            upper, jnp.concatenate([other, block], axis=0), jnp.concatenate([block, other], axis=0)
        )
    return block


def scattered(parts):
    index = lax.axis_index("seq")
    size = lax.axis_size("seq")
    rest = parts.shape[1:]
    lead = parts.shape[0]
    held = parts.reshape((size, lead // size) + rest)
    for bit in bits_of(size):
        half = held.reshape((held.shape[0] // 2, 2) + held.shape[1:])
        upper = (index & bit) != 0
        mine = jnp.where(upper, half[:, 1], half[:, 0])
        theirs = jnp.where(upper, half[:, 0], half[:, 1]).astype(bf16)
        held = mine.astype(f32) + swapped(theirs, bit).astype(f32)
    return held[0]


def padded(rows, width):
    return jnp.pad(rows, ((0, 0), (0, width - rows.shape[1])))


def shards(
    hidden, segments, cotangent, norm_gain, in_weight, conv_weight, conv_bias, step_bias, log_rate,
    skip_gain, gate_gain, out_weight,
):
    n_seqs, block, n_width = hidden.shape
    size = lax.axis_size("seq")
    groups = lax.axis_size("dp")
    index = lax.axis_index("seq")
    tokens = size * block
    n_inner = gate_gain.shape[0]
    n_heads = step_bias.shape[0]
    n_taps = conv_weight.shape[0]
    n_mixed = conv_bias.shape[0]
    n_state = (n_mixed - n_inner) // 2
    head = n_inner // n_heads
    own_inner = n_inner // size
    own_heads = n_heads // size
    own_bc = 2 * n_state // size
    q = min(128, block)
    in_rows = in_weight.shape[0]

    in_low = in_weight.astype(bf16)
    z_cols = in_low[:, :n_inner].reshape(in_rows, size, own_inner)
    x_cols = in_low[:, n_inner : 2 * n_inner].reshape(in_rows, size, own_inner)
    bc_cols = in_low[:, 2 * n_inner : n_inner + n_mixed].reshape(in_rows, size, own_bc)
    dt_cols = in_low[:, n_inner + n_mixed :].reshape(in_rows, size, own_heads)
    gap = jnp.zeros((in_rows, size, LANES - own_heads - own_bc), bf16)
    laid = jnp.concatenate([x_cols, dt_cols, gap, bc_cols, z_cols], axis=2).transpose(1, 0, 2)
    mine = lax.all_to_all(laid, "seq", 0, 0, tiled=True)
    mine = mine.reshape(size * in_rows, -1)
    n_first = own_inner + LANES
    w_first = lax.all_gather(mine[:, :n_first], "dp", axis=0, tiled=True)
    w_z = lax.all_gather(mine[:, n_first:], "dp", axis=0, tiled=True)
    order = [(f, (f % groups) * size + f // groups) for f in range(groups * size)]
    back = [(b, a) for a, b in order]
    out_moved = lax.ppermute(out_weight.astype(bf16), ("dp", "seq"), order)
    w_out = lax.all_gather(out_moved, "dp", axis=0, tiled=True)

    flat = hidden.reshape(block, n_width).astype(f32)
    inv = lax.rsqrt(jnp.mean(flat * flat, axis=-1, keepdims=True) + epsilon)
    unit = flat * inv
    normed = gathered((unit * norm_gain).astype(bf16))
    cot_own = cotangent.reshape(block, n_width)
    cot = gathered(cot_own)
    docs = lax.all_gather(segments.reshape(block), "seq", axis=0, tiled=True).astype(f32)
    dcol = jnp.broadcast_to(docs[:, None], (tokens, LANES))
    drow = jnp.broadcast_to(docs[None, :], (8, tokens))

    def own_part(vector, parts):
        return lax.dynamic_slice_in_dim(vector, index * parts, parts, vector.ndim - 1)

    w_x, w_small = w_first[:, :own_inner], w_first[:, own_inner:]
    small = mm(normed, w_small, NN)
    x_in = mm(normed, w_x, NN).astype(bf16)
    z = mm(normed, w_z, NN)
    conv_x = own_part(conv_weight[:, :n_inner], own_inner)
    bias_x = own_part(conv_bias[None, :n_inner], own_inner)
    conv_bc = own_part(conv_weight[:, n_inner:], own_bc)
    bias_bc = own_part(conv_bias[None, n_inner:], own_bc)
    sb = padded(own_part(step_bias[None], own_heads), LANES)
    rate = padded(jnp.exp(own_part(log_rate[None], own_heads)), LANES)
    skip = jnp.repeat(own_part(skip_gain[None], own_heads), head, axis=1)
    gain = own_part(gate_gain[None], own_inner)

    head_lanes = jnp.arange(LANES) < own_heads
    bc_in = small[:, LANES - own_bc :].astype(bf16).astype(f32)
    small_dt = jnp.where(head_lanes, small, 0.0)

    def earlier(rows, lag):
        return jnp.pad(rows, ((lag, 0), (0, 0)))[:tokens]

    def later(rows, lag):
        return jnp.pad(rows, ((0, lag), (0, 0)))[lag:]

    same = [None] + [
        jnp.where(jnp.pad(docs, (lag, 0), constant_values=-1.0)[:tokens] == docs, 1.0, 0.0)[:, None]
        for lag in range(1, n_taps)
    ]
    bc_conv = bias_bc + conv_bc[0:1] * bc_in
    for lag in range(1, n_taps):
        bc_conv = bc_conv + conv_bc[lag : lag + 1] * earlier(bc_in, lag) * same[lag]
    bc_sig = jax.nn.sigmoid(bc_conv)
    bct = lax.all_gather((bc_conv * bc_sig).astype(bf16).T, "seq", axis=0, tiled=True)

    y, states = run_forward(
        q, x_in, small_dt, bct, dcol, drow, conv_x, bias_x, sb, rate, skip, head
    )

    d_gn = mm(cot, w_out, NT)
    z_sig = jax.nn.sigmoid(z)
    z_act = z * z_sig
    gated = y * z_act
    scaled = d_gn * gain
    both = jnp.stack([jnp.sum(gated * gated, axis=1), jnp.sum(scaled * gated, axis=1)])
    both = lax.psum(both, "seq")
    g_inv = lax.rsqrt(both[0] / n_inner + epsilon)[:, None]
    g_dot = both[1][:, None] / n_inner
    gate_low = (gated * g_inv * gain).astype(bf16)
    d_gated = g_inv * scaled - gated * (g_inv * g_inv * g_inv * g_dot)
    d_gain = jnp.sum(d_gn * gated * g_inv, axis=0)
    d_z = (d_gated * y * (z_sig * (1.0 + z * (1.0 - z_sig)))).astype(bf16)
    d_y = d_gated * z_act

    branch = scattered(mm(gate_low, w_out, NN).astype(bf16))
    result = (flat + branch).reshape(n_seqs, block, n_width).astype(bf16)
    out_term = mm(gate_low, cot, TN).astype(bf16)
    z_term = mm(normed, d_z, TN).astype(bf16)
    out_part = lax.psum_scatter(out_term, "dp", scatter_dimension=0, tiled=True)
    z_part = lax.psum_scatter(z_term, "dp", scatter_dimension=0, tiled=True)
    d_out_weight = lax.ppermute(out_part, ("dp", "seq"), back).astype(f32)

    d_x, d_dt, d_bct, d_conv_x, d_heads = run_backward(
        q, x_in, small_dt, bct, dcol, drow, conv_x, bias_x, sb, rate, skip, d_y, states, head
    )
    d_bc = scattered(d_bct).T
    d_bcc = d_bc * (bc_sig * (1.0 + bc_conv * (1.0 - bc_sig)))
    d_bc_in = conv_bc[0:1] * d_bcc
    w_sums = [jnp.sum(d_bcc * bc_in, axis=0)]
    for lag in range(1, n_taps):
        held = d_bcc * same[lag]
        d_bc_in = d_bc_in + conv_bc[lag : lag + 1] * later(held, lag)
        w_sums.append(jnp.sum(held * earlier(bc_in, lag), axis=0))
    w_sums.append(jnp.sum(d_bcc, axis=0))
    d_small = jnp.concatenate([d_dt[:, : LANES - own_bc], d_bc_in], axis=1).astype(bf16)
    d_first = jnp.concatenate([d_x, d_small], axis=1)
    first_term = mm(normed, d_first, TN).astype(bf16)
    first_part = lax.psum_scatter(first_term, "dp", scatter_dimension=0, tiled=True)
    d_normed = mm(d_first, w_first, NT) + mm(d_z, w_z, NT)
    d_norm = scattered(d_normed.astype(bf16))

    term = jnp.concatenate([first_part, z_part], axis=1).reshape(size, in_rows, -1)
    moved = lax.all_to_all(term, "seq", 0, 0, tiled=True).transpose(1, 0, 2).astype(f32)
    d_in_weight = jnp.concatenate(
        [
            moved[:, :, n_first:].reshape(in_rows, n_inner),
            moved[:, :, :own_inner].reshape(in_rows, n_inner),
            moved[:, :, n_first - own_bc : n_first].reshape(in_rows, 2 * n_state),
            moved[:, :, own_inner : own_inner + own_heads].reshape(in_rows, n_heads),
        ],
        axis=1,
    )

    d_norm_gain = jnp.sum(d_norm * unit, axis=0)
    lifted = d_norm * norm_gain
    d_flat = inv * lifted - flat * (
        inv * inv * inv * jnp.mean(lifted * flat, axis=-1, keepdims=True)
    )
    d_hidden = (cot_own.astype(f32) + d_flat).reshape(n_seqs, block, n_width)

    d_skip = jnp.sum(d_conv_x[n_taps + 1].reshape(own_heads, head), axis=1)
    packed = jnp.concatenate(
        [
            d_conv_x[: n_taps + 1].reshape(-1),
            jnp.stack(w_sums).reshape(-1),
            d_gain,
            d_heads[0, :own_heads],
            d_heads[1, :own_heads],
            d_skip,
            d_norm_gain,
        ]
    )
    packed = jnp.sum(lax.all_gather(packed, "dp", axis=0), axis=0)
    packed = lax.all_gather(packed, "seq", axis=0)
    at = 0

    def take(count):
        nonlocal at
        at += count
        return packed[:, at - count : at]

    got_x = take((n_taps + 1) * own_inner).reshape(size, n_taps + 1, own_inner)
    got_bc = take((n_taps + 1) * own_bc).reshape(size, n_taps + 1, own_bc)
    got_x = got_x.transpose(1, 0, 2).reshape(n_taps + 1, n_inner)
    got_bc = got_bc.transpose(1, 0, 2).reshape(n_taps + 1, 2 * n_state)
    conv_all = jnp.concatenate([got_x, got_bc], axis=1)
    d_gate_gain = take(own_inner).reshape(n_inner)
    d_step_bias = take(own_heads).reshape(n_heads)
    d_log_rate = take(own_heads).reshape(n_heads)
    d_skip_gain = take(own_heads).reshape(n_heads)
    d_norm_all = jnp.sum(take(n_width), axis=0)
    return (
        result,
        d_hidden,
        d_norm_all,
        d_in_weight,
        conv_all[:n_taps],
        conv_all[n_taps],
        d_step_bias,
        d_log_rate,
        d_skip_gain,
        d_gate_gain,
        d_out_weight,
    )


def solution(mesh):
    tokens = P("dp", "seq", None)
    rows = P(("dp", "seq"), None)
    return jax.shard_map(
        shards,
        mesh=mesh,
        in_specs=(tokens, P("dp", "seq"), tokens, P(), rows, P(), P(), P(), P(), P(), P(), rows),
        out_specs=(tokens, tokens, P(), rows, P(), P(), P(), P(), P(), P(), rows),
        check_vma=False,
    )
```

```python
import functools

import jax
import jax.numpy as jnp
from jax import lax
from jax.experimental import pallas as pl
from jax.experimental.pallas import tpu as pltpu
from jax.sharding import PartitionSpec as P

epsilon = 1e-05
highest = lax.Precision.HIGHEST
f32 = jnp.float32
bf16 = jnp.bfloat16
LANES = 128
HALO = 16
NEG = -1e30


def mm(a, b, dims, out=f32):
    return lax.dot_general(a, b, (dims, ((), ())), preferred_element_type=out)


NN = ((1,), (0,))
NT = ((1,), (1,))
TN = ((0,), (0,))


def exact(a, b, dims):
    return lax.dot_general(a, b, (dims, ((), ())), precision=highest, preferred_element_type=f32)


def softplus(v):
    return jnp.maximum(v, 0.0) + jnp.log1p(jnp.exp(-jnp.abs(v)))


def sigmoid(v):
    return 1.0 / (1.0 + jnp.exp(-v))


def lane_iota(shape):
    return lax.broadcasted_iota(jnp.int32, shape, len(shape) - 1)


def spread(columns, first, second, wide):
    rows = columns.shape[0]
    left = jnp.broadcast_to(columns[:, first : first + 1], (rows, LANES))
    right = jnp.broadcast_to(columns[:, second : second + 1], (rows, LANES))
    return jnp.where(wide, left, right)


def step_parts(raw, rate, q):
    row = lax.broadcasted_iota(jnp.int32, (q, q), 0)
    col = lax.broadcasted_iota(jnp.int32, (q, q), 1)
    tri = jnp.where(row >= col, 1.0, 0.0).astype(f32)
    step = softplus(raw)
    decay = -step * rate
    total = exact(tri, decay, NN)
    return step, decay, total, tri, row >= col


def convolve(ext, docs_ext, own, weights, bias, lanes, q, taps):
    running = bias + weights[0:1, lanes] * ext[pl.ds(HALO, q), lanes]
    for lag in range(1, taps):
        same = jnp.where(docs_ext[pl.ds(HALO - lag, q), :] == own, 1.0, 0.0)
        running = running + weights[lag : lag + 1, lanes] * ext[pl.ds(HALO - lag, q), lanes] * same
    return running


def scan_forward(
    q, taps, pairs, head,
    x_ref, small_ref, bct_ref, dcol_ref, drow_ref, w_ref, b_ref, sb_ref, rate_ref, skip_ref,
    y_ref, states_ref,
    state, ext, docs_ext, xs, xt, last_doc,
):
    c = pl.program_id(0)
    n = bct_ref.shape[0] // 2

    @pl.when(c == 0)
    def _():
        state[...] = jnp.zeros_like(state)
        ext[pl.ds(0, HALO), :] = jnp.zeros((HALO, ext.shape[1]), f32)
        docs_ext[pl.ds(0, HALO), :] = jnp.full((HALO, LANES), -1.0, f32)
        last_doc[...] = jnp.full(last_doc.shape, -1.0, f32)

    own = dcol_ref[...]
    ext[pl.ds(HALO, q), :] = x_ref[...].astype(f32)
    docs_ext[pl.ds(HALO, q), :] = own
    step, _, cum, _, causal = step_parts(small_ref[...] + sb_ref[...], rate_ref[...], q)
    step_t = step.T
    cum_t = cum.T
    end = cum[q - 1 : q, :]
    id_in = last_doc[0:1, :]
    final = own[q - 1 : q, :]
    linked = jnp.where(final == id_in, 1.0, 0.0)
    fade = linked * jnp.exp(end)
    entering = jnp.where(own == id_in, 1.0, 0.0) * jnp.exp(cum)
    to_end = jnp.where(own == final, 1.0, 0.0) * jnp.exp(end - cum) * step
    same_doc = jnp.broadcast_to(own[:, 0:1], (q, q)) == jnp.broadcast_to(drow_ref[0:1, :], (q, q))
    hide = jnp.where(jnp.logical_and(causal, same_doc), 0.0, NEG)
    bt = bct_ref[0:n, :]
    ct = bct_ref[n : 2 * n, :]
    scores = mm(ct, bt, TN)
    states_ref[0] = state[...]
    old = state[...].astype(bf16)
    wide = lane_iota((q, LANES)) < head
    wide_row = lane_iota((1, LANES)) < head
    for k in range(pairs):
        lanes = slice(k * LANES, (k + 1) * LANES)
        h0, h1 = 2 * k, 2 * k + 1
        conv = convolve(ext, docs_ext, own, w_ref, b_ref[:, lanes], lanes, q, taps)
        x = conv * sigmoid(conv)
        xd = x * spread(step, h0, h1, wide)
        xt[:, lanes] = (x * spread(to_end, h0, h1, wide)).astype(bf16)
        mats = []
        for h in (h0, h1):
            gap = cum[:, h : h + 1] - cum_t[h : h + 1, :] + hide
            mats.append((jnp.exp(gap) * scores).astype(bf16))
        out = mm(mats[0], jnp.where(wide, xd, 0.0).astype(bf16), NN)
        out = out + mm(mats[1], jnp.where(wide, 0.0, xd).astype(bf16), NN)
        out = out + mm(ct, old[:, lanes], TN) * spread(entering, h0, h1, wide)
        y_ref[:, lanes] = out + skip_ref[:, lanes] * x
    update = mm(bt, xt[...], NN)
    for k in range(pairs):
        lanes = slice(k * LANES, (k + 1) * LANES)
        state[:, lanes] = state[:, lanes] * spread(fade, 2 * k, 2 * k + 1, wide_row) + update[:, lanes]
    ext[pl.ds(0, HALO), :] = ext[pl.ds(q, HALO), :]
    docs_ext[pl.ds(0, HALO), :] = docs_ext[pl.ds(q, HALO), :]
    last_doc[...] = jnp.broadcast_to(final, last_doc.shape)


def scan_backward(
    q, taps, pairs, head, chunks,
    x_ref, xp_ref, small_ref, bct_ref, dcol_ref, dcolp_ref, drow_ref, w_ref, b_ref, sb_ref, rate_ref,
    skip_ref, dy_ref, states_ref,
    dx_ref, dsmall_ref, dbct_ref, dconv_ref, dhead_ref,
    dstate, ext, docs_ext, dcv, docs_after, dye, xt, col_t,
):
    step_at = pl.program_id(0)
    c = chunks - 1 - step_at
    n = bct_ref.shape[0] // 2
    width = x_ref.shape[1]

    @pl.when(step_at == 0)
    def _():
        dstate[...] = jnp.zeros_like(dstate)
        dcv[pl.ds(q, HALO), :] = jnp.zeros((HALO, width), f32)
        docs_after[pl.ds(q, HALO), :] = jnp.full((HALO, LANES), -1.0, f32)
        dconv_ref[...] = jnp.zeros_like(dconv_ref)
        dhead_ref[...] = jnp.zeros_like(dhead_ref)
        col_t[...] = jnp.zeros_like(col_t)

    first = c == 0
    own = dcol_ref[...]
    before = jnp.where(first, -1.0, dcolp_ref[...])
    ext[pl.ds(0, HALO), :] = xp_ref[...].astype(f32)
    ext[pl.ds(HALO, q), :] = x_ref[...].astype(f32)
    docs_ext[pl.ds(0, HALO), :] = before
    docs_ext[pl.ds(HALO, q), :] = own
    docs_after[pl.ds(0, q), :] = own
    raw = small_ref[...] + sb_ref[...]
    rate = rate_ref[...]
    step, decay, cum, tri, causal = step_parts(raw, rate, q)
    step_t = step.T
    cum_t = cum.T
    end = cum[q - 1 : q, :]
    id_in = before[HALO - 1 : HALO, :]
    final = own[q - 1 : q, :]
    linked = jnp.where(final == id_in, 1.0, 0.0)
    fade = linked * jnp.exp(end)
    entering = jnp.where(own == id_in, 1.0, 0.0) * jnp.exp(cum)
    tail = jnp.where(own == final, 1.0, 0.0) * jnp.exp(end - cum)
    to_end = tail * step
    same_doc = jnp.broadcast_to(own[:, 0:1], (q, q)) == jnp.broadcast_to(drow_ref[0:1, :], (q, q))
    hide = jnp.where(jnp.logical_and(causal, same_doc), 0.0, NEG)
    bt = bct_ref[0:n, :]
    ct = bct_ref[n : 2 * n, :]
    scores = mm(ct, bt, TN)
    old = states_ref[0].astype(bf16)
    after = dstate[...].astype(bf16)
    wide = lane_iota((q, LANES)) < head
    wide_row = lane_iota((1, LANES)) < head
    lane = lane_iota((q, LANES))
    d_scores = jnp.zeros((q, q), f32)
    rows = jnp.zeros((q, LANES), f32)
    d_enter = jnp.zeros((q, LANES), f32)
    d_toend = jnp.zeros((q, LANES), f32)
    d_fade = jnp.zeros((8, LANES), f32)
    part = lax.broadcasted_iota(jnp.int32, (LANES, LANES), 0) // head
    to = lane_iota((LANES, LANES))
    for k in range(pairs):
        lanes = slice(k * LANES, (k + 1) * LANES)
        h0, h1 = 2 * k, 2 * k + 1
        pick = jnp.where(part + 2 * k == to, 1.0, 0.0)
        conv = convolve(ext, docs_ext, own, w_ref, b_ref[:, lanes], lanes, q, taps)
        sig = sigmoid(conv)
        x = conv * sig
        xb = x.astype(bf16)
        dy = dy_ref[:, lanes]
        halves = (jnp.where(wide, dy, 0.0).astype(bf16), jnp.where(wide, 0.0, dy).astype(bf16))
        dxd = jnp.zeros((q, LANES), f32)
        for h, half in ((h0, halves[0]), (h1, halves[1])):
            inner = mm(half, xb, NT)
            keep = jnp.exp(cum[:, h : h + 1] - cum_t[h : h + 1, :] + hide)
            grown = keep * inner
            mat = keep * scores
            dt = step_t[h : h + 1, :]
            g = grown * scores
            d_scores = d_scores + grown * dt
            rows = jnp.where(lane == h, jnp.sum(g * dt, axis=1, keepdims=True), rows)
            col_t[h : h + 1, :] = jnp.sum(g, axis=0, keepdims=True)
            dxd = dxd + mm(mat.astype(bf16), half, TN)
        v = mm(bt, after[:, lanes], TN)
        u = mm(ct, old[:, lanes], TN)
        enter_k = spread(entering, h0, h1, wide)
        end_k = spread(to_end, h0, h1, wide)
        d_enter = d_enter + exact(dy * u, pick, NN)
        d_toend = d_toend + exact(x * v, pick, NN)
        hh = jnp.sum(dstate[:, lanes] * states_ref[0, :, lanes], axis=0, keepdims=True)
        d_fade = d_fade + exact(jnp.broadcast_to(hh, (8, LANES)), pick, NN)
        dye[:, lanes] = (dy * enter_k).astype(bf16)
        xt[:, lanes] = (x * end_k).astype(bf16)
        dx = dxd * spread(step, h0, h1, wide) + end_k * v + skip_ref[:, lanes] * dy
        dconv = dx * (sig * (1.0 + conv * (1.0 - sig)))
        dcv[pl.ds(0, q), lanes] = dconv
        sums = [jnp.sum(dconv * ext[pl.ds(HALO, q), lanes], axis=0, keepdims=True)]
        dxin = w_ref[0:1, lanes] * dconv
        for lag in range(1, taps):
            same = jnp.where(docs_ext[pl.ds(HALO - lag, q), :] == own, 1.0, 0.0)
            sums.append(jnp.sum(dconv * same * ext[pl.ds(HALO - lag, q), lanes], axis=0, keepdims=True))
            follow = jnp.where(docs_after[pl.ds(lag, q), :] == own, 1.0, 0.0)
            dxin = dxin + w_ref[lag : lag + 1, lanes] * dcv[pl.ds(lag, q), lanes] * follow
        sums.append(jnp.sum(dconv, axis=0, keepdims=True))
        sums.append(jnp.sum(dy * x, axis=0, keepdims=True))
        dx_ref[:, lanes] = dxin.astype(bf16)
        for i, s in enumerate(sums):
            dconv_ref[i : i + 1, lanes] = dconv_ref[i : i + 1, lanes] + s
    dsb = d_scores.astype(bf16)
    dbct_ref[0:n, :] = mm(ct, dsb, NN) + mm(after, xt[...], NT)
    dbct_ref[n : 2 * n, :] = mm(bt, dsb, NT) + mm(old, dye[...], NT)
    new = mm(ct, dye[...], NN)
    for k in range(pairs):
        lanes = slice(k * LANES, (k + 1) * LANES)
        dstate[:, lanes] = dstate[:, lanes] * spread(fade, 2 * k, 2 * k + 1, wide_row) + new[:, lanes]
    cols = col_t[...].T
    pulled = d_toend * to_end
    at_end = jnp.sum(pulled, axis=0, keepdims=True) + fade * d_fade[0:1, :]
    d_cum = rows - step * cols + d_enter * entering - pulled
    last_row = lax.broadcasted_iota(jnp.int32, (q, LANES), 0) == q - 1
    d_cum = d_cum + jnp.where(last_row, at_end, 0.0)
    d_decay = exact(tri, d_cum, TN)
    d_step = cols + d_toend * tail - rate * d_decay
    d_raw = d_step * sigmoid(raw)
    dsmall_ref[...] = d_raw
    dhead_ref[0:1, :] = dhead_ref[0:1, :] + jnp.sum(d_raw, axis=0, keepdims=True)
    dhead_ref[1:2, :] = dhead_ref[1:2, :] + jnp.sum(d_decay * decay, axis=0, keepdims=True)
    dcv[pl.ds(q, HALO), :] = dcv[pl.ds(0, HALO), :]
    docs_after[pl.ds(q, HALO), :] = docs_after[pl.ds(0, HALO), :]


def whole(array):
    return pl.BlockSpec(array.shape, lambda c: (0,) * array.ndim)


def run_forward(q, x_in, small, bct, dcol, drow, conv_w, conv_b, sb, rate, skip, head):
    tokens, width = x_in.shape
    n = bct.shape[0] // 2
    chunks = tokens // q
    pairs = width // LANES
    taps = conv_w.shape[0]
    return pl.pallas_call(
        functools.partial(scan_forward, q, taps, pairs, head),
        grid=(chunks,),
        in_specs=[
            pl.BlockSpec((q, width), lambda c: (c, 0)),
            pl.BlockSpec((q, LANES), lambda c: (c, 0)),
            pl.BlockSpec((2 * n, q), lambda c: (0, c)),
            pl.BlockSpec((q, LANES), lambda c: (c, 0)),
            pl.BlockSpec((8, q), lambda c: (0, c)),
            whole(conv_w), whole(conv_b), whole(sb), whole(rate), whole(skip),
        ],
        out_specs=[
            pl.BlockSpec((q, width), lambda c: (c, 0)),
            pl.BlockSpec((1, n, width), lambda c: (c, 0, 0)),
        ],
        out_shape=[
            jax.ShapeDtypeStruct((tokens, width), f32),
            jax.ShapeDtypeStruct((chunks, n, width), f32),
        ],
        scratch_shapes=[
            pltpu.VMEM((n, width), f32),
            pltpu.VMEM((HALO + q, width), f32),
            pltpu.VMEM((HALO + q, LANES), f32),
            pltpu.VMEM((8, LANES), f32),
            pltpu.VMEM((q, width), bf16),
            pltpu.VMEM((8, LANES), f32),
        ],
        name="scan_forward",
    )(x_in, small, bct, dcol, drow, conv_w, conv_b, sb, rate, skip)


def run_backward(q, x_in, small, bct, dcol, drow, conv_w, conv_b, sb, rate, skip, dy, states, head):
    tokens, width = x_in.shape
    n = bct.shape[0] // 2
    chunks = tokens // q
    pairs = width // LANES
    taps = conv_w.shape[0]
    per = q // HALO

    def at(c):
        return chunks - 1 - c

    def prior(c):
        return jnp.maximum((chunks - 1 - c) * per - 1, 0)

    return pl.pallas_call(
        functools.partial(scan_backward, q, taps, pairs, head, chunks),
        grid=(chunks,),
        in_specs=[
            pl.BlockSpec((q, width), lambda c: (at(c), 0)),
            pl.BlockSpec((HALO, width), lambda c: (prior(c), 0)),
            pl.BlockSpec((q, LANES), lambda c: (at(c), 0)),
            pl.BlockSpec((2 * n, q), lambda c: (0, at(c))),
            pl.BlockSpec((q, LANES), lambda c: (at(c), 0)),
            pl.BlockSpec((HALO, LANES), lambda c: (prior(c), 0)),
            pl.BlockSpec((8, q), lambda c: (0, at(c))),
            whole(conv_w), whole(conv_b), whole(sb), whole(rate), whole(skip),
            pl.BlockSpec((q, width), lambda c: (at(c), 0)),
            pl.BlockSpec((1, n, width), lambda c: (at(c), 0, 0)),
        ],
        out_specs=[
            pl.BlockSpec((q, width), lambda c: (at(c), 0)),
            pl.BlockSpec((q, LANES), lambda c: (at(c), 0)),
            pl.BlockSpec((2 * n, q), lambda c: (0, at(c))),
            pl.BlockSpec((8, width), lambda c: (0, 0)),
            pl.BlockSpec((8, LANES), lambda c: (0, 0)),
        ],
        out_shape=[
            jax.ShapeDtypeStruct((tokens, width), bf16),
            jax.ShapeDtypeStruct((tokens, LANES), f32),
            jax.ShapeDtypeStruct((2 * n, tokens), f32),
            jax.ShapeDtypeStruct((8, width), f32),
            jax.ShapeDtypeStruct((8, LANES), f32),
        ],
        scratch_shapes=[
            pltpu.VMEM((n, width), f32),
            pltpu.VMEM((HALO + q, width), f32),
            pltpu.VMEM((HALO + q, LANES), f32),
            pltpu.VMEM((q + HALO, width), f32),
            pltpu.VMEM((q + HALO, LANES), f32),
            pltpu.VMEM((q, width), bf16),
            pltpu.VMEM((q, width), bf16),
            pltpu.VMEM((LANES, q), f32),
        ],
        name="scan_backward",
    )(x_in, x_in, small, bct, dcol, dcol, drow, conv_w, conv_b, sb, rate, skip, dy, states)


def swapped(block, bit):
    size = lax.axis_size("seq")
    return lax.ppermute(block, "seq", [(i, i ^ bit) for i in range(size)])


def bits_of(size):
    bits, bit = [], 1
    while bit < size:
        bits.append(bit)
        bit *= 2
    return bits


def gathered(block):
    index = lax.axis_index("seq")
    for bit in bits_of(lax.axis_size("seq")):
        other = swapped(block, bit)
        upper = (index & bit) != 0
        block = jnp.where(
            upper, jnp.concatenate([other, block], axis=0), jnp.concatenate([block, other], axis=0)
        )
    return block


def scattered(parts):
    index = lax.axis_index("seq")
    size = lax.axis_size("seq")
    rest = parts.shape[1:]
    lead = parts.shape[0]
    held = parts.reshape((size, lead // size) + rest)
    for bit in bits_of(size):
        half = held.reshape((held.shape[0] // 2, 2) + held.shape[1:])
        upper = (index & bit) != 0
        mine = jnp.where(upper, half[:, 1], half[:, 0])
        theirs = jnp.where(upper, half[:, 0], half[:, 1]).astype(bf16)
        held = mine.astype(f32) + swapped(theirs, bit).astype(f32)
    return held[0]


def summed(block):
    count = lax.axis_size("dp")
    for bit in bits_of(count):
        block = block + lax.ppermute(block, "dp", [(i, i ^ bit) for i in range(count)])
    return block


def folded(rows, lead, width):
    cut = rows.reshape(lead, rows.shape[0] // lead, rows.shape[1] // width, width)
    cut = cut.transpose(0, 2, 1, 3).reshape(lead, -1, width)
    return cut[0] if lead == 1 else cut


def unfolded(pieces, width):
    lead, stacked, narrow = pieces.shape
    cut = pieces.reshape(lead, width // narrow, stacked * narrow // width, narrow)
    return cut.transpose(0, 2, 1, 3).reshape(-1, width)


def padded(rows, width):
    return jnp.pad(rows, ((0, 0), (0, width - rows.shape[1])))


def shards(
    hidden, segments, cotangent, norm_gain, in_weight, conv_weight, conv_bias, step_bias, log_rate,
    skip_gain, gate_gain, out_weight,
):
    n_seqs, block, n_width = hidden.shape
    size = lax.axis_size("seq")
    groups = lax.axis_size("dp")
    index = lax.axis_index("seq")
    tokens = size * block
    n_inner = gate_gain.shape[0]
    n_heads = step_bias.shape[0]
    n_taps = conv_weight.shape[0]
    n_mixed = conv_bias.shape[0]
    n_state = (n_mixed - n_inner) // 2
    head = n_inner // n_heads
    own_inner = n_inner // size
    own_heads = n_heads // size
    own_bc = 2 * n_state // size
    q = min(128, block)
    in_rows = in_weight.shape[0]

    in_low = in_weight.astype(bf16)
    z_cols = in_low[:, :n_inner].reshape(in_rows, size, own_inner)
    x_cols = in_low[:, n_inner : 2 * n_inner].reshape(in_rows, size, own_inner)
    bc_cols = in_low[:, 2 * n_inner : n_inner + n_mixed].reshape(in_rows, size, own_bc)
    dt_cols = in_low[:, n_inner + n_mixed :].reshape(in_rows, size, own_heads)
    gap = jnp.zeros((in_rows, size, LANES - own_heads - own_bc), bf16)
    laid = jnp.concatenate([x_cols, dt_cols, gap, bc_cols, z_cols], axis=2).transpose(1, 0, 2)
    mine = lax.all_to_all(laid, "seq", 0, 0, tiled=True)
    mine = mine.reshape(size * in_rows, -1)
    n_first = own_inner + LANES
    w_first = lax.all_gather(mine[:, :n_first], "dp", axis=0, tiled=True)
    order = [(f, (f % groups) * size + f // groups) for f in range(groups * size)]
    back = [(b, a) for a, b in order]
    out_moved = lax.ppermute(out_weight.astype(bf16), ("dp", "seq"), order)
    z_block = jnp.concatenate([mine[:, n_first:], folded(out_moved, 1, own_inner)], axis=0)

    flat = hidden.reshape(block, n_width).astype(f32)
    inv = lax.rsqrt(jnp.mean(flat * flat, axis=-1, keepdims=True) + epsilon)
    unit = flat * inv
    normed = gathered((unit * norm_gain).astype(bf16))
    normed, z_block = lax.optimization_barrier((normed, z_block))
    joined = lax.all_gather(z_block, "dp", axis=0, tiled=True).reshape(groups, -1, own_inner)
    z_rows = size * in_rows
    w_z = joined[:, :z_rows].reshape(-1, own_inner)
    w_out = unfolded(joined[:, z_rows:], n_width)
    cot_own = cotangent.reshape(block, n_width)
    cot = gathered(cot_own)
    docs = lax.all_gather(segments.reshape(block), "seq", axis=0, tiled=True).astype(f32)
    dcol = jnp.broadcast_to(docs[:, None], (tokens, LANES))
    drow = jnp.broadcast_to(docs[None, :], (8, tokens))

    def own_part(vector, parts):
        return lax.dynamic_slice_in_dim(vector, index * parts, parts, vector.ndim - 1)

    w_x, w_small = w_first[:, :own_inner], w_first[:, own_inner:]
    small = mm(normed, w_small, NN)
    x_in = mm(normed, w_x, NN).astype(bf16)
    z = mm(normed, w_z, NN)
    conv_x = own_part(conv_weight[:, :n_inner], own_inner)
    bias_x = own_part(conv_bias[None, :n_inner], own_inner)
    conv_bc = own_part(conv_weight[:, n_inner:], own_bc)
    bias_bc = own_part(conv_bias[None, n_inner:], own_bc)
    sb = padded(own_part(step_bias[None], own_heads), LANES)
    rate = padded(jnp.exp(own_part(log_rate[None], own_heads)), LANES)
    skip = jnp.repeat(own_part(skip_gain[None], own_heads), head, axis=1)
    gain = own_part(gate_gain[None], own_inner)

    head_lanes = jnp.arange(LANES) < own_heads
    bc_in = small[:, LANES - own_bc :].astype(bf16).astype(f32)
    small_dt = jnp.where(head_lanes, small, 0.0)

    def earlier(rows, lag):
        return jnp.pad(rows, ((lag, 0), (0, 0)))[:tokens]

    def later(rows, lag):
        return jnp.pad(rows, ((0, lag), (0, 0)))[lag:]

    same = [None] + [
        jnp.where(jnp.pad(docs, (lag, 0), constant_values=-1.0)[:tokens] == docs, 1.0, 0.0)[:, None]
        for lag in range(1, n_taps)
    ]
    bc_conv = bias_bc + conv_bc[0:1] * bc_in
    for lag in range(1, n_taps):
        bc_conv = bc_conv + conv_bc[lag : lag + 1] * earlier(bc_in, lag) * same[lag]
    bc_sig = jax.nn.sigmoid(bc_conv)
    bct = lax.all_gather((bc_conv * bc_sig).astype(bf16).T, "seq", axis=0, tiled=True)

    y, states = run_forward(
        q, x_in, small_dt, bct, dcol, drow, conv_x, bias_x, sb, rate, skip, head
    )

    d_gn = mm(cot, w_out, NT)
    z_sig = jax.nn.sigmoid(z)
    z_act = z * z_sig
    gated = y * z_act
    scaled = d_gn * gain
    both = jnp.stack([jnp.sum(gated * gated, axis=1), jnp.sum(scaled * gated, axis=1)])
    both = lax.psum(both, "seq")
    g_inv = lax.rsqrt(both[0] / n_inner + epsilon)[:, None]
    g_dot = both[1][:, None] / n_inner
    gate_low = (gated * g_inv * gain).astype(bf16)
    d_gated = g_inv * scaled - gated * (g_inv * g_inv * g_inv * g_dot)
    d_gain = jnp.sum(d_gn * gated * g_inv, axis=0)
    d_z = (d_gated * y * (z_sig * (1.0 + z * (1.0 - z_sig)))).astype(bf16)
    d_y = d_gated * z_act

    branch = scattered(mm(gate_low, w_out, NN).astype(bf16))
    result = (flat + branch).reshape(n_seqs, block, n_width).astype(bf16)
    out_term = mm(gate_low, cot, TN).astype(bf16)
    z_term = mm(normed, d_z, TN).astype(bf16).reshape(groups, z_rows, own_inner)
    terms = jnp.concatenate([z_term, folded(out_term, groups, own_inner)], axis=1)
    terms, d_y = lax.optimization_barrier((terms.reshape(-1, own_inner), d_y))
    parts = lax.psum_scatter(terms, "dp", scatter_dimension=0, tiled=True)
    z_part = parts[:z_rows]
    out_part = unfolded(parts[None, z_rows:], n_width)
    d_out_weight = lax.ppermute(out_part, ("dp", "seq"), back).astype(f32)

    d_x, d_dt, d_bct, d_conv_x, d_heads = run_backward(
        q, x_in, small_dt, bct, dcol, drow, conv_x, bias_x, sb, rate, skip, d_y, states, head
    )
    d_bc = scattered(d_bct).T
    d_bcc = d_bc * (bc_sig * (1.0 + bc_conv * (1.0 - bc_sig)))
    d_bc_in = conv_bc[0:1] * d_bcc
    w_sums = [jnp.sum(d_bcc * bc_in, axis=0)]
    for lag in range(1, n_taps):
        held = d_bcc * same[lag]
        d_bc_in = d_bc_in + conv_bc[lag : lag + 1] * later(held, lag)
        w_sums.append(jnp.sum(held * earlier(bc_in, lag), axis=0))
    w_sums.append(jnp.sum(d_bcc, axis=0))
    d_small = jnp.concatenate([d_dt[:, : LANES - own_bc], d_bc_in], axis=1).astype(bf16)
    d_first = jnp.concatenate([d_x, d_small], axis=1)
    first_term = mm(normed, d_first, TN).astype(bf16)
    first_part = lax.psum_scatter(first_term, "dp", scatter_dimension=0, tiled=True)
    d_normed = mm(d_first, w_first, NT) + mm(d_z, w_z, NT)
    d_norm = scattered(d_normed.astype(bf16))

    term = jnp.concatenate([first_part, z_part], axis=1).reshape(size, in_rows, -1)
    moved = lax.all_to_all(term, "seq", 0, 0, tiled=True).transpose(1, 0, 2).astype(f32)
    d_in_weight = jnp.concatenate(
        [
            moved[:, :, n_first:].reshape(in_rows, n_inner),
            moved[:, :, :own_inner].reshape(in_rows, n_inner),
            moved[:, :, n_first - own_bc : n_first].reshape(in_rows, 2 * n_state),
            moved[:, :, own_inner : own_inner + own_heads].reshape(in_rows, n_heads),
        ],
        axis=1,
    )

    d_norm_gain = jnp.sum(d_norm * unit, axis=0)
    lifted = d_norm * norm_gain
    d_flat = inv * lifted - flat * (
        inv * inv * inv * jnp.mean(lifted * flat, axis=-1, keepdims=True)
    )
    d_hidden = (cot_own.astype(f32) + d_flat).reshape(n_seqs, block, n_width)

    d_skip = jnp.sum(d_conv_x[n_taps + 1].reshape(own_heads, head), axis=1)
    packed = jnp.concatenate(
        [
            d_conv_x[: n_taps + 1].reshape(-1),
            jnp.stack(w_sums).reshape(-1),
            d_gain,
            d_heads[0, :own_heads],
            d_heads[1, :own_heads],
            d_skip,
            d_norm_gain,
        ]
    )
    packed = gathered(summed(packed)[None])
    at = 0

    def take(count):
        nonlocal at
        at += count
        return packed[:, at - count : at]

    got_x = take((n_taps + 1) * own_inner).reshape(size, n_taps + 1, own_inner)
    got_bc = take((n_taps + 1) * own_bc).reshape(size, n_taps + 1, own_bc)
    got_x = got_x.transpose(1, 0, 2).reshape(n_taps + 1, n_inner)
    got_bc = got_bc.transpose(1, 0, 2).reshape(n_taps + 1, 2 * n_state)
    conv_all = jnp.concatenate([got_x, got_bc], axis=1)
    d_gate_gain = take(own_inner).reshape(n_inner)
    d_step_bias = take(own_heads).reshape(n_heads)
    d_log_rate = take(own_heads).reshape(n_heads)
    d_skip_gain = take(own_heads).reshape(n_heads)
    d_norm_all = jnp.sum(take(n_width), axis=0)
    return (
        result,
        d_hidden,
        d_norm_all,
        d_in_weight,
        conv_all[:n_taps],
        conv_all[n_taps],
        d_step_bias,
        d_log_rate,
        d_skip_gain,
        d_gate_gain,
        d_out_weight,
    )


def solution(mesh):
    tokens = P("dp", "seq", None)
    rows = P(("dp", "seq"), None)
    return jax.shard_map(
        shards,
        mesh=mesh,
        in_specs=(tokens, P("dp", "seq"), tokens, P(), rows, P(), P(), P(), P(), P(), P(), rows),
        out_specs=(tokens, tokens, P(), rows, P(), P(), P(), P(), P(), P(), rows),
        check_vma=False,
    )
```

```python
import functools

import jax
import jax.numpy as jnp
from jax import lax
from jax.experimental import pallas as pl
from jax.experimental.pallas import tpu as pltpu
from jax.sharding import PartitionSpec as P

epsilon = 1e-05
highest = lax.Precision.HIGHEST
f32 = jnp.float32
bf16 = jnp.bfloat16
LANES = 128
HALO = 16
NEG = -1e30


def mm(a, b, dims, out=f32):
    return lax.dot_general(a, b, (dims, ((), ())), preferred_element_type=out)


NN = ((1,), (0,))
NT = ((1,), (1,))
TN = ((0,), (0,))


def exact(a, b, dims):
    return lax.dot_general(a, b, (dims, ((), ())), precision=highest, preferred_element_type=f32)


def softplus(v):
    return jnp.maximum(v, 0.0) + jnp.log1p(jnp.exp(-jnp.abs(v)))


def sigmoid(v):
    return 1.0 / (1.0 + jnp.exp(-v))


def lane_iota(shape):
    return lax.broadcasted_iota(jnp.int32, shape, len(shape) - 1)


def spread(columns, first, second, wide):
    rows = columns.shape[0]
    left = jnp.broadcast_to(columns[:, first : first + 1], (rows, LANES))
    right = jnp.broadcast_to(columns[:, second : second + 1], (rows, LANES))
    return jnp.where(wide, left, right)


def step_parts(raw, rate, q):
    row = lax.broadcasted_iota(jnp.int32, (q, q), 0)
    col = lax.broadcasted_iota(jnp.int32, (q, q), 1)
    tri = jnp.where(row >= col, 1.0, 0.0).astype(f32)
    step = softplus(raw)
    decay = -step * rate
    total = exact(tri, decay, NN)
    return step, decay, total, tri, row >= col


def convolve(ext, docs_ext, own, weights, bias, lanes, q, taps):
    running = bias + weights[0:1, lanes] * ext[pl.ds(HALO, q), lanes]
    for lag in range(1, taps):
        same = jnp.where(docs_ext[pl.ds(HALO - lag, q), :] == own, 1.0, 0.0)
        running = running + weights[lag : lag + 1, lanes] * ext[pl.ds(HALO - lag, q), lanes] * same
    return running


def scan_forward(
    q, taps, pairs, head,
    x_ref, small_ref, bct_ref, dcol_ref, drow_ref, w_ref, b_ref, sb_ref, rate_ref, skip_ref,
    y_ref, states_ref,
    state, ext, docs_ext, xs, xt, last_doc,
):
    c = pl.program_id(0)
    n = bct_ref.shape[0] // 2

    @pl.when(c == 0)
    def _():
        state[...] = jnp.zeros_like(state)
        ext[pl.ds(0, HALO), :] = jnp.zeros((HALO, ext.shape[1]), f32)
        docs_ext[pl.ds(0, HALO), :] = jnp.full((HALO, LANES), -1.0, f32)
        last_doc[...] = jnp.full(last_doc.shape, -1.0, f32)

    own = dcol_ref[...]
    ext[pl.ds(HALO, q), :] = x_ref[...].astype(f32)
    docs_ext[pl.ds(HALO, q), :] = own
    step, _, cum, _, causal = step_parts(small_ref[...] + sb_ref[...], rate_ref[...], q)
    step_t = step.T
    cum_t = cum.T
    end = cum[q - 1 : q, :]
    id_in = last_doc[0:1, :]
    final = own[q - 1 : q, :]
    linked = jnp.where(final == id_in, 1.0, 0.0)
    fade = linked * jnp.exp(end)
    entering = jnp.where(own == id_in, 1.0, 0.0) * jnp.exp(cum)
    to_end = jnp.where(own == final, 1.0, 0.0) * jnp.exp(end - cum) * step
    same_doc = jnp.broadcast_to(own[:, 0:1], (q, q)) == jnp.broadcast_to(drow_ref[0:1, :], (q, q))
    hide = jnp.where(jnp.logical_and(causal, same_doc), 0.0, NEG)
    bt = bct_ref[0:n, :]
    ct = bct_ref[n : 2 * n, :]
    scores = mm(ct, bt, TN)
    states_ref[0] = state[...]
    old = state[...].astype(bf16)
    wide = lane_iota((q, LANES)) < head
    wide_row = lane_iota((1, LANES)) < head
    for k in range(pairs):
        lanes = slice(k * LANES, (k + 1) * LANES)
        h0, h1 = 2 * k, 2 * k + 1
        conv = convolve(ext, docs_ext, own, w_ref, b_ref[:, lanes], lanes, q, taps)
        x = conv * sigmoid(conv)
        xd = x * spread(step, h0, h1, wide)
        xt[:, lanes] = (x * spread(to_end, h0, h1, wide)).astype(bf16)
        mats = []
        for h in (h0, h1):
            gap = cum[:, h : h + 1] - cum_t[h : h + 1, :] + hide
            mats.append((jnp.exp(gap) * scores).astype(bf16))
        out = mm(mats[0], jnp.where(wide, xd, 0.0).astype(bf16), NN)
        out = out + mm(mats[1], jnp.where(wide, 0.0, xd).astype(bf16), NN)
        out = out + mm(ct, old[:, lanes], TN) * spread(entering, h0, h1, wide)
        y_ref[:, lanes] = out + skip_ref[:, lanes] * x
    update = mm(bt, xt[...], NN)
    for k in range(pairs):
        lanes = slice(k * LANES, (k + 1) * LANES)
        state[:, lanes] = state[:, lanes] * spread(fade, 2 * k, 2 * k + 1, wide_row) + update[:, lanes]
    ext[pl.ds(0, HALO), :] = ext[pl.ds(q, HALO), :]
    docs_ext[pl.ds(0, HALO), :] = docs_ext[pl.ds(q, HALO), :]
    last_doc[...] = jnp.broadcast_to(final, last_doc.shape)


def scan_backward(
    q, taps, pairs, head, chunks,
    x_ref, xp_ref, small_ref, bct_ref, dcol_ref, dcolp_ref, drow_ref, w_ref, b_ref, sb_ref, rate_ref,
    skip_ref, dy_ref, states_ref,
    dx_ref, dsmall_ref, dbct_ref, dconv_ref, dhead_ref,
    dstate, ext, docs_ext, dcv, docs_after, dye, xt, col_t,
):
    step_at = pl.program_id(0)
    c = chunks - 1 - step_at
    n = bct_ref.shape[0] // 2
    width = x_ref.shape[1]

    @pl.when(step_at == 0)
    def _():
        dstate[...] = jnp.zeros_like(dstate)
        dcv[pl.ds(q, HALO), :] = jnp.zeros((HALO, width), f32)
        docs_after[pl.ds(q, HALO), :] = jnp.full((HALO, LANES), -1.0, f32)
        dconv_ref[...] = jnp.zeros_like(dconv_ref)
        dhead_ref[...] = jnp.zeros_like(dhead_ref)
        col_t[...] = jnp.zeros_like(col_t)

    first = c == 0
    own = dcol_ref[...]
    before = jnp.where(first, -1.0, dcolp_ref[...])
    ext[pl.ds(0, HALO), :] = xp_ref[...].astype(f32)
    ext[pl.ds(HALO, q), :] = x_ref[...].astype(f32)
    docs_ext[pl.ds(0, HALO), :] = before
    docs_ext[pl.ds(HALO, q), :] = own
    docs_after[pl.ds(0, q), :] = own
    raw = small_ref[...] + sb_ref[...]
    rate = rate_ref[...]
    step, decay, cum, tri, causal = step_parts(raw, rate, q)
    step_t = step.T
    cum_t = cum.T
    end = cum[q - 1 : q, :]
    id_in = before[HALO - 1 : HALO, :]
    final = own[q - 1 : q, :]
    linked = jnp.where(final == id_in, 1.0, 0.0)
    fade = linked * jnp.exp(end)
    entering = jnp.where(own == id_in, 1.0, 0.0) * jnp.exp(cum)
    tail = jnp.where(own == final, 1.0, 0.0) * jnp.exp(end - cum)
    to_end = tail * step
    same_doc = jnp.broadcast_to(own[:, 0:1], (q, q)) == jnp.broadcast_to(drow_ref[0:1, :], (q, q))
    hide = jnp.where(jnp.logical_and(causal, same_doc), 0.0, NEG)
    bt = bct_ref[0:n, :]
    ct = bct_ref[n : 2 * n, :]
    scores = mm(ct, bt, TN)
    old = states_ref[0].astype(bf16)
    after = dstate[...].astype(bf16)
    wide = lane_iota((q, LANES)) < head
    wide_row = lane_iota((1, LANES)) < head
    lane = lane_iota((q, LANES))
    d_scores = jnp.zeros((q, q), f32)
    rows = jnp.zeros((q, LANES), f32)
    d_enter = jnp.zeros((q, LANES), f32)
    d_toend = jnp.zeros((q, LANES), f32)
    d_fade = jnp.zeros((8, LANES), f32)
    part = lax.broadcasted_iota(jnp.int32, (LANES, LANES), 0) // head
    to = lane_iota((LANES, LANES))
    for k in range(pairs):
        lanes = slice(k * LANES, (k + 1) * LANES)
        h0, h1 = 2 * k, 2 * k + 1
        pick = jnp.where(part + 2 * k == to, 1.0, 0.0)
        conv = convolve(ext, docs_ext, own, w_ref, b_ref[:, lanes], lanes, q, taps)
        sig = sigmoid(conv)
        x = conv * sig
        xb = x.astype(bf16)
        dy = dy_ref[:, lanes]
        halves = (jnp.where(wide, dy, 0.0).astype(bf16), jnp.where(wide, 0.0, dy).astype(bf16))
        dxd = jnp.zeros((q, LANES), f32)
        for h, half in ((h0, halves[0]), (h1, halves[1])):
            inner = mm(half, xb, NT)
            keep = jnp.exp(cum[:, h : h + 1] - cum_t[h : h + 1, :] + hide)
            grown = keep * inner
            mat = keep * scores
            dt = step_t[h : h + 1, :]
            g = grown * scores
            d_scores = d_scores + grown * dt
            rows = jnp.where(lane == h, jnp.sum(g * dt, axis=1, keepdims=True), rows)
            col_t[h : h + 1, :] = jnp.sum(g, axis=0, keepdims=True)
            dxd = dxd + mm(mat.astype(bf16), half, TN)
        v = mm(bt, after[:, lanes], TN)
        u = mm(ct, old[:, lanes], TN)
        enter_k = spread(entering, h0, h1, wide)
        end_k = spread(to_end, h0, h1, wide)
        d_enter = d_enter + exact(dy * u, pick, NN)
        d_toend = d_toend + exact(x * v, pick, NN)
        hh = jnp.sum(dstate[:, lanes] * states_ref[0, :, lanes], axis=0, keepdims=True)
        d_fade = d_fade + exact(jnp.broadcast_to(hh, (8, LANES)), pick, NN)
        dye[:, lanes] = (dy * enter_k).astype(bf16)
        xt[:, lanes] = (x * end_k).astype(bf16)
        dx = dxd * spread(step, h0, h1, wide) + end_k * v + skip_ref[:, lanes] * dy
        dconv = dx * (sig * (1.0 + conv * (1.0 - sig)))
        dcv[pl.ds(0, q), lanes] = dconv
        sums = [jnp.sum(dconv * ext[pl.ds(HALO, q), lanes], axis=0, keepdims=True)]
        dxin = w_ref[0:1, lanes] * dconv
        for lag in range(1, taps):
            same = jnp.where(docs_ext[pl.ds(HALO - lag, q), :] == own, 1.0, 0.0)
            sums.append(jnp.sum(dconv * same * ext[pl.ds(HALO - lag, q), lanes], axis=0, keepdims=True))
            follow = jnp.where(docs_after[pl.ds(lag, q), :] == own, 1.0, 0.0)
            dxin = dxin + w_ref[lag : lag + 1, lanes] * dcv[pl.ds(lag, q), lanes] * follow
        sums.append(jnp.sum(dconv, axis=0, keepdims=True))
        sums.append(jnp.sum(dy * x, axis=0, keepdims=True))
        dx_ref[:, lanes] = dxin.astype(bf16)
        for i, s in enumerate(sums):
            dconv_ref[i : i + 1, lanes] = dconv_ref[i : i + 1, lanes] + s
    dsb = d_scores.astype(bf16)
    dbct_ref[0:n, :] = mm(ct, dsb, NN) + mm(after, xt[...], NT)
    dbct_ref[n : 2 * n, :] = mm(bt, dsb, NT) + mm(old, dye[...], NT)
    new = mm(ct, dye[...], NN)
    for k in range(pairs):
        lanes = slice(k * LANES, (k + 1) * LANES)
        dstate[:, lanes] = dstate[:, lanes] * spread(fade, 2 * k, 2 * k + 1, wide_row) + new[:, lanes]
    cols = col_t[...].T
    pulled = d_toend * to_end
    at_end = jnp.sum(pulled, axis=0, keepdims=True) + fade * d_fade[0:1, :]
    d_cum = rows - step * cols + d_enter * entering - pulled
    last_row = lax.broadcasted_iota(jnp.int32, (q, LANES), 0) == q - 1
    d_cum = d_cum + jnp.where(last_row, at_end, 0.0)
    d_decay = exact(tri, d_cum, TN)
    d_step = cols + d_toend * tail - rate * d_decay
    d_raw = d_step * sigmoid(raw)
    dsmall_ref[...] = d_raw
    dhead_ref[0:1, :] = dhead_ref[0:1, :] + jnp.sum(d_raw, axis=0, keepdims=True)
    dhead_ref[1:2, :] = dhead_ref[1:2, :] + jnp.sum(d_decay * decay, axis=0, keepdims=True)
    dcv[pl.ds(q, HALO), :] = dcv[pl.ds(0, HALO), :]
    docs_after[pl.ds(q, HALO), :] = docs_after[pl.ds(0, HALO), :]


def whole(array):
    return pl.BlockSpec(array.shape, lambda c: (0,) * array.ndim)


def run_forward(q, x_in, small, bct, dcol, drow, conv_w, conv_b, sb, rate, skip, head):
    tokens, width = x_in.shape
    n = bct.shape[0] // 2
    chunks = tokens // q
    pairs = width // LANES
    taps = conv_w.shape[0]
    return pl.pallas_call(
        functools.partial(scan_forward, q, taps, pairs, head),
        grid=(chunks,),
        in_specs=[
            pl.BlockSpec((q, width), lambda c: (c, 0)),
            pl.BlockSpec((q, LANES), lambda c: (c, 0)),
            pl.BlockSpec((2 * n, q), lambda c: (0, c)),
            pl.BlockSpec((q, LANES), lambda c: (c, 0)),
            pl.BlockSpec((8, q), lambda c: (0, c)),
            whole(conv_w), whole(conv_b), whole(sb), whole(rate), whole(skip),
        ],
        out_specs=[
            pl.BlockSpec((q, width), lambda c: (c, 0)),
            pl.BlockSpec((1, n, width), lambda c: (c, 0, 0)),
        ],
        out_shape=[
            jax.ShapeDtypeStruct((tokens, width), f32),
            jax.ShapeDtypeStruct((chunks, n, width), f32),
        ],
        scratch_shapes=[
            pltpu.VMEM((n, width), f32),
            pltpu.VMEM((HALO + q, width), f32),
            pltpu.VMEM((HALO + q, LANES), f32),
            pltpu.VMEM((8, LANES), f32),
            pltpu.VMEM((q, width), bf16),
            pltpu.VMEM((8, LANES), f32),
        ],
        name="scan_forward",
    )(x_in, small, bct, dcol, drow, conv_w, conv_b, sb, rate, skip)


def run_backward(q, x_in, small, bct, dcol, drow, conv_w, conv_b, sb, rate, skip, dy, states, head):
    tokens, width = x_in.shape
    n = bct.shape[0] // 2
    chunks = tokens // q
    pairs = width // LANES
    taps = conv_w.shape[0]
    per = q // HALO

    def at(c):
        return chunks - 1 - c

    def prior(c):
        return jnp.maximum((chunks - 1 - c) * per - 1, 0)

    return pl.pallas_call(
        functools.partial(scan_backward, q, taps, pairs, head, chunks),
        grid=(chunks,),
        in_specs=[
            pl.BlockSpec((q, width), lambda c: (at(c), 0)),
            pl.BlockSpec((HALO, width), lambda c: (prior(c), 0)),
            pl.BlockSpec((q, LANES), lambda c: (at(c), 0)),
            pl.BlockSpec((2 * n, q), lambda c: (0, at(c))),
            pl.BlockSpec((q, LANES), lambda c: (at(c), 0)),
            pl.BlockSpec((HALO, LANES), lambda c: (prior(c), 0)),
            pl.BlockSpec((8, q), lambda c: (0, at(c))),
            whole(conv_w), whole(conv_b), whole(sb), whole(rate), whole(skip),
            pl.BlockSpec((q, width), lambda c: (at(c), 0)),
            pl.BlockSpec((1, n, width), lambda c: (at(c), 0, 0)),
        ],
        out_specs=[
            pl.BlockSpec((q, width), lambda c: (at(c), 0)),
            pl.BlockSpec((q, LANES), lambda c: (at(c), 0)),
            pl.BlockSpec((2 * n, q), lambda c: (0, at(c))),
            pl.BlockSpec((8, width), lambda c: (0, 0)),
            pl.BlockSpec((8, LANES), lambda c: (0, 0)),
        ],
        out_shape=[
            jax.ShapeDtypeStruct((tokens, width), bf16),
            jax.ShapeDtypeStruct((tokens, LANES), f32),
            jax.ShapeDtypeStruct((2 * n, tokens), f32),
            jax.ShapeDtypeStruct((8, width), f32),
            jax.ShapeDtypeStruct((8, LANES), f32),
        ],
        scratch_shapes=[
            pltpu.VMEM((n, width), f32),
            pltpu.VMEM((HALO + q, width), f32),
            pltpu.VMEM((HALO + q, LANES), f32),
            pltpu.VMEM((q + HALO, width), f32),
            pltpu.VMEM((q + HALO, LANES), f32),
            pltpu.VMEM((q, width), bf16),
            pltpu.VMEM((q, width), bf16),
            pltpu.VMEM((LANES, q), f32),
        ],
        name="scan_backward",
    )(x_in, x_in, small, bct, dcol, dcol, drow, conv_w, conv_b, sb, rate, skip, dy, states)


def swapped(block, bit):
    size = lax.axis_size("seq")
    return lax.ppermute(block, "seq", [(i, i ^ bit) for i in range(size)])


def bits_of(size):
    bits, bit = [], 1
    while bit < size:
        bits.append(bit)
        bit *= 2
    return bits


def gathered(block):
    index = lax.axis_index("seq")
    block = block[None]
    for bit in reversed(bits_of(lax.axis_size("seq"))):
        other = swapped(block, bit)
        upper = (index & bit) != 0
        block = jnp.where(
            upper, jnp.stack([other, block], axis=1), jnp.stack([block, other], axis=1)
        )
        block = block.reshape((-1,) + block.shape[2:])
    return block.reshape((-1,) + block.shape[2:])


def scattered(parts, between=lambda held: held):
    index = lax.axis_index("seq")
    size = lax.axis_size("seq")
    rest = parts.shape[1:]
    lead = parts.shape[0]
    held = parts.reshape((size, lead // size) + rest)
    for bit in bits_of(size):
        half = held.reshape((held.shape[0] // 2, 2) + held.shape[1:])
        upper = (index & bit) != 0
        mine = jnp.where(upper, half[:, 1], half[:, 0])
        theirs = jnp.where(upper, half[:, 0], half[:, 1]).astype(bf16)
        held = between(mine.astype(f32) + swapped(theirs, bit).astype(f32))
    return held[0]


def summed(block):
    count = lax.axis_size("dp")
    for bit in bits_of(count):
        block = block + lax.ppermute(block, "dp", [(i, i ^ bit) for i in range(count)])
    return block


def moved_by(block, step):
    count = lax.axis_size("dp")
    route = [(i, i + 2 * step) for i in range(count) if 0 <= i + 2 * step < count]
    return lax.ppermute(block, "dp", route)


def crossed(block, bits):
    return lax.ppermute(block, "dp", [(i, i ^ bits) for i in range(lax.axis_size("dp"))])


def gathered_rows(block):
    count = lax.axis_size("dp")
    length = count // 2
    if not is_small(count):
        return lax.all_gather(block, "dp", axis=0, tiled=True)
    at = lax.axis_index("dp")
    place, side = at // 2, at % 2
    rows = block.shape[0]
    whole_rows = jnp.zeros((count * rows, block.shape[1]), block.dtype)

    def put(into, piece, pair, half):
        return lax.dynamic_update_slice(into, piece, ((pair * 2 + half) * rows, 0))

    whole_rows = put(whole_rows, block, place, side)
    whole_rows = put(whole_rows, crossed(block, 1), place, 1 - side)
    up, down, ready = block, block, []
    both = jnp.minimum(place, length - 1 - place)
    for hop in range(1, length):
        up, down = moved_by(up, 1), moved_by(down, -1)
        ready.append((down, up))
        piece, pair = None, None
        for spot in range(length):
            near = min(spot, length - 1 - spot)
            if hop <= 2 * near:
                away, from_below = (hop + 1) // 2, hop % 2 == 0
            else:
                away, from_below = hop - near, spot > length - 1 - spot
            chosen = ready[away - 1][1 if from_below else 0]
            source = spot - away if from_below else spot + away
            here = place == spot
            piece = chosen if piece is None else jnp.where(here, chosen, piece)
            pair = source if pair is None else jnp.where(here, source, pair)
        whole_rows = put(whole_rows, piece, pair, side)
        whole_rows = put(whole_rows, crossed(piece, 1), pair, 1 - side)
    return whole_rows


def is_small(count):
    return count <= 8 and count & (count - 1) == 0


def halved_rows(term):
    count = lax.axis_size("dp")
    if not is_small(count):
        return term
    at = lax.axis_index("dp")
    pairs = term.reshape(count // 2, 2, -1, term.shape[1])

    def side(which):
        return lax.dynamic_index_in_dim(pairs, which, 1, keepdims=False)

    came = crossed(side((at & 1) ^ 1), 1)
    return (side(at & 1).astype(f32) + came.astype(f32)).astype(bf16)


def finished_rows(lines):
    count = lax.axis_size("dp")
    if not is_small(count):
        return lax.psum_scatter(lines, "dp", scatter_dimension=0, tiled=True)
    at = lax.axis_index("dp")

    def part(owner):
        return lax.dynamic_index_in_dim(lines, owner // 2, 0, keepdims=False)

    came = [crossed(part(at ^ bits), bits) for bits in range(2, count, 2)]
    return sum([piece.astype(f32) for piece in came], part(at).astype(f32)).astype(bf16)


def after(value, other):
    return lax.optimization_barrier((value, other))[0]


def turned(blocks):
    size = lax.axis_size("seq")
    index = lax.axis_index("seq")
    if size & (size - 1):
        return lax.all_to_all(blocks, "seq", 0, 0, tiled=True)
    out = blocks
    for bits in range(1, size):
        piece = lax.dynamic_slice_in_dim(blocks, index ^ bits, 1, 0)
        piece = lax.ppermute(piece, "seq", [(i, i ^ bits) for i in range(size)])
        out = lax.dynamic_update_slice_in_dim(out, piece, index ^ bits, 0)
    return out


def folded(rows, lead, width):
    cut = rows.reshape(lead, rows.shape[0] // lead, rows.shape[1] // width, width)
    cut = cut.transpose(0, 2, 1, 3).reshape(lead, -1, width)
    return cut[0] if lead == 1 else cut


def unfolded(pieces, width):
    lead, stacked, narrow = pieces.shape
    cut = pieces.reshape(lead, width // narrow, stacked * narrow // width, narrow)
    return cut.transpose(0, 2, 1, 3).reshape(-1, width)


def padded(rows, width):
    return jnp.pad(rows, ((0, 0), (0, width - rows.shape[1])))


def shards(
    hidden, segments, cotangent, norm_gain, in_weight, conv_weight, conv_bias, step_bias, log_rate,
    skip_gain, gate_gain, out_weight,
):
    n_seqs, block, n_width = hidden.shape
    size = lax.axis_size("seq")
    groups = lax.axis_size("dp")
    index = lax.axis_index("seq")
    tokens = size * block
    n_inner = gate_gain.shape[0]
    n_heads = step_bias.shape[0]
    n_taps = conv_weight.shape[0]
    n_mixed = conv_bias.shape[0]
    n_state = (n_mixed - n_inner) // 2
    head = n_inner // n_heads
    own_inner = n_inner // size
    own_heads = n_heads // size
    own_bc = 2 * n_state // size
    q = min(128, block)
    in_rows = in_weight.shape[0]

    in_low = in_weight.astype(bf16)
    z_cols = in_low[:, :n_inner].reshape(in_rows, size, own_inner)
    x_cols = in_low[:, n_inner : 2 * n_inner].reshape(in_rows, size, own_inner)
    bc_cols = in_low[:, 2 * n_inner : n_inner + n_mixed].reshape(in_rows, size, own_bc)
    dt_cols = in_low[:, n_inner + n_mixed :].reshape(in_rows, size, own_heads)
    gap = jnp.zeros((in_rows, size, LANES - own_heads - own_bc), bf16)
    laid = jnp.concatenate([x_cols, dt_cols, gap, bc_cols, z_cols], axis=2).transpose(1, 0, 2)
    mine = lax.all_to_all(laid, "seq", 0, 0, tiled=True)
    flat = hidden.reshape(block, n_width).astype(f32)
    inv = lax.rsqrt(jnp.mean(flat * flat, axis=-1, keepdims=True) + epsilon)
    unit = flat * inv
    normed_own = (unit * norm_gain).astype(bf16)
    mine, normed_own = lax.optimization_barrier((mine, normed_own))
    mine = mine.reshape(size * in_rows, -1)
    n_first = own_inner + LANES
    w_first = gathered_rows(mine[:, :n_first])
    order = [(f, (f % groups) * size + f // groups) for f in range(groups * size)]
    back = [(b, a) for a, b in order]
    out_moved = lax.ppermute(out_weight.astype(bf16), ("dp", "seq"), order)
    z_block = jnp.concatenate([mine[:, n_first:], folded(out_moved, 1, own_inner)], axis=0)

    normed = gathered(normed_own)
    joined = lax.all_gather(z_block, "dp", axis=0, tiled=True).reshape(groups, -1, own_inner)
    z_rows = size * in_rows
    w_z = joined[:, :z_rows].reshape(-1, own_inner)
    w_out = unfolded(joined[:, z_rows:], n_width)
    cot_own = cotangent.reshape(block, n_width)
    cot = gathered(cot_own)
    docs = lax.all_gather(segments.reshape(block), "seq", axis=0, tiled=True).astype(f32)
    dcol = jnp.broadcast_to(docs[:, None], (tokens, LANES))
    drow = jnp.broadcast_to(docs[None, :], (8, tokens))

    def own_part(vector, parts):
        return lax.dynamic_slice_in_dim(vector, index * parts, parts, vector.ndim - 1)

    w_x, w_small = w_first[:, :own_inner], w_first[:, own_inner:]
    small = mm(normed, w_small, NN)
    x_in = mm(normed, w_x, NN).astype(bf16)
    z = mm(normed, w_z, NN)
    conv_x = own_part(conv_weight[:, :n_inner], own_inner)
    bias_x = own_part(conv_bias[None, :n_inner], own_inner)
    conv_bc = own_part(conv_weight[:, n_inner:], own_bc)
    bias_bc = own_part(conv_bias[None, n_inner:], own_bc)
    sb = padded(own_part(step_bias[None], own_heads), LANES)
    rate = padded(jnp.exp(own_part(log_rate[None], own_heads)), LANES)
    skip = jnp.repeat(own_part(skip_gain[None], own_heads), head, axis=1)
    gain = own_part(gate_gain[None], own_inner)

    head_lanes = jnp.arange(LANES) < own_heads
    bc_in = small[:, LANES - own_bc :].astype(bf16).astype(f32)
    small_dt = jnp.where(head_lanes, small, 0.0)

    def earlier(rows, lag):
        return jnp.pad(rows, ((lag, 0), (0, 0)))[:tokens]

    def later(rows, lag):
        return jnp.pad(rows, ((0, lag), (0, 0)))[lag:]

    same = [None] + [
        jnp.where(jnp.pad(docs, (lag, 0), constant_values=-1.0)[:tokens] == docs, 1.0, 0.0)[:, None]
        for lag in range(1, n_taps)
    ]
    bc_conv = bias_bc + conv_bc[0:1] * bc_in
    for lag in range(1, n_taps):
        bc_conv = bc_conv + conv_bc[lag : lag + 1] * earlier(bc_in, lag) * same[lag]
    bc_sig = jax.nn.sigmoid(bc_conv)
    bct = gathered((bc_conv * bc_sig).astype(bf16).T)

    y, states = run_forward(
        q, x_in, small_dt, bct, dcol, drow, conv_x, bias_x, sb, rate, skip, head
    )

    d_gn = mm(cot, w_out, NT)
    z_sig = jax.nn.sigmoid(z)
    z_act = z * z_sig
    gated = y * z_act
    scaled = d_gn * gain
    both = jnp.stack([jnp.sum(gated * gated, axis=1), jnp.sum(scaled * gated, axis=1)])
    both = lax.psum(both, "seq")
    g_inv = lax.rsqrt(both[0] / n_inner + epsilon)[:, None]
    g_dot = both[1][:, None] / n_inner
    gate_low = (gated * g_inv * gain).astype(bf16)
    d_gated = g_inv * scaled - gated * (g_inv * g_inv * g_inv * g_dot)
    d_gain = jnp.sum(d_gn * gated * g_inv, axis=0)
    d_z = (d_gated * y * (z_sig * (1.0 + z * (1.0 - z_sig)))).astype(bf16)
    d_y = d_gated * z_act

    terms = [mm(normed, d_z, TN)]
    for k in range(0, n_width, own_inner):
        terms.append(mm(gate_low, cot[:, k : k + own_inner], TN))
    terms = [term.astype(bf16).reshape(groups, -1, own_inner) for term in terms]
    terms = jnp.concatenate(terms, axis=1).reshape(-1, own_inner)
    terms, d_y = lax.optimization_barrier((terms, d_y))
    parts = lax.psum_scatter(terms, "dp", scatter_dimension=0, tiled=True)

    d_x, d_dt, d_bct, d_conv_x, d_heads = run_backward(
        q, x_in, small_dt, bct, dcol, drow, conv_x, bias_x, sb, rate, skip, d_y, states, head
    )
    d_bc = scattered(d_bct).T
    d_bcc = d_bc * (bc_sig * (1.0 + bc_conv * (1.0 - bc_sig)))
    d_bc_in = conv_bc[0:1] * d_bcc
    w_sums = [jnp.sum(d_bcc * bc_in, axis=0)]
    for lag in range(1, n_taps):
        held = d_bcc * same[lag]
        d_bc_in = d_bc_in + conv_bc[lag : lag + 1] * later(held, lag)
        w_sums.append(jnp.sum(held * earlier(bc_in, lag), axis=0))
    w_sums.append(jnp.sum(d_bcc, axis=0))
    d_small = jnp.concatenate([d_dt[:, : LANES - own_bc], d_bc_in], axis=1).astype(bf16)
    d_first = jnp.concatenate([d_x, d_small], axis=1)
    first_term = mm(normed, d_first, TN).astype(bf16)
    first_term, d_first = lax.optimization_barrier((first_term, d_first))
    d_normed = (mm(d_first, w_first, NT) + mm(d_z, w_z, NT)).astype(bf16)
    lines = after(halved_rows(first_term), d_normed)
    first_part = finished_rows(lines)
    d_norm = scattered(d_normed, lambda held: after(held, lines))
    parts = after(parts, lines)
    branch = after(mm(gate_low, w_out, NN).astype(bf16), parts)
    branch = lax.psum_scatter(branch, "seq", scatter_dimension=0, tiled=True)
    result = (flat + branch.astype(f32)).reshape(n_seqs, block, n_width).astype(bf16)

    def own_rows(part):
        out = turned(part.reshape(size, in_rows, -1))
        return out.transpose(1, 0, 2).astype(f32)

    out_part = unfolded(parts[None, z_rows:], n_width)
    d_out_weight = lax.ppermute(out_part, ("dp", "seq"), back).astype(f32)
    in_z = own_rows(parts[:z_rows])
    in_first = own_rows(first_part)
    d_in_weight = jnp.concatenate(
        [
            in_z.reshape(in_rows, n_inner),
            in_first[:, :, :own_inner].reshape(in_rows, n_inner),
            in_first[:, :, n_first - own_bc :].reshape(in_rows, 2 * n_state),
            in_first[:, :, own_inner : own_inner + own_heads].reshape(in_rows, n_heads),
        ],
        axis=1,
    )

    d_norm_gain = jnp.sum(d_norm * unit, axis=0)
    lifted = d_norm * norm_gain
    d_flat = inv * lifted - flat * (
        inv * inv * inv * jnp.mean(lifted * flat, axis=-1, keepdims=True)
    )
    d_hidden = (cot_own.astype(f32) + d_flat).reshape(n_seqs, block, n_width)

    d_skip = jnp.sum(d_conv_x[n_taps + 1].reshape(own_heads, head), axis=1)
    packed = jnp.concatenate(
        [
            d_conv_x[: n_taps + 1].reshape(-1),
            jnp.stack(w_sums).reshape(-1),
            d_gain,
            d_heads[0, :own_heads],
            d_heads[1, :own_heads],
            d_skip,
            d_norm_gain,
        ]
    )
    packed = gathered(summed(after(packed, first_part))[None])
    at = 0

    def take(count):
        nonlocal at
        at += count
        return packed[:, at - count : at]

    got_x = take((n_taps + 1) * own_inner).reshape(size, n_taps + 1, own_inner)
    got_bc = take((n_taps + 1) * own_bc).reshape(size, n_taps + 1, own_bc)
    got_x = got_x.transpose(1, 0, 2).reshape(n_taps + 1, n_inner)
    got_bc = got_bc.transpose(1, 0, 2).reshape(n_taps + 1, 2 * n_state)
    conv_all = jnp.concatenate([got_x, got_bc], axis=1)
    d_gate_gain = take(own_inner).reshape(n_inner)
    d_step_bias = take(own_heads).reshape(n_heads)
    d_log_rate = take(own_heads).reshape(n_heads)
    d_skip_gain = take(own_heads).reshape(n_heads)
    d_norm_all = jnp.sum(take(n_width), axis=0)
    return (
        result,
        d_hidden,
        d_norm_all,
        d_in_weight,
        conv_all[:n_taps],
        conv_all[n_taps],
        d_step_bias,
        d_log_rate,
        d_skip_gain,
        d_gate_gain,
        d_out_weight,
    )


def solution(mesh):
    tokens = P("dp", "seq", None)
    rows = P(("dp", "seq"), None)
    return jax.shard_map(
        shards,
        mesh=mesh,
        in_specs=(tokens, P("dp", "seq"), tokens, P(), rows, P(), P(), P(), P(), P(), P(), rows),
        out_specs=(tokens, tokens, P(), rows, P(), P(), P(), P(), P(), P(), rows),
        check_vma=False,
    )
```

```python
import functools

import jax
import jax.numpy as jnp
from jax import lax
from jax.experimental import pallas as pl
from jax.experimental.layout import Layout, with_layout_constraint
from jax.experimental.pallas import tpu as pltpu
from jax.sharding import PartitionSpec as P

epsilon = 1e-05
highest = lax.Precision.HIGHEST
f32 = jnp.float32
bf16 = jnp.bfloat16
LANES = 128
HALO = 16
NEG = -1e30


def mm(a, b, dims, out=f32):
    return lax.dot_general(a, b, (dims, ((), ())), preferred_element_type=out)


NN = ((1,), (0,))
NT = ((1,), (1,))
TN = ((0,), (0,))


def exact(a, b, dims):
    return lax.dot_general(a, b, (dims, ((), ())), precision=highest, preferred_element_type=f32)


def softplus(v):
    return jnp.maximum(v, 0.0) + jnp.log1p(jnp.exp(-jnp.abs(v)))


def sigmoid(v):
    return 1.0 / (1.0 + jnp.exp(-v))


def lane_iota(shape):
    return lax.broadcasted_iota(jnp.int32, shape, len(shape) - 1)


def spread(columns, first, second, wide):
    rows = columns.shape[0]
    left = jnp.broadcast_to(columns[:, first : first + 1], (rows, LANES))
    right = jnp.broadcast_to(columns[:, second : second + 1], (rows, LANES))
    return jnp.where(wide, left, right)


def step_parts(raw, rate, q):
    row = lax.broadcasted_iota(jnp.int32, (q, q), 0)
    col = lax.broadcasted_iota(jnp.int32, (q, q), 1)
    tri = jnp.where(row >= col, 1.0, 0.0).astype(f32)
    step = softplus(raw)
    decay = -step * rate
    total = exact(tri, decay, NN)
    return step, decay, total, tri, row >= col


def convolve(ext, docs_ext, own, weights, bias, lanes, q, taps):
    running = bias + weights[0:1, lanes] * ext[pl.ds(HALO, q), lanes]
    for lag in range(1, taps):
        same = jnp.where(docs_ext[pl.ds(HALO - lag, q), :] == own, 1.0, 0.0)
        running = running + weights[lag : lag + 1, lanes] * ext[pl.ds(HALO - lag, q), lanes] * same
    return running


def scan_forward(
    q, taps, pairs, head,
    x_ref, small_ref, bct_ref, dcol_ref, drow_ref, w_ref, b_ref, sb_ref, rate_ref, skip_ref,
    y_ref, states_ref,
    state, ext, docs_ext, xs, xt, last_doc,
):
    c = pl.program_id(0)
    n = bct_ref.shape[0] // 2

    @pl.when(c == 0)
    def _():
        state[...] = jnp.zeros_like(state)
        ext[pl.ds(0, HALO), :] = jnp.zeros((HALO, ext.shape[1]), f32)
        docs_ext[pl.ds(0, HALO), :] = jnp.full((HALO, LANES), -1.0, f32)
        last_doc[...] = jnp.full(last_doc.shape, -1.0, f32)

    own = dcol_ref[...]
    ext[pl.ds(HALO, q), :] = x_ref[...].astype(f32)
    docs_ext[pl.ds(HALO, q), :] = own
    step, _, cum, _, causal = step_parts(small_ref[...] + sb_ref[...], rate_ref[...], q)
    step_t = step.T
    cum_t = cum.T
    end = cum[q - 1 : q, :]
    id_in = last_doc[0:1, :]
    final = own[q - 1 : q, :]
    linked = jnp.where(final == id_in, 1.0, 0.0)
    fade = linked * jnp.exp(end)
    entering = jnp.where(own == id_in, 1.0, 0.0) * jnp.exp(cum)
    to_end = jnp.where(own == final, 1.0, 0.0) * jnp.exp(end - cum) * step
    same_doc = jnp.broadcast_to(own[:, 0:1], (q, q)) == jnp.broadcast_to(drow_ref[0:1, :], (q, q))
    hide = jnp.where(jnp.logical_and(causal, same_doc), 0.0, NEG)
    bt = bct_ref[0:n, :]
    ct = bct_ref[n : 2 * n, :]
    scores = mm(ct, bt, TN)
    states_ref[0] = state[...]
    old = state[...].astype(bf16)
    wide = lane_iota((q, LANES)) < head
    wide_row = lane_iota((1, LANES)) < head
    for k in range(pairs):
        lanes = slice(k * LANES, (k + 1) * LANES)
        h0, h1 = 2 * k, 2 * k + 1
        conv = convolve(ext, docs_ext, own, w_ref, b_ref[:, lanes], lanes, q, taps)
        x = conv * sigmoid(conv)
        xd = x * spread(step, h0, h1, wide)
        xt[:, lanes] = (x * spread(to_end, h0, h1, wide)).astype(bf16)
        mats = []
        for h in (h0, h1):
            gap = cum[:, h : h + 1] - cum_t[h : h + 1, :] + hide
            mats.append((jnp.exp(gap) * scores).astype(bf16))
        out = mm(mats[0], jnp.where(wide, xd, 0.0).astype(bf16), NN)
        out = out + mm(mats[1], jnp.where(wide, 0.0, xd).astype(bf16), NN)
        out = out + mm(ct, old[:, lanes], TN) * spread(entering, h0, h1, wide)
        y_ref[:, lanes] = out + skip_ref[:, lanes] * x
    update = mm(bt, xt[...], NN)
    for k in range(pairs):
        lanes = slice(k * LANES, (k + 1) * LANES)
        state[:, lanes] = state[:, lanes] * spread(fade, 2 * k, 2 * k + 1, wide_row) + update[:, lanes]
    ext[pl.ds(0, HALO), :] = ext[pl.ds(q, HALO), :]
    docs_ext[pl.ds(0, HALO), :] = docs_ext[pl.ds(q, HALO), :]
    last_doc[...] = jnp.broadcast_to(final, last_doc.shape)


def scan_backward(
    q, taps, pairs, head, chunks,
    x_ref, xp_ref, small_ref, bct_ref, dcol_ref, dcolp_ref, drow_ref, w_ref, b_ref, sb_ref, rate_ref,
    skip_ref, dy_ref, states_ref,
    dx_ref, dsmall_ref, dbct_ref, dconv_ref, dhead_ref,
    dstate, ext, docs_ext, dcv, docs_after, dye, xt, col_t,
):
    step_at = pl.program_id(0)
    c = chunks - 1 - step_at
    n = bct_ref.shape[0] // 2
    width = x_ref.shape[1]

    @pl.when(step_at == 0)
    def _():
        dstate[...] = jnp.zeros_like(dstate)
        dcv[pl.ds(q, HALO), :] = jnp.zeros((HALO, width), f32)
        docs_after[pl.ds(q, HALO), :] = jnp.full((HALO, LANES), -1.0, f32)
        dconv_ref[...] = jnp.zeros_like(dconv_ref)
        dhead_ref[...] = jnp.zeros_like(dhead_ref)
        col_t[...] = jnp.zeros_like(col_t)

    first = c == 0
    own = dcol_ref[...]
    before = jnp.where(first, -1.0, dcolp_ref[...])
    ext[pl.ds(0, HALO), :] = xp_ref[...].astype(f32)
    ext[pl.ds(HALO, q), :] = x_ref[...].astype(f32)
    docs_ext[pl.ds(0, HALO), :] = before
    docs_ext[pl.ds(HALO, q), :] = own
    docs_after[pl.ds(0, q), :] = own
    raw = small_ref[...] + sb_ref[...]
    rate = rate_ref[...]
    step, decay, cum, tri, causal = step_parts(raw, rate, q)
    step_t = step.T
    cum_t = cum.T
    end = cum[q - 1 : q, :]
    id_in = before[HALO - 1 : HALO, :]
    final = own[q - 1 : q, :]
    linked = jnp.where(final == id_in, 1.0, 0.0)
    fade = linked * jnp.exp(end)
    entering = jnp.where(own == id_in, 1.0, 0.0) * jnp.exp(cum)
    tail = jnp.where(own == final, 1.0, 0.0) * jnp.exp(end - cum)
    to_end = tail * step
    same_doc = jnp.broadcast_to(own[:, 0:1], (q, q)) == jnp.broadcast_to(drow_ref[0:1, :], (q, q))
    hide = jnp.where(jnp.logical_and(causal, same_doc), 0.0, NEG)
    bt = bct_ref[0:n, :]
    ct = bct_ref[n : 2 * n, :]
    scores = mm(ct, bt, TN)
    old = states_ref[0].astype(bf16)
    after = dstate[...].astype(bf16)
    wide = lane_iota((q, LANES)) < head
    wide_row = lane_iota((1, LANES)) < head
    lane = lane_iota((q, LANES))
    d_scores = jnp.zeros((q, q), f32)
    rows = jnp.zeros((q, LANES), f32)
    d_enter = jnp.zeros((q, LANES), f32)
    d_toend = jnp.zeros((q, LANES), f32)
    d_fade = jnp.zeros((8, LANES), f32)
    part = lax.broadcasted_iota(jnp.int32, (LANES, LANES), 0) // head
    to = lane_iota((LANES, LANES))
    for k in range(pairs):
        lanes = slice(k * LANES, (k + 1) * LANES)
        h0, h1 = 2 * k, 2 * k + 1
        pick = jnp.where(part + 2 * k == to, 1.0, 0.0)
        conv = convolve(ext, docs_ext, own, w_ref, b_ref[:, lanes], lanes, q, taps)
        sig = sigmoid(conv)
        x = conv * sig
        xb = x.astype(bf16)
        dy = dy_ref[:, lanes]
        halves = (jnp.where(wide, dy, 0.0).astype(bf16), jnp.where(wide, 0.0, dy).astype(bf16))
        dxd = jnp.zeros((q, LANES), f32)
        for h, half in ((h0, halves[0]), (h1, halves[1])):
            inner = mm(half, xb, NT)
            keep = jnp.exp(cum[:, h : h + 1] - cum_t[h : h + 1, :] + hide)
            grown = keep * inner
            mat = keep * scores
            dt = step_t[h : h + 1, :]
            g = grown * scores
            d_scores = d_scores + grown * dt
            rows = jnp.where(lane == h, jnp.sum(g * dt, axis=1, keepdims=True), rows)
            col_t[h : h + 1, :] = jnp.sum(g, axis=0, keepdims=True)
            dxd = dxd + mm(mat.astype(bf16), half, TN)
        v = mm(bt, after[:, lanes], TN)
        u = mm(ct, old[:, lanes], TN)
        enter_k = spread(entering, h0, h1, wide)
        end_k = spread(to_end, h0, h1, wide)
        d_enter = d_enter + exact(dy * u, pick, NN)
        d_toend = d_toend + exact(x * v, pick, NN)
        hh = jnp.sum(dstate[:, lanes] * states_ref[0, :, lanes], axis=0, keepdims=True)
        d_fade = d_fade + exact(jnp.broadcast_to(hh, (8, LANES)), pick, NN)
        dye[:, lanes] = (dy * enter_k).astype(bf16)
        xt[:, lanes] = (x * end_k).astype(bf16)
        dx = dxd * spread(step, h0, h1, wide) + end_k * v + skip_ref[:, lanes] * dy
        dconv = dx * (sig * (1.0 + conv * (1.0 - sig)))
        dcv[pl.ds(0, q), lanes] = dconv
        sums = [jnp.sum(dconv * ext[pl.ds(HALO, q), lanes], axis=0, keepdims=True)]
        dxin = w_ref[0:1, lanes] * dconv
        for lag in range(1, taps):
            same = jnp.where(docs_ext[pl.ds(HALO - lag, q), :] == own, 1.0, 0.0)
            sums.append(jnp.sum(dconv * same * ext[pl.ds(HALO - lag, q), lanes], axis=0, keepdims=True))
            follow = jnp.where(docs_after[pl.ds(lag, q), :] == own, 1.0, 0.0)
            dxin = dxin + w_ref[lag : lag + 1, lanes] * dcv[pl.ds(lag, q), lanes] * follow
        sums.append(jnp.sum(dconv, axis=0, keepdims=True))
        sums.append(jnp.sum(dy * x, axis=0, keepdims=True))
        dx_ref[:, lanes] = dxin.astype(bf16)
        for i, s in enumerate(sums):
            dconv_ref[i : i + 1, lanes] = dconv_ref[i : i + 1, lanes] + s
    dsb = d_scores.astype(bf16)
    dbct_ref[0:n, :] = mm(ct, dsb, NN) + mm(after, xt[...], NT)
    dbct_ref[n : 2 * n, :] = mm(bt, dsb, NT) + mm(old, dye[...], NT)
    new = mm(ct, dye[...], NN)
    for k in range(pairs):
        lanes = slice(k * LANES, (k + 1) * LANES)
        dstate[:, lanes] = dstate[:, lanes] * spread(fade, 2 * k, 2 * k + 1, wide_row) + new[:, lanes]
    cols = col_t[...].T
    pulled = d_toend * to_end
    at_end = jnp.sum(pulled, axis=0, keepdims=True) + fade * d_fade[0:1, :]
    d_cum = rows - step * cols + d_enter * entering - pulled
    last_row = lax.broadcasted_iota(jnp.int32, (q, LANES), 0) == q - 1
    d_cum = d_cum + jnp.where(last_row, at_end, 0.0)
    d_decay = exact(tri, d_cum, TN)
    d_step = cols + d_toend * tail - rate * d_decay
    d_raw = d_step * sigmoid(raw)
    dsmall_ref[...] = d_raw
    dhead_ref[0:1, :] = dhead_ref[0:1, :] + jnp.sum(d_raw, axis=0, keepdims=True)
    dhead_ref[1:2, :] = dhead_ref[1:2, :] + jnp.sum(d_decay * decay, axis=0, keepdims=True)
    dcv[pl.ds(q, HALO), :] = dcv[pl.ds(0, HALO), :]
    docs_after[pl.ds(q, HALO), :] = docs_after[pl.ds(0, HALO), :]


def whole(array):
    return pl.BlockSpec(array.shape, lambda c: (0,) * array.ndim)


def run_forward(q, x_in, small, bct, dcol, drow, conv_w, conv_b, sb, rate, skip, head):
    tokens, width = x_in.shape
    n = bct.shape[0] // 2
    chunks = tokens // q
    pairs = width // LANES
    taps = conv_w.shape[0]
    return pl.pallas_call(
        functools.partial(scan_forward, q, taps, pairs, head),
        grid=(chunks,),
        in_specs=[
            pl.BlockSpec((q, width), lambda c: (c, 0)),
            pl.BlockSpec((q, LANES), lambda c: (c, 0)),
            pl.BlockSpec((2 * n, q), lambda c: (0, c)),
            pl.BlockSpec((q, LANES), lambda c: (c, 0)),
            pl.BlockSpec((8, q), lambda c: (0, c)),
            whole(conv_w), whole(conv_b), whole(sb), whole(rate), whole(skip),
        ],
        out_specs=[
            pl.BlockSpec((q, width), lambda c: (c, 0)),
            pl.BlockSpec((1, n, width), lambda c: (c, 0, 0)),
        ],
        out_shape=[
            jax.ShapeDtypeStruct((tokens, width), f32),
            jax.ShapeDtypeStruct((chunks, n, width), f32),
        ],
        scratch_shapes=[
            pltpu.VMEM((n, width), f32),
            pltpu.VMEM((HALO + q, width), f32),
            pltpu.VMEM((HALO + q, LANES), f32),
            pltpu.VMEM((8, LANES), f32),
            pltpu.VMEM((q, width), bf16),
            pltpu.VMEM((8, LANES), f32),
        ],
        name="scan_forward",
    )(x_in, small, bct, dcol, drow, conv_w, conv_b, sb, rate, skip)


def run_backward(q, x_in, small, bct, dcol, drow, conv_w, conv_b, sb, rate, skip, dy, states, head):
    tokens, width = x_in.shape
    n = bct.shape[0] // 2
    chunks = tokens // q
    pairs = width // LANES
    taps = conv_w.shape[0]
    per = q // HALO

    def at(c):
        return chunks - 1 - c

    def prior(c):
        return jnp.maximum((chunks - 1 - c) * per - 1, 0)

    return pl.pallas_call(
        functools.partial(scan_backward, q, taps, pairs, head, chunks),
        grid=(chunks,),
        in_specs=[
            pl.BlockSpec((q, width), lambda c: (at(c), 0)),
            pl.BlockSpec((HALO, width), lambda c: (prior(c), 0)),
            pl.BlockSpec((q, LANES), lambda c: (at(c), 0)),
            pl.BlockSpec((2 * n, q), lambda c: (0, at(c))),
            pl.BlockSpec((q, LANES), lambda c: (at(c), 0)),
            pl.BlockSpec((HALO, LANES), lambda c: (prior(c), 0)),
            pl.BlockSpec((8, q), lambda c: (0, at(c))),
            whole(conv_w), whole(conv_b), whole(sb), whole(rate), whole(skip),
            pl.BlockSpec((q, width), lambda c: (at(c), 0)),
            pl.BlockSpec((1, n, width), lambda c: (at(c), 0, 0)),
        ],
        out_specs=[
            pl.BlockSpec((q, width), lambda c: (at(c), 0)),
            pl.BlockSpec((q, LANES), lambda c: (at(c), 0)),
            pl.BlockSpec((2 * n, q), lambda c: (0, at(c))),
            pl.BlockSpec((8, width), lambda c: (0, 0)),
            pl.BlockSpec((8, LANES), lambda c: (0, 0)),
        ],
        out_shape=[
            jax.ShapeDtypeStruct((tokens, width), bf16),
            jax.ShapeDtypeStruct((tokens, LANES), f32),
            jax.ShapeDtypeStruct((2 * n, tokens), f32),
            jax.ShapeDtypeStruct((8, width), f32),
            jax.ShapeDtypeStruct((8, LANES), f32),
        ],
        scratch_shapes=[
            pltpu.VMEM((n, width), f32),
            pltpu.VMEM((HALO + q, width), f32),
            pltpu.VMEM((HALO + q, LANES), f32),
            pltpu.VMEM((q + HALO, width), f32),
            pltpu.VMEM((q + HALO, LANES), f32),
            pltpu.VMEM((q, width), bf16),
            pltpu.VMEM((q, width), bf16),
            pltpu.VMEM((LANES, q), f32),
        ],
        name="scan_backward",
    )(x_in, x_in, small, bct, dcol, dcol, drow, conv_w, conv_b, sb, rate, skip, dy, states)


def swapped(block, bit):
    size = lax.axis_size("seq")
    return lax.ppermute(block, "seq", [(i, i ^ bit) for i in range(size)])


def bits_of(size):
    bits, bit = [], 1
    while bit < size:
        bits.append(bit)
        bit *= 2
    return bits


def gathered(block):
    index = lax.axis_index("seq")
    block = block[None]
    for bit in reversed(bits_of(lax.axis_size("seq"))):
        other = swapped(block, bit)
        upper = (index & bit) != 0
        block = jnp.where(
            upper, jnp.stack([other, block], axis=1), jnp.stack([block, other], axis=1)
        )
        block = block.reshape((-1,) + block.shape[2:])
    return block.reshape((-1,) + block.shape[2:])


def scattered(parts, between=lambda held: held):
    index = lax.axis_index("seq")
    size = lax.axis_size("seq")
    rest = parts.shape[1:]
    lead = parts.shape[0]
    held = parts.reshape((size, lead // size) + rest)
    for bit in bits_of(size):
        half = held.reshape((held.shape[0] // 2, 2) + held.shape[1:])
        upper = (index & bit) != 0
        mine = jnp.where(upper, half[:, 1], half[:, 0])
        theirs = jnp.where(upper, half[:, 0], half[:, 1]).astype(bf16)
        held = between(mine.astype(f32) + swapped(theirs, bit).astype(f32))
    return held[0]


def summed(block):
    count = lax.axis_size("dp")
    for bit in bits_of(count):
        block = block + lax.ppermute(block, "dp", [(i, i ^ bit) for i in range(count)])
    return block


def moved_by(block, step):
    count = lax.axis_size("dp")
    route = [(i, i + 2 * step) for i in range(count) if 0 <= i + 2 * step < count]
    return lax.ppermute(block, "dp", route)


def crossed(block, bits):
    return lax.ppermute(block, "dp", [(i, i ^ bits) for i in range(lax.axis_size("dp"))])


def gathered_rows(block):
    count = lax.axis_size("dp")
    length = count // 2
    if not is_small(count):
        return lax.all_gather(block, "dp", axis=0, tiled=True), block
    at = lax.axis_index("dp")
    place, side = at // 2, at % 2
    rows = block.shape[0]
    whole_rows = jnp.zeros((count * rows, block.shape[1]), block.dtype)

    def put(into, piece, pair, half):
        return lax.dynamic_update_slice(into, piece, ((pair * 2 + half) * rows, 0))

    whole_rows = put(whole_rows, block, place, side)
    whole_rows = put(whole_rows, crossed(block, 1), place, 1 - side)
    up, down, ready = block, block, []
    both = jnp.minimum(place, length - 1 - place)
    for hop in range(1, length):
        up, down = moved_by(up, 1), moved_by(down, -1)
        ready.append((down, up))
        piece, pair = None, None
        for spot in range(length):
            near = min(spot, length - 1 - spot)
            if hop <= 2 * near:
                away, from_below = (hop + 1) // 2, hop % 2 == 0
            else:
                away, from_below = hop - near, spot > length - 1 - spot
            chosen = ready[away - 1][1 if from_below else 0]
            source = spot - away if from_below else spot + away
            here = place == spot
            piece = chosen if piece is None else jnp.where(here, chosen, piece)
            pair = source if pair is None else jnp.where(here, source, pair)
        whole_rows = put(whole_rows, piece, pair, side)
        whole_rows = put(whole_rows, crossed(piece, 1), pair, 1 - side)
    return whole_rows, ready[0]


def is_small(count):
    return count <= 8 and count & (count - 1) == 0


def halved_rows(term):
    count = lax.axis_size("dp")
    if not is_small(count):
        return term
    at = lax.axis_index("dp")
    pairs = term.reshape(count // 2, 2, -1, term.shape[1])

    def side(which):
        return lax.dynamic_index_in_dim(pairs, which, 1, keepdims=False)

    came = crossed(side((at & 1) ^ 1), 1)
    return (side(at & 1).astype(f32) + came.astype(f32)).astype(bf16)


def shared_rows(lines):
    count = lax.axis_size("dp")
    if not is_small(count):
        return [lax.psum_scatter(lines, "dp", scatter_dimension=0, tiled=True)]
    at = lax.axis_index("dp")

    def part(owner):
        return lax.dynamic_index_in_dim(lines, owner // 2, 0, keepdims=False)

    return [part(at)] + [crossed(part(at ^ bits), bits) for bits in range(2, count, 2)]


def after(value, other):
    return lax.optimization_barrier((value, other))[0]


def turned(blocks):
    size = lax.axis_size("seq")
    index = lax.axis_index("seq")
    if size & (size - 1):
        return lax.all_to_all(blocks, "seq", 0, 0, tiled=True)
    out = blocks
    for bits in range(1, size):
        piece = lax.dynamic_slice_in_dim(blocks, index ^ bits, 1, 0)
        piece = lax.ppermute(piece, "seq", [(i, i ^ bits) for i in range(size)])
        out = lax.dynamic_update_slice_in_dim(out, piece, index ^ bits, 0)
    return out


def folded(rows, lead, width):
    cut = rows.reshape(lead, rows.shape[0] // lead, rows.shape[1] // width, width)
    cut = cut.transpose(0, 2, 1, 3).reshape(lead, -1, width)
    return cut[0] if lead == 1 else cut


def unfolded(pieces, width):
    lead, stacked, narrow = pieces.shape
    cut = pieces.reshape(lead, width // narrow, stacked * narrow // width, narrow)
    return cut.transpose(0, 2, 1, 3).reshape(-1, width)


def exchanged(parts):
    size = lax.axis_size("seq")
    index = lax.axis_index("seq")
    held = parts.reshape((size, -1) + parts.shape[1:])

    def part(owner):
        return lax.dynamic_index_in_dim(held, owner, 0, keepdims=False)

    came = [
        lax.ppermute(part(index ^ bits).astype(bf16), "seq", [(i, i ^ bits) for i in range(size)])
        for bits in range(1, size)
    ]
    return sum([piece.astype(f32) for piece in came], part(index))


def by_rows(array):
    return with_layout_constraint(array, Layout(major_to_minor=(0, 1)))


def padded(rows, width):
    return jnp.pad(rows, ((0, 0), (0, width - rows.shape[1])))


def shards(
    hidden, segments, cotangent, norm_gain, in_weight, conv_weight, conv_bias, step_bias, log_rate,
    skip_gain, gate_gain, out_weight,
):
    n_seqs, block, n_width = hidden.shape
    size = lax.axis_size("seq")
    groups = lax.axis_size("dp")
    index = lax.axis_index("seq")
    tokens = size * block
    n_inner = gate_gain.shape[0]
    n_heads = step_bias.shape[0]
    n_taps = conv_weight.shape[0]
    n_mixed = conv_bias.shape[0]
    n_state = (n_mixed - n_inner) // 2
    head = n_inner // n_heads
    own_inner = n_inner // size
    own_heads = n_heads // size
    own_bc = 2 * n_state // size
    q = min(128, block)
    in_rows = in_weight.shape[0]

    in_low = in_weight.astype(bf16)
    z_cols = in_low[:, :n_inner].reshape(in_rows, size, own_inner)
    x_cols = in_low[:, n_inner : 2 * n_inner].reshape(in_rows, size, own_inner)
    bc_cols = in_low[:, 2 * n_inner : n_inner + n_mixed].reshape(in_rows, size, own_bc)
    dt_cols = in_low[:, n_inner + n_mixed :].reshape(in_rows, size, own_heads)
    gap = jnp.zeros((in_rows, size, LANES - own_heads - own_bc), bf16)
    laid = jnp.concatenate([x_cols, dt_cols, gap, bc_cols, z_cols], axis=2).transpose(1, 0, 2)
    mine = lax.all_to_all(laid, "seq", 0, 0, tiled=True)
    flat = hidden.reshape(block, n_width).astype(f32)
    inv = lax.rsqrt(jnp.mean(flat * flat, axis=-1, keepdims=True) + epsilon)
    unit = flat * inv
    normed_own = (unit * norm_gain).astype(bf16)
    mine, normed_own = lax.optimization_barrier((mine, normed_own))
    mine = mine.reshape(size * in_rows, -1)
    n_first = own_inner + LANES
    w_first, first_hop = gathered_rows(mine[:, :n_first])
    order = [(f, (f % groups) * size + f // groups) for f in range(groups * size)]
    back = [(b, a) for a, b in order]
    out_moved = lax.ppermute(out_weight.astype(bf16), ("dp", "seq"), order)
    z_block = jnp.concatenate([mine[:, n_first:], folded(out_moved, 1, own_inner)], axis=0)

    normed = gathered(normed_own)
    joined = lax.all_gather(after(z_block, first_hop), "dp", axis=0, tiled=True).reshape(groups, -1, own_inner)
    z_rows = size * in_rows
    w_z = joined[:, :z_rows].reshape(-1, own_inner)
    w_out = unfolded(joined[:, z_rows:], n_width)
    cot_own = cotangent.reshape(block, n_width)
    cot = gathered(cot_own)
    docs = lax.all_gather(segments.reshape(block), "seq", axis=0, tiled=True).astype(f32)
    dcol = jnp.broadcast_to(docs[:, None], (tokens, LANES))
    drow = jnp.broadcast_to(docs[None, :], (8, tokens))

    def own_part(vector, parts):
        return lax.dynamic_slice_in_dim(vector, index * parts, parts, vector.ndim - 1)

    w_x, w_small = w_first[:, :own_inner], w_first[:, own_inner:]
    small = mm(normed, w_small, NN)
    x_in = mm(normed, w_x, NN).astype(bf16)
    z = mm(normed, w_z, NN)
    conv_x = own_part(conv_weight[:, :n_inner], own_inner)
    bias_x = own_part(conv_bias[None, :n_inner], own_inner)
    conv_bc = own_part(conv_weight[:, n_inner:], own_bc)
    bias_bc = own_part(conv_bias[None, n_inner:], own_bc)
    sb = padded(own_part(step_bias[None], own_heads), LANES)
    rate = padded(jnp.exp(own_part(log_rate[None], own_heads)), LANES)
    skip = jnp.repeat(own_part(skip_gain[None], own_heads), head, axis=1)
    gain = own_part(gate_gain[None], own_inner)

    head_lanes = jnp.arange(LANES) < own_heads
    bc_in = small[:, LANES - own_bc :].astype(bf16).astype(f32)
    small_dt = jnp.where(head_lanes, small, 0.0)

    def earlier(rows, lag):
        return jnp.pad(rows, ((lag, 0), (0, 0)))[:tokens]

    def later(rows, lag):
        return jnp.pad(rows, ((0, lag), (0, 0)))[lag:]

    same = [None] + [
        jnp.where(jnp.pad(docs, (lag, 0), constant_values=-1.0)[:tokens] == docs, 1.0, 0.0)[:, None]
        for lag in range(1, n_taps)
    ]
    bc_conv = bias_bc + conv_bc[0:1] * bc_in
    for lag in range(1, n_taps):
        bc_conv = bc_conv + conv_bc[lag : lag + 1] * earlier(bc_in, lag) * same[lag]
    bc_sig = jax.nn.sigmoid(bc_conv)
    bct = gathered(by_rows((bc_conv * bc_sig).astype(bf16).T))

    y, states = run_forward(
        q, x_in, small_dt, bct, dcol, drow, conv_x, bias_x, sb, rate, skip, head
    )

    d_gn = mm(cot, w_out, NT)
    z_sig = jax.nn.sigmoid(z)
    z_act = z * z_sig
    gated = y * z_act
    scaled = d_gn * gain
    both = jnp.stack([jnp.sum(gated * gated, axis=1), jnp.sum(scaled * gated, axis=1)])
    both = lax.psum(both, "seq")
    g_inv = lax.rsqrt(both[0] / n_inner + epsilon)[:, None]
    g_dot = both[1][:, None] / n_inner
    gate_low = (gated * g_inv * gain).astype(bf16)
    d_gated = g_inv * scaled - gated * (g_inv * g_inv * g_inv * g_dot)
    d_gain = jnp.sum(d_gn * gated * g_inv, axis=0)
    d_z = (d_gated * y * (z_sig * (1.0 + z * (1.0 - z_sig)))).astype(bf16)
    d_y = d_gated * z_act

    terms = [mm(normed, d_z, TN)]
    for k in range(0, n_width, own_inner):
        terms.append(mm(gate_low, cot[:, k : k + own_inner], TN))
    terms = [term.astype(bf16).reshape(groups, -1, own_inner) for term in terms]
    terms = jnp.concatenate(terms, axis=1).reshape(-1, own_inner)
    terms, d_y = lax.optimization_barrier((terms, d_y))
    parts = lax.psum_scatter(terms, "dp", scatter_dimension=0, tiled=True)

    d_x, d_dt, d_bct, d_conv_x, d_heads = run_backward(
        q, x_in, small_dt, bct, dcol, drow, conv_x, bias_x, sb, rate, skip, d_y, states, head
    )
    d_bc = by_rows(exchanged(d_bct)).T
    d_bcc = d_bc * (bc_sig * (1.0 + bc_conv * (1.0 - bc_sig)))
    d_bc_in = conv_bc[0:1] * d_bcc
    w_sums = [jnp.sum(d_bcc * bc_in, axis=0)]
    for lag in range(1, n_taps):
        held = d_bcc * same[lag]
        d_bc_in = d_bc_in + conv_bc[lag : lag + 1] * later(held, lag)
        w_sums.append(jnp.sum(held * earlier(bc_in, lag), axis=0))
    w_sums.append(jnp.sum(d_bcc, axis=0))
    d_small = jnp.concatenate([d_dt[:, : LANES - own_bc], d_bc_in], axis=1).astype(bf16)
    d_first = jnp.concatenate([d_x, d_small], axis=1)
    first_term = mm(normed, d_first, TN).astype(bf16)
    first_term, d_first = lax.optimization_barrier((first_term, d_first))
    branch = scattered(mm(gate_low, w_out, NN).astype(bf16))
    result = (flat + branch).reshape(n_seqs, block, n_width).astype(bf16)
    d_normed = mm(d_first, w_first, NT) + mm(d_z, w_z, NT)
    d_norm_gain = jnp.sum(d_normed * normed.astype(f32), axis=0) / norm_gain
    d_skip = jnp.sum(d_conv_x[n_taps + 1].reshape(own_heads, head), axis=1)
    packed = jnp.concatenate(
        [
            d_conv_x[: n_taps + 1].reshape(-1),
            jnp.stack(w_sums).reshape(-1),
            d_gain,
            d_heads[0, :own_heads],
            d_heads[1, :own_heads],
            d_skip,
            d_norm_gain,
        ]
    )
    lines = halved_rows(first_term)
    packed = gathered(after(summed(packed), lines)[None])
    shares = shared_rows(lines)
    parts = after(parts, (lines, result))
    d_norm = after(d_normed.astype(bf16), parts)
    d_norm = lax.psum_scatter(d_norm, "seq", scatter_dimension=0, tiled=True).astype(f32)

    def own_rows(part):
        out = turned(part.reshape(size, in_rows, -1))
        return out.transpose(1, 0, 2).astype(f32)

    out_part = unfolded(parts[None, z_rows:], n_width)
    d_out_weight = lax.ppermute(out_part, ("dp", "seq"), back).astype(f32)
    in_z = own_rows(parts[:z_rows])
    shares = after(shares, (in_z, d_out_weight))
    first_part = sum(share.astype(f32) for share in shares)
    in_first = own_rows(first_part.astype(bf16))
    d_in_weight = jnp.concatenate(
        [
            in_z.reshape(in_rows, n_inner),
            in_first[:, :, :own_inner].reshape(in_rows, n_inner),
            in_first[:, :, n_first - own_bc :].reshape(in_rows, 2 * n_state),
            in_first[:, :, own_inner : own_inner + own_heads].reshape(in_rows, n_heads),
        ],
        axis=1,
    )

    lifted = d_norm * norm_gain
    d_flat = inv * lifted - flat * (
        inv * inv * inv * jnp.mean(lifted * flat, axis=-1, keepdims=True)
    )
    d_hidden = (cot_own.astype(f32) + d_flat).reshape(n_seqs, block, n_width)

    at = 0

    def take(count):
        nonlocal at
        at += count
        return packed[:, at - count : at]

    got_x = take((n_taps + 1) * own_inner).reshape(size, n_taps + 1, own_inner)
    got_bc = take((n_taps + 1) * own_bc).reshape(size, n_taps + 1, own_bc)
    got_x = got_x.transpose(1, 0, 2).reshape(n_taps + 1, n_inner)
    got_bc = got_bc.transpose(1, 0, 2).reshape(n_taps + 1, 2 * n_state)
    conv_all = jnp.concatenate([got_x, got_bc], axis=1)
    d_gate_gain = take(own_inner).reshape(n_inner)
    d_step_bias = take(own_heads).reshape(n_heads)
    d_log_rate = take(own_heads).reshape(n_heads)
    d_skip_gain = take(own_heads).reshape(n_heads)
    d_norm_all = jnp.sum(take(n_width), axis=0)
    return (
        result,
        d_hidden,
        d_norm_all,
        d_in_weight,
        conv_all[:n_taps],
        conv_all[n_taps],
        d_step_bias,
        d_log_rate,
        d_skip_gain,
        d_gate_gain,
        d_out_weight,
    )


def solution(mesh):
    tokens = P("dp", "seq", None)
    rows = P(("dp", "seq"), None)
    return jax.shard_map(
        shards,
        mesh=mesh,
        in_specs=(tokens, P("dp", "seq"), tokens, P(), rows, P(), P(), P(), P(), P(), P(), rows),
        out_specs=(tokens, tokens, P(), rows, P(), P(), P(), P(), P(), P(), rows),
        check_vma=False,
    )
```

```python
import functools

import jax
import jax.numpy as jnp
from jax import lax
from jax.experimental import pallas as pl
from jax.experimental.layout import Layout, with_layout_constraint
from jax.experimental.pallas import tpu as pltpu
from jax.sharding import PartitionSpec as P

epsilon = 1e-05
highest = lax.Precision.HIGHEST
f32 = jnp.float32
bf16 = jnp.bfloat16
LANES = 128
HALO = 16
NEG = -1e30


def mm(a, b, dims, out=f32):
    return lax.dot_general(a, b, (dims, ((), ())), preferred_element_type=out)


NN = ((1,), (0,))
NT = ((1,), (1,))
TN = ((0,), (0,))


def exact(a, b, dims):
    return lax.dot_general(a, b, (dims, ((), ())), precision=highest, preferred_element_type=f32)


def softplus(v):
    return jnp.maximum(v, 0.0) + jnp.log1p(jnp.exp(-jnp.abs(v)))


def sigmoid(v):
    return 1.0 / (1.0 + jnp.exp(-v))


def lane_iota(shape):
    return lax.broadcasted_iota(jnp.int32, shape, len(shape) - 1)


def spread(columns, first, second, wide):
    rows = columns.shape[0]
    left = jnp.broadcast_to(columns[:, first : first + 1], (rows, LANES))
    right = jnp.broadcast_to(columns[:, second : second + 1], (rows, LANES))
    return jnp.where(wide, left, right)


def step_parts(raw, rate, q):
    row = lax.broadcasted_iota(jnp.int32, (q, q), 0)
    col = lax.broadcasted_iota(jnp.int32, (q, q), 1)
    tri = jnp.where(row >= col, 1.0, 0.0).astype(f32)
    step = softplus(raw)
    decay = -step * rate
    total = exact(tri, decay, NN)
    return step, decay, total, tri, row >= col


def convolve(ext, docs_ext, own, weights, bias, lanes, q, taps):
    running = bias + weights[0:1, lanes] * ext[pl.ds(HALO, q), lanes]
    for lag in range(1, taps):
        same = jnp.where(docs_ext[pl.ds(HALO - lag, q), :] == own, 1.0, 0.0)
        running = running + weights[lag : lag + 1, lanes] * ext[pl.ds(HALO - lag, q), lanes] * same
    return running


def scan_forward(
    q, taps, pairs, head,
    x_ref, small_ref, bct_ref, dcol_ref, drow_ref, w_ref, b_ref, sb_ref, rate_ref, skip_ref,
    y_ref, states_ref,
    state, ext, docs_ext, xs, xt, last_doc,
):
    c = pl.program_id(0)
    n = bct_ref.shape[0] // 2

    @pl.when(c == 0)
    def _():
        state[...] = jnp.zeros_like(state)
        ext[pl.ds(0, HALO), :] = jnp.zeros((HALO, ext.shape[1]), f32)
        docs_ext[pl.ds(0, HALO), :] = jnp.full((HALO, LANES), -1.0, f32)
        last_doc[...] = jnp.full(last_doc.shape, -1.0, f32)

    own = dcol_ref[...]
    ext[pl.ds(HALO, q), :] = x_ref[...].astype(f32)
    docs_ext[pl.ds(HALO, q), :] = own
    step, _, cum, _, causal = step_parts(small_ref[...] + sb_ref[...], rate_ref[...], q)
    step_t = step.T
    cum_t = cum.T
    end = cum[q - 1 : q, :]
    id_in = last_doc[0:1, :]
    final = own[q - 1 : q, :]
    linked = jnp.where(final == id_in, 1.0, 0.0)
    fade = linked * jnp.exp(end)
    entering = jnp.where(own == id_in, 1.0, 0.0) * jnp.exp(cum)
    to_end = jnp.where(own == final, 1.0, 0.0) * jnp.exp(end - cum) * step
    same_doc = jnp.broadcast_to(own[:, 0:1], (q, q)) == jnp.broadcast_to(drow_ref[0:1, :], (q, q))
    hide = jnp.where(jnp.logical_and(causal, same_doc), 0.0, NEG)
    bt = bct_ref[0:n, :]
    ct = bct_ref[n : 2 * n, :]
    scores = mm(ct, bt, TN)
    states_ref[0] = state[...]
    old = state[...].astype(bf16)
    wide = lane_iota((q, LANES)) < head
    wide_row = lane_iota((1, LANES)) < head
    for k in range(pairs):
        lanes = slice(k * LANES, (k + 1) * LANES)
        h0, h1 = 2 * k, 2 * k + 1
        conv = convolve(ext, docs_ext, own, w_ref, b_ref[:, lanes], lanes, q, taps)
        x = conv * sigmoid(conv)
        xd = x * spread(step, h0, h1, wide)
        xt[:, lanes] = (x * spread(to_end, h0, h1, wide)).astype(bf16)
        mats = []
        for h in (h0, h1):
            gap = cum[:, h : h + 1] - cum_t[h : h + 1, :] + hide
            mats.append((jnp.exp(gap) * scores).astype(bf16))
        out = mm(mats[0], jnp.where(wide, xd, 0.0).astype(bf16), NN)
        out = out + mm(mats[1], jnp.where(wide, 0.0, xd).astype(bf16), NN)
        out = out + mm(ct, old[:, lanes], TN) * spread(entering, h0, h1, wide)
        y_ref[:, lanes] = out + skip_ref[:, lanes] * x
    update = mm(bt, xt[...], NN)
    for k in range(pairs):
        lanes = slice(k * LANES, (k + 1) * LANES)
        state[:, lanes] = state[:, lanes] * spread(fade, 2 * k, 2 * k + 1, wide_row) + update[:, lanes]
    ext[pl.ds(0, HALO), :] = ext[pl.ds(q, HALO), :]
    docs_ext[pl.ds(0, HALO), :] = docs_ext[pl.ds(q, HALO), :]
    last_doc[...] = jnp.broadcast_to(final, last_doc.shape)


def scan_backward(
    q, taps, pairs, head, chunks,
    x_ref, xp_ref, small_ref, bct_ref, dcol_ref, dcolp_ref, drow_ref, w_ref, b_ref, sb_ref, rate_ref,
    skip_ref, dy_ref, states_ref,
    dx_ref, dsmall_ref, dbct_ref, dconv_ref, dhead_ref,
    dstate, ext, docs_ext, dcv, docs_after, dye, xt, col_t,
):
    step_at = pl.program_id(0)
    c = chunks - 1 - step_at
    n = bct_ref.shape[0] // 2
    width = x_ref.shape[1]

    @pl.when(step_at == 0)
    def _():
        dstate[...] = jnp.zeros_like(dstate)
        dcv[pl.ds(q, HALO), :] = jnp.zeros((HALO, width), f32)
        docs_after[pl.ds(q, HALO), :] = jnp.full((HALO, LANES), -1.0, f32)
        dconv_ref[...] = jnp.zeros_like(dconv_ref)
        dhead_ref[...] = jnp.zeros_like(dhead_ref)
        col_t[...] = jnp.zeros_like(col_t)

    first = c == 0
    own = dcol_ref[...]
    before = jnp.where(first, -1.0, dcolp_ref[...])
    ext[pl.ds(0, HALO), :] = xp_ref[...].astype(f32)
    ext[pl.ds(HALO, q), :] = x_ref[...].astype(f32)
    docs_ext[pl.ds(0, HALO), :] = before
    docs_ext[pl.ds(HALO, q), :] = own
    docs_after[pl.ds(0, q), :] = own
    raw = small_ref[...] + sb_ref[...]
    rate = rate_ref[...]
    step, decay, cum, tri, causal = step_parts(raw, rate, q)
    step_t = step.T
    cum_t = cum.T
    end = cum[q - 1 : q, :]
    id_in = before[HALO - 1 : HALO, :]
    final = own[q - 1 : q, :]
    linked = jnp.where(final == id_in, 1.0, 0.0)
    fade = linked * jnp.exp(end)
    entering = jnp.where(own == id_in, 1.0, 0.0) * jnp.exp(cum)
    tail = jnp.where(own == final, 1.0, 0.0) * jnp.exp(end - cum)
    to_end = tail * step
    same_doc = jnp.broadcast_to(own[:, 0:1], (q, q)) == jnp.broadcast_to(drow_ref[0:1, :], (q, q))
    hide = jnp.where(jnp.logical_and(causal, same_doc), 0.0, NEG)
    bt = bct_ref[0:n, :]
    ct = bct_ref[n : 2 * n, :]
    scores = mm(ct, bt, TN)
    old = states_ref[0].astype(bf16)
    after = dstate[...].astype(bf16)
    wide = lane_iota((q, LANES)) < head
    wide_row = lane_iota((1, LANES)) < head
    lane = lane_iota((q, LANES))
    d_scores = jnp.zeros((q, q), f32)
    rows = jnp.zeros((q, LANES), f32)
    d_enter = jnp.zeros((q, LANES), f32)
    d_toend = jnp.zeros((q, LANES), f32)
    d_fade = jnp.zeros((8, LANES), f32)
    part = lax.broadcasted_iota(jnp.int32, (LANES, LANES), 0) // head
    to = lane_iota((LANES, LANES))
    for k in range(pairs):
        lanes = slice(k * LANES, (k + 1) * LANES)
        h0, h1 = 2 * k, 2 * k + 1
        pick = jnp.where(part + 2 * k == to, 1.0, 0.0)
        conv = convolve(ext, docs_ext, own, w_ref, b_ref[:, lanes], lanes, q, taps)
        sig = sigmoid(conv)
        x = conv * sig
        xb = x.astype(bf16)
        dy = dy_ref[:, lanes]
        halves = (jnp.where(wide, dy, 0.0).astype(bf16), jnp.where(wide, 0.0, dy).astype(bf16))
        dxd = jnp.zeros((q, LANES), f32)
        for h, half in ((h0, halves[0]), (h1, halves[1])):
            inner = mm(half, xb, NT)
            keep = jnp.exp(cum[:, h : h + 1] - cum_t[h : h + 1, :] + hide)
            grown = keep * inner
            mat = keep * scores
            dt = step_t[h : h + 1, :]
            g = grown * scores
            d_scores = d_scores + grown * dt
            rows = jnp.where(lane == h, jnp.sum(g * dt, axis=1, keepdims=True), rows)
            col_t[h : h + 1, :] = jnp.sum(g, axis=0, keepdims=True)
            dxd = dxd + mm(mat.astype(bf16), half, TN)
        v = mm(bt, after[:, lanes], TN)
        u = mm(ct, old[:, lanes], TN)
        enter_k = spread(entering, h0, h1, wide)
        end_k = spread(to_end, h0, h1, wide)
        d_enter = d_enter + exact(dy * u, pick, NN)
        d_toend = d_toend + exact(x * v, pick, NN)
        hh = jnp.sum(dstate[:, lanes] * states_ref[0, :, lanes], axis=0, keepdims=True)
        d_fade = d_fade + exact(jnp.broadcast_to(hh, (8, LANES)), pick, NN)
        dye[:, lanes] = (dy * enter_k).astype(bf16)
        xt[:, lanes] = (x * end_k).astype(bf16)
        dx = dxd * spread(step, h0, h1, wide) + end_k * v + skip_ref[:, lanes] * dy
        dconv = dx * (sig * (1.0 + conv * (1.0 - sig)))
        dcv[pl.ds(0, q), lanes] = dconv
        sums = [jnp.sum(dconv * ext[pl.ds(HALO, q), lanes], axis=0, keepdims=True)]
        dxin = w_ref[0:1, lanes] * dconv
        for lag in range(1, taps):
            same = jnp.where(docs_ext[pl.ds(HALO - lag, q), :] == own, 1.0, 0.0)
            sums.append(jnp.sum(dconv * same * ext[pl.ds(HALO - lag, q), lanes], axis=0, keepdims=True))
            follow = jnp.where(docs_after[pl.ds(lag, q), :] == own, 1.0, 0.0)
            dxin = dxin + w_ref[lag : lag + 1, lanes] * dcv[pl.ds(lag, q), lanes] * follow
        sums.append(jnp.sum(dconv, axis=0, keepdims=True))
        sums.append(jnp.sum(dy * x, axis=0, keepdims=True))
        dx_ref[:, lanes] = dxin.astype(bf16)
        for i, s in enumerate(sums):
            dconv_ref[i : i + 1, lanes] = dconv_ref[i : i + 1, lanes] + s
    dsb = d_scores.astype(bf16)
    dbct_ref[0:n, :] = mm(ct, dsb, NN) + mm(after, xt[...], NT)
    dbct_ref[n : 2 * n, :] = mm(bt, dsb, NT) + mm(old, dye[...], NT)
    new = mm(ct, dye[...], NN)
    for k in range(pairs):
        lanes = slice(k * LANES, (k + 1) * LANES)
        dstate[:, lanes] = dstate[:, lanes] * spread(fade, 2 * k, 2 * k + 1, wide_row) + new[:, lanes]
    cols = col_t[...].T
    pulled = d_toend * to_end
    at_end = jnp.sum(pulled, axis=0, keepdims=True) + fade * d_fade[0:1, :]
    d_cum = rows - step * cols + d_enter * entering - pulled
    last_row = lax.broadcasted_iota(jnp.int32, (q, LANES), 0) == q - 1
    d_cum = d_cum + jnp.where(last_row, at_end, 0.0)
    d_decay = exact(tri, d_cum, TN)
    d_step = cols + d_toend * tail - rate * d_decay
    d_raw = d_step * sigmoid(raw)
    dsmall_ref[...] = d_raw
    dhead_ref[0:1, :] = dhead_ref[0:1, :] + jnp.sum(d_raw, axis=0, keepdims=True)
    dhead_ref[1:2, :] = dhead_ref[1:2, :] + jnp.sum(d_decay * decay, axis=0, keepdims=True)
    dcv[pl.ds(q, HALO), :] = dcv[pl.ds(0, HALO), :]
    docs_after[pl.ds(q, HALO), :] = docs_after[pl.ds(0, HALO), :]


def whole(array):
    return pl.BlockSpec(array.shape, lambda c: (0,) * array.ndim)


def run_forward(q, x_in, small, bct, dcol, drow, conv_w, conv_b, sb, rate, skip, head):
    tokens, width = x_in.shape
    n = bct.shape[0] // 2
    chunks = tokens // q
    pairs = width // LANES
    taps = conv_w.shape[0]
    return pl.pallas_call(
        functools.partial(scan_forward, q, taps, pairs, head),
        grid=(chunks,),
        in_specs=[
            pl.BlockSpec((q, width), lambda c: (c, 0)),
            pl.BlockSpec((q, LANES), lambda c: (c, 0)),
            pl.BlockSpec((2 * n, q), lambda c: (0, c)),
            pl.BlockSpec((q, LANES), lambda c: (c, 0)),
            pl.BlockSpec((8, q), lambda c: (0, c)),
            whole(conv_w), whole(conv_b), whole(sb), whole(rate), whole(skip),
        ],
        out_specs=[
            pl.BlockSpec((q, width), lambda c: (c, 0)),
            pl.BlockSpec((1, n, width), lambda c: (c, 0, 0)),
        ],
        out_shape=[
            jax.ShapeDtypeStruct((tokens, width), f32),
            jax.ShapeDtypeStruct((chunks, n, width), f32),
        ],
        scratch_shapes=[
            pltpu.VMEM((n, width), f32),
            pltpu.VMEM((HALO + q, width), f32),
            pltpu.VMEM((HALO + q, LANES), f32),
            pltpu.VMEM((8, LANES), f32),
            pltpu.VMEM((q, width), bf16),
            pltpu.VMEM((8, LANES), f32),
        ],
        name="scan_forward",
    )(x_in, small, bct, dcol, drow, conv_w, conv_b, sb, rate, skip)


def run_backward(q, x_in, small, bct, dcol, drow, conv_w, conv_b, sb, rate, skip, dy, states, head):
    tokens, width = x_in.shape
    n = bct.shape[0] // 2
    chunks = tokens // q
    pairs = width // LANES
    taps = conv_w.shape[0]
    per = q // HALO

    def at(c):
        return chunks - 1 - c

    def prior(c):
        return jnp.maximum((chunks - 1 - c) * per - 1, 0)

    return pl.pallas_call(
        functools.partial(scan_backward, q, taps, pairs, head, chunks),
        grid=(chunks,),
        in_specs=[
            pl.BlockSpec((q, width), lambda c: (at(c), 0)),
            pl.BlockSpec((HALO, width), lambda c: (prior(c), 0)),
            pl.BlockSpec((q, LANES), lambda c: (at(c), 0)),
            pl.BlockSpec((2 * n, q), lambda c: (0, at(c))),
            pl.BlockSpec((q, LANES), lambda c: (at(c), 0)),
            pl.BlockSpec((HALO, LANES), lambda c: (prior(c), 0)),
            pl.BlockSpec((8, q), lambda c: (0, at(c))),
            whole(conv_w), whole(conv_b), whole(sb), whole(rate), whole(skip),
            pl.BlockSpec((q, width), lambda c: (at(c), 0)),
            pl.BlockSpec((1, n, width), lambda c: (at(c), 0, 0)),
        ],
        out_specs=[
            pl.BlockSpec((q, width), lambda c: (at(c), 0)),
            pl.BlockSpec((q, LANES), lambda c: (at(c), 0)),
            pl.BlockSpec((2 * n, q), lambda c: (0, at(c))),
            pl.BlockSpec((8, width), lambda c: (0, 0)),
            pl.BlockSpec((8, LANES), lambda c: (0, 0)),
        ],
        out_shape=[
            jax.ShapeDtypeStruct((tokens, width), bf16),
            jax.ShapeDtypeStruct((tokens, LANES), f32),
            jax.ShapeDtypeStruct((2 * n, tokens), f32),
            jax.ShapeDtypeStruct((8, width), f32),
            jax.ShapeDtypeStruct((8, LANES), f32),
        ],
        scratch_shapes=[
            pltpu.VMEM((n, width), f32),
            pltpu.VMEM((HALO + q, width), f32),
            pltpu.VMEM((HALO + q, LANES), f32),
            pltpu.VMEM((q + HALO, width), f32),
            pltpu.VMEM((q + HALO, LANES), f32),
            pltpu.VMEM((q, width), bf16),
            pltpu.VMEM((q, width), bf16),
            pltpu.VMEM((LANES, q), f32),
        ],
        name="scan_backward",
    )(x_in, x_in, small, bct, dcol, dcol, drow, conv_w, conv_b, sb, rate, skip, dy, states)


def swapped(block, bit):
    size = lax.axis_size("seq")
    return lax.ppermute(block, "seq", [(i, i ^ bit) for i in range(size)])


def bits_of(size):
    bits, bit = [], 1
    while bit < size:
        bits.append(bit)
        bit *= 2
    return bits


def joined_by(held, bit):
    other = swapped(held, bit)
    upper = (lax.axis_index("seq") & bit) != 0
    both = jnp.where(upper, jnp.stack([other, held], axis=1), jnp.stack([held, other], axis=1))
    return both.reshape((-1,) + both.shape[2:])


def opened(block):
    bits = bits_of(lax.axis_size("seq"))
    return joined_by(block[None], bits[-1]) if bits else block[None]


def gathered(block, held=None):
    held = opened(block) if held is None else held
    for bit in reversed(bits_of(lax.axis_size("seq"))[:-1]):
        held = joined_by(held, bit)
    return held.reshape((-1,) + held.shape[2:])


def scattered(parts, between=lambda held: held):
    index = lax.axis_index("seq")
    size = lax.axis_size("seq")
    rest = parts.shape[1:]
    lead = parts.shape[0]
    held = parts.reshape((size, lead // size) + rest)
    for bit in bits_of(size):
        half = held.reshape((held.shape[0] // 2, 2) + held.shape[1:])
        upper = (index & bit) != 0
        mine = jnp.where(upper, half[:, 1], half[:, 0])
        theirs = jnp.where(upper, half[:, 0], half[:, 1]).astype(bf16)
        held = between(mine.astype(f32) + swapped(theirs, bit).astype(f32))
    return held[0]


def summed(block, between):
    count = lax.axis_size("dp")
    for bit in reversed(bits_of(count)):
        if bit == 1:
            block = between(block)
        block = block + lax.ppermute(block, "dp", [(i, i ^ bit) for i in range(count)])
    return block


def moved_by(block, step):
    count = lax.axis_size("dp")
    route = [(i, i + 2 * step) for i in range(count) if 0 <= i + 2 * step < count]
    return lax.ppermute(block, "dp", route)


def crossed(block, bits):
    return lax.ppermute(block, "dp", [(i, i ^ bits) for i in range(lax.axis_size("dp"))])


def gathered_rows(block, waits):
    count = lax.axis_size("dp")
    length = count // 2
    if not is_small(count):
        return lax.all_gather(block, "dp", axis=0, tiled=True), block
    at = lax.axis_index("dp")
    place, side = at // 2, at % 2
    rows = block.shape[0]
    whole_rows = jnp.zeros((count * rows, block.shape[1]), block.dtype)

    def put(into, piece, pair, half):
        return lax.dynamic_update_slice(into, piece, ((pair * 2 + half) * rows, 0))

    whole_rows = put(whole_rows, block, place, side)
    other = crossed(block, 1)
    whole_rows = put(whole_rows, other, place, 1 - side)
    up, down, ready = block, block, []
    for hop in range(1, length):
        up, down = after((moved_by(up, 1), moved_by(down, -1)), (other, waits[hop - 1 : hop]))
        ready.append((down, up))
        piece, pair = None, None
        for spot in range(length):
            near = min(spot, length - 1 - spot)
            if hop <= 2 * near:
                away, from_below = (hop + 1) // 2, hop % 2 == 0
            else:
                away, from_below = hop - near, spot > length - 1 - spot
            chosen = ready[away - 1][1 if from_below else 0]
            source = spot - away if from_below else spot + away
            here = place == spot
            piece = chosen if piece is None else jnp.where(here, chosen, piece)
            pair = source if pair is None else jnp.where(here, source, pair)
        whole_rows = put(whole_rows, piece, pair, side)
        other = crossed(piece, 1)
        whole_rows = put(whole_rows, other, pair, 1 - side)
    return whole_rows, ready[min(1, length - 2)]


def is_small(count):
    return count <= 8 and count & (count - 1) == 0


def halved_rows(term):
    count = lax.axis_size("dp")
    if not is_small(count):
        return term
    at = lax.axis_index("dp")
    pairs = term.reshape(count // 2, 2, -1, term.shape[1])

    def side(which):
        return lax.dynamic_index_in_dim(pairs, which, 1, keepdims=False)

    came = crossed(side((at & 1) ^ 1), 1)
    return (side(at & 1).astype(f32) + came.astype(f32)).astype(bf16)


def shared_rows(lines):
    count = lax.axis_size("dp")
    if not is_small(count):
        return [lax.psum_scatter(lines, "dp", scatter_dimension=0, tiled=True)]
    at = lax.axis_index("dp")

    def part(owner):
        return lax.dynamic_index_in_dim(lines, owner // 2, 0, keepdims=False)

    return [part(at)] + [crossed(part(at ^ bits), bits) for bits in range(2, count, 2)]


def after(value, other):
    return lax.optimization_barrier((value, other))[0]


def turned(blocks):
    size = lax.axis_size("seq")
    index = lax.axis_index("seq")
    if size & (size - 1):
        return lax.all_to_all(blocks, "seq", 0, 0, tiled=True)
    out = blocks
    for bits in range(1, size):
        piece = lax.dynamic_slice_in_dim(blocks, index ^ bits, 1, 0)
        piece = lax.ppermute(piece, "seq", [(i, i ^ bits) for i in range(size)])
        out = lax.dynamic_update_slice_in_dim(out, piece, index ^ bits, 0)
    return out


def folded(rows, lead, width):
    cut = rows.reshape(lead, rows.shape[0] // lead, rows.shape[1] // width, width)
    cut = cut.transpose(0, 2, 1, 3).reshape(lead, -1, width)
    return cut[0] if lead == 1 else cut


def unfolded(pieces, width):
    lead, stacked, narrow = pieces.shape
    cut = pieces.reshape(lead, width // narrow, stacked * narrow // width, narrow)
    return cut.transpose(0, 2, 1, 3).reshape(-1, width)


def exchanged(parts):
    size = lax.axis_size("seq")
    index = lax.axis_index("seq")
    held = parts.reshape((size, -1) + parts.shape[1:])

    def part(owner):
        return lax.dynamic_index_in_dim(held, owner, 0, keepdims=False)

    came = [
        lax.ppermute(part(index ^ bits).astype(bf16), "seq", [(i, i ^ bits) for i in range(size)])
        for bits in range(1, size)
    ]
    return sum([piece.astype(f32) for piece in came], part(index))


def by_rows(array):
    return with_layout_constraint(array, Layout(major_to_minor=(0, 1)))


def padded(rows, width):
    return jnp.pad(rows, ((0, 0), (0, width - rows.shape[1])))


def shards(
    hidden, segments, cotangent, norm_gain, in_weight, conv_weight, conv_bias, step_bias, log_rate,
    skip_gain, gate_gain, out_weight,
):
    n_seqs, block, n_width = hidden.shape
    size = lax.axis_size("seq")
    groups = lax.axis_size("dp")
    index = lax.axis_index("seq")
    tokens = size * block
    n_inner = gate_gain.shape[0]
    n_heads = step_bias.shape[0]
    n_taps = conv_weight.shape[0]
    n_mixed = conv_bias.shape[0]
    n_state = (n_mixed - n_inner) // 2
    head = n_inner // n_heads
    own_inner = n_inner // size
    own_heads = n_heads // size
    own_bc = 2 * n_state // size
    q = min(128, block)
    in_rows = in_weight.shape[0]

    in_low = in_weight.astype(bf16)
    z_cols = in_low[:, :n_inner].reshape(in_rows, size, own_inner)
    x_cols = in_low[:, n_inner : 2 * n_inner].reshape(in_rows, size, own_inner)
    bc_cols = in_low[:, 2 * n_inner : n_inner + n_mixed].reshape(in_rows, size, own_bc)
    dt_cols = in_low[:, n_inner + n_mixed :].reshape(in_rows, size, own_heads)
    gap = jnp.zeros((in_rows, size, LANES - own_heads - own_bc), bf16)
    laid = jnp.concatenate([x_cols, dt_cols, gap, bc_cols, z_cols], axis=2).transpose(1, 0, 2)
    mine = lax.all_to_all(laid, "seq", 0, 0, tiled=True)
    flat = hidden.reshape(block, n_width).astype(f32)
    inv = lax.rsqrt(jnp.mean(flat * flat, axis=-1, keepdims=True) + epsilon)
    unit = flat * inv
    normed_own = (unit * norm_gain).astype(bf16)
    docs = gathered(segments).reshape(tokens).astype(f32)
    order = [(f, (f % groups) * size + f // groups) for f in range(groups * size)]
    back = [(b, a) for a, b in order]
    out_moved = lax.ppermute(out_weight.astype(bf16), ("dp", "seq"), order)
    mine, normed_own = lax.optimization_barrier((after(mine, (docs, out_moved)), normed_own))
    mine = mine.reshape(size * in_rows, -1)
    n_first = own_inner + LANES
    cot_own = cotangent.reshape(block, n_width)
    normed_held = opened(normed_own)
    cot_held = opened(after(cot_own, mine))
    w_first, hopped = gathered_rows(mine[:, :n_first], [normed_held, cot_held])
    z_block = jnp.concatenate([mine[:, n_first:], folded(out_moved, 1, own_inner)], axis=0)

    normed = gathered(normed_own, normed_held)
    joined = lax.all_gather(after(z_block, hopped), "dp", axis=0, tiled=True).reshape(groups, -1, own_inner)
    z_rows = size * in_rows
    w_z = joined[:, :z_rows].reshape(-1, own_inner)
    w_out = unfolded(joined[:, z_rows:], n_width)
    cot = gathered(cot_own, cot_held)
    dcol = jnp.broadcast_to(docs[:, None], (tokens, LANES))
    drow = jnp.broadcast_to(docs[None, :], (8, tokens))

    def own_part(vector, parts):
        return lax.dynamic_slice_in_dim(vector, index * parts, parts, vector.ndim - 1)

    w_x, w_small = w_first[:, :own_inner], w_first[:, own_inner:]
    small = mm(normed, w_small, NN)
    x_in = mm(normed, w_x, NN).astype(bf16)
    z = mm(normed, w_z, NN)
    conv_x = own_part(conv_weight[:, :n_inner], own_inner)
    bias_x = own_part(conv_bias[None, :n_inner], own_inner)
    conv_bc = own_part(conv_weight[:, n_inner:], own_bc)
    bias_bc = own_part(conv_bias[None, n_inner:], own_bc)
    sb = padded(own_part(step_bias[None], own_heads), LANES)
    rate = padded(jnp.exp(own_part(log_rate[None], own_heads)), LANES)
    skip = jnp.repeat(own_part(skip_gain[None], own_heads), head, axis=1)
    gain = own_part(gate_gain[None], own_inner)

    head_lanes = jnp.arange(LANES) < own_heads
    bc_in = small[:, LANES - own_bc :].astype(bf16).astype(f32)
    small_dt = jnp.where(head_lanes, small, 0.0)

    def earlier(rows, lag):
        return jnp.pad(rows, ((lag, 0), (0, 0)))[:tokens]

    def later(rows, lag):
        return jnp.pad(rows, ((0, lag), (0, 0)))[lag:]

    same = [None] + [
        jnp.where(jnp.pad(docs, (lag, 0), constant_values=-1.0)[:tokens] == docs, 1.0, 0.0)[:, None]
        for lag in range(1, n_taps)
    ]
    bc_conv = bias_bc + conv_bc[0:1] * bc_in
    for lag in range(1, n_taps):
        bc_conv = bc_conv + conv_bc[lag : lag + 1] * earlier(bc_in, lag) * same[lag]
    bc_sig = jax.nn.sigmoid(bc_conv)
    bct = gathered(by_rows((bc_conv * bc_sig).astype(bf16).T))

    y, states = run_forward(
        q, x_in, small_dt, bct, dcol, drow, conv_x, bias_x, sb, rate, skip, head
    )

    d_gn = mm(cot, w_out, NT)
    z_sig = jax.nn.sigmoid(z)
    z_act = z * z_sig
    gated = y * z_act
    scaled = d_gn * gain
    both = jnp.stack([jnp.sum(gated * gated, axis=1), jnp.sum(scaled * gated, axis=1)])
    both = lax.psum(both, "seq")
    g_inv = lax.rsqrt(both[0] / n_inner + epsilon)[:, None]
    g_dot = both[1][:, None] / n_inner
    gate_low = (gated * g_inv * gain).astype(bf16)
    d_gated = g_inv * scaled - gated * (g_inv * g_inv * g_inv * g_dot)
    d_gain = jnp.sum(d_gn * gated * g_inv, axis=0)
    d_z = (d_gated * y * (z_sig * (1.0 + z * (1.0 - z_sig)))).astype(bf16)
    d_y = d_gated * z_act

    terms = [mm(normed, d_z, TN)]
    for k in range(0, n_width, own_inner):
        terms.append(mm(gate_low, cot[:, k : k + own_inner], TN))
    terms = [term.astype(bf16).reshape(groups, -1, own_inner) for term in terms]
    terms = jnp.concatenate(terms, axis=1).reshape(-1, own_inner)
    terms, d_y = lax.optimization_barrier((terms, d_y))
    parts = lax.psum_scatter(terms, "dp", scatter_dimension=0, tiled=True)

    d_x, d_dt, d_bct, d_conv_x, d_heads = run_backward(
        q, x_in, small_dt, bct, dcol, drow, conv_x, bias_x, sb, rate, skip, d_y, states, head
    )
    x_term = mm(normed, d_x, TN).astype(bf16)
    x_term, d_bct = lax.optimization_barrier((x_term, d_bct))
    x_lines = halved_rows(x_term)
    d_bc = by_rows(exchanged(d_bct)).T
    d_bcc = d_bc * (bc_sig * (1.0 + bc_conv * (1.0 - bc_sig)))
    d_bc_in = conv_bc[0:1] * d_bcc
    w_sums = [jnp.sum(d_bcc * bc_in, axis=0)]
    for lag in range(1, n_taps):
        held = d_bcc * same[lag]
        d_bc_in = d_bc_in + conv_bc[lag : lag + 1] * later(held, lag)
        w_sums.append(jnp.sum(held * earlier(bc_in, lag), axis=0))
    w_sums.append(jnp.sum(d_bcc, axis=0))
    d_small = jnp.concatenate([d_dt[:, : LANES - own_bc], d_bc_in], axis=1).astype(bf16)
    d_first = jnp.concatenate([d_x, d_small], axis=1)
    small_lines = halved_rows(mm(normed, d_small, TN).astype(bf16))
    branch = scattered(mm(gate_low, w_out, NN).astype(bf16))
    result = (flat + branch).reshape(n_seqs, block, n_width).astype(bf16)
    d_normed = mm(d_first, w_first, NT) + mm(d_z, w_z, NT)
    d_norm_gain = jnp.sum(d_normed * normed.astype(f32), axis=0) / norm_gain
    d_skip = jnp.sum(d_conv_x[n_taps + 1].reshape(own_heads, head), axis=1)
    packed = jnp.concatenate(
        [
            d_conv_x[: n_taps + 1].reshape(-1),
            jnp.stack(w_sums).reshape(-1),
            d_gain,
            d_heads[0, :own_heads],
            d_heads[1, :own_heads],
            d_skip,
            d_norm_gain,
        ]
    )
    lines = jnp.concatenate([x_lines, small_lines], axis=-1)
    packed = gathered(summed(packed, lambda held: after(held, lines))[None])
    shares = shared_rows(lines)
    parts = after(parts, (lines, result))
    d_norm = after(d_normed.astype(bf16), parts)
    d_norm = lax.psum_scatter(d_norm, "seq", scatter_dimension=0, tiled=True).astype(f32)

    def own_rows(part):
        out = turned(part.reshape(size, in_rows, -1))
        return out.transpose(1, 0, 2).astype(f32)

    out_part = unfolded(parts[None, z_rows:], n_width)
    d_out_weight = lax.ppermute(out_part, ("dp", "seq"), back).astype(f32)
    in_z = own_rows(parts[:z_rows])
    shares = after(shares, (in_z, d_out_weight))
    first_part = sum(share.astype(f32) for share in shares)
    in_first = own_rows(first_part.astype(bf16))
    d_in_weight = jnp.concatenate(
        [
            in_z.reshape(in_rows, n_inner),
            in_first[:, :, :own_inner].reshape(in_rows, n_inner),
            in_first[:, :, n_first - own_bc :].reshape(in_rows, 2 * n_state),
            in_first[:, :, own_inner : own_inner + own_heads].reshape(in_rows, n_heads),
        ],
        axis=1,
    )

    lifted = d_norm * norm_gain
    d_flat = inv * lifted - flat * (
        inv * inv * inv * jnp.mean(lifted * flat, axis=-1, keepdims=True)
    )
    d_hidden = (cot_own.astype(f32) + d_flat).reshape(n_seqs, block, n_width)

    at = 0

    def take(count):
        nonlocal at
        at += count
        return packed[:, at - count : at]

    got_x = take((n_taps + 1) * own_inner).reshape(size, n_taps + 1, own_inner)
    got_bc = take((n_taps + 1) * own_bc).reshape(size, n_taps + 1, own_bc)
    got_x = got_x.transpose(1, 0, 2).reshape(n_taps + 1, n_inner)
    got_bc = got_bc.transpose(1, 0, 2).reshape(n_taps + 1, 2 * n_state)
    conv_all = jnp.concatenate([got_x, got_bc], axis=1)
    d_gate_gain = take(own_inner).reshape(n_inner)
    d_step_bias = take(own_heads).reshape(n_heads)
    d_log_rate = take(own_heads).reshape(n_heads)
    d_skip_gain = take(own_heads).reshape(n_heads)
    d_norm_all = jnp.sum(take(n_width), axis=0)
    return (
        result,
        d_hidden,
        d_norm_all,
        d_in_weight,
        conv_all[:n_taps],
        conv_all[n_taps],
        d_step_bias,
        d_log_rate,
        d_skip_gain,
        d_gate_gain,
        d_out_weight,
    )


def solution(mesh):
    tokens = P("dp", "seq", None)
    rows = P(("dp", "seq"), None)
    return jax.shard_map(
        shards,
        mesh=mesh,
        in_specs=(tokens, P("dp", "seq"), tokens, P(), rows, P(), P(), P(), P(), P(), P(), rows),
        out_specs=(tokens, tokens, P(), rows, P(), P(), P(), P(), P(), P(), rows),
        check_vma=False,
    )
```

```python
import functools

import jax
import jax.numpy as jnp
from jax import lax
from jax.experimental import pallas as pl
from jax.experimental.layout import Layout, with_layout_constraint
from jax.experimental.pallas import tpu as pltpu
from jax.sharding import PartitionSpec as P

epsilon = 1e-05
highest = lax.Precision.HIGHEST
f32 = jnp.float32
bf16 = jnp.bfloat16
LANES = 128
HALO = 16
NEG = -1e30


def mm(a, b, dims, out=f32):
    return lax.dot_general(a, b, (dims, ((), ())), preferred_element_type=out)


NN = ((1,), (0,))
NT = ((1,), (1,))
TN = ((0,), (0,))


def exact(a, b, dims):
    return lax.dot_general(a, b, (dims, ((), ())), precision=highest, preferred_element_type=f32)


def softplus(v):
    return jnp.maximum(v, 0.0) + jnp.log1p(jnp.exp(-jnp.abs(v)))


def sigmoid(v):
    return 1.0 / (1.0 + jnp.exp(-v))


def lane_iota(shape):
    return lax.broadcasted_iota(jnp.int32, shape, len(shape) - 1)


def spread(columns, first, second, wide):
    rows = columns.shape[0]
    left = jnp.broadcast_to(columns[:, first : first + 1], (rows, LANES))
    right = jnp.broadcast_to(columns[:, second : second + 1], (rows, LANES))
    return jnp.where(wide, left, right)


def step_parts(raw, rate, q):
    row = lax.broadcasted_iota(jnp.int32, (q, q), 0)
    col = lax.broadcasted_iota(jnp.int32, (q, q), 1)
    tri = jnp.where(row >= col, 1.0, 0.0).astype(f32)
    step = softplus(raw)
    decay = -step * rate
    total = exact(tri, decay, NN)
    return step, decay, total, tri, row >= col


def convolve(ext, docs_ext, own, weights, bias, lanes, q, taps):
    running = bias + weights[0:1, lanes] * ext[pl.ds(HALO, q), lanes]
    for lag in range(1, taps):
        same = jnp.where(docs_ext[pl.ds(HALO - lag, q), :] == own, 1.0, 0.0)
        running = running + weights[lag : lag + 1, lanes] * ext[pl.ds(HALO - lag, q), lanes] * same
    return running


def scan_forward(
    q, taps, pairs, head,
    x_ref, small_ref, bct_ref, dcol_ref, drow_ref, w_ref, b_ref, sb_ref, rate_ref, skip_ref,
    y_ref, states_ref,
    state, ext, docs_ext, xs, xt, last_doc,
):
    c = pl.program_id(0)
    n = bct_ref.shape[0] // 2

    @pl.when(c == 0)
    def _():
        state[...] = jnp.zeros_like(state)
        ext[pl.ds(0, HALO), :] = jnp.zeros((HALO, ext.shape[1]), f32)
        docs_ext[pl.ds(0, HALO), :] = jnp.full((HALO, LANES), -1.0, f32)
        last_doc[...] = jnp.full(last_doc.shape, -1.0, f32)

    own = dcol_ref[...]
    ext[pl.ds(HALO, q), :] = x_ref[...].astype(f32)
    docs_ext[pl.ds(HALO, q), :] = own
    step, _, cum, _, causal = step_parts(small_ref[...] + sb_ref[...], rate_ref[...], q)
    step_t = step.T
    cum_t = cum.T
    end = cum[q - 1 : q, :]
    id_in = last_doc[0:1, :]
    final = own[q - 1 : q, :]
    linked = jnp.where(final == id_in, 1.0, 0.0)
    fade = linked * jnp.exp(end)
    entering = jnp.where(own == id_in, 1.0, 0.0) * jnp.exp(cum)
    to_end = jnp.where(own == final, 1.0, 0.0) * jnp.exp(end - cum) * step
    same_doc = jnp.broadcast_to(own[:, 0:1], (q, q)) == jnp.broadcast_to(drow_ref[0:1, :], (q, q))
    hide = jnp.where(jnp.logical_and(causal, same_doc), 0.0, NEG)
    bt = bct_ref[0:n, :]
    ct = bct_ref[n : 2 * n, :]
    scores = mm(ct, bt, TN)
    states_ref[0] = state[...]
    old = state[...].astype(bf16)
    wide = lane_iota((q, LANES)) < head
    wide_row = lane_iota((1, LANES)) < head
    for k in range(pairs):
        lanes = slice(k * LANES, (k + 1) * LANES)
        h0, h1 = 2 * k, 2 * k + 1
        conv = convolve(ext, docs_ext, own, w_ref, b_ref[:, lanes], lanes, q, taps)
        x = conv * sigmoid(conv)
        xd = x * spread(step, h0, h1, wide)
        xt[:, lanes] = (x * spread(to_end, h0, h1, wide)).astype(bf16)
        mats = []
        for h in (h0, h1):
            gap = cum[:, h : h + 1] - cum_t[h : h + 1, :] + hide
            mats.append((jnp.exp(gap) * scores).astype(bf16))
        out = mm(mats[0], jnp.where(wide, xd, 0.0).astype(bf16), NN)
        out = out + mm(mats[1], jnp.where(wide, 0.0, xd).astype(bf16), NN)
        out = out + mm(ct, old[:, lanes], TN) * spread(entering, h0, h1, wide)
        y_ref[:, lanes] = out + skip_ref[:, lanes] * x
    update = mm(bt, xt[...], NN)
    for k in range(pairs):
        lanes = slice(k * LANES, (k + 1) * LANES)
        state[:, lanes] = state[:, lanes] * spread(fade, 2 * k, 2 * k + 1, wide_row) + update[:, lanes]
    ext[pl.ds(0, HALO), :] = ext[pl.ds(q, HALO), :]
    docs_ext[pl.ds(0, HALO), :] = docs_ext[pl.ds(q, HALO), :]
    last_doc[...] = jnp.broadcast_to(final, last_doc.shape)


def scan_backward(
    q, taps, pairs, head, chunks,
    x_ref, xp_ref, small_ref, bct_ref, dcol_ref, dcolp_ref, drow_ref, w_ref, b_ref, sb_ref, rate_ref,
    skip_ref, dy_ref, states_ref,
    dx_ref, dsmall_ref, dbct_ref, dconv_ref, dhead_ref,
    dstate, ext, docs_ext, dcv, docs_after, dye, xt, col_t,
):
    step_at = pl.program_id(0)
    c = chunks - 1 - step_at
    n = bct_ref.shape[0] // 2
    width = x_ref.shape[1]

    @pl.when(step_at == 0)
    def _():
        dstate[...] = jnp.zeros_like(dstate)
        dcv[pl.ds(q, HALO), :] = jnp.zeros((HALO, width), f32)
        docs_after[pl.ds(q, HALO), :] = jnp.full((HALO, LANES), -1.0, f32)
        dconv_ref[...] = jnp.zeros_like(dconv_ref)
        dhead_ref[...] = jnp.zeros_like(dhead_ref)
        col_t[...] = jnp.zeros_like(col_t)

    first = c == 0
    own = dcol_ref[...]
    before = jnp.where(first, -1.0, dcolp_ref[...])
    ext[pl.ds(0, HALO), :] = xp_ref[...].astype(f32)
    ext[pl.ds(HALO, q), :] = x_ref[...].astype(f32)
    docs_ext[pl.ds(0, HALO), :] = before
    docs_ext[pl.ds(HALO, q), :] = own
    docs_after[pl.ds(0, q), :] = own
    raw = small_ref[...] + sb_ref[...]
    rate = rate_ref[...]
    step, decay, cum, tri, causal = step_parts(raw, rate, q)
    step_t = step.T
    cum_t = cum.T
    end = cum[q - 1 : q, :]
    id_in = before[HALO - 1 : HALO, :]
    final = own[q - 1 : q, :]
    linked = jnp.where(final == id_in, 1.0, 0.0)
    fade = linked * jnp.exp(end)
    entering = jnp.where(own == id_in, 1.0, 0.0) * jnp.exp(cum)
    tail = jnp.where(own == final, 1.0, 0.0) * jnp.exp(end - cum)
    to_end = tail * step
    same_doc = jnp.broadcast_to(own[:, 0:1], (q, q)) == jnp.broadcast_to(drow_ref[0:1, :], (q, q))
    hide = jnp.where(jnp.logical_and(causal, same_doc), 0.0, NEG)
    bt = bct_ref[0:n, :]
    ct = bct_ref[n : 2 * n, :]
    scores = mm(ct, bt, TN)
    old = states_ref[0].astype(bf16)
    after = dstate[...].astype(bf16)
    wide = lane_iota((q, LANES)) < head
    wide_row = lane_iota((1, LANES)) < head
    lane = lane_iota((q, LANES))
    d_scores = jnp.zeros((q, q), f32)
    rows = jnp.zeros((q, LANES), f32)
    d_enter = jnp.zeros((q, LANES), f32)
    d_toend = jnp.zeros((q, LANES), f32)
    d_fade = jnp.zeros((8, LANES), f32)
    part = lax.broadcasted_iota(jnp.int32, (LANES, LANES), 0) // head
    to = lane_iota((LANES, LANES))
    for k in range(pairs):
        lanes = slice(k * LANES, (k + 1) * LANES)
        h0, h1 = 2 * k, 2 * k + 1
        pick = jnp.where(part + 2 * k == to, 1.0, 0.0)
        conv = convolve(ext, docs_ext, own, w_ref, b_ref[:, lanes], lanes, q, taps)
        sig = sigmoid(conv)
        x = conv * sig
        xb = x.astype(bf16)
        dy = dy_ref[:, lanes]
        halves = (jnp.where(wide, dy, 0.0).astype(bf16), jnp.where(wide, 0.0, dy).astype(bf16))
        dxd = jnp.zeros((q, LANES), f32)
        for h, half in ((h0, halves[0]), (h1, halves[1])):
            inner = mm(half, xb, NT)
            keep = jnp.exp(cum[:, h : h + 1] - cum_t[h : h + 1, :] + hide)
            grown = keep * inner
            mat = keep * scores
            dt = step_t[h : h + 1, :]
            g = grown * scores
            d_scores = d_scores + grown * dt
            rows = jnp.where(lane == h, jnp.sum(g * dt, axis=1, keepdims=True), rows)
            col_t[h : h + 1, :] = jnp.sum(g, axis=0, keepdims=True)
            dxd = dxd + mm(mat.astype(bf16), half, TN)
        v = mm(bt, after[:, lanes], TN)
        u = mm(ct, old[:, lanes], TN)
        enter_k = spread(entering, h0, h1, wide)
        end_k = spread(to_end, h0, h1, wide)
        d_enter = d_enter + exact(dy * u, pick, NN)
        d_toend = d_toend + exact(x * v, pick, NN)
        hh = jnp.sum(dstate[:, lanes] * states_ref[0, :, lanes], axis=0, keepdims=True)
        d_fade = d_fade + exact(jnp.broadcast_to(hh, (8, LANES)), pick, NN)
        dye[:, lanes] = (dy * enter_k).astype(bf16)
        xt[:, lanes] = (x * end_k).astype(bf16)
        dx = dxd * spread(step, h0, h1, wide) + end_k * v + skip_ref[:, lanes] * dy
        dconv = dx * (sig * (1.0 + conv * (1.0 - sig)))
        dcv[pl.ds(0, q), lanes] = dconv
        sums = [jnp.sum(dconv * ext[pl.ds(HALO, q), lanes], axis=0, keepdims=True)]
        dxin = w_ref[0:1, lanes] * dconv
        for lag in range(1, taps):
            same = jnp.where(docs_ext[pl.ds(HALO - lag, q), :] == own, 1.0, 0.0)
            sums.append(jnp.sum(dconv * same * ext[pl.ds(HALO - lag, q), lanes], axis=0, keepdims=True))
            follow = jnp.where(docs_after[pl.ds(lag, q), :] == own, 1.0, 0.0)
            dxin = dxin + w_ref[lag : lag + 1, lanes] * dcv[pl.ds(lag, q), lanes] * follow
        sums.append(jnp.sum(dconv, axis=0, keepdims=True))
        sums.append(jnp.sum(dy * x, axis=0, keepdims=True))
        dx_ref[:, lanes] = dxin.astype(bf16)
        for i, s in enumerate(sums):
            dconv_ref[i : i + 1, lanes] = dconv_ref[i : i + 1, lanes] + s
    dsb = d_scores.astype(bf16)
    dbct_ref[0:n, :] = mm(ct, dsb, NN) + mm(after, xt[...], NT)
    dbct_ref[n : 2 * n, :] = mm(bt, dsb, NT) + mm(old, dye[...], NT)
    new = mm(ct, dye[...], NN)
    for k in range(pairs):
        lanes = slice(k * LANES, (k + 1) * LANES)
        dstate[:, lanes] = dstate[:, lanes] * spread(fade, 2 * k, 2 * k + 1, wide_row) + new[:, lanes]
    cols = col_t[...].T
    pulled = d_toend * to_end
    at_end = jnp.sum(pulled, axis=0, keepdims=True) + fade * d_fade[0:1, :]
    d_cum = rows - step * cols + d_enter * entering - pulled
    last_row = lax.broadcasted_iota(jnp.int32, (q, LANES), 0) == q - 1
    d_cum = d_cum + jnp.where(last_row, at_end, 0.0)
    d_decay = exact(tri, d_cum, TN)
    d_step = cols + d_toend * tail - rate * d_decay
    d_raw = d_step * sigmoid(raw)
    dsmall_ref[...] = d_raw
    dhead_ref[0:1, :] = dhead_ref[0:1, :] + jnp.sum(d_raw, axis=0, keepdims=True)
    dhead_ref[1:2, :] = dhead_ref[1:2, :] + jnp.sum(d_decay * decay, axis=0, keepdims=True)
    dcv[pl.ds(q, HALO), :] = dcv[pl.ds(0, HALO), :]
    docs_after[pl.ds(q, HALO), :] = docs_after[pl.ds(0, HALO), :]


def whole(array):
    return pl.BlockSpec(array.shape, lambda c: (0,) * array.ndim)


def run_forward(q, x_in, small, bct, dcol, drow, conv_w, conv_b, sb, rate, skip, head):
    tokens, width = x_in.shape
    n = bct.shape[0] // 2
    chunks = tokens // q
    pairs = width // LANES
    taps = conv_w.shape[0]
    return pl.pallas_call(
        functools.partial(scan_forward, q, taps, pairs, head),
        grid=(chunks,),
        in_specs=[
            pl.BlockSpec((q, width), lambda c: (c, 0)),
            pl.BlockSpec((q, LANES), lambda c: (c, 0)),
            pl.BlockSpec((2 * n, q), lambda c: (0, c)),
            pl.BlockSpec((q, LANES), lambda c: (c, 0)),
            pl.BlockSpec((8, q), lambda c: (0, c)),
            whole(conv_w), whole(conv_b), whole(sb), whole(rate), whole(skip),
        ],
        out_specs=[
            pl.BlockSpec((q, width), lambda c: (c, 0)),
            pl.BlockSpec((1, n, width), lambda c: (c, 0, 0)),
        ],
        out_shape=[
            jax.ShapeDtypeStruct((tokens, width), f32),
            jax.ShapeDtypeStruct((chunks, n, width), f32),
        ],
        scratch_shapes=[
            pltpu.VMEM((n, width), f32),
            pltpu.VMEM((HALO + q, width), f32),
            pltpu.VMEM((HALO + q, LANES), f32),
            pltpu.VMEM((8, LANES), f32),
            pltpu.VMEM((q, width), bf16),
            pltpu.VMEM((8, LANES), f32),
        ],
        name="scan_forward",
    )(x_in, small, bct, dcol, drow, conv_w, conv_b, sb, rate, skip)


def run_backward(q, x_in, small, bct, dcol, drow, conv_w, conv_b, sb, rate, skip, dy, states, head):
    tokens, width = x_in.shape
    n = bct.shape[0] // 2
    chunks = tokens // q
    pairs = width // LANES
    taps = conv_w.shape[0]
    per = q // HALO

    def at(c):
        return chunks - 1 - c

    def prior(c):
        return jnp.maximum((chunks - 1 - c) * per - 1, 0)

    return pl.pallas_call(
        functools.partial(scan_backward, q, taps, pairs, head, chunks),
        grid=(chunks,),
        in_specs=[
            pl.BlockSpec((q, width), lambda c: (at(c), 0)),
            pl.BlockSpec((HALO, width), lambda c: (prior(c), 0)),
            pl.BlockSpec((q, LANES), lambda c: (at(c), 0)),
            pl.BlockSpec((2 * n, q), lambda c: (0, at(c))),
            pl.BlockSpec((q, LANES), lambda c: (at(c), 0)),
            pl.BlockSpec((HALO, LANES), lambda c: (prior(c), 0)),
            pl.BlockSpec((8, q), lambda c: (0, at(c))),
            whole(conv_w), whole(conv_b), whole(sb), whole(rate), whole(skip),
            pl.BlockSpec((q, width), lambda c: (at(c), 0)),
            pl.BlockSpec((1, n, width), lambda c: (at(c), 0, 0)),
        ],
        out_specs=[
            pl.BlockSpec((q, width), lambda c: (at(c), 0)),
            pl.BlockSpec((q, LANES), lambda c: (at(c), 0)),
            pl.BlockSpec((2 * n, q), lambda c: (0, at(c))),
            pl.BlockSpec((8, width), lambda c: (0, 0)),
            pl.BlockSpec((8, LANES), lambda c: (0, 0)),
        ],
        out_shape=[
            jax.ShapeDtypeStruct((tokens, width), bf16),
            jax.ShapeDtypeStruct((tokens, LANES), f32),
            jax.ShapeDtypeStruct((2 * n, tokens), f32),
            jax.ShapeDtypeStruct((8, width), f32),
            jax.ShapeDtypeStruct((8, LANES), f32),
        ],
        scratch_shapes=[
            pltpu.VMEM((n, width), f32),
            pltpu.VMEM((HALO + q, width), f32),
            pltpu.VMEM((HALO + q, LANES), f32),
            pltpu.VMEM((q + HALO, width), f32),
            pltpu.VMEM((q + HALO, LANES), f32),
            pltpu.VMEM((q, width), bf16),
            pltpu.VMEM((q, width), bf16),
            pltpu.VMEM((LANES, q), f32),
        ],
        name="scan_backward",
    )(x_in, x_in, small, bct, dcol, dcol, drow, conv_w, conv_b, sb, rate, skip, dy, states)


def gate_forward(
    groups, z_rows, tall,
    normed_ref, cot_ref, joined_ref, y_ref, gain_ref, z_ref, dgn_ref, sums_ref, wz, wo,
):
    parts, held, width = wo.shape

    @pl.when(pl.program_id(0) == 0)
    def _():
        for g in range(groups):
            wz[pl.ds(g * z_rows, z_rows), :] = joined_ref[g, pl.ds(0, z_rows), :]
            for k in range(parts):
                wo[k, pl.ds(g * tall, tall), :] = joined_ref[g, pl.ds(z_rows + k * tall, tall), :]

    z = mm(normed_ref[...], wz[...], NN)
    d_gn = mm(cot_ref[:, 0:width], wo[0], NT)
    for k in range(1, parts):
        d_gn = d_gn + mm(cot_ref[:, k * width : (k + 1) * width], wo[k], NT)
    z_ref[...] = z
    dgn_ref[...] = d_gn
    gated = y_ref[...] * (z * sigmoid(z))
    square = jnp.sum(gated * gated, axis=1, keepdims=True)
    cross = jnp.sum(d_gn * gain_ref[...] * gated, axis=1, keepdims=True)
    lane = lane_iota((square.shape[0], LANES))
    sums_ref[...] = jnp.where(lane == 0, square, jnp.where(lane == 1, cross, 0.0)).T[0:8, :]


def gate_backward(
    blocks, tile, z_rows, tall, channels,
    normed_ref, cot_ref, y_ref, z_ref, dgn_ref, sums_ref, gain_ref,
    gate_ref, dz_ref, dy_ref, dgain_ref, terms_ref,
):
    step = pl.program_id(0)
    rows, width = y_ref.shape
    parts = normed_ref.shape[1] // width

    @pl.when(step == 0)
    def _():
        dgain_ref[...] = jnp.zeros_like(dgain_ref)

    @pl.when(step < blocks)
    def _():
        own = pl.ds(pl.multiple_of(step * rows, rows), rows)
        columns = jnp.concatenate([sums_ref[...], jnp.zeros((LANES - 8, rows), f32)], axis=0).T
        inv = lax.rsqrt(columns[:, 0:1] / channels + epsilon)
        slope = inv * inv * inv * (columns[:, 1:2] / channels)
        for k in range(width // LANES):
            lanes = slice(k * LANES, (k + 1) * LANES)
            y, z, d_gn, gain = y_ref[:, lanes], z_ref[:, lanes], dgn_ref[:, lanes], gain_ref[:, lanes]
            sig = sigmoid(z)
            act = z * sig
            gated = y * act
            scaled = gated * inv
            gate_ref[own, lanes] = (scaled * gain).astype(bf16)
            dgain_ref[0:1, lanes] = dgain_ref[0:1, lanes] + jnp.sum(d_gn * scaled, axis=0, keepdims=True)
            d_gated = inv * (d_gn * gain) - gated * slope
            dz_ref[own, lanes] = (d_gated * y * (sig * (1.0 + z * (1.0 - sig)))).astype(bf16)
            dy_ref[:, lanes] = d_gated * act

    def store(term, at, within, base):
        if within >= tile:
            start = pl.multiple_of(base + at * tile, 16)
            terms_ref[0, pl.ds(start, tile), :] = term
        else:
            for n in range(tile // within):
                piece = term[n * within : (n + 1) * within]
                terms_ref[at * (tile // within) + n, pl.ds(base, within), :] = piece

    @pl.when(step >= blocks)
    def _():
        i = step - blocks
        lanes = pl.ds(pl.multiple_of(i * tile, LANES), tile)
        store(mm(normed_ref[:, lanes], dz_ref[...], TN).astype(bf16), i, z_rows, 0)
        j = i // parts
        lanes = pl.ds(pl.multiple_of(j * tile, LANES), tile)
        left = gate_ref[:, lanes]
        for k in range(parts):

            @pl.when(i % parts == k)
            def _():
                right = cot_ref[:, k * width : (k + 1) * width]
                store(mm(left, right, TN).astype(bf16), j, tall, z_rows + k * tall)


def run_gate_forward(joined, z_rows, normed, cot, y, gain):
    groups, deep, width = joined.shape
    tokens, n_width = normed.shape
    parts = n_width // width
    tall = (deep - z_rows) // parts
    rows = min(256, tokens)

    def tokens_of(columns):
        return pl.BlockSpec((rows, columns), lambda c: (c, 0))

    return pl.pallas_call(
        functools.partial(gate_forward, groups, z_rows, tall),
        grid=(tokens // rows,),
        in_specs=[tokens_of(n_width), tokens_of(n_width), whole(joined), tokens_of(width), whole(gain)],
        out_specs=[tokens_of(width), tokens_of(width), pl.BlockSpec((8, rows), lambda c: (0, c))],
        out_shape=[
            jax.ShapeDtypeStruct((tokens, width), f32),
            jax.ShapeDtypeStruct((tokens, width), f32),
            jax.ShapeDtypeStruct((8, tokens), f32),
        ],
        scratch_shapes=[
            pltpu.VMEM((groups * z_rows, width), bf16),
            pltpu.VMEM((parts, groups * tall, width), bf16),
        ],
        name="gate_forward",
    )(normed, cot, joined, y, gain)


def run_gate_backward(groups, z_rows, tall, channels, normed, cot, y, z, d_gn, sums, gain):
    tokens, n_width = normed.shape
    width = y.shape[1]
    parts = n_width // width
    rows = min(256, tokens)
    blocks = tokens // rows
    tile = 3 * LANES
    deep = z_rows + parts * tall

    def tokens_of(columns):
        return pl.BlockSpec((rows, columns), lambda c: (jnp.minimum(c, blocks - 1), 0))

    return pl.pallas_call(
        functools.partial(gate_backward, blocks, tile, z_rows, tall, channels),
        grid=(blocks + n_width // tile,),
        in_specs=[
            whole(normed), whole(cot), tokens_of(width), tokens_of(width), tokens_of(width),
            pl.BlockSpec((8, rows), lambda c: (0, jnp.minimum(c, blocks - 1))), whole(gain),
        ],
        out_specs=[
            pl.BlockSpec((tokens, width), lambda c: (0, 0)),
            pl.BlockSpec((tokens, width), lambda c: (0, 0)),
            tokens_of(width),
            pl.BlockSpec((8, width), lambda c: (0, 0)),
            pl.BlockSpec((groups, deep, width), lambda c: (0, 0, 0)),
        ],
        out_shape=[
            jax.ShapeDtypeStruct((tokens, width), bf16),
            jax.ShapeDtypeStruct((tokens, width), bf16),
            jax.ShapeDtypeStruct((tokens, width), f32),
            jax.ShapeDtypeStruct((8, width), f32),
            jax.ShapeDtypeStruct((groups, deep, width), bf16),
        ],
        name="gate_backward",
    )(normed, cot, y, z, d_gn, sums, gain)


def swapped(block, bit):
    size = lax.axis_size("seq")
    return lax.ppermute(block, "seq", [(i, i ^ bit) for i in range(size)])


def bits_of(size):
    bits, bit = [], 1
    while bit < size:
        bits.append(bit)
        bit *= 2
    return bits


def joined_by(held, bit):
    other = swapped(held, bit)
    upper = (lax.axis_index("seq") & bit) != 0
    both = jnp.where(upper, jnp.stack([other, held], axis=1), jnp.stack([held, other], axis=1))
    return both.reshape((-1,) + both.shape[2:])


def opened(block):
    bits = bits_of(lax.axis_size("seq"))
    return joined_by(block[None], bits[-1]) if bits else block[None]


def gathered(block, held=None):
    held = opened(block) if held is None else held
    for bit in reversed(bits_of(lax.axis_size("seq"))[:-1]):
        held = joined_by(held, bit)
    return held.reshape((-1,) + held.shape[2:])


def scattered(parts, between=lambda held: held):
    index = lax.axis_index("seq")
    size = lax.axis_size("seq")
    rest = parts.shape[1:]
    lead = parts.shape[0]
    held = parts.reshape((size, lead // size) + rest)
    for bit in bits_of(size):
        half = held.reshape((held.shape[0] // 2, 2) + held.shape[1:])
        upper = (index & bit) != 0
        mine = jnp.where(upper, half[:, 1], half[:, 0])
        theirs = jnp.where(upper, half[:, 0], half[:, 1]).astype(bf16)
        held = between(mine.astype(f32) + swapped(theirs, bit).astype(f32))
    return held[0]


def added_over(block, bits):
    for bit in bits:
        block = block + crossed(block, bit)
    return block


def moved_by(block, step):
    count = lax.axis_size("dp")
    route = [(i, i + 2 * step) for i in range(count) if 0 <= i + 2 * step < count]
    return lax.ppermute(block, "dp", route)


def crossed(block, bits):
    return lax.ppermute(block, "dp", [(i, i ^ bits) for i in range(lax.axis_size("dp"))])


def gathered_rows(block, waits):
    count = lax.axis_size("dp")
    length = count // 2
    if not is_small(count):
        return lax.all_gather(block, "dp", axis=0, tiled=True), block
    at = lax.axis_index("dp")
    place, side = at // 2, at % 2
    rows = block.shape[0]
    whole_rows = jnp.zeros((count * rows, block.shape[1]), block.dtype)

    def put(into, piece, pair, half):
        return lax.dynamic_update_slice(into, piece, ((pair * 2 + half) * rows, 0))

    whole_rows = put(whole_rows, block, place, side)
    other = crossed(block, 1)
    whole_rows = put(whole_rows, other, place, 1 - side)
    up, down, ready = block, block, []
    for hop in range(1, length):
        up, down = after((moved_by(up, 1), moved_by(down, -1)), (other, waits[hop - 1 : hop]))
        ready.append((down, up))
        piece, pair = None, None
        for spot in range(length):
            near = min(spot, length - 1 - spot)
            if hop <= 2 * near:
                away, from_below = (hop + 1) // 2, hop % 2 == 0
            else:
                away, from_below = hop - near, spot > length - 1 - spot
            chosen = ready[away - 1][1 if from_below else 0]
            source = spot - away if from_below else spot + away
            here = place == spot
            piece = chosen if piece is None else jnp.where(here, chosen, piece)
            pair = source if pair is None else jnp.where(here, source, pair)
        whole_rows = put(whole_rows, piece, pair, side)
        other = crossed(piece, 1)
        whole_rows = put(whole_rows, other, pair, 1 - side)
    return whole_rows, ready[min(1, length - 2)]


def is_small(count):
    return count <= 8 and count & (count - 1) == 0


def halved_rows(term):
    count = lax.axis_size("dp")
    if not is_small(count):
        return term
    at = lax.axis_index("dp")
    pairs = term.reshape(count // 2, 2, -1, term.shape[1])

    def side(which):
        return lax.dynamic_index_in_dim(pairs, which, 1, keepdims=False)

    came = crossed(side((at & 1) ^ 1), 1)
    return (side(at & 1).astype(f32) + came.astype(f32)).astype(bf16)


def shared_rows(lines):
    count = lax.axis_size("dp")
    if not is_small(count):
        return [lax.psum_scatter(lines, "dp", scatter_dimension=0, tiled=True)]
    at = lax.axis_index("dp")

    def part(owner):
        return lax.dynamic_index_in_dim(lines, owner // 2, 0, keepdims=False)

    return [part(at)] + [crossed(part(at ^ bits), bits) for bits in range(2, count, 2)]


def after(value, other):
    return lax.optimization_barrier((value, other))[0]


def turned(blocks):
    size = lax.axis_size("seq")
    index = lax.axis_index("seq")
    if size & (size - 1):
        return lax.all_to_all(blocks, "seq", 0, 0, tiled=True)
    out = blocks
    for bits in range(1, size):
        piece = lax.dynamic_slice_in_dim(blocks, index ^ bits, 1, 0)
        piece = lax.ppermute(piece, "seq", [(i, i ^ bits) for i in range(size)])
        out = lax.dynamic_update_slice_in_dim(out, piece, index ^ bits, 0)
    return out


def folded(rows, lead, width):
    cut = rows.reshape(lead, rows.shape[0] // lead, rows.shape[1] // width, width)
    cut = cut.transpose(0, 2, 1, 3).reshape(lead, -1, width)
    return cut[0] if lead == 1 else cut


def unfolded(pieces, width):
    lead, stacked, narrow = pieces.shape
    cut = pieces.reshape(lead, width // narrow, stacked * narrow // width, narrow)
    return cut.transpose(0, 2, 1, 3).reshape(-1, width)


def exchanged(parts):
    size = lax.axis_size("seq")
    index = lax.axis_index("seq")
    held = parts.reshape((size, -1) + parts.shape[1:])

    def part(owner):
        return lax.dynamic_index_in_dim(held, owner, 0, keepdims=False)

    came = [
        lax.ppermute(part(index ^ bits).astype(bf16), "seq", [(i, i ^ bits) for i in range(size)])
        for bits in range(1, size)
    ]
    return sum([piece.astype(f32) for piece in came], part(index))


def by_rows(array):
    return with_layout_constraint(array, Layout(major_to_minor=(0, 1)))


def padded(rows, width):
    return jnp.pad(rows, ((0, 0), (0, width - rows.shape[1])))


def shards(
    hidden, segments, cotangent, norm_gain, in_weight, conv_weight, conv_bias, step_bias, log_rate,
    skip_gain, gate_gain, out_weight,
):
    n_seqs, block, n_width = hidden.shape
    size = lax.axis_size("seq")
    groups = lax.axis_size("dp")
    index = lax.axis_index("seq")
    tokens = size * block
    n_inner = gate_gain.shape[0]
    n_heads = step_bias.shape[0]
    n_taps = conv_weight.shape[0]
    n_mixed = conv_bias.shape[0]
    n_state = (n_mixed - n_inner) // 2
    head = n_inner // n_heads
    own_inner = n_inner // size
    own_heads = n_heads // size
    own_bc = 2 * n_state // size
    q = min(128, block)
    in_rows = in_weight.shape[0]

    in_low = in_weight.astype(bf16)
    z_cols = in_low[:, :n_inner].reshape(in_rows, size, own_inner)
    x_cols = in_low[:, n_inner : 2 * n_inner].reshape(in_rows, size, own_inner)
    bc_cols = in_low[:, 2 * n_inner : n_inner + n_mixed].reshape(in_rows, size, own_bc)
    dt_cols = in_low[:, n_inner + n_mixed :].reshape(in_rows, size, own_heads)
    gap = jnp.zeros((in_rows, size, LANES - own_heads - own_bc), bf16)
    laid = jnp.concatenate([x_cols, dt_cols, gap, bc_cols, z_cols], axis=2).transpose(1, 0, 2)
    mine = lax.all_to_all(laid, "seq", 0, 0, tiled=True)
    flat = hidden.reshape(block, n_width).astype(f32)
    inv = lax.rsqrt(jnp.mean(flat * flat, axis=-1, keepdims=True) + epsilon)
    unit = flat * inv
    normed_own = (unit * norm_gain).astype(bf16)
    docs = gathered(segments).reshape(tokens).astype(f32)
    order = [(f, (f % groups) * size + f // groups) for f in range(groups * size)]
    back = [(b, a) for a, b in order]
    out_moved = lax.ppermute(out_weight.astype(bf16), ("dp", "seq"), order)
    mine, normed_own = lax.optimization_barrier((after(mine, docs), normed_own))
    mine = mine.reshape(size * in_rows, -1)
    n_first = own_inner + LANES
    cot_own = cotangent.reshape(block, n_width)
    normed_held = opened(normed_own)
    cot_held = opened(after(cot_own, mine))
    w_first, hopped = gathered_rows(mine[:, :n_first], [normed_held, cot_held])
    z_block = jnp.concatenate([mine[:, n_first:], folded(after(out_moved, hopped), 1, own_inner)], axis=0)

    normed = gathered(normed_own, normed_held)
    joined = lax.all_gather(z_block, "dp", axis=0, tiled=True).reshape(groups, -1, own_inner)
    z_rows = size * in_rows
    w_z = joined[:, :z_rows].reshape(-1, own_inner)
    w_out = unfolded(joined[:, z_rows:], n_width)
    cot = gathered(cot_own, cot_held)
    dcol = jnp.broadcast_to(docs[:, None], (tokens, LANES))
    drow = jnp.broadcast_to(docs[None, :], (8, tokens))

    def own_part(vector, parts):
        return lax.dynamic_slice_in_dim(vector, index * parts, parts, vector.ndim - 1)

    w_x, w_small = w_first[:, :own_inner], w_first[:, own_inner:]
    small = mm(normed, w_small, NN)
    x_in = mm(normed, w_x, NN).astype(bf16)
    conv_x = own_part(conv_weight[:, :n_inner], own_inner)
    bias_x = own_part(conv_bias[None, :n_inner], own_inner)
    conv_bc = own_part(conv_weight[:, n_inner:], own_bc)
    bias_bc = own_part(conv_bias[None, n_inner:], own_bc)
    sb = padded(own_part(step_bias[None], own_heads), LANES)
    rate = padded(jnp.exp(own_part(log_rate[None], own_heads)), LANES)
    skip = jnp.repeat(own_part(skip_gain[None], own_heads), head, axis=1)
    gain = own_part(gate_gain[None], own_inner)

    head_lanes = jnp.arange(LANES) < own_heads
    bc_in = small[:, LANES - own_bc :].astype(bf16).astype(f32)
    small_dt = jnp.where(head_lanes, small, 0.0)

    def earlier(rows, lag):
        return jnp.pad(rows, ((lag, 0), (0, 0)))[:tokens]

    def later(rows, lag):
        return jnp.pad(rows, ((0, lag), (0, 0)))[lag:]

    same = [None] + [
        jnp.where(jnp.pad(docs, (lag, 0), constant_values=-1.0)[:tokens] == docs, 1.0, 0.0)[:, None]
        for lag in range(1, n_taps)
    ]
    bc_conv = bias_bc + conv_bc[0:1] * bc_in
    for lag in range(1, n_taps):
        bc_conv = bc_conv + conv_bc[lag : lag + 1] * earlier(bc_in, lag) * same[lag]
    bc_sig = jax.nn.sigmoid(bc_conv)
    bct = gathered(by_rows((bc_conv * bc_sig).astype(bf16).T))

    y, states = run_forward(
        q, x_in, small_dt, bct, dcol, drow, conv_x, bias_x, sb, rate, skip, head
    )

    out_rows = own_inner // groups
    tiled = z_rows % 16 == 0 and out_rows % 16 == 0
    if tiled:
        lead, deep, tall, gate_in = groups, z_rows, out_rows, joined
    else:
        lead, deep, tall = 1, groups * z_rows, own_inner
        gate_in = jnp.concatenate([w_z, folded(w_out, 1, own_inner)], axis=0)[None]
    z, d_gn, sums = run_gate_forward(gate_in, deep, normed, cot, y, gain)
    sums = lax.psum(sums[:2], "seq")
    sums = jnp.pad(sums, ((0, 6), (0, 0)))
    gate_low, d_z, d_y, d_gain, terms = run_gate_backward(
        lead, deep, tall, n_inner, normed, cot, y, z, d_gn, sums, gain
    )
    d_gain = d_gain[0]
    if not tiled:
        z_term = terms[0, :deep].reshape(groups, z_rows, own_inner)
        out_term = terms[0, deep:].reshape(n_width // own_inner, groups, out_rows, own_inner)
        out_term = out_term.transpose(1, 0, 2, 3).reshape(groups, -1, own_inner)
        terms = jnp.concatenate([z_term, out_term], axis=1)
    terms = terms.reshape(-1, own_inner)
    parts = lax.psum_scatter(terms, "dp", scatter_dimension=0, tiled=True)

    d_x, d_dt, d_bct, d_conv_x, d_heads = run_backward(
        q, x_in, small_dt, bct, dcol, drow, conv_x, bias_x, sb, rate, skip, d_y, states, head
    )
    x_term = mm(normed, d_x, TN).astype(bf16)
    x_term, d_bct = lax.optimization_barrier((x_term, d_bct))
    x_lines = halved_rows(x_term)
    d_bc = by_rows(exchanged(d_bct)).T
    d_bcc = d_bc * (bc_sig * (1.0 + bc_conv * (1.0 - bc_sig)))
    d_bc_in = conv_bc[0:1] * d_bcc
    w_sums = [jnp.sum(d_bcc * bc_in, axis=0)]
    for lag in range(1, n_taps):
        held = d_bcc * same[lag]
        d_bc_in = d_bc_in + conv_bc[lag : lag + 1] * later(held, lag)
        w_sums.append(jnp.sum(held * earlier(bc_in, lag), axis=0))
    w_sums.append(jnp.sum(d_bcc, axis=0))
    d_small = jnp.concatenate([d_dt[:, : LANES - own_bc], d_bc_in], axis=1).astype(bf16)
    d_first = jnp.concatenate([d_x, d_small], axis=1)
    small_lines = halved_rows(mm(normed, d_small, TN).astype(bf16))
    branch = scattered(mm(after(gate_low, d_bc), w_out, NN).astype(bf16))
    result = (flat + branch).reshape(n_seqs, block, n_width).astype(bf16)
    d_first = after(d_first, x_lines)
    d_normed = mm(d_first, w_first, NT) + mm(d_z, w_z, NT)
    d_norm_gain = jnp.sum(d_normed * normed.astype(f32), axis=0) / norm_gain
    d_skip = jnp.sum(d_conv_x[n_taps + 1].reshape(own_heads, head), axis=1)
    packed = jnp.concatenate(
        [
            d_conv_x[: n_taps + 1].reshape(-1),
            jnp.stack(w_sums).reshape(-1),
            d_gain,
            d_heads[0, :own_heads],
            d_heads[1, :own_heads],
            d_skip,
            d_norm_gain,
        ]
    )
    lines = jnp.concatenate([x_lines, small_lines], axis=-1)
    packed = added_over(packed, reversed(bits_of(groups)[1:]))
    lines, packed = lax.optimization_barrier((lines, packed))
    shares = shared_rows(lines)
    packed = gathered(added_over(packed, bits_of(groups)[:1])[None])
    parts, result = lax.optimization_barrier((after(parts, shares[:2]), result))
    d_norm = after(d_normed.astype(bf16), parts)
    d_norm = lax.psum_scatter(d_norm, "seq", scatter_dimension=0, tiled=True).astype(f32)

    def own_rows(part):
        out = turned(part.reshape(size, in_rows, -1))
        return out.transpose(1, 0, 2).astype(f32)

    out_part = unfolded(parts[None, z_rows:], n_width)
    d_out_weight = lax.ppermute(out_part, ("dp", "seq"), back).astype(f32)
    in_z = own_rows(parts[:z_rows])
    shares, in_z, d_out_weight = lax.optimization_barrier((shares, in_z, d_out_weight))
    first_part = sum(share.astype(f32) for share in shares)
    in_first = own_rows(first_part.astype(bf16))
    d_in_weight = jnp.concatenate(
        [
            in_z.reshape(in_rows, n_inner),
            in_first[:, :, :own_inner].reshape(in_rows, n_inner),
            in_first[:, :, n_first - own_bc :].reshape(in_rows, 2 * n_state),
            in_first[:, :, own_inner : own_inner + own_heads].reshape(in_rows, n_heads),
        ],
        axis=1,
    )

    lifted = d_norm * norm_gain
    d_flat = inv * lifted - flat * (
        inv * inv * inv * jnp.mean(lifted * flat, axis=-1, keepdims=True)
    )
    d_hidden = (cot_own.astype(f32) + d_flat).reshape(n_seqs, block, n_width)

    at = 0

    def take(count):
        nonlocal at
        at += count
        return packed[:, at - count : at]

    got_x = take((n_taps + 1) * own_inner).reshape(size, n_taps + 1, own_inner)
    got_bc = take((n_taps + 1) * own_bc).reshape(size, n_taps + 1, own_bc)
    got_x = got_x.transpose(1, 0, 2).reshape(n_taps + 1, n_inner)
    got_bc = got_bc.transpose(1, 0, 2).reshape(n_taps + 1, 2 * n_state)
    conv_all = jnp.concatenate([got_x, got_bc], axis=1)
    d_gate_gain = take(own_inner).reshape(n_inner)
    d_step_bias = take(own_heads).reshape(n_heads)
    d_log_rate = take(own_heads).reshape(n_heads)
    d_skip_gain = take(own_heads).reshape(n_heads)
    d_norm_all = jnp.sum(take(n_width), axis=0)
    return (
        result,
        d_hidden,
        d_norm_all,
        d_in_weight,
        conv_all[:n_taps],
        conv_all[n_taps],
        d_step_bias,
        d_log_rate,
        d_skip_gain,
        d_gate_gain,
        d_out_weight,
    )


def solution(mesh):
    tokens = P("dp", "seq", None)
    rows = P(("dp", "seq"), None)
    return jax.shard_map(
        shards,
        mesh=mesh,
        in_specs=(tokens, P("dp", "seq"), tokens, P(), rows, P(), P(), P(), P(), P(), P(), rows),
        out_specs=(tokens, tokens, P(), rows, P(), P(), P(), P(), P(), P(), rows),
        check_vma=False,
    )
```

```python
import functools

import jax
import jax.numpy as jnp
from jax import lax
from jax.experimental import pallas as pl
from jax.experimental.layout import Layout, with_layout_constraint
from jax.experimental.pallas import tpu as pltpu
from jax.sharding import PartitionSpec as P

epsilon = 1e-05
highest = lax.Precision.HIGHEST
f32 = jnp.float32
bf16 = jnp.bfloat16
LANES = 128
HALO = 16
NEG = -1e30


def mm(a, b, dims, out=f32):
    return lax.dot_general(a, b, (dims, ((), ())), preferred_element_type=out)


NN = ((1,), (0,))
NT = ((1,), (1,))
TN = ((0,), (0,))


def exact(a, b, dims):
    return lax.dot_general(a, b, (dims, ((), ())), precision=highest, preferred_element_type=f32)


def softplus(v):
    return jnp.maximum(v, 0.0) + jnp.log1p(jnp.exp(-jnp.abs(v)))


def sigmoid(v):
    return 1.0 / (1.0 + jnp.exp(-v))


def lane_iota(shape):
    return lax.broadcasted_iota(jnp.int32, shape, len(shape) - 1)


def spread(columns, first, second, wide):
    rows = columns.shape[0]
    left = jnp.broadcast_to(columns[:, first : first + 1], (rows, LANES))
    right = jnp.broadcast_to(columns[:, second : second + 1], (rows, LANES))
    return jnp.where(wide, left, right)


def step_parts(raw, rate, q):
    row = lax.broadcasted_iota(jnp.int32, (q, q), 0)
    col = lax.broadcasted_iota(jnp.int32, (q, q), 1)
    tri = jnp.where(row >= col, 1.0, 0.0).astype(f32)
    step = softplus(raw)
    decay = -step * rate
    total = exact(tri, decay, NN)
    return step, decay, total, tri, row >= col


def convolve(ext, docs_ext, own, weights, bias, lanes, q, taps):
    running = bias + weights[0:1, lanes] * ext[pl.ds(HALO, q), lanes]
    for lag in range(1, taps):
        same = jnp.where(docs_ext[pl.ds(HALO - lag, q), :] == own, 1.0, 0.0)
        running = running + weights[lag : lag + 1, lanes] * ext[pl.ds(HALO - lag, q), lanes] * same
    return running


def scan_forward(
    q, taps, pairs, head,
    x_ref, small_ref, bct_ref, dcol_ref, drow_ref, w_ref, b_ref, sb_ref, rate_ref, skip_ref,
    y_ref, states_ref,
    state, ext, docs_ext, xs, xt, last_doc,
):
    c = pl.program_id(0)
    n = bct_ref.shape[0] // 2

    @pl.when(c == 0)
    def _():
        state[...] = jnp.zeros_like(state)
        ext[pl.ds(0, HALO), :] = jnp.zeros((HALO, ext.shape[1]), f32)
        docs_ext[pl.ds(0, HALO), :] = jnp.full((HALO, LANES), -1.0, f32)
        last_doc[...] = jnp.full(last_doc.shape, -1.0, f32)

    own = dcol_ref[...]
    ext[pl.ds(HALO, q), :] = x_ref[...].astype(f32)
    docs_ext[pl.ds(HALO, q), :] = own
    step, _, cum, _, causal = step_parts(small_ref[...] + sb_ref[...], rate_ref[...], q)
    step_t = step.T
    cum_t = cum.T
    end = cum[q - 1 : q, :]
    id_in = last_doc[0:1, :]
    final = own[q - 1 : q, :]
    linked = jnp.where(final == id_in, 1.0, 0.0)
    fade = linked * jnp.exp(end)
    entering = jnp.where(own == id_in, 1.0, 0.0) * jnp.exp(cum)
    to_end = jnp.where(own == final, 1.0, 0.0) * jnp.exp(end - cum) * step
    same_doc = jnp.broadcast_to(own[:, 0:1], (q, q)) == jnp.broadcast_to(drow_ref[0:1, :], (q, q))
    hide = jnp.where(jnp.logical_and(causal, same_doc), 0.0, NEG)
    bt = bct_ref[0:n, :]
    ct = bct_ref[n : 2 * n, :]
    scores = mm(ct, bt, TN)
    states_ref[0] = state[...]
    old = state[...].astype(bf16)
    wide = lane_iota((q, LANES)) < head
    wide_row = lane_iota((1, LANES)) < head
    for k in range(pairs):
        lanes = slice(k * LANES, (k + 1) * LANES)
        h0, h1 = 2 * k, 2 * k + 1
        conv = convolve(ext, docs_ext, own, w_ref, b_ref[:, lanes], lanes, q, taps)
        x = conv * sigmoid(conv)
        xd = x * spread(step, h0, h1, wide)
        xt[:, lanes] = (x * spread(to_end, h0, h1, wide)).astype(bf16)
        mats = []
        for h in (h0, h1):
            gap = cum[:, h : h + 1] - cum_t[h : h + 1, :] + hide
            mats.append((jnp.exp(gap) * scores).astype(bf16))
        out = mm(mats[0], jnp.where(wide, xd, 0.0).astype(bf16), NN)
        out = out + mm(mats[1], jnp.where(wide, 0.0, xd).astype(bf16), NN)
        out = out + mm(ct, old[:, lanes], TN) * spread(entering, h0, h1, wide)
        y_ref[:, lanes] = out + skip_ref[:, lanes] * x
    update = mm(bt, xt[...], NN)
    for k in range(pairs):
        lanes = slice(k * LANES, (k + 1) * LANES)
        state[:, lanes] = state[:, lanes] * spread(fade, 2 * k, 2 * k + 1, wide_row) + update[:, lanes]
    ext[pl.ds(0, HALO), :] = ext[pl.ds(q, HALO), :]
    docs_ext[pl.ds(0, HALO), :] = docs_ext[pl.ds(q, HALO), :]
    last_doc[...] = jnp.broadcast_to(final, last_doc.shape)


def scan_backward(
    q, taps, pairs, head, chunks,
    x_ref, xp_ref, small_ref, bct_ref, dcol_ref, dcolp_ref, drow_ref, w_ref, b_ref, sb_ref, rate_ref,
    skip_ref, dy_ref, states_ref,
    dx_ref, dsmall_ref, dbct_ref, dconv_ref, dhead_ref,
    dstate, ext, docs_ext, dcv, docs_after, dye, xt, col_t,
):
    step_at = pl.program_id(0)
    c = chunks - 1 - step_at
    n = bct_ref.shape[0] // 2
    width = x_ref.shape[1]

    @pl.when(step_at == 0)
    def _():
        dstate[...] = jnp.zeros_like(dstate)
        dcv[pl.ds(q, HALO), :] = jnp.zeros((HALO, width), f32)
        docs_after[pl.ds(q, HALO), :] = jnp.full((HALO, LANES), -1.0, f32)
        dconv_ref[...] = jnp.zeros_like(dconv_ref)
        dhead_ref[...] = jnp.zeros_like(dhead_ref)
        col_t[...] = jnp.zeros_like(col_t)

    first = c == 0
    own = dcol_ref[...]
    before = jnp.where(first, -1.0, dcolp_ref[...])
    ext[pl.ds(0, HALO), :] = xp_ref[...].astype(f32)
    ext[pl.ds(HALO, q), :] = x_ref[...].astype(f32)
    docs_ext[pl.ds(0, HALO), :] = before
    docs_ext[pl.ds(HALO, q), :] = own
    docs_after[pl.ds(0, q), :] = own
    raw = small_ref[...] + sb_ref[...]
    rate = rate_ref[...]
    step, decay, cum, tri, causal = step_parts(raw, rate, q)
    step_t = step.T
    cum_t = cum.T
    end = cum[q - 1 : q, :]
    id_in = before[HALO - 1 : HALO, :]
    final = own[q - 1 : q, :]
    linked = jnp.where(final == id_in, 1.0, 0.0)
    fade = linked * jnp.exp(end)
    entering = jnp.where(own == id_in, 1.0, 0.0) * jnp.exp(cum)
    tail = jnp.where(own == final, 1.0, 0.0) * jnp.exp(end - cum)
    to_end = tail * step
    same_doc = jnp.broadcast_to(own[:, 0:1], (q, q)) == jnp.broadcast_to(drow_ref[0:1, :], (q, q))
    hide = jnp.where(jnp.logical_and(causal, same_doc), 0.0, NEG)
    bt = bct_ref[0:n, :]
    ct = bct_ref[n : 2 * n, :]
    scores = mm(ct, bt, TN)
    old = states_ref[0].astype(bf16)
    after = dstate[...].astype(bf16)
    wide = lane_iota((q, LANES)) < head
    wide_row = lane_iota((1, LANES)) < head
    lane = lane_iota((q, LANES))
    d_scores = jnp.zeros((q, q), f32)
    rows = jnp.zeros((q, LANES), f32)
    d_enter = jnp.zeros((q, LANES), f32)
    d_toend = jnp.zeros((q, LANES), f32)
    d_fade = jnp.zeros((8, LANES), f32)
    part = lax.broadcasted_iota(jnp.int32, (LANES, LANES), 0) // head
    to = lane_iota((LANES, LANES))
    for k in range(pairs):
        lanes = slice(k * LANES, (k + 1) * LANES)
        h0, h1 = 2 * k, 2 * k + 1
        pick = jnp.where(part + 2 * k == to, 1.0, 0.0)
        conv = convolve(ext, docs_ext, own, w_ref, b_ref[:, lanes], lanes, q, taps)
        sig = sigmoid(conv)
        x = conv * sig
        xb = x.astype(bf16)
        dy = dy_ref[:, lanes]
        halves = (jnp.where(wide, dy, 0.0).astype(bf16), jnp.where(wide, 0.0, dy).astype(bf16))
        dxd = jnp.zeros((q, LANES), f32)
        for h, half in ((h0, halves[0]), (h1, halves[1])):
            inner = mm(half, xb, NT)
            keep = jnp.exp(cum[:, h : h + 1] - cum_t[h : h + 1, :] + hide)
            grown = keep * inner
            mat = keep * scores
            dt = step_t[h : h + 1, :]
            g = grown * scores
            d_scores = d_scores + grown * dt
            rows = jnp.where(lane == h, jnp.sum(g * dt, axis=1, keepdims=True), rows)
            col_t[h : h + 1, :] = jnp.sum(g, axis=0, keepdims=True)
            dxd = dxd + mm(mat.astype(bf16), half, TN)
        v = mm(bt, after[:, lanes], TN)
        u = mm(ct, old[:, lanes], TN)
        enter_k = spread(entering, h0, h1, wide)
        end_k = spread(to_end, h0, h1, wide)
        d_enter = d_enter + exact(dy * u, pick, NN)
        d_toend = d_toend + exact(x * v, pick, NN)
        hh = jnp.sum(dstate[:, lanes] * states_ref[0, :, lanes], axis=0, keepdims=True)
        d_fade = d_fade + exact(jnp.broadcast_to(hh, (8, LANES)), pick, NN)
        dye[:, lanes] = (dy * enter_k).astype(bf16)
        xt[:, lanes] = (x * end_k).astype(bf16)
        dx = dxd * spread(step, h0, h1, wide) + end_k * v + skip_ref[:, lanes] * dy
        dconv = dx * (sig * (1.0 + conv * (1.0 - sig)))
        dcv[pl.ds(0, q), lanes] = dconv
        sums = [jnp.sum(dconv * ext[pl.ds(HALO, q), lanes], axis=0, keepdims=True)]
        dxin = w_ref[0:1, lanes] * dconv
        for lag in range(1, taps):
            same = jnp.where(docs_ext[pl.ds(HALO - lag, q), :] == own, 1.0, 0.0)
            sums.append(jnp.sum(dconv * same * ext[pl.ds(HALO - lag, q), lanes], axis=0, keepdims=True))
            follow = jnp.where(docs_after[pl.ds(lag, q), :] == own, 1.0, 0.0)
            dxin = dxin + w_ref[lag : lag + 1, lanes] * dcv[pl.ds(lag, q), lanes] * follow
        sums.append(jnp.sum(dconv, axis=0, keepdims=True))
        sums.append(jnp.sum(dy * x, axis=0, keepdims=True))
        dx_ref[:, lanes] = dxin.astype(bf16)
        for i, s in enumerate(sums):
            dconv_ref[i : i + 1, lanes] = dconv_ref[i : i + 1, lanes] + s
    dsb = d_scores.astype(bf16)
    dbct_ref[0:n, :] = mm(ct, dsb, NN) + mm(after, xt[...], NT)
    dbct_ref[n : 2 * n, :] = mm(bt, dsb, NT) + mm(old, dye[...], NT)
    new = mm(ct, dye[...], NN)
    for k in range(pairs):
        lanes = slice(k * LANES, (k + 1) * LANES)
        dstate[:, lanes] = dstate[:, lanes] * spread(fade, 2 * k, 2 * k + 1, wide_row) + new[:, lanes]
    cols = col_t[...].T
    pulled = d_toend * to_end
    at_end = jnp.sum(pulled, axis=0, keepdims=True) + fade * d_fade[0:1, :]
    d_cum = rows - step * cols + d_enter * entering - pulled
    last_row = lax.broadcasted_iota(jnp.int32, (q, LANES), 0) == q - 1
    d_cum = d_cum + jnp.where(last_row, at_end, 0.0)
    d_decay = exact(tri, d_cum, TN)
    d_step = cols + d_toend * tail - rate * d_decay
    d_raw = d_step * sigmoid(raw)
    dsmall_ref[...] = d_raw
    dhead_ref[0:1, :] = dhead_ref[0:1, :] + jnp.sum(d_raw, axis=0, keepdims=True)
    dhead_ref[1:2, :] = dhead_ref[1:2, :] + jnp.sum(d_decay * decay, axis=0, keepdims=True)
    dcv[pl.ds(q, HALO), :] = dcv[pl.ds(0, HALO), :]
    docs_after[pl.ds(q, HALO), :] = docs_after[pl.ds(0, HALO), :]


def whole(array):
    return pl.BlockSpec(array.shape, lambda c: (0,) * array.ndim)


def run_forward(q, x_in, small, bct, dcol, drow, conv_w, conv_b, sb, rate, skip, head):
    tokens, width = x_in.shape
    n = bct.shape[0] // 2
    chunks = tokens // q
    pairs = width // LANES
    taps = conv_w.shape[0]
    return pl.pallas_call(
        functools.partial(scan_forward, q, taps, pairs, head),
        grid=(chunks,),
        in_specs=[
            pl.BlockSpec((q, width), lambda c: (c, 0)),
            pl.BlockSpec((q, LANES), lambda c: (c, 0)),
            pl.BlockSpec((2 * n, q), lambda c: (0, c)),
            pl.BlockSpec((q, LANES), lambda c: (c, 0)),
            pl.BlockSpec((8, q), lambda c: (0, c)),
            whole(conv_w), whole(conv_b), whole(sb), whole(rate), whole(skip),
        ],
        out_specs=[
            pl.BlockSpec((q, width), lambda c: (c, 0)),
            pl.BlockSpec((1, n, width), lambda c: (c, 0, 0)),
        ],
        out_shape=[
            jax.ShapeDtypeStruct((tokens, width), f32),
            jax.ShapeDtypeStruct((chunks, n, width), f32),
        ],
        scratch_shapes=[
            pltpu.VMEM((n, width), f32),
            pltpu.VMEM((HALO + q, width), f32),
            pltpu.VMEM((HALO + q, LANES), f32),
            pltpu.VMEM((8, LANES), f32),
            pltpu.VMEM((q, width), bf16),
            pltpu.VMEM((8, LANES), f32),
        ],
        name="scan_forward",
    )(x_in, small, bct, dcol, drow, conv_w, conv_b, sb, rate, skip)


def run_backward(q, x_in, small, bct, dcol, drow, conv_w, conv_b, sb, rate, skip, dy, states, head):
    tokens, width = x_in.shape
    n = bct.shape[0] // 2
    chunks = tokens // q
    pairs = width // LANES
    taps = conv_w.shape[0]
    per = q // HALO

    def at(c):
        return chunks - 1 - c

    def prior(c):
        return jnp.maximum((chunks - 1 - c) * per - 1, 0)

    return pl.pallas_call(
        functools.partial(scan_backward, q, taps, pairs, head, chunks),
        grid=(chunks,),
        in_specs=[
            pl.BlockSpec((q, width), lambda c: (at(c), 0)),
            pl.BlockSpec((HALO, width), lambda c: (prior(c), 0)),
            pl.BlockSpec((q, LANES), lambda c: (at(c), 0)),
            pl.BlockSpec((2 * n, q), lambda c: (0, at(c))),
            pl.BlockSpec((q, LANES), lambda c: (at(c), 0)),
            pl.BlockSpec((HALO, LANES), lambda c: (prior(c), 0)),
            pl.BlockSpec((8, q), lambda c: (0, at(c))),
            whole(conv_w), whole(conv_b), whole(sb), whole(rate), whole(skip),
            pl.BlockSpec((q, width), lambda c: (at(c), 0)),
            pl.BlockSpec((1, n, width), lambda c: (at(c), 0, 0)),
        ],
        out_specs=[
            pl.BlockSpec((q, width), lambda c: (at(c), 0)),
            pl.BlockSpec((q, LANES), lambda c: (at(c), 0)),
            pl.BlockSpec((2 * n, q), lambda c: (0, at(c))),
            pl.BlockSpec((8, width), lambda c: (0, 0)),
            pl.BlockSpec((8, LANES), lambda c: (0, 0)),
        ],
        out_shape=[
            jax.ShapeDtypeStruct((tokens, width), bf16),
            jax.ShapeDtypeStruct((tokens, LANES), f32),
            jax.ShapeDtypeStruct((2 * n, tokens), f32),
            jax.ShapeDtypeStruct((8, width), f32),
            jax.ShapeDtypeStruct((8, LANES), f32),
        ],
        scratch_shapes=[
            pltpu.VMEM((n, width), f32),
            pltpu.VMEM((HALO + q, width), f32),
            pltpu.VMEM((HALO + q, LANES), f32),
            pltpu.VMEM((q + HALO, width), f32),
            pltpu.VMEM((q + HALO, LANES), f32),
            pltpu.VMEM((q, width), bf16),
            pltpu.VMEM((q, width), bf16),
            pltpu.VMEM((LANES, q), f32),
        ],
        name="scan_backward",
    )(x_in, x_in, small, bct, dcol, dcol, drow, conv_w, conv_b, sb, rate, skip, dy, states)


def gate_forward(
    groups, z_rows, tall,
    normed_ref, cot_ref, joined_ref, y_ref, gain_ref, z_ref, dgn_ref, sums_ref, wz, wo,
):
    parts, held, width = wo.shape

    @pl.when(pl.program_id(0) == 0)
    def _():
        for g in range(groups):
            wz[pl.ds(g * z_rows, z_rows), :] = joined_ref[g, pl.ds(0, z_rows), :]
            for k in range(parts):
                wo[k, pl.ds(g * tall, tall), :] = joined_ref[g, pl.ds(z_rows + k * tall, tall), :]

    z = mm(normed_ref[...], wz[...], NN)
    d_gn = mm(cot_ref[:, 0:width], wo[0], NT)
    for k in range(1, parts):
        d_gn = d_gn + mm(cot_ref[:, k * width : (k + 1) * width], wo[k], NT)
    z_ref[...] = z
    dgn_ref[...] = d_gn
    gated = y_ref[...] * (z * sigmoid(z))
    square = jnp.sum(gated * gated, axis=1, keepdims=True)
    cross = jnp.sum(d_gn * gain_ref[...] * gated, axis=1, keepdims=True)
    lane = lane_iota((square.shape[0], LANES))
    sums_ref[...] = jnp.where(lane == 0, square, jnp.where(lane == 1, cross, 0.0)).T[0:8, :]


def gate_backward(
    channels,
    y_ref, z_ref, dgn_ref, sums_ref, gain_ref,
    gate_ref, dz_ref, dy_ref, dgain_ref,
):
    rows, width = y_ref.shape

    @pl.when(pl.program_id(0) == 0)
    def _():
        dgain_ref[...] = jnp.zeros_like(dgain_ref)

    columns = jnp.concatenate([sums_ref[...], jnp.zeros((LANES - 8, rows), f32)], axis=0).T
    inv = lax.rsqrt(columns[:, 0:1] / channels + epsilon)
    slope = inv * inv * inv * (columns[:, 1:2] / channels)

    def column(k, _):
        lanes = pl.ds(pl.multiple_of(k * LANES, LANES), LANES)
        y, z, d_gn, gain = y_ref[:, lanes], z_ref[:, lanes], dgn_ref[:, lanes], gain_ref[:, lanes]
        sig = sigmoid(z)
        act = z * sig
        gated = y * act
        scaled = gated * inv
        gate_ref[:, lanes] = (scaled * gain).astype(bf16)
        dgain_ref[0:1, lanes] = dgain_ref[0:1, lanes] + jnp.sum(d_gn * scaled, axis=0, keepdims=True)
        d_gated = inv * (d_gn * gain) - gated * slope
        dz_ref[:, lanes] = (d_gated * y * (sig * (1.0 + z * (1.0 - sig)))).astype(bf16)
        dy_ref[:, lanes] = d_gated * act
        return 0

    lax.fori_loop(0, width // LANES, column, 0)


def run_gate_forward(joined, z_rows, normed, cot, y, gain):
    groups, deep, width = joined.shape
    tokens, n_width = normed.shape
    parts = n_width // width
    tall = (deep - z_rows) // parts
    rows = min(256, tokens)

    def tokens_of(columns):
        return pl.BlockSpec((rows, columns), lambda c: (c, 0))

    return pl.pallas_call(
        functools.partial(gate_forward, groups, z_rows, tall),
        grid=(tokens // rows,),
        in_specs=[tokens_of(n_width), tokens_of(n_width), whole(joined), tokens_of(width), whole(gain)],
        out_specs=[tokens_of(width), tokens_of(width), pl.BlockSpec((8, rows), lambda c: (0, c))],
        out_shape=[
            jax.ShapeDtypeStruct((tokens, width), f32),
            jax.ShapeDtypeStruct((tokens, width), f32),
            jax.ShapeDtypeStruct((8, tokens), f32),
        ],
        scratch_shapes=[
            pltpu.VMEM((groups * z_rows, width), bf16),
            pltpu.VMEM((parts, groups * tall, width), bf16),
        ],
        name="gate_forward",
    )(normed, cot, joined, y, gain)


def run_gate_backward(channels, y, z, d_gn, sums, gain):
    tokens, width = y.shape
    rows = min(256, tokens)
    part = pl.BlockSpec((rows, width), lambda c: (c, 0))
    return pl.pallas_call(
        functools.partial(gate_backward, channels),
        grid=(tokens // rows,),
        in_specs=[part, part, part, pl.BlockSpec((8, rows), lambda c: (0, c)), whole(gain)],
        out_specs=[part, part, part, pl.BlockSpec((8, width), lambda c: (0, 0))],
        out_shape=[
            jax.ShapeDtypeStruct((tokens, width), bf16),
            jax.ShapeDtypeStruct((tokens, width), bf16),
            jax.ShapeDtypeStruct((tokens, width), f32),
            jax.ShapeDtypeStruct((8, width), f32),
        ],
        name="gate_backward",
    )(y, z, d_gn, sums, gain)


def swapped(block, bit):
    size = lax.axis_size("seq")
    return lax.ppermute(block, "seq", [(i, i ^ bit) for i in range(size)])


def bits_of(size):
    bits, bit = [], 1
    while bit < size:
        bits.append(bit)
        bit *= 2
    return bits


def joined_by(held, bit):
    other = swapped(held, bit)
    upper = (lax.axis_index("seq") & bit) != 0
    both = jnp.where(upper, jnp.stack([other, held], axis=1), jnp.stack([held, other], axis=1))
    return both.reshape((-1,) + both.shape[2:])


def opened(block):
    bits = bits_of(lax.axis_size("seq"))
    return joined_by(block[None], bits[-1]) if bits else block[None]


def gathered(block, held=None):
    held = opened(block) if held is None else held
    for bit in reversed(bits_of(lax.axis_size("seq"))[:-1]):
        held = joined_by(held, bit)
    return held.reshape((-1,) + held.shape[2:])


def scattered(parts, between=lambda held: held):
    index = lax.axis_index("seq")
    size = lax.axis_size("seq")
    rest = parts.shape[1:]
    lead = parts.shape[0]
    held = parts.reshape((size, lead // size) + rest)
    for bit in bits_of(size):
        half = held.reshape((held.shape[0] // 2, 2) + held.shape[1:])
        upper = (index & bit) != 0
        mine = jnp.where(upper, half[:, 1], half[:, 0])
        theirs = jnp.where(upper, half[:, 0], half[:, 1]).astype(bf16)
        held = between(mine.astype(f32) + swapped(theirs, bit).astype(f32))
    return held[0]


def added_over(block, bits):
    for bit in bits:
        block = block + crossed(block, bit)
    return block


def moved_by(block, step):
    count = lax.axis_size("dp")
    route = [(i, i + 2 * step) for i in range(count) if 0 <= i + 2 * step < count]
    return lax.ppermute(block, "dp", route)


def crossed(block, bits):
    return lax.ppermute(block, "dp", [(i, i ^ bits) for i in range(lax.axis_size("dp"))])


def gathered_rows(block, waits):
    count = lax.axis_size("dp")
    length = count // 2
    if not is_small(count):
        return lax.all_gather(block, "dp", axis=0, tiled=True), block
    at = lax.axis_index("dp")
    place, side = at // 2, at % 2
    rows = block.shape[0]
    whole_rows = jnp.zeros((count * rows, block.shape[1]), block.dtype)

    def put(into, piece, pair, half):
        return lax.dynamic_update_slice(into, piece, ((pair * 2 + half) * rows, 0))

    whole_rows = put(whole_rows, block, place, side)
    other = crossed(block, 1)
    whole_rows = put(whole_rows, other, place, 1 - side)
    up, down, ready = block, block, []
    for hop in range(1, length):
        up, down = after((moved_by(up, 1), moved_by(down, -1)), (other, waits[hop - 1 : hop]))
        ready.append((down, up))
        piece, pair = None, None
        for spot in range(length):
            near = min(spot, length - 1 - spot)
            if hop <= 2 * near:
                away, from_below = (hop + 1) // 2, hop % 2 == 0
            else:
                away, from_below = hop - near, spot > length - 1 - spot
            chosen = ready[away - 1][1 if from_below else 0]
            source = spot - away if from_below else spot + away
            here = place == spot
            piece = chosen if piece is None else jnp.where(here, chosen, piece)
            pair = source if pair is None else jnp.where(here, source, pair)
        whole_rows = put(whole_rows, piece, pair, side)
        other = crossed(piece, 1)
        whole_rows = put(whole_rows, other, pair, 1 - side)
    return whole_rows, ready[min(1, length - 2)]


def is_small(count):
    return count <= 8 and count & (count - 1) == 0


def halved_rows(term):
    count = lax.axis_size("dp")
    if not is_small(count):
        return term
    at = lax.axis_index("dp")
    pairs = term.reshape(count // 2, 2, -1, term.shape[1])

    def side(which):
        return lax.dynamic_index_in_dim(pairs, which, 1, keepdims=False)

    came = crossed(side((at & 1) ^ 1), 1)
    return (side(at & 1).astype(f32) + came.astype(f32)).astype(bf16)


def shared_rows(lines):
    count = lax.axis_size("dp")
    if not is_small(count):
        return [lax.psum_scatter(lines, "dp", scatter_dimension=0, tiled=True)]
    at = lax.axis_index("dp")

    def part(owner):
        return lax.dynamic_index_in_dim(lines, owner // 2, 0, keepdims=False)

    return [part(at)] + [crossed(part(at ^ bits), bits) for bits in range(2, count, 2)]


def after(value, other):
    return lax.optimization_barrier((value, other))[0]


def turned(blocks):
    size = lax.axis_size("seq")
    index = lax.axis_index("seq")
    if size & (size - 1):
        return lax.all_to_all(blocks, "seq", 0, 0, tiled=True)
    out = blocks
    for bits in range(1, size):
        piece = lax.dynamic_slice_in_dim(blocks, index ^ bits, 1, 0)
        piece = lax.ppermute(piece, "seq", [(i, i ^ bits) for i in range(size)])
        out = lax.dynamic_update_slice_in_dim(out, piece, index ^ bits, 0)
    return out


def folded(rows, lead, width):
    cut = rows.reshape(lead, rows.shape[0] // lead, rows.shape[1] // width, width)
    cut = cut.transpose(0, 2, 1, 3).reshape(lead, -1, width)
    return cut[0] if lead == 1 else cut


def unfolded(pieces, width):
    lead, stacked, narrow = pieces.shape
    cut = pieces.reshape(lead, width // narrow, stacked * narrow // width, narrow)
    return cut.transpose(0, 2, 1, 3).reshape(-1, width)


def exchanged(parts):
    size = lax.axis_size("seq")
    index = lax.axis_index("seq")
    held = parts.reshape((size, -1) + parts.shape[1:])

    def part(owner):
        return lax.dynamic_index_in_dim(held, owner, 0, keepdims=False)

    came = [
        lax.ppermute(part(index ^ bits).astype(bf16), "seq", [(i, i ^ bits) for i in range(size)])
        for bits in range(1, size)
    ]
    return sum([piece.astype(f32) for piece in came], part(index))


def by_rows(array):
    return with_layout_constraint(array, Layout(major_to_minor=(0, 1)))


def padded(rows, width):
    return jnp.pad(rows, ((0, 0), (0, width - rows.shape[1])))


def shards(
    hidden, segments, cotangent, norm_gain, in_weight, conv_weight, conv_bias, step_bias, log_rate,
    skip_gain, gate_gain, out_weight,
):
    n_seqs, block, n_width = hidden.shape
    size = lax.axis_size("seq")
    groups = lax.axis_size("dp")
    index = lax.axis_index("seq")
    tokens = size * block
    n_inner = gate_gain.shape[0]
    n_heads = step_bias.shape[0]
    n_taps = conv_weight.shape[0]
    n_mixed = conv_bias.shape[0]
    n_state = (n_mixed - n_inner) // 2
    head = n_inner // n_heads
    own_inner = n_inner // size
    own_heads = n_heads // size
    own_bc = 2 * n_state // size
    q = min(128, block)
    in_rows = in_weight.shape[0]

    in_low = in_weight.astype(bf16)
    runs = 2 if groups % 2 == 0 else 1

    def dealt(columns):
        cut = columns.reshape(columns.shape[0], runs, size, -1)
        return cut.transpose(0, 2, 1, 3).reshape(columns.shape[0], size, -1)

    def undealt(columns):
        cut = columns.reshape(columns.shape[0], size, runs, -1)
        return cut.transpose(0, 2, 1, 3).reshape(columns.shape[0], -1)

    z_cols = dealt(in_low[:, :n_inner])
    x_cols = dealt(in_low[:, n_inner : 2 * n_inner])
    bc_cols = in_low[:, 2 * n_inner : n_inner + n_mixed].reshape(in_rows, size, own_bc)
    dt_cols = dealt(in_low[:, n_inner + n_mixed :])
    gap = jnp.zeros((in_rows, size, LANES - own_heads - own_bc), bf16)
    laid = jnp.concatenate([x_cols, dt_cols, gap, bc_cols, z_cols], axis=2).transpose(1, 0, 2)
    mine = lax.all_to_all(laid, "seq", 0, 0, tiled=True)
    flat = hidden.reshape(block, n_width).astype(f32)
    inv = lax.rsqrt(jnp.mean(flat * flat, axis=-1, keepdims=True) + epsilon)
    unit = flat * inv
    normed_own = (unit * norm_gain).astype(bf16)
    docs = gathered(segments).reshape(tokens).astype(f32)
    half = groups // runs
    order = []
    for f in range(groups * size):
        run, owner, spot = f // (half * size), f // half % size, f % half
        order.append((f, (run * half + spot) * size + owner))
    back = [(b, a) for a, b in order]
    out_moved = lax.ppermute(out_weight.astype(bf16), ("dp", "seq"), order)
    mine, normed_own = lax.optimization_barrier((after(mine, (docs, out_moved)), normed_own))
    mine = mine.reshape(size * in_rows, -1)
    n_first = own_inner + LANES
    cot_own = cotangent.reshape(block, n_width)
    normed_held = opened(normed_own)
    cot_held = opened(after(cot_own, mine))
    w_first, hopped = gathered_rows(mine[:, :n_first], [normed_held, cot_held])
    z_block = jnp.concatenate([mine[:, n_first:], folded(out_moved, 1, own_inner)], axis=0)

    normed = gathered(normed_own, normed_held)
    joined = lax.all_gather(after(z_block, hopped), "dp", axis=0, tiled=True).reshape(groups, -1, own_inner)
    z_rows = size * in_rows
    w_z = joined[:, :z_rows].reshape(-1, own_inner)
    w_out = unfolded(joined[:, z_rows:], n_width)
    cot = gathered(cot_own, cot_held)
    dcol = jnp.broadcast_to(docs[:, None], (tokens, LANES))
    drow = jnp.broadcast_to(docs[None, :], (8, tokens))

    def own_part(vector, parts):
        return lax.dynamic_slice_in_dim(vector, index * parts, parts, vector.ndim - 1)

    def own_heads_of(vector):
        return lax.dynamic_index_in_dim(dealt(vector), index, 1, keepdims=False)

    w_x, w_small = w_first[:, :own_inner], w_first[:, own_inner:]
    small = mm(normed, w_small, NN)
    x_in = mm(normed, w_x, NN).astype(bf16)
    conv_x = own_heads_of(conv_weight[:, :n_inner])
    bias_x = own_heads_of(conv_bias[None, :n_inner])
    conv_bc = own_part(conv_weight[:, n_inner:], own_bc)
    bias_bc = own_part(conv_bias[None, n_inner:], own_bc)
    sb = padded(own_heads_of(step_bias[None]), LANES)
    rate = padded(jnp.exp(own_heads_of(log_rate[None])), LANES)
    skip = jnp.repeat(own_heads_of(skip_gain[None]), head, axis=1)
    gain = own_heads_of(gate_gain[None])

    head_lanes = jnp.arange(LANES) < own_heads
    bc_in = small[:, LANES - own_bc :].astype(bf16).astype(f32)
    small_dt = jnp.where(head_lanes, small, 0.0)

    def earlier(rows, lag):
        return jnp.pad(rows, ((lag, 0), (0, 0)))[:tokens]

    def later(rows, lag):
        return jnp.pad(rows, ((0, lag), (0, 0)))[lag:]

    same = [None] + [
        jnp.where(jnp.pad(docs, (lag, 0), constant_values=-1.0)[:tokens] == docs, 1.0, 0.0)[:, None]
        for lag in range(1, n_taps)
    ]
    bc_conv = bias_bc + conv_bc[0:1] * bc_in
    for lag in range(1, n_taps):
        bc_conv = bc_conv + conv_bc[lag : lag + 1] * earlier(bc_in, lag) * same[lag]
    bc_sig = jax.nn.sigmoid(bc_conv)
    bct = gathered(by_rows((bc_conv * bc_sig).astype(bf16).T))

    y, states = run_forward(
        q, x_in, small_dt, bct, dcol, drow, conv_x, bias_x, sb, rate, skip, head
    )

    out_rows = own_inner // groups
    tiled = z_rows % 16 == 0 and out_rows % 16 == 0
    if tiled:
        lead, deep, tall, gate_in = groups, z_rows, out_rows, joined
    else:
        lead, deep, tall = 1, groups * z_rows, own_inner
        gate_in = jnp.concatenate([w_z, folded(w_out, 1, own_inner)], axis=0)[None]
    z, d_gn, sums = run_gate_forward(gate_in, deep, normed, cot, y, gain)
    sums = lax.psum(sums[:2], "seq")
    sums = jnp.pad(sums, ((0, 6), (0, 0)))
    gate_low, d_z, d_y, d_gain = run_gate_backward(n_inner, y, z, d_gn, sums, gain)
    d_gain = d_gain[0]
    terms = [mm(normed, d_z, TN)]
    for k in range(0, n_width, own_inner):
        terms.append(mm(gate_low, cot[:, k : k + own_inner], TN))
    terms = [term.astype(bf16).reshape(groups, -1, own_inner) for term in terms]
    terms = jnp.concatenate(terms, axis=1).reshape(-1, own_inner)
    terms, d_y = lax.optimization_barrier((terms, d_y))
    parts = lax.psum_scatter(terms, "dp", scatter_dimension=0, tiled=True)

    d_x, d_dt, d_bct, d_conv_x, d_heads = run_backward(
        q, x_in, small_dt, bct, dcol, drow, conv_x, bias_x, sb, rate, skip, d_y, states, head
    )
    x_term = mm(normed, d_x, TN).astype(bf16)
    x_term, d_bct = lax.optimization_barrier((x_term, d_bct))
    x_lines = halved_rows(x_term)
    d_bc = by_rows(exchanged(d_bct)).T
    d_bcc = d_bc * (bc_sig * (1.0 + bc_conv * (1.0 - bc_sig)))
    d_bc_in = conv_bc[0:1] * d_bcc
    w_sums = [jnp.sum(d_bcc * bc_in, axis=0)]
    for lag in range(1, n_taps):
        held = d_bcc * same[lag]
        d_bc_in = d_bc_in + conv_bc[lag : lag + 1] * later(held, lag)
        w_sums.append(jnp.sum(held * earlier(bc_in, lag), axis=0))
    w_sums.append(jnp.sum(d_bcc, axis=0))
    d_small = jnp.concatenate([d_dt[:, : LANES - own_bc], d_bc_in], axis=1).astype(bf16)
    d_first = jnp.concatenate([d_x, d_small], axis=1)
    small_lines = halved_rows(mm(normed, d_small, TN).astype(bf16))
    branch = scattered(mm(after(gate_low, d_bc), w_out, NN).astype(bf16))
    result = (flat + branch).reshape(n_seqs, block, n_width).astype(bf16)
    x_shares = shared_rows(x_lines)
    d_first = after(d_first, x_lines)
    d_normed = mm(d_first, w_first, NT) + mm(d_z, w_z, NT)
    d_norm_gain = jnp.sum(d_normed * normed.astype(f32), axis=0) / norm_gain
    d_skip = jnp.sum(d_conv_x[n_taps + 1].reshape(own_heads, head), axis=1)
    packed = jnp.concatenate(
        [
            d_conv_x[: n_taps + 1].reshape(-1),
            jnp.stack(w_sums).reshape(-1),
            d_gain,
            d_heads[0, :own_heads],
            d_heads[1, :own_heads],
            d_skip,
            d_norm_gain,
        ]
    )
    lines = jnp.concatenate([x_lines, small_lines], axis=-1)
    packed = added_over(after(packed, x_shares[:2]), reversed(bits_of(groups)[1:]))
    parts, result = lax.optimization_barrier((after(parts, x_shares[:2]), result))
    packed = added_over(after(packed, (x_shares[:3], parts)), bits_of(groups)[:1])
    packed = gathered(after(packed, x_shares)[None])
    small_shares = shared_rows(small_lines)
    d_norm = after(d_normed.astype(bf16), parts)
    d_norm = lax.psum_scatter(d_norm, "seq", scatter_dimension=0, tiled=True).astype(f32)

    def own_rows(part):
        out = turned(part.reshape(size, in_rows, -1))
        return out.transpose(1, 0, 2).astype(f32)

    out_part = unfolded(parts[None, z_rows:], n_width)
    d_out_weight = lax.ppermute(out_part, ("dp", "seq"), back).astype(f32)
    in_z = own_rows(parts[:z_rows])
    x_shares, in_z, d_out_weight = lax.optimization_barrier((x_shares, in_z, d_out_weight))
    first_part = [sum(piece.astype(f32) for piece in own) for own in (x_shares, small_shares)]
    first_part = jnp.concatenate(first_part, axis=1)
    in_first = own_rows(first_part.astype(bf16))
    d_in_weight = jnp.concatenate(
        [
            undealt(in_z),
            undealt(in_first[:, :, :own_inner]),
            in_first[:, :, n_first - own_bc :].reshape(in_rows, 2 * n_state),
            undealt(in_first[:, :, own_inner : own_inner + own_heads]),
        ],
        axis=1,
    )

    lifted = d_norm * norm_gain
    d_flat = inv * lifted - flat * (
        inv * inv * inv * jnp.mean(lifted * flat, axis=-1, keepdims=True)
    )
    d_hidden = (cot_own.astype(f32) + d_flat).reshape(n_seqs, block, n_width)

    at = 0

    def take(count):
        nonlocal at
        at += count
        return packed[:, at - count : at]

    got_x = take((n_taps + 1) * own_inner).reshape(size, n_taps + 1, own_inner)
    got_bc = take((n_taps + 1) * own_bc).reshape(size, n_taps + 1, own_bc)
    got_x = undealt(got_x.transpose(1, 0, 2))
    got_bc = got_bc.transpose(1, 0, 2).reshape(n_taps + 1, 2 * n_state)
    conv_all = jnp.concatenate([got_x, got_bc], axis=1)
    d_gate_gain = undealt(take(own_inner)[None])[0]
    d_step_bias = undealt(take(own_heads)[None])[0]
    d_log_rate = undealt(take(own_heads)[None])[0]
    d_skip_gain = undealt(take(own_heads)[None])[0]
    d_norm_all = jnp.sum(take(n_width), axis=0)
    return (
        result,
        d_hidden,
        d_norm_all,
        d_in_weight,
        conv_all[:n_taps],
        conv_all[n_taps],
        d_step_bias,
        d_log_rate,
        d_skip_gain,
        d_gate_gain,
        d_out_weight,
    )


def solution(mesh):
    tokens = P("dp", "seq", None)
    rows = P(("dp", "seq"), None)
    return jax.shard_map(
        shards,
        mesh=mesh,
        in_specs=(tokens, P("dp", "seq"), tokens, P(), rows, P(), P(), P(), P(), P(), P(), rows),
        out_specs=(tokens, tokens, P(), rows, P(), P(), P(), P(), P(), P(), rows),
        check_vma=False,
    )
```

```python
import functools

import jax
import jax.numpy as jnp
from jax import lax
from jax.experimental import pallas as pl
from jax.experimental.layout import Layout, with_layout_constraint
from jax.experimental.pallas import tpu as pltpu
from jax.sharding import PartitionSpec as P

epsilon = 1e-05
highest = lax.Precision.HIGHEST
f32 = jnp.float32
bf16 = jnp.bfloat16
LANES = 128
HALO = 16
NEG = -1e30


def mm(a, b, dims, out=f32):
    return lax.dot_general(a, b, (dims, ((), ())), preferred_element_type=out)


NN = ((1,), (0,))
NT = ((1,), (1,))
TN = ((0,), (0,))


def exact(a, b, dims):
    return lax.dot_general(a, b, (dims, ((), ())), precision=highest, preferred_element_type=f32)


def softplus(v):
    return jnp.maximum(v, 0.0) + jnp.log1p(jnp.exp(-jnp.abs(v)))


def sigmoid(v):
    return 1.0 / (1.0 + jnp.exp(-v))


def lane_iota(shape):
    return lax.broadcasted_iota(jnp.int32, shape, len(shape) - 1)


def spread(columns, first, second, wide):
    rows = columns.shape[0]
    left = jnp.broadcast_to(columns[:, first : first + 1], (rows, LANES))
    right = jnp.broadcast_to(columns[:, second : second + 1], (rows, LANES))
    return jnp.where(wide, left, right)


def step_parts(raw, rate, q):
    row = lax.broadcasted_iota(jnp.int32, (q, q), 0)
    col = lax.broadcasted_iota(jnp.int32, (q, q), 1)
    tri = jnp.where(row >= col, 1.0, 0.0).astype(f32)
    step = softplus(raw)
    decay = -step * rate
    total = exact(tri, decay, NN)
    return step, decay, total, tri, row >= col


def convolve(ext, docs_ext, own, weights, bias, lanes, q, taps):
    running = bias + weights[0:1, lanes] * ext[pl.ds(HALO, q), lanes]
    for lag in range(1, taps):
        same = jnp.where(docs_ext[pl.ds(HALO - lag, q), :] == own, 1.0, 0.0)
        running = running + weights[lag : lag + 1, lanes] * ext[pl.ds(HALO - lag, q), lanes] * same
    return running


def scan_forward(
    q, taps, pairs, head,
    x_ref, small_ref, bct_ref, dcol_ref, drow_ref, w_ref, b_ref, sb_ref, rate_ref, skip_ref,
    y_ref, states_ref,
    state, ext, docs_ext, xs, xt, last_doc,
):
    c = pl.program_id(0)
    n = bct_ref.shape[0] // 2

    @pl.when(c == 0)
    def _():
        state[...] = jnp.zeros_like(state)
        ext[pl.ds(0, HALO), :] = jnp.zeros((HALO, ext.shape[1]), f32)
        docs_ext[pl.ds(0, HALO), :] = jnp.full((HALO, LANES), -1.0, f32)
        last_doc[...] = jnp.full(last_doc.shape, -1.0, f32)

    own = dcol_ref[...]
    ext[pl.ds(HALO, q), :] = x_ref[...].astype(f32)
    docs_ext[pl.ds(HALO, q), :] = own
    step, _, cum, _, causal = step_parts(small_ref[...] + sb_ref[...], rate_ref[...], q)
    step_t = step.T
    cum_t = cum.T
    end = cum[q - 1 : q, :]
    id_in = last_doc[0:1, :]
    final = own[q - 1 : q, :]
    linked = jnp.where(final == id_in, 1.0, 0.0)
    fade = linked * jnp.exp(end)
    entering = jnp.where(own == id_in, 1.0, 0.0) * jnp.exp(cum)
    to_end = jnp.where(own == final, 1.0, 0.0) * jnp.exp(end - cum) * step
    same_doc = jnp.broadcast_to(own[:, 0:1], (q, q)) == jnp.broadcast_to(drow_ref[0:1, :], (q, q))
    hide = jnp.where(jnp.logical_and(causal, same_doc), 0.0, NEG)
    bt = bct_ref[0:n, :]
    ct = bct_ref[n : 2 * n, :]
    scores = mm(ct, bt, TN)
    states_ref[0] = state[...]
    old = state[...].astype(bf16)
    wide = lane_iota((q, LANES)) < head
    wide_row = lane_iota((1, LANES)) < head
    for k in range(pairs):
        lanes = slice(k * LANES, (k + 1) * LANES)
        h0, h1 = 2 * k, 2 * k + 1
        conv = convolve(ext, docs_ext, own, w_ref, b_ref[:, lanes], lanes, q, taps)
        x = conv * sigmoid(conv)
        xd = x * spread(step, h0, h1, wide)
        xt[:, lanes] = (x * spread(to_end, h0, h1, wide)).astype(bf16)
        mats = []
        for h in (h0, h1):
            gap = cum[:, h : h + 1] - cum_t[h : h + 1, :] + hide
            mats.append((jnp.exp(gap) * scores).astype(bf16))
        out = mm(mats[0], jnp.where(wide, xd, 0.0).astype(bf16), NN)
        out = out + mm(mats[1], jnp.where(wide, 0.0, xd).astype(bf16), NN)
        out = out + mm(ct, old[:, lanes], TN) * spread(entering, h0, h1, wide)
        y_ref[:, lanes] = out + skip_ref[:, lanes] * x
    update = mm(bt, xt[...], NN)
    for k in range(pairs):
        lanes = slice(k * LANES, (k + 1) * LANES)
        state[:, lanes] = state[:, lanes] * spread(fade, 2 * k, 2 * k + 1, wide_row) + update[:, lanes]
    ext[pl.ds(0, HALO), :] = ext[pl.ds(q, HALO), :]
    docs_ext[pl.ds(0, HALO), :] = docs_ext[pl.ds(q, HALO), :]
    last_doc[...] = jnp.broadcast_to(final, last_doc.shape)


def scan_backward(
    q, taps, pairs, head, chunks,
    x_ref, xp_ref, small_ref, bct_ref, dcol_ref, dcolp_ref, drow_ref, w_ref, b_ref, sb_ref, rate_ref,
    skip_ref, dy_ref, states_ref,
    dx_ref, dsmall_ref, dbct_ref, dconv_ref, dhead_ref,
    dstate, ext, docs_ext, dcv, docs_after, dye, xt, col_t,
):
    step_at = pl.program_id(0)
    c = chunks - 1 - step_at
    n = bct_ref.shape[0] // 2
    width = x_ref.shape[1]

    @pl.when(step_at == 0)
    def _():
        dstate[...] = jnp.zeros_like(dstate)
        dcv[pl.ds(q, HALO), :] = jnp.zeros((HALO, width), f32)
        docs_after[pl.ds(q, HALO), :] = jnp.full((HALO, LANES), -1.0, f32)
        dconv_ref[...] = jnp.zeros_like(dconv_ref)
        dhead_ref[...] = jnp.zeros_like(dhead_ref)
        col_t[...] = jnp.zeros_like(col_t)

    first = c == 0
    own = dcol_ref[...]
    before = jnp.where(first, -1.0, dcolp_ref[...])
    ext[pl.ds(0, HALO), :] = xp_ref[...].astype(f32)
    ext[pl.ds(HALO, q), :] = x_ref[...].astype(f32)
    docs_ext[pl.ds(0, HALO), :] = before
    docs_ext[pl.ds(HALO, q), :] = own
    docs_after[pl.ds(0, q), :] = own
    raw = small_ref[...] + sb_ref[...]
    rate = rate_ref[...]
    step, decay, cum, tri, causal = step_parts(raw, rate, q)
    step_t = step.T
    cum_t = cum.T
    end = cum[q - 1 : q, :]
    id_in = before[HALO - 1 : HALO, :]
    final = own[q - 1 : q, :]
    linked = jnp.where(final == id_in, 1.0, 0.0)
    fade = linked * jnp.exp(end)
    entering = jnp.where(own == id_in, 1.0, 0.0) * jnp.exp(cum)
    tail = jnp.where(own == final, 1.0, 0.0) * jnp.exp(end - cum)
    to_end = tail * step
    same_doc = jnp.broadcast_to(own[:, 0:1], (q, q)) == jnp.broadcast_to(drow_ref[0:1, :], (q, q))
    hide = jnp.where(jnp.logical_and(causal, same_doc), 0.0, NEG)
    bt = bct_ref[0:n, :]
    ct = bct_ref[n : 2 * n, :]
    scores = mm(ct, bt, TN)
    old = states_ref[0].astype(bf16)
    after = dstate[...].astype(bf16)
    wide = lane_iota((q, LANES)) < head
    wide_row = lane_iota((1, LANES)) < head
    lane = lane_iota((q, LANES))
    d_scores = jnp.zeros((q, q), f32)
    rows = jnp.zeros((q, LANES), f32)
    d_enter = jnp.zeros((q, LANES), f32)
    d_toend = jnp.zeros((q, LANES), f32)
    d_fade = jnp.zeros((8, LANES), f32)
    part = lax.broadcasted_iota(jnp.int32, (LANES, LANES), 0) // head
    to = lane_iota((LANES, LANES))
    for k in range(pairs):
        lanes = slice(k * LANES, (k + 1) * LANES)
        h0, h1 = 2 * k, 2 * k + 1
        pick = jnp.where(part + 2 * k == to, 1.0, 0.0)
        conv = convolve(ext, docs_ext, own, w_ref, b_ref[:, lanes], lanes, q, taps)
        sig = sigmoid(conv)
        x = conv * sig
        xb = x.astype(bf16)
        dy = dy_ref[:, lanes]
        halves = (jnp.where(wide, dy, 0.0).astype(bf16), jnp.where(wide, 0.0, dy).astype(bf16))
        dxd = jnp.zeros((q, LANES), f32)
        for h, half in ((h0, halves[0]), (h1, halves[1])):
            inner = mm(half, xb, NT)
            keep = jnp.exp(cum[:, h : h + 1] - cum_t[h : h + 1, :] + hide)
            grown = keep * inner
            mat = keep * scores
            dt = step_t[h : h + 1, :]
            g = grown * scores
            d_scores = d_scores + grown * dt
            rows = jnp.where(lane == h, jnp.sum(g * dt, axis=1, keepdims=True), rows)
            col_t[h : h + 1, :] = jnp.sum(g, axis=0, keepdims=True)
            dxd = dxd + mm(mat.astype(bf16), half, TN)
        v = mm(bt, after[:, lanes], TN)
        u = mm(ct, old[:, lanes], TN)
        enter_k = spread(entering, h0, h1, wide)
        end_k = spread(to_end, h0, h1, wide)
        d_enter = d_enter + exact(dy * u, pick, NN)
        d_toend = d_toend + exact(x * v, pick, NN)
        hh = jnp.sum(dstate[:, lanes] * states_ref[0, :, lanes], axis=0, keepdims=True)
        d_fade = d_fade + exact(jnp.broadcast_to(hh, (8, LANES)), pick, NN)
        dye[:, lanes] = (dy * enter_k).astype(bf16)
        xt[:, lanes] = (x * end_k).astype(bf16)
        dx = dxd * spread(step, h0, h1, wide) + end_k * v + skip_ref[:, lanes] * dy
        dconv = dx * (sig * (1.0 + conv * (1.0 - sig)))
        dcv[pl.ds(0, q), lanes] = dconv
        sums = [jnp.sum(dconv * ext[pl.ds(HALO, q), lanes], axis=0, keepdims=True)]
        dxin = w_ref[0:1, lanes] * dconv
        for lag in range(1, taps):
            same = jnp.where(docs_ext[pl.ds(HALO - lag, q), :] == own, 1.0, 0.0)
            sums.append(jnp.sum(dconv * same * ext[pl.ds(HALO - lag, q), lanes], axis=0, keepdims=True))
            follow = jnp.where(docs_after[pl.ds(lag, q), :] == own, 1.0, 0.0)
            dxin = dxin + w_ref[lag : lag + 1, lanes] * dcv[pl.ds(lag, q), lanes] * follow
        sums.append(jnp.sum(dconv, axis=0, keepdims=True))
        sums.append(jnp.sum(dy * x, axis=0, keepdims=True))
        dx_ref[:, lanes] = dxin.astype(bf16)
        for i, s in enumerate(sums):
            dconv_ref[i : i + 1, lanes] = dconv_ref[i : i + 1, lanes] + s
    dsb = d_scores.astype(bf16)
    dbct_ref[0:n, :] = mm(ct, dsb, NN) + mm(after, xt[...], NT)
    dbct_ref[n : 2 * n, :] = mm(bt, dsb, NT) + mm(old, dye[...], NT)
    new = mm(ct, dye[...], NN)
    for k in range(pairs):
        lanes = slice(k * LANES, (k + 1) * LANES)
        dstate[:, lanes] = dstate[:, lanes] * spread(fade, 2 * k, 2 * k + 1, wide_row) + new[:, lanes]
    cols = col_t[...].T
    pulled = d_toend * to_end
    at_end = jnp.sum(pulled, axis=0, keepdims=True) + fade * d_fade[0:1, :]
    d_cum = rows - step * cols + d_enter * entering - pulled
    last_row = lax.broadcasted_iota(jnp.int32, (q, LANES), 0) == q - 1
    d_cum = d_cum + jnp.where(last_row, at_end, 0.0)
    d_decay = exact(tri, d_cum, TN)
    d_step = cols + d_toend * tail - rate * d_decay
    d_raw = d_step * sigmoid(raw)
    dsmall_ref[...] = d_raw
    dhead_ref[0:1, :] = dhead_ref[0:1, :] + jnp.sum(d_raw, axis=0, keepdims=True)
    dhead_ref[1:2, :] = dhead_ref[1:2, :] + jnp.sum(d_decay * decay, axis=0, keepdims=True)
    dcv[pl.ds(q, HALO), :] = dcv[pl.ds(0, HALO), :]
    docs_after[pl.ds(q, HALO), :] = docs_after[pl.ds(0, HALO), :]


def whole(array):
    return pl.BlockSpec(array.shape, lambda c: (0,) * array.ndim)


def run_forward(q, x_in, small, bct, dcol, drow, conv_w, conv_b, sb, rate, skip, head):
    tokens, width = x_in.shape
    n = bct.shape[0] // 2
    chunks = tokens // q
    pairs = width // LANES
    taps = conv_w.shape[0]
    return pl.pallas_call(
        functools.partial(scan_forward, q, taps, pairs, head),
        grid=(chunks,),
        in_specs=[
            pl.BlockSpec((q, width), lambda c: (c, 0)),
            pl.BlockSpec((q, LANES), lambda c: (c, 0)),
            pl.BlockSpec((2 * n, q), lambda c: (0, c)),
            pl.BlockSpec((q, LANES), lambda c: (c, 0)),
            pl.BlockSpec((8, q), lambda c: (0, c)),
            whole(conv_w), whole(conv_b), whole(sb), whole(rate), whole(skip),
        ],
        out_specs=[
            pl.BlockSpec((q, width), lambda c: (c, 0)),
            pl.BlockSpec((1, n, width), lambda c: (c, 0, 0)),
        ],
        out_shape=[
            jax.ShapeDtypeStruct((tokens, width), f32),
            jax.ShapeDtypeStruct((chunks, n, width), f32),
        ],
        scratch_shapes=[
            pltpu.VMEM((n, width), f32),
            pltpu.VMEM((HALO + q, width), f32),
            pltpu.VMEM((HALO + q, LANES), f32),
            pltpu.VMEM((8, LANES), f32),
            pltpu.VMEM((q, width), bf16),
            pltpu.VMEM((8, LANES), f32),
        ],
        name="scan_forward",
    )(x_in, small, bct, dcol, drow, conv_w, conv_b, sb, rate, skip)


def run_backward(q, x_in, small, bct, dcol, drow, conv_w, conv_b, sb, rate, skip, dy, states, head):
    tokens, width = x_in.shape
    n = bct.shape[0] // 2
    chunks = tokens // q
    pairs = width // LANES
    taps = conv_w.shape[0]
    per = q // HALO

    def at(c):
        return chunks - 1 - c

    def prior(c):
        return jnp.maximum((chunks - 1 - c) * per - 1, 0)

    return pl.pallas_call(
        functools.partial(scan_backward, q, taps, pairs, head, chunks),
        grid=(chunks,),
        in_specs=[
            pl.BlockSpec((q, width), lambda c: (at(c), 0)),
            pl.BlockSpec((HALO, width), lambda c: (prior(c), 0)),
            pl.BlockSpec((q, LANES), lambda c: (at(c), 0)),
            pl.BlockSpec((2 * n, q), lambda c: (0, at(c))),
            pl.BlockSpec((q, LANES), lambda c: (at(c), 0)),
            pl.BlockSpec((HALO, LANES), lambda c: (prior(c), 0)),
            pl.BlockSpec((8, q), lambda c: (0, at(c))),
            whole(conv_w), whole(conv_b), whole(sb), whole(rate), whole(skip),
            pl.BlockSpec((q, width), lambda c: (at(c), 0)),
            pl.BlockSpec((1, n, width), lambda c: (at(c), 0, 0)),
        ],
        out_specs=[
            pl.BlockSpec((q, width), lambda c: (at(c), 0)),
            pl.BlockSpec((q, LANES), lambda c: (at(c), 0)),
            pl.BlockSpec((2 * n, q), lambda c: (0, at(c))),
            pl.BlockSpec((8, width), lambda c: (0, 0)),
            pl.BlockSpec((8, LANES), lambda c: (0, 0)),
        ],
        out_shape=[
            jax.ShapeDtypeStruct((tokens, width), bf16),
            jax.ShapeDtypeStruct((tokens, LANES), f32),
            jax.ShapeDtypeStruct((2 * n, tokens), f32),
            jax.ShapeDtypeStruct((8, width), f32),
            jax.ShapeDtypeStruct((8, LANES), f32),
        ],
        scratch_shapes=[
            pltpu.VMEM((n, width), f32),
            pltpu.VMEM((HALO + q, width), f32),
            pltpu.VMEM((HALO + q, LANES), f32),
            pltpu.VMEM((q + HALO, width), f32),
            pltpu.VMEM((q + HALO, LANES), f32),
            pltpu.VMEM((q, width), bf16),
            pltpu.VMEM((q, width), bf16),
            pltpu.VMEM((LANES, q), f32),
        ],
        name="scan_backward",
    )(x_in, x_in, small, bct, dcol, dcol, drow, conv_w, conv_b, sb, rate, skip, dy, states)


def gate_forward(
    groups, z_rows, tall,
    normed_ref, cot_ref, joined_ref, y_ref, gain_ref, z_ref, dgn_ref, sums_ref, wz, wo,
):
    parts, held, width = wo.shape

    @pl.when(pl.program_id(0) == 0)
    def _():
        for g in range(groups):
            wz[pl.ds(g * z_rows, z_rows), :] = joined_ref[g, pl.ds(0, z_rows), :]
            for k in range(parts):
                wo[k, pl.ds(g * tall, tall), :] = joined_ref[g, pl.ds(z_rows + k * tall, tall), :]

    z = mm(normed_ref[...], wz[...], NN)
    d_gn = mm(cot_ref[:, 0:width], wo[0], NT)
    for k in range(1, parts):
        d_gn = d_gn + mm(cot_ref[:, k * width : (k + 1) * width], wo[k], NT)
    z_ref[...] = z
    dgn_ref[...] = d_gn
    gated = y_ref[...] * (z * sigmoid(z))
    square = jnp.sum(gated * gated, axis=1, keepdims=True)
    cross = jnp.sum(d_gn * gain_ref[...] * gated, axis=1, keepdims=True)
    lane = lane_iota((square.shape[0], LANES))
    sums_ref[...] = jnp.where(lane == 0, square, jnp.where(lane == 1, cross, 0.0)).T[0:8, :]


def gate_backward(
    channels,
    y_ref, z_ref, dgn_ref, sums_ref, gain_ref,
    gate_ref, dz_ref, dy_ref, dgain_ref,
):
    rows, width = y_ref.shape

    @pl.when(pl.program_id(0) == 0)
    def _():
        dgain_ref[...] = jnp.zeros_like(dgain_ref)

    columns = jnp.concatenate([sums_ref[...], jnp.zeros((LANES - 8, rows), f32)], axis=0).T
    inv = lax.rsqrt(columns[:, 0:1] / channels + epsilon)
    slope = inv * inv * inv * (columns[:, 1:2] / channels)

    def column(k, _):
        lanes = pl.ds(pl.multiple_of(k * LANES, LANES), LANES)
        y, z, d_gn, gain = y_ref[:, lanes], z_ref[:, lanes], dgn_ref[:, lanes], gain_ref[:, lanes]
        sig = sigmoid(z)
        act = z * sig
        gated = y * act
        scaled = gated * inv
        gate_ref[:, lanes] = (scaled * gain).astype(bf16)
        dgain_ref[0:1, lanes] = dgain_ref[0:1, lanes] + jnp.sum(d_gn * scaled, axis=0, keepdims=True)
        d_gated = inv * (d_gn * gain) - gated * slope
        dz_ref[:, lanes] = (d_gated * y * (sig * (1.0 + z * (1.0 - sig)))).astype(bf16)
        dy_ref[:, lanes] = d_gated * act
        return 0

    lax.fori_loop(0, width // LANES, column, 0)


def run_gate_forward(joined, z_rows, normed, cot, y, gain):
    groups, deep, width = joined.shape
    tokens, n_width = normed.shape
    parts = n_width // width
    tall = (deep - z_rows) // parts
    rows = min(256, tokens)

    def tokens_of(columns):
        return pl.BlockSpec((rows, columns), lambda c: (c, 0))

    return pl.pallas_call(
        functools.partial(gate_forward, groups, z_rows, tall),
        grid=(tokens // rows,),
        in_specs=[tokens_of(n_width), tokens_of(n_width), whole(joined), tokens_of(width), whole(gain)],
        out_specs=[tokens_of(width), tokens_of(width), pl.BlockSpec((8, rows), lambda c: (0, c))],
        out_shape=[
            jax.ShapeDtypeStruct((tokens, width), f32),
            jax.ShapeDtypeStruct((tokens, width), f32),
            jax.ShapeDtypeStruct((8, tokens), f32),
        ],
        scratch_shapes=[
            pltpu.VMEM((groups * z_rows, width), bf16),
            pltpu.VMEM((parts, groups * tall, width), bf16),
        ],
        name="gate_forward",
    )(normed, cot, joined, y, gain)


def run_gate_backward(channels, y, z, d_gn, sums, gain):
    tokens, width = y.shape
    rows = min(256, tokens)
    part = pl.BlockSpec((rows, width), lambda c: (c, 0))
    return pl.pallas_call(
        functools.partial(gate_backward, channels),
        grid=(tokens // rows,),
        in_specs=[part, part, part, pl.BlockSpec((8, rows), lambda c: (0, c)), whole(gain)],
        out_specs=[part, part, part, pl.BlockSpec((8, width), lambda c: (0, 0))],
        out_shape=[
            jax.ShapeDtypeStruct((tokens, width), bf16),
            jax.ShapeDtypeStruct((tokens, width), bf16),
            jax.ShapeDtypeStruct((tokens, width), f32),
            jax.ShapeDtypeStruct((8, width), f32),
        ],
        name="gate_backward",
    )(y, z, d_gn, sums, gain)


def swapped(block, bit):
    size = lax.axis_size("seq")
    return lax.ppermute(block, "seq", [(i, i ^ bit) for i in range(size)])


def bits_of(size):
    bits, bit = [], 1
    while bit < size:
        bits.append(bit)
        bit *= 2
    return bits


def joined_by(held, bit):
    other = swapped(held, bit)
    upper = (lax.axis_index("seq") & bit) != 0
    both = jnp.where(upper, jnp.stack([other, held], axis=1), jnp.stack([held, other], axis=1))
    return both.reshape((-1,) + both.shape[2:])


def opened(block):
    bits = bits_of(lax.axis_size("seq"))
    return joined_by(block[None], bits[-1]) if bits else block[None]


def gathered(block, held=None):
    held = opened(block) if held is None else held
    for bit in reversed(bits_of(lax.axis_size("seq"))[:-1]):
        held = joined_by(held, bit)
    return held.reshape((-1,) + held.shape[2:])


def scattered(parts, between=lambda held: held):
    index = lax.axis_index("seq")
    size = lax.axis_size("seq")
    rest = parts.shape[1:]
    lead = parts.shape[0]
    held = parts.reshape((size, lead // size) + rest)
    for bit in bits_of(size):
        half = held.reshape((held.shape[0] // 2, 2) + held.shape[1:])
        upper = (index & bit) != 0
        mine = jnp.where(upper, half[:, 1], half[:, 0])
        theirs = jnp.where(upper, half[:, 0], half[:, 1]).astype(bf16)
        held = between(mine.astype(f32) + swapped(theirs, bit).astype(f32))
    return held[0]


def added_over(block, bits):
    for bit in bits:
        block = block + crossed(block, bit)
    return block


def moved_by(block, step):
    count = lax.axis_size("dp")
    route = [(i, i + 2 * step) for i in range(count) if 0 <= i + 2 * step < count]
    return lax.ppermute(block, "dp", route)


def crossed(block, bits):
    return lax.ppermute(block, "dp", [(i, i ^ bits) for i in range(lax.axis_size("dp"))])


def gathered_rows(block, waits):
    count = lax.axis_size("dp")
    length = count // 2
    if not is_small(count):
        return lax.all_gather(block, "dp", axis=0, tiled=True), block
    at = lax.axis_index("dp")
    place, side = at // 2, at % 2
    rows = block.shape[0]
    whole_rows = jnp.zeros((count * rows, block.shape[1]), block.dtype)

    def put(into, piece, pair, half):
        return lax.dynamic_update_slice(into, piece, ((pair * 2 + half) * rows, 0))

    whole_rows = put(whole_rows, block, place, side)
    other = crossed(block, 1)
    whole_rows = put(whole_rows, other, place, 1 - side)
    up, down, ready = block, block, []
    for hop in range(1, length):
        up, down = after((moved_by(up, 1), moved_by(down, -1)), (other, waits[hop - 1 : hop]))
        ready.append((down, up))
        piece, pair = None, None
        for spot in range(length):
            near = min(spot, length - 1 - spot)
            if hop <= 2 * near:
                away, from_below = (hop + 1) // 2, hop % 2 == 0
            else:
                away, from_below = hop - near, spot > length - 1 - spot
            chosen = ready[away - 1][1 if from_below else 0]
            source = spot - away if from_below else spot + away
            here = place == spot
            piece = chosen if piece is None else jnp.where(here, chosen, piece)
            pair = source if pair is None else jnp.where(here, source, pair)
        whole_rows = put(whole_rows, piece, pair, side)
        other = crossed(piece, 1)
        whole_rows = put(whole_rows, other, pair, 1 - side)
    return whole_rows, ready[0]


def is_small(count):
    return count <= 8 and count & (count - 1) == 0


def cut_rows(held, bit):
    upper = (lax.axis_index("dp") & bit) != 0
    pair = held.reshape((2, -1) + held.shape[1:])
    mine = lax.dynamic_index_in_dim(pair, upper.astype(jnp.int32), 0, keepdims=False)
    theirs = lax.dynamic_index_in_dim(pair, 1 - upper.astype(jnp.int32), 0, keepdims=False)
    return mine, theirs


def first_cut(term):
    count = lax.axis_size("dp")
    blocks = term.reshape(count // 2, 2, -1, term.shape[1])
    side = lax.axis_index("dp") & 1
    mine = lax.dynamic_index_in_dim(blocks, side, 1, keepdims=False)
    theirs = lax.dynamic_index_in_dim(blocks, 1 - side, 1, keepdims=False)
    return mine, theirs


def added_to(mine, theirs, bit):
    return (mine.astype(f32) + crossed(theirs, bit).astype(f32)).astype(bf16)


def after(value, other):
    return lax.optimization_barrier((value, other))[0]


def turned(blocks):
    size = lax.axis_size("seq")
    index = lax.axis_index("seq")
    if size & (size - 1):
        return lax.all_to_all(blocks, "seq", 0, 0, tiled=True)
    out = blocks
    for bits in range(1, size):
        piece = lax.dynamic_slice_in_dim(blocks, index ^ bits, 1, 0)
        piece = lax.ppermute(piece, "seq", [(i, i ^ bits) for i in range(size)])
        out = lax.dynamic_update_slice_in_dim(out, piece, index ^ bits, 0)
    return out


def folded(rows, lead, width):
    cut = rows.reshape(lead, rows.shape[0] // lead, rows.shape[1] // width, width)
    cut = cut.transpose(0, 2, 1, 3).reshape(lead, -1, width)
    return cut[0] if lead == 1 else cut


def unfolded(pieces, width):
    lead, stacked, narrow = pieces.shape
    cut = pieces.reshape(lead, width // narrow, stacked * narrow // width, narrow)
    return cut.transpose(0, 2, 1, 3).reshape(-1, width)


def exchanged(parts):
    size = lax.axis_size("seq")
    index = lax.axis_index("seq")
    held = parts.reshape((size, -1) + parts.shape[1:])

    def part(owner):
        return lax.dynamic_index_in_dim(held, owner, 0, keepdims=False)

    came = [
        lax.ppermute(part(index ^ bits).astype(bf16), "seq", [(i, i ^ bits) for i in range(size)])
        for bits in range(1, size)
    ]
    return sum([piece.astype(f32) for piece in came], part(index))


def by_rows(array):
    return with_layout_constraint(array, Layout(major_to_minor=(0, 1)))


def padded(rows, width):
    return jnp.pad(rows, ((0, 0), (0, width - rows.shape[1])))


def shards(
    hidden, segments, cotangent, norm_gain, in_weight, conv_weight, conv_bias, step_bias, log_rate,
    skip_gain, gate_gain, out_weight,
):
    n_seqs, block, n_width = hidden.shape
    size = lax.axis_size("seq")
    groups = lax.axis_size("dp")
    index = lax.axis_index("seq")
    tokens = size * block
    n_inner = gate_gain.shape[0]
    n_heads = step_bias.shape[0]
    n_taps = conv_weight.shape[0]
    n_mixed = conv_bias.shape[0]
    n_state = (n_mixed - n_inner) // 2
    head = n_inner // n_heads
    own_inner = n_inner // size
    own_heads = n_heads // size
    own_bc = 2 * n_state // size
    q = min(128, block)
    in_rows = in_weight.shape[0]

    in_low = in_weight.astype(bf16)
    z_cols = in_low[:, :n_inner].reshape(in_rows, size, own_inner)
    x_cols = in_low[:, n_inner : 2 * n_inner].reshape(in_rows, size, own_inner)
    bc_cols = in_low[:, 2 * n_inner : n_inner + n_mixed].reshape(in_rows, size, own_bc)
    dt_cols = in_low[:, n_inner + n_mixed :].reshape(in_rows, size, own_heads)
    gap = jnp.zeros((in_rows, size, LANES - own_heads - own_bc), bf16)
    laid = jnp.concatenate([x_cols, dt_cols, gap, bc_cols, z_cols], axis=2).transpose(1, 0, 2)
    mine = lax.all_to_all(laid, "seq", 0, 0, tiled=True)
    flat = hidden.reshape(block, n_width).astype(f32)
    inv = lax.rsqrt(jnp.mean(flat * flat, axis=-1, keepdims=True) + epsilon)
    unit = flat * inv
    normed_own = (unit * norm_gain).astype(bf16)
    docs = gathered(segments).reshape(tokens).astype(f32)
    order = [(f, (f % groups) * size + f // groups) for f in range(groups * size)]
    back = [(b, a) for a, b in order]
    out_moved = lax.ppermute(out_weight.astype(bf16), ("dp", "seq"), order)
    mine, normed_own = lax.optimization_barrier((after(mine, (docs, out_moved)), normed_own))
    mine = mine.reshape(size * in_rows, -1)
    n_first = own_inner + LANES
    cot_own = cotangent.reshape(block, n_width)
    normed_held = opened(normed_own)
    cot_held = opened(after(cot_own, mine))
    w_first, hopped = gathered_rows(mine[:, :n_first], [normed_held, cot_held])
    z_block = jnp.concatenate([mine[:, n_first:], folded(out_moved, 1, own_inner)], axis=0)

    normed = gathered(normed_own, normed_held)
    joined = lax.all_gather(after(z_block, hopped), "dp", axis=0, tiled=True).reshape(groups, -1, own_inner)
    z_rows = size * in_rows
    w_z = joined[:, :z_rows].reshape(-1, own_inner)
    w_out = unfolded(joined[:, z_rows:], n_width)
    cot = gathered(cot_own, cot_held)
    dcol = jnp.broadcast_to(docs[:, None], (tokens, LANES))
    drow = jnp.broadcast_to(docs[None, :], (8, tokens))

    def own_part(vector, parts):
        return lax.dynamic_slice_in_dim(vector, index * parts, parts, vector.ndim - 1)

    w_x, w_small = w_first[:, :own_inner], w_first[:, own_inner:]
    small = mm(normed, w_small, NN)
    x_in = mm(normed, w_x, NN).astype(bf16)
    conv_x = own_part(conv_weight[:, :n_inner], own_inner)
    bias_x = own_part(conv_bias[None, :n_inner], own_inner)
    conv_bc = own_part(conv_weight[:, n_inner:], own_bc)
    bias_bc = own_part(conv_bias[None, n_inner:], own_bc)
    sb = padded(own_part(step_bias[None], own_heads), LANES)
    rate = padded(jnp.exp(own_part(log_rate[None], own_heads)), LANES)
    skip = jnp.repeat(own_part(skip_gain[None], own_heads), head, axis=1)
    gain = own_part(gate_gain[None], own_inner)

    head_lanes = jnp.arange(LANES) < own_heads
    bc_in = small[:, LANES - own_bc :].astype(bf16).astype(f32)
    small_dt = jnp.where(head_lanes, small, 0.0)

    def earlier(rows, lag):
        return jnp.pad(rows, ((lag, 0), (0, 0)))[:tokens]

    def later(rows, lag):
        return jnp.pad(rows, ((0, lag), (0, 0)))[lag:]

    same = [None] + [
        jnp.where(jnp.pad(docs, (lag, 0), constant_values=-1.0)[:tokens] == docs, 1.0, 0.0)[:, None]
        for lag in range(1, n_taps)
    ]
    bc_conv = bias_bc + conv_bc[0:1] * bc_in
    for lag in range(1, n_taps):
        bc_conv = bc_conv + conv_bc[lag : lag + 1] * earlier(bc_in, lag) * same[lag]
    bc_sig = jax.nn.sigmoid(bc_conv)
    bct = gathered(by_rows((bc_conv * bc_sig).astype(bf16).T))

    y, states = run_forward(
        q, x_in, small_dt, bct, dcol, drow, conv_x, bias_x, sb, rate, skip, head
    )

    out_rows = own_inner // groups
    tiled = z_rows % 16 == 0 and out_rows % 16 == 0
    if tiled:
        lead, deep, tall, gate_in = groups, z_rows, out_rows, joined
    else:
        lead, deep, tall = 1, groups * z_rows, own_inner
        gate_in = jnp.concatenate([w_z, folded(w_out, 1, own_inner)], axis=0)[None]
    z, d_gn, sums = run_gate_forward(gate_in, deep, normed, cot, y, gain)
    sums = lax.psum(sums[:2], "seq")
    sums = jnp.pad(sums, ((0, 6), (0, 0)))
    gate_low, d_z, d_y, d_gain = run_gate_backward(n_inner, y, z, d_gn, sums, gain)
    d_gain = d_gain[0]
    terms = [mm(normed, d_z, TN)]
    for k in range(0, n_width, own_inner):
        terms.append(mm(gate_low, cot[:, k : k + own_inner], TN))
    terms = [term.astype(bf16).reshape(groups, -1, own_inner) for term in terms]
    terms = jnp.concatenate(terms, axis=1).reshape(-1, own_inner)
    terms, d_y = lax.optimization_barrier((terms, d_y))
    parts = lax.psum_scatter(terms, "dp", scatter_dimension=0, tiled=True)

    d_x, d_dt, d_bct, d_conv_x, d_heads = run_backward(
        q, x_in, small_dt, bct, dcol, drow, conv_x, bias_x, sb, rate, skip, d_y, states, head
    )
    x_term = mm(normed, d_x, TN).astype(bf16)
    x_term, d_bct = lax.optimization_barrier((x_term, d_bct))
    if is_small(groups):
        x_mine, x_theirs = first_cut(x_term)
        x_theirs, d_bct = lax.optimization_barrier((x_theirs, d_bct))
        x_lines = added_to(x_mine, x_theirs, 1)
    d_bc = by_rows(exchanged(d_bct)).T
    d_bcc = d_bc * (bc_sig * (1.0 + bc_conv * (1.0 - bc_sig)))
    d_bc_in = conv_bc[0:1] * d_bcc
    w_sums = [jnp.sum(d_bcc * bc_in, axis=0)]
    for lag in range(1, n_taps):
        held = d_bcc * same[lag]
        d_bc_in = d_bc_in + conv_bc[lag : lag + 1] * later(held, lag)
        w_sums.append(jnp.sum(held * earlier(bc_in, lag), axis=0))
    w_sums.append(jnp.sum(d_bcc, axis=0))
    d_small = jnp.concatenate([d_dt[:, : LANES - own_bc], d_bc_in], axis=1).astype(bf16)
    d_first = jnp.concatenate([d_x, d_small], axis=1)
    small_term = mm(normed, d_small, TN).astype(bf16)
    branch = scattered(mm(after(gate_low, d_bc), w_out, NN).astype(bf16))
    result = (flat + branch).reshape(n_seqs, block, n_width).astype(bf16)
    d_normed = mm(d_first, w_first, NT) + mm(after(d_z, d_bc), w_z, NT)
    d_norm_gain = jnp.sum(d_normed * normed.astype(f32), axis=0) / norm_gain
    d_skip = jnp.sum(d_conv_x[n_taps + 1].reshape(own_heads, head), axis=1)
    packed = jnp.concatenate(
        [
            d_conv_x[: n_taps + 1].reshape(-1),
            jnp.stack(w_sums).reshape(-1),
            d_gain,
            d_heads[0, :own_heads],
            d_heads[1, :own_heads],
            d_skip,
            d_norm_gain,
        ]
    )
    if is_small(groups):
        lines = jnp.concatenate([x_lines, added_to(*first_cut(small_term), 1)], axis=-1)
        packed = added_over(packed, reversed(bits_of(groups)[1:]))
        bit = groups // 2
        while bit > 1:
            lines = added_to(*cut_rows(lines, bit), bit)
            if bit == groups // 2:
                packed = after(packed, lines)
                parts = after(parts, lines)
            bit //= 2
        first_part = lines[0]
        packed = gathered(added_over(packed, bits_of(groups)[:1])[None])
    else:
        lines = jnp.concatenate([x_term, small_term], axis=-1)
        first_part = lax.psum_scatter(lines, "dp", scatter_dimension=0, tiled=True)
        packed = gathered(lax.psum(packed, "dp")[None])
    parts, result = lax.optimization_barrier((parts, result))
    d_norm = after(d_normed.astype(bf16), parts)
    d_norm = lax.psum_scatter(d_norm, "seq", scatter_dimension=0, tiled=True).astype(f32)

    def own_rows(part):
        out = turned(part.reshape(size, in_rows, -1))
        return out.transpose(1, 0, 2).astype(f32)

    out_part = unfolded(parts[None, z_rows:], n_width)
    d_out_weight = lax.ppermute(out_part, ("dp", "seq"), back).astype(f32)
    in_z = own_rows(parts[:z_rows])
    first_part, in_z, d_out_weight = lax.optimization_barrier((first_part, in_z, d_out_weight))
    in_first = own_rows(first_part)
    d_in_weight = jnp.concatenate(
        [
            in_z.reshape(in_rows, n_inner),
            in_first[:, :, :own_inner].reshape(in_rows, n_inner),
            in_first[:, :, n_first - own_bc :].reshape(in_rows, 2 * n_state),
            in_first[:, :, own_inner : own_inner + own_heads].reshape(in_rows, n_heads),
        ],
        axis=1,
    )

    lifted = d_norm * norm_gain
    d_flat = inv * lifted - flat * (
        inv * inv * inv * jnp.mean(lifted * flat, axis=-1, keepdims=True)
    )
    d_hidden = (cot_own.astype(f32) + d_flat).reshape(n_seqs, block, n_width)

    at = 0

    def take(count):
        nonlocal at
        at += count
        return packed[:, at - count : at]

    got_x = take((n_taps + 1) * own_inner).reshape(size, n_taps + 1, own_inner)
    got_bc = take((n_taps + 1) * own_bc).reshape(size, n_taps + 1, own_bc)
    got_x = got_x.transpose(1, 0, 2).reshape(n_taps + 1, n_inner)
    got_bc = got_bc.transpose(1, 0, 2).reshape(n_taps + 1, 2 * n_state)
    conv_all = jnp.concatenate([got_x, got_bc], axis=1)
    d_gate_gain = take(own_inner).reshape(n_inner)
    d_step_bias = take(own_heads).reshape(n_heads)
    d_log_rate = take(own_heads).reshape(n_heads)
    d_skip_gain = take(own_heads).reshape(n_heads)
    d_norm_all = jnp.sum(take(n_width), axis=0)
    return (
        result,
        d_hidden,
        d_norm_all,
        d_in_weight,
        conv_all[:n_taps],
        conv_all[n_taps],
        d_step_bias,
        d_log_rate,
        d_skip_gain,
        d_gate_gain,
        d_out_weight,
    )


def solution(mesh):
    tokens = P("dp", "seq", None)
    rows = P(("dp", "seq"), None)
    return jax.shard_map(
        shards,
        mesh=mesh,
        in_specs=(tokens, P("dp", "seq"), tokens, P(), rows, P(), P(), P(), P(), P(), P(), rows),
        out_specs=(tokens, tokens, P(), rows, P(), P(), P(), P(), P(), P(), rows),
        check_vma=False,
    )
```

```python
import functools

import jax
import jax.numpy as jnp
from jax import lax
from jax.experimental import pallas as pl
from jax.experimental.layout import Layout, with_layout_constraint
from jax.experimental.pallas import tpu as pltpu
from jax.sharding import PartitionSpec as P

epsilon = 1e-05
highest = lax.Precision.HIGHEST
f32 = jnp.float32
bf16 = jnp.bfloat16
LANES = 128
HALO = 16
NEG = -1e30


def mm(a, b, dims, out=f32):
    return lax.dot_general(a, b, (dims, ((), ())), preferred_element_type=out)


NN = ((1,), (0,))
NT = ((1,), (1,))
TN = ((0,), (0,))


def exact(a, b, dims):
    return lax.dot_general(a, b, (dims, ((), ())), precision=highest, preferred_element_type=f32)


def softplus(v):
    return jnp.maximum(v, 0.0) + jnp.log1p(jnp.exp(-jnp.abs(v)))


def sigmoid(v):
    return 1.0 / (1.0 + jnp.exp(-v))


def lane_iota(shape):
    return lax.broadcasted_iota(jnp.int32, shape, len(shape) - 1)


def spread(columns, first, second, wide):
    rows = columns.shape[0]
    left = jnp.broadcast_to(columns[:, first : first + 1], (rows, LANES))
    right = jnp.broadcast_to(columns[:, second : second + 1], (rows, LANES))
    return jnp.where(wide, left, right)


def step_parts(raw, rate, q):
    row = lax.broadcasted_iota(jnp.int32, (q, q), 0)
    col = lax.broadcasted_iota(jnp.int32, (q, q), 1)
    tri = jnp.where(row >= col, 1.0, 0.0).astype(f32)
    step = softplus(raw)
    decay = -step * rate
    total = exact(tri, decay, NN)
    return step, decay, total, tri, row >= col


def convolve(ext, docs_ext, own, weights, bias, lanes, q, taps):
    running = bias + weights[0:1, lanes] * ext[pl.ds(HALO, q), lanes]
    for lag in range(1, taps):
        same = jnp.where(docs_ext[pl.ds(HALO - lag, q), :] == own, 1.0, 0.0)
        running = running + weights[lag : lag + 1, lanes] * ext[pl.ds(HALO - lag, q), lanes] * same
    return running


def scan_forward(
    q, taps, pairs, head,
    x_ref, small_ref, bct_ref, dcol_ref, drow_ref, w_ref, b_ref, sb_ref, rate_ref, skip_ref,
    y_ref, states_ref,
    state, ext, docs_ext, xs, xt, last_doc,
):
    c = pl.program_id(0)
    n = bct_ref.shape[0] // 2

    @pl.when(c == 0)
    def _():
        state[...] = jnp.zeros_like(state)
        ext[pl.ds(0, HALO), :] = jnp.zeros((HALO, ext.shape[1]), f32)
        docs_ext[pl.ds(0, HALO), :] = jnp.full((HALO, LANES), -1.0, f32)
        last_doc[...] = jnp.full(last_doc.shape, -1.0, f32)

    own = dcol_ref[...]
    ext[pl.ds(HALO, q), :] = x_ref[...].astype(f32)
    docs_ext[pl.ds(HALO, q), :] = own
    step, _, cum, _, causal = step_parts(small_ref[...] + sb_ref[...], rate_ref[...], q)
    step_t = step.T
    cum_t = cum.T
    end = cum[q - 1 : q, :]
    id_in = last_doc[0:1, :]
    final = own[q - 1 : q, :]
    linked = jnp.where(final == id_in, 1.0, 0.0)
    fade = linked * jnp.exp(end)
    entering = jnp.where(own == id_in, 1.0, 0.0) * jnp.exp(cum)
    to_end = jnp.where(own == final, 1.0, 0.0) * jnp.exp(end - cum) * step
    same_doc = jnp.broadcast_to(own[:, 0:1], (q, q)) == jnp.broadcast_to(drow_ref[0:1, :], (q, q))
    hide = jnp.where(jnp.logical_and(causal, same_doc), 0.0, NEG)
    bt = bct_ref[0:n, :]
    ct = bct_ref[n : 2 * n, :]
    scores = mm(ct, bt, TN)
    states_ref[0] = state[...]
    old = state[...].astype(bf16)
    wide = lane_iota((q, LANES)) < head
    wide_row = lane_iota((1, LANES)) < head
    for k in range(pairs):
        lanes = slice(k * LANES, (k + 1) * LANES)
        h0, h1 = 2 * k, 2 * k + 1
        conv = convolve(ext, docs_ext, own, w_ref, b_ref[:, lanes], lanes, q, taps)
        x = conv * sigmoid(conv)
        xd = x * spread(step, h0, h1, wide)
        xt[:, lanes] = (x * spread(to_end, h0, h1, wide)).astype(bf16)
        mats = []
        for h in (h0, h1):
            gap = cum[:, h : h + 1] - cum_t[h : h + 1, :] + hide
            mats.append((jnp.exp(gap) * scores).astype(bf16))
        out = mm(mats[0], jnp.where(wide, xd, 0.0).astype(bf16), NN)
        out = out + mm(mats[1], jnp.where(wide, 0.0, xd).astype(bf16), NN)
        out = out + mm(ct, old[:, lanes], TN) * spread(entering, h0, h1, wide)
        y_ref[:, lanes] = out + skip_ref[:, lanes] * x
    update = mm(bt, xt[...], NN)
    for k in range(pairs):
        lanes = slice(k * LANES, (k + 1) * LANES)
        state[:, lanes] = state[:, lanes] * spread(fade, 2 * k, 2 * k + 1, wide_row) + update[:, lanes]
    ext[pl.ds(0, HALO), :] = ext[pl.ds(q, HALO), :]
    docs_ext[pl.ds(0, HALO), :] = docs_ext[pl.ds(q, HALO), :]
    last_doc[...] = jnp.broadcast_to(final, last_doc.shape)


def scan_backward(
    q, taps, pairs, head, chunks,
    x_ref, xp_ref, small_ref, bct_ref, dcol_ref, dcolp_ref, drow_ref, w_ref, b_ref, sb_ref, rate_ref,
    skip_ref, dy_ref, states_ref,
    dx_ref, dsmall_ref, dbct_ref, dconv_ref, dhead_ref,
    dstate, ext, docs_ext, dcv, docs_after, dye, xt, col_t,
):
    step_at = pl.program_id(0)
    c = chunks - 1 - step_at
    n = bct_ref.shape[0] // 2
    width = x_ref.shape[1]

    @pl.when(step_at == 0)
    def _():
        dstate[...] = jnp.zeros_like(dstate)
        dcv[pl.ds(q, HALO), :] = jnp.zeros((HALO, width), f32)
        docs_after[pl.ds(q, HALO), :] = jnp.full((HALO, LANES), -1.0, f32)
        dconv_ref[...] = jnp.zeros_like(dconv_ref)
        dhead_ref[...] = jnp.zeros_like(dhead_ref)
        col_t[...] = jnp.zeros_like(col_t)

    first = c == 0
    own = dcol_ref[...]
    before = jnp.where(first, -1.0, dcolp_ref[...])
    ext[pl.ds(0, HALO), :] = xp_ref[...].astype(f32)
    ext[pl.ds(HALO, q), :] = x_ref[...].astype(f32)
    docs_ext[pl.ds(0, HALO), :] = before
    docs_ext[pl.ds(HALO, q), :] = own
    docs_after[pl.ds(0, q), :] = own
    raw = small_ref[...] + sb_ref[...]
    rate = rate_ref[...]
    step, decay, cum, tri, causal = step_parts(raw, rate, q)
    step_t = step.T
    cum_t = cum.T
    end = cum[q - 1 : q, :]
    id_in = before[HALO - 1 : HALO, :]
    final = own[q - 1 : q, :]
    linked = jnp.where(final == id_in, 1.0, 0.0)
    fade = linked * jnp.exp(end)
    entering = jnp.where(own == id_in, 1.0, 0.0) * jnp.exp(cum)
    tail = jnp.where(own == final, 1.0, 0.0) * jnp.exp(end - cum)
    to_end = tail * step
    same_doc = jnp.broadcast_to(own[:, 0:1], (q, q)) == jnp.broadcast_to(drow_ref[0:1, :], (q, q))
    hide = jnp.where(jnp.logical_and(causal, same_doc), 0.0, NEG)
    bt = bct_ref[0:n, :]
    ct = bct_ref[n : 2 * n, :]
    scores = mm(ct, bt, TN)
    old = states_ref[0].astype(bf16)
    after = dstate[...].astype(bf16)
    wide = lane_iota((q, LANES)) < head
    wide_row = lane_iota((1, LANES)) < head
    lane = lane_iota((q, LANES))
    d_scores = jnp.zeros((q, q), f32)
    rows = jnp.zeros((q, LANES), f32)
    d_enter = jnp.zeros((q, LANES), f32)
    d_toend = jnp.zeros((q, LANES), f32)
    d_fade = jnp.zeros((8, LANES), f32)
    part = lax.broadcasted_iota(jnp.int32, (LANES, LANES), 0) // head
    to = lane_iota((LANES, LANES))
    for k in range(pairs):
        lanes = slice(k * LANES, (k + 1) * LANES)
        h0, h1 = 2 * k, 2 * k + 1
        pick = jnp.where(part + 2 * k == to, 1.0, 0.0)
        conv = convolve(ext, docs_ext, own, w_ref, b_ref[:, lanes], lanes, q, taps)
        sig = sigmoid(conv)
        x = conv * sig
        xb = x.astype(bf16)
        dy = dy_ref[:, lanes]
        halves = (jnp.where(wide, dy, 0.0).astype(bf16), jnp.where(wide, 0.0, dy).astype(bf16))
        dxd = jnp.zeros((q, LANES), f32)
        for h, half in ((h0, halves[0]), (h1, halves[1])):
            inner = mm(half, xb, NT)
            keep = jnp.exp(cum[:, h : h + 1] - cum_t[h : h + 1, :] + hide)
            grown = keep * inner
            mat = keep * scores
            dt = step_t[h : h + 1, :]
            g = grown * scores
            d_scores = d_scores + grown * dt
            rows = jnp.where(lane == h, jnp.sum(g * dt, axis=1, keepdims=True), rows)
            col_t[h : h + 1, :] = jnp.sum(g, axis=0, keepdims=True)
            dxd = dxd + mm(mat.astype(bf16), half, TN)
        v = mm(bt, after[:, lanes], TN)
        u = mm(ct, old[:, lanes], TN)
        enter_k = spread(entering, h0, h1, wide)
        end_k = spread(to_end, h0, h1, wide)
        d_enter = d_enter + exact(dy * u, pick, NN)
        d_toend = d_toend + exact(x * v, pick, NN)
        hh = jnp.sum(dstate[:, lanes] * states_ref[0, :, lanes], axis=0, keepdims=True)
        d_fade = d_fade + exact(jnp.broadcast_to(hh, (8, LANES)), pick, NN)
        dye[:, lanes] = (dy * enter_k).astype(bf16)
        xt[:, lanes] = (x * end_k).astype(bf16)
        dx = dxd * spread(step, h0, h1, wide) + end_k * v + skip_ref[:, lanes] * dy
        dconv = dx * (sig * (1.0 + conv * (1.0 - sig)))
        dcv[pl.ds(0, q), lanes] = dconv
        sums = [jnp.sum(dconv * ext[pl.ds(HALO, q), lanes], axis=0, keepdims=True)]
        dxin = w_ref[0:1, lanes] * dconv
        for lag in range(1, taps):
            same = jnp.where(docs_ext[pl.ds(HALO - lag, q), :] == own, 1.0, 0.0)
            sums.append(jnp.sum(dconv * same * ext[pl.ds(HALO - lag, q), lanes], axis=0, keepdims=True))
            follow = jnp.where(docs_after[pl.ds(lag, q), :] == own, 1.0, 0.0)
            dxin = dxin + w_ref[lag : lag + 1, lanes] * dcv[pl.ds(lag, q), lanes] * follow
        sums.append(jnp.sum(dconv, axis=0, keepdims=True))
        sums.append(jnp.sum(dy * x, axis=0, keepdims=True))
        dx_ref[:, lanes] = dxin.astype(bf16)
        for i, s in enumerate(sums):
            dconv_ref[i : i + 1, lanes] = dconv_ref[i : i + 1, lanes] + s
    dsb = d_scores.astype(bf16)
    dbct_ref[0:n, :] = mm(ct, dsb, NN) + mm(after, xt[...], NT)
    dbct_ref[n : 2 * n, :] = mm(bt, dsb, NT) + mm(old, dye[...], NT)
    new = mm(ct, dye[...], NN)
    for k in range(pairs):
        lanes = slice(k * LANES, (k + 1) * LANES)
        dstate[:, lanes] = dstate[:, lanes] * spread(fade, 2 * k, 2 * k + 1, wide_row) + new[:, lanes]
    cols = col_t[...].T
    pulled = d_toend * to_end
    at_end = jnp.sum(pulled, axis=0, keepdims=True) + fade * d_fade[0:1, :]
    d_cum = rows - step * cols + d_enter * entering - pulled
    last_row = lax.broadcasted_iota(jnp.int32, (q, LANES), 0) == q - 1
    d_cum = d_cum + jnp.where(last_row, at_end, 0.0)
    d_decay = exact(tri, d_cum, TN)
    d_step = cols + d_toend * tail - rate * d_decay
    d_raw = d_step * sigmoid(raw)
    dsmall_ref[...] = d_raw
    dhead_ref[0:1, :] = dhead_ref[0:1, :] + jnp.sum(d_raw, axis=0, keepdims=True)
    dhead_ref[1:2, :] = dhead_ref[1:2, :] + jnp.sum(d_decay * decay, axis=0, keepdims=True)
    dcv[pl.ds(q, HALO), :] = dcv[pl.ds(0, HALO), :]
    docs_after[pl.ds(q, HALO), :] = docs_after[pl.ds(0, HALO), :]


def whole(array):
    return pl.BlockSpec(array.shape, lambda c: (0,) * array.ndim)


def run_forward(q, x_in, small, bct, dcol, drow, conv_w, conv_b, sb, rate, skip, head):
    tokens, width = x_in.shape
    n = bct.shape[0] // 2
    chunks = tokens // q
    pairs = width // LANES
    taps = conv_w.shape[0]
    return pl.pallas_call(
        functools.partial(scan_forward, q, taps, pairs, head),
        grid=(chunks,),
        in_specs=[
            pl.BlockSpec((q, width), lambda c: (c, 0)),
            pl.BlockSpec((q, LANES), lambda c: (c, 0)),
            pl.BlockSpec((2 * n, q), lambda c: (0, c)),
            pl.BlockSpec((q, LANES), lambda c: (c, 0)),
            pl.BlockSpec((8, q), lambda c: (0, c)),
            whole(conv_w), whole(conv_b), whole(sb), whole(rate), whole(skip),
        ],
        out_specs=[
            pl.BlockSpec((q, width), lambda c: (c, 0)),
            pl.BlockSpec((1, n, width), lambda c: (c, 0, 0)),
        ],
        out_shape=[
            jax.ShapeDtypeStruct((tokens, width), f32),
            jax.ShapeDtypeStruct((chunks, n, width), f32),
        ],
        scratch_shapes=[
            pltpu.VMEM((n, width), f32),
            pltpu.VMEM((HALO + q, width), f32),
            pltpu.VMEM((HALO + q, LANES), f32),
            pltpu.VMEM((8, LANES), f32),
            pltpu.VMEM((q, width), bf16),
            pltpu.VMEM((8, LANES), f32),
        ],
        name="scan_forward",
    )(x_in, small, bct, dcol, drow, conv_w, conv_b, sb, rate, skip)


def run_backward(q, x_in, small, bct, dcol, drow, conv_w, conv_b, sb, rate, skip, dy, states, head):
    tokens, width = x_in.shape
    n = bct.shape[0] // 2
    chunks = tokens // q
    pairs = width // LANES
    taps = conv_w.shape[0]
    per = q // HALO

    def at(c):
        return chunks - 1 - c

    def prior(c):
        return jnp.maximum((chunks - 1 - c) * per - 1, 0)

    return pl.pallas_call(
        functools.partial(scan_backward, q, taps, pairs, head, chunks),
        grid=(chunks,),
        in_specs=[
            pl.BlockSpec((q, width), lambda c: (at(c), 0)),
            pl.BlockSpec((HALO, width), lambda c: (prior(c), 0)),
            pl.BlockSpec((q, LANES), lambda c: (at(c), 0)),
            pl.BlockSpec((2 * n, q), lambda c: (0, at(c))),
            pl.BlockSpec((q, LANES), lambda c: (at(c), 0)),
            pl.BlockSpec((HALO, LANES), lambda c: (prior(c), 0)),
            pl.BlockSpec((8, q), lambda c: (0, at(c))),
            whole(conv_w), whole(conv_b), whole(sb), whole(rate), whole(skip),
            pl.BlockSpec((q, width), lambda c: (at(c), 0)),
            pl.BlockSpec((1, n, width), lambda c: (at(c), 0, 0)),
        ],
        out_specs=[
            pl.BlockSpec((q, width), lambda c: (at(c), 0)),
            pl.BlockSpec((q, LANES), lambda c: (at(c), 0)),
            pl.BlockSpec((2 * n, q), lambda c: (0, at(c))),
            pl.BlockSpec((8, width), lambda c: (0, 0)),
            pl.BlockSpec((8, LANES), lambda c: (0, 0)),
        ],
        out_shape=[
            jax.ShapeDtypeStruct((tokens, width), bf16),
            jax.ShapeDtypeStruct((tokens, LANES), f32),
            jax.ShapeDtypeStruct((2 * n, tokens), f32),
            jax.ShapeDtypeStruct((8, width), f32),
            jax.ShapeDtypeStruct((8, LANES), f32),
        ],
        scratch_shapes=[
            pltpu.VMEM((n, width), f32),
            pltpu.VMEM((HALO + q, width), f32),
            pltpu.VMEM((HALO + q, LANES), f32),
            pltpu.VMEM((q + HALO, width), f32),
            pltpu.VMEM((q + HALO, LANES), f32),
            pltpu.VMEM((q, width), bf16),
            pltpu.VMEM((q, width), bf16),
            pltpu.VMEM((LANES, q), f32),
        ],
        name="scan_backward",
    )(x_in, x_in, small, bct, dcol, dcol, drow, conv_w, conv_b, sb, rate, skip, dy, states)


def gate_forward(
    groups, z_rows, tall,
    normed_ref, cot_ref, joined_ref, y_ref, gain_ref, z_ref, dgn_ref, sums_ref, wz, wo,
):
    parts, held, width = wo.shape

    @pl.when(pl.program_id(0) == 0)
    def _():
        for g in range(groups):
            wz[pl.ds(g * z_rows, z_rows), :] = joined_ref[g, pl.ds(0, z_rows), :]
            for k in range(parts):
                wo[k, pl.ds(g * tall, tall), :] = joined_ref[g, pl.ds(z_rows + k * tall, tall), :]

    z = mm(normed_ref[...], wz[...], NN)
    d_gn = mm(cot_ref[:, 0:width], wo[0], NT)
    for k in range(1, parts):
        d_gn = d_gn + mm(cot_ref[:, k * width : (k + 1) * width], wo[k], NT)
    z_ref[...] = z
    dgn_ref[...] = d_gn
    gated = y_ref[...] * (z * sigmoid(z))
    square = jnp.sum(gated * gated, axis=1, keepdims=True)
    cross = jnp.sum(d_gn * gain_ref[...] * gated, axis=1, keepdims=True)
    lane = lane_iota((square.shape[0], LANES))
    sums_ref[...] = jnp.where(lane == 0, square, jnp.where(lane == 1, cross, 0.0)).T[0:8, :]


def gate_backward(
    blocks, tile, z_rows, tall, channels,
    normed_ref, cot_ref, y_ref, z_ref, dgn_ref, sums_ref, gain_ref,
    gate_ref, dz_ref, dy_ref, dgain_ref, terms_ref,
):
    step = pl.program_id(0)
    rows, width = y_ref.shape
    parts = normed_ref.shape[1] // width

    @pl.when(step == 0)
    def _():
        dgain_ref[...] = jnp.zeros_like(dgain_ref)

    @pl.when(step < blocks)
    def _():
        own = pl.ds(pl.multiple_of(step * rows, rows), rows)
        columns = jnp.concatenate([sums_ref[...], jnp.zeros((LANES - 8, rows), f32)], axis=0).T
        inv = lax.rsqrt(columns[:, 0:1] / channels + epsilon)
        slope = inv * inv * inv * (columns[:, 1:2] / channels)
        for k in range(width // LANES):
            lanes = slice(k * LANES, (k + 1) * LANES)
            y, z, d_gn, gain = y_ref[:, lanes], z_ref[:, lanes], dgn_ref[:, lanes], gain_ref[:, lanes]
            sig = sigmoid(z)
            act = z * sig
            gated = y * act
            scaled = gated * inv
            gate_ref[own, lanes] = (scaled * gain).astype(bf16)
            dgain_ref[0:1, lanes] = dgain_ref[0:1, lanes] + jnp.sum(d_gn * scaled, axis=0, keepdims=True)
            d_gated = inv * (d_gn * gain) - gated * slope
            dz_ref[own, lanes] = (d_gated * y * (sig * (1.0 + z * (1.0 - sig)))).astype(bf16)
            dy_ref[:, lanes] = d_gated * act

    def store(term, at, within, base):
        if within >= tile:
            start = pl.multiple_of(base + at * tile, 16)
            terms_ref[0, pl.ds(start, tile), :] = term
        else:
            for n in range(tile // within):
                piece = term[n * within : (n + 1) * within]
                terms_ref[at * (tile // within) + n, pl.ds(base, within), :] = piece

    @pl.when(step >= blocks)
    def _():
        i = step - blocks
        lanes = pl.ds(pl.multiple_of(i * tile, LANES), tile)
        store(mm(normed_ref[:, lanes], dz_ref[...], TN).astype(bf16), i, z_rows, 0)
        j = i // parts
        lanes = pl.ds(pl.multiple_of(j * tile, LANES), tile)
        left = gate_ref[:, lanes]
        for k in range(parts):

            @pl.when(i % parts == k)
            def _():
                right = cot_ref[:, k * width : (k + 1) * width]
                store(mm(left, right, TN).astype(bf16), j, tall, z_rows + k * tall)


def run_gate_forward(joined, z_rows, normed, cot, y, gain):
    groups, deep, width = joined.shape
    tokens, n_width = normed.shape
    parts = n_width // width
    tall = (deep - z_rows) // parts
    rows = min(256, tokens)

    def tokens_of(columns):
        return pl.BlockSpec((rows, columns), lambda c: (c, 0))

    return pl.pallas_call(
        functools.partial(gate_forward, groups, z_rows, tall),
        grid=(tokens // rows,),
        in_specs=[tokens_of(n_width), tokens_of(n_width), whole(joined), tokens_of(width), whole(gain)],
        out_specs=[
            tokens_of(width), tokens_of(width), pl.BlockSpec((8, rows), lambda c: (0, c)),
            pl.BlockSpec((groups * z_rows, width), lambda c: (0, 0)),
            pl.BlockSpec((parts, groups * tall, width), lambda c: (0, 0, 0)),
        ],
        out_shape=[
            jax.ShapeDtypeStruct((tokens, width), f32),
            jax.ShapeDtypeStruct((tokens, width), f32),
            jax.ShapeDtypeStruct((8, tokens), f32),
            jax.ShapeDtypeStruct((groups * z_rows, width), bf16),
            jax.ShapeDtypeStruct((parts, groups * tall, width), bf16),
        ],
        name="gate_forward",
    )(normed, cot, joined, y, gain)


def run_gate_backward(groups, z_rows, tall, channels, normed, cot, y, z, d_gn, sums, gain):
    tokens, n_width = normed.shape
    width = y.shape[1]
    parts = n_width // width
    rows = min(256, tokens)
    blocks = tokens // rows
    tile = 3 * LANES
    deep = z_rows + parts * tall

    def tokens_of(columns):
        return pl.BlockSpec((rows, columns), lambda c: (jnp.minimum(c, blocks - 1), 0))

    return pl.pallas_call(
        functools.partial(gate_backward, blocks, tile, z_rows, tall, channels),
        grid=(blocks + n_width // tile,),
        in_specs=[
            whole(normed), whole(cot), tokens_of(width), tokens_of(width), tokens_of(width),
            pl.BlockSpec((8, rows), lambda c: (0, jnp.minimum(c, blocks - 1))), whole(gain),
        ],
        out_specs=[
            pl.BlockSpec((tokens, width), lambda c: (0, 0)),
            pl.BlockSpec((tokens, width), lambda c: (0, 0)),
            tokens_of(width),
            pl.BlockSpec((8, width), lambda c: (0, 0)),
            pl.BlockSpec((groups, deep, width), lambda c: (0, 0, 0)),
        ],
        out_shape=[
            jax.ShapeDtypeStruct((tokens, width), bf16),
            jax.ShapeDtypeStruct((tokens, width), bf16),
            jax.ShapeDtypeStruct((tokens, width), f32),
            jax.ShapeDtypeStruct((8, width), f32),
            jax.ShapeDtypeStruct((groups, deep, width), bf16),
        ],
        name="gate_backward",
    )(normed, cot, y, z, d_gn, sums, gain)


def swapped(block, bit):
    size = lax.axis_size("seq")
    return lax.ppermute(block, "seq", [(i, i ^ bit) for i in range(size)])


def bits_of(size):
    bits, bit = [], 1
    while bit < size:
        bits.append(bit)
        bit *= 2
    return bits


def joined_by(held, bit):
    other = swapped(held, bit)
    upper = (lax.axis_index("seq") & bit) != 0
    both = jnp.where(upper, jnp.stack([other, held], axis=1), jnp.stack([held, other], axis=1))
    return both.reshape((-1,) + both.shape[2:])


def opened(block):
    bits = bits_of(lax.axis_size("seq"))
    return joined_by(block[None], bits[-1]) if bits else block[None]


def gathered(block, held=None):
    held = opened(block) if held is None else held
    for bit in reversed(bits_of(lax.axis_size("seq"))[:-1]):
        held = joined_by(held, bit)
    return held.reshape((-1,) + held.shape[2:])


def scattered(parts, between=lambda held: held):
    index = lax.axis_index("seq")
    size = lax.axis_size("seq")
    rest = parts.shape[1:]
    lead = parts.shape[0]
    held = parts.reshape((size, lead // size) + rest)
    for bit in bits_of(size):
        half = held.reshape((held.shape[0] // 2, 2) + held.shape[1:])
        upper = (index & bit) != 0
        mine = jnp.where(upper, half[:, 1], half[:, 0])
        theirs = jnp.where(upper, half[:, 0], half[:, 1]).astype(bf16)
        held = between(mine.astype(f32) + swapped(theirs, bit).astype(f32))
    return held[0]


def added_over(block, bits):
    for bit in bits:
        block = block + crossed(block, bit)
    return block


def moved_by(block, step):
    count = lax.axis_size("dp")
    route = [(i, i + 2 * step) for i in range(count) if 0 <= i + 2 * step < count]
    return lax.ppermute(block, "dp", route)


def crossed(block, bits):
    return lax.ppermute(block, "dp", [(i, i ^ bits) for i in range(lax.axis_size("dp"))])


def gathered_rows(block, waits):
    count = lax.axis_size("dp")
    length = count // 2
    if not is_small(count):
        return lax.all_gather(block, "dp", axis=0, tiled=True), block
    at = lax.axis_index("dp")
    place, side = at // 2, at % 2
    rows = block.shape[0]
    whole_rows = jnp.zeros((count * rows, block.shape[1]), block.dtype)

    def put(into, piece, pair, half):
        return lax.dynamic_update_slice(into, piece, ((pair * 2 + half) * rows, 0))

    whole_rows = put(whole_rows, block, place, side)
    other = crossed(block, 1)
    whole_rows = put(whole_rows, other, place, 1 - side)
    up, down, ready = block, block, []
    for hop in range(1, length):
        up, down = after((moved_by(up, 1), moved_by(down, -1)), (other, waits[hop - 1 : hop]))
        ready.append((down, up))
        piece, pair = None, None
        for spot in range(length):
            near = min(spot, length - 1 - spot)
            if hop <= 2 * near:
                away, from_below = (hop + 1) // 2, hop % 2 == 0
            else:
                away, from_below = hop - near, spot > length - 1 - spot
            chosen = ready[away - 1][1 if from_below else 0]
            source = spot - away if from_below else spot + away
            here = place == spot
            piece = chosen if piece is None else jnp.where(here, chosen, piece)
            pair = source if pair is None else jnp.where(here, source, pair)
        whole_rows = put(whole_rows, piece, pair, side)
        other = crossed(piece, 1)
        whole_rows = put(whole_rows, other, pair, 1 - side)
    return whole_rows, ready[min(1, length - 2)]


def is_small(count):
    return count <= 8 and count & (count - 1) == 0


def halved_rows(term):
    count = lax.axis_size("dp")
    if not is_small(count):
        return term
    at = lax.axis_index("dp")
    pairs = term.reshape(count // 2, 2, -1, term.shape[1])

    def side(which):
        return lax.dynamic_index_in_dim(pairs, which, 1, keepdims=False)

    came = crossed(side((at & 1) ^ 1), 1)
    return (side(at & 1).astype(f32) + came.astype(f32)).astype(bf16)


def shared_rows(lines):
    count = lax.axis_size("dp")
    if not is_small(count):
        return [lax.psum_scatter(lines, "dp", scatter_dimension=0, tiled=True)]
    at = lax.axis_index("dp")

    def part(owner):
        return lax.dynamic_index_in_dim(lines, owner // 2, 0, keepdims=False)

    return [part(at)] + [crossed(part(at ^ bits), bits) for bits in range(2, count, 2)]


def after(value, other):
    return lax.optimization_barrier((value, other))[0]


def turned(blocks):
    size = lax.axis_size("seq")
    index = lax.axis_index("seq")
    if size & (size - 1):
        return lax.all_to_all(blocks, "seq", 0, 0, tiled=True)
    out = blocks
    for bits in range(1, size):
        piece = lax.dynamic_slice_in_dim(blocks, index ^ bits, 1, 0)
        piece = lax.ppermute(piece, "seq", [(i, i ^ bits) for i in range(size)])
        out = lax.dynamic_update_slice_in_dim(out, piece, index ^ bits, 0)
    return out


def folded(rows, lead, width):
    cut = rows.reshape(lead, rows.shape[0] // lead, rows.shape[1] // width, width)
    cut = cut.transpose(0, 2, 1, 3).reshape(lead, -1, width)
    return cut[0] if lead == 1 else cut


def unfolded(pieces, width):
    lead, stacked, narrow = pieces.shape
    cut = pieces.reshape(lead, width // narrow, stacked * narrow // width, narrow)
    return cut.transpose(0, 2, 1, 3).reshape(-1, width)


def exchanged(parts):
    size = lax.axis_size("seq")
    index = lax.axis_index("seq")
    held = parts.reshape((size, -1) + parts.shape[1:])

    def part(owner):
        return lax.dynamic_index_in_dim(held, owner, 0, keepdims=False)

    came = [
        lax.ppermute(part(index ^ bits).astype(bf16), "seq", [(i, i ^ bits) for i in range(size)])
        for bits in range(1, size)
    ]
    return sum([piece.astype(f32) for piece in came], part(index))


def by_rows(array):
    return with_layout_constraint(array, Layout(major_to_minor=(0, 1)))


def padded(rows, width):
    return jnp.pad(rows, ((0, 0), (0, width - rows.shape[1])))


def shards(
    hidden, segments, cotangent, norm_gain, in_weight, conv_weight, conv_bias, step_bias, log_rate,
    skip_gain, gate_gain, out_weight,
):
    n_seqs, block, n_width = hidden.shape
    size = lax.axis_size("seq")
    groups = lax.axis_size("dp")
    index = lax.axis_index("seq")
    tokens = size * block
    n_inner = gate_gain.shape[0]
    n_heads = step_bias.shape[0]
    n_taps = conv_weight.shape[0]
    n_mixed = conv_bias.shape[0]
    n_state = (n_mixed - n_inner) // 2
    head = n_inner // n_heads
    own_inner = n_inner // size
    own_heads = n_heads // size
    own_bc = 2 * n_state // size
    q = min(128, block)
    in_rows = in_weight.shape[0]

    in_low = in_weight.astype(bf16)
    z_cols = in_low[:, :n_inner].reshape(in_rows, size, own_inner)
    x_cols = in_low[:, n_inner : 2 * n_inner].reshape(in_rows, size, own_inner)
    bc_cols = in_low[:, 2 * n_inner : n_inner + n_mixed].reshape(in_rows, size, own_bc)
    dt_cols = in_low[:, n_inner + n_mixed :].reshape(in_rows, size, own_heads)
    gap = jnp.zeros((in_rows, size, LANES - own_heads - own_bc), bf16)
    laid = jnp.concatenate([x_cols, dt_cols, gap, bc_cols, z_cols], axis=2).transpose(1, 0, 2)
    mine = lax.all_to_all(laid, "seq", 0, 0, tiled=True)
    flat = hidden.reshape(block, n_width).astype(f32)
    inv = lax.rsqrt(jnp.mean(flat * flat, axis=-1, keepdims=True) + epsilon)
    unit = flat * inv
    normed_own = (unit * norm_gain).astype(bf16)
    docs = gathered(segments).reshape(tokens).astype(f32)
    order = [(f, (f % groups) * size + f // groups) for f in range(groups * size)]
    back = [(b, a) for a, b in order]
    out_moved = lax.ppermute(out_weight.astype(bf16), ("dp", "seq"), order)
    mine, normed_own = lax.optimization_barrier((after(mine, (docs, out_moved)), normed_own))
    mine = mine.reshape(size * in_rows, -1)
    n_first = own_inner + LANES
    cot_own = cotangent.reshape(block, n_width)
    normed_held = opened(normed_own)
    cot_held = opened(after(cot_own, mine))
    w_first, hopped = gathered_rows(mine[:, :n_first], [normed_held, cot_held])
    z_block = jnp.concatenate([mine[:, n_first:], folded(out_moved, 1, own_inner)], axis=0)

    normed = gathered(normed_own, normed_held)
    joined = lax.all_gather(after(z_block, hopped), "dp", axis=0, tiled=True).reshape(groups, -1, own_inner)
    z_rows = size * in_rows
    cot = gathered(cot_own, cot_held)
    dcol = jnp.broadcast_to(docs[:, None], (tokens, LANES))
    drow = jnp.broadcast_to(docs[None, :], (8, tokens))

    def own_part(vector, parts):
        return lax.dynamic_slice_in_dim(vector, index * parts, parts, vector.ndim - 1)

    w_x, w_small = w_first[:, :own_inner], w_first[:, own_inner:]
    small = mm(normed, w_small, NN)
    x_in = mm(normed, w_x, NN).astype(bf16)
    conv_x = own_part(conv_weight[:, :n_inner], own_inner)
    bias_x = own_part(conv_bias[None, :n_inner], own_inner)
    conv_bc = own_part(conv_weight[:, n_inner:], own_bc)
    bias_bc = own_part(conv_bias[None, n_inner:], own_bc)
    sb = padded(own_part(step_bias[None], own_heads), LANES)
    rate = padded(jnp.exp(own_part(log_rate[None], own_heads)), LANES)
    skip = jnp.repeat(own_part(skip_gain[None], own_heads), head, axis=1)
    gain = own_part(gate_gain[None], own_inner)

    head_lanes = jnp.arange(LANES) < own_heads
    bc_in = small[:, LANES - own_bc :].astype(bf16).astype(f32)
    small_dt = jnp.where(head_lanes, small, 0.0)

    def earlier(rows, lag):
        return jnp.pad(rows, ((lag, 0), (0, 0)))[:tokens]

    def later(rows, lag):
        return jnp.pad(rows, ((0, lag), (0, 0)))[lag:]

    same = [None] + [
        jnp.where(jnp.pad(docs, (lag, 0), constant_values=-1.0)[:tokens] == docs, 1.0, 0.0)[:, None]
        for lag in range(1, n_taps)
    ]
    bc_conv = bias_bc + conv_bc[0:1] * bc_in
    for lag in range(1, n_taps):
        bc_conv = bc_conv + conv_bc[lag : lag + 1] * earlier(bc_in, lag) * same[lag]
    bc_sig = jax.nn.sigmoid(bc_conv)
    bct = gathered(by_rows((bc_conv * bc_sig).astype(bf16).T))

    y, states = run_forward(
        q, x_in, small_dt, bct, dcol, drow, conv_x, bias_x, sb, rate, skip, head
    )

    out_rows = own_inner // groups
    tiled = z_rows % 16 == 0 and out_rows % 16 == 0
    if tiled:
        lead, deep, tall, gate_in = groups, z_rows, out_rows, joined
    else:
        lead, deep, tall = 1, groups * z_rows, own_inner
        w_out = unfolded(joined[:, z_rows:], n_width)
        gate_in = [joined[:, :z_rows].reshape(-1, own_inner), folded(w_out, 1, own_inner)]
        gate_in = jnp.concatenate(gate_in, axis=0)[None]
    z, d_gn, sums, w_z, w_out = run_gate_forward(gate_in, deep, normed, cot, y, gain)
    w_out = jnp.concatenate(list(w_out), axis=1)
    sums = lax.psum(sums[:2], "seq")
    sums = jnp.pad(sums, ((0, 6), (0, 0)))
    gate_low, d_z, d_y, d_gain, terms = run_gate_backward(
        lead, deep, tall, n_inner, normed, cot, y, z, d_gn, sums, gain
    )
    d_gain = d_gain[0]
    if not tiled:
        z_term = terms[0, :deep].reshape(groups, z_rows, own_inner)
        out_term = terms[0, deep:].reshape(n_width // own_inner, groups, out_rows, own_inner)
        out_term = out_term.transpose(1, 0, 2, 3).reshape(groups, -1, own_inner)
        terms = jnp.concatenate([z_term, out_term], axis=1)
    terms = terms.reshape(-1, own_inner)
    parts = lax.psum_scatter(terms, "dp", scatter_dimension=0, tiled=True)

    d_x, d_dt, d_bct, d_conv_x, d_heads = run_backward(
        q, x_in, small_dt, bct, dcol, drow, conv_x, bias_x, sb, rate, skip, d_y, states, head
    )
    x_term = mm(normed, d_x, TN).astype(bf16)
    x_term, d_bct = lax.optimization_barrier((x_term, d_bct))
    x_lines = halved_rows(x_term)
    d_bc = by_rows(exchanged(d_bct)).T
    d_bcc = d_bc * (bc_sig * (1.0 + bc_conv * (1.0 - bc_sig)))
    d_bc_in = conv_bc[0:1] * d_bcc
    w_sums = [jnp.sum(d_bcc * bc_in, axis=0)]
    for lag in range(1, n_taps):
        held = d_bcc * same[lag]
        d_bc_in = d_bc_in + conv_bc[lag : lag + 1] * later(held, lag)
        w_sums.append(jnp.sum(held * earlier(bc_in, lag), axis=0))
    w_sums.append(jnp.sum(d_bcc, axis=0))
    d_small = jnp.concatenate([d_dt[:, : LANES - own_bc], d_bc_in], axis=1).astype(bf16)
    d_first = jnp.concatenate([d_x, d_small], axis=1)
    small_lines = halved_rows(mm(normed, d_small, TN).astype(bf16))
    branch = scattered(mm(after(gate_low, d_bc), w_out, NN).astype(bf16))
    result = (flat + branch).reshape(n_seqs, block, n_width).astype(bf16)
    d_normed = mm(d_first, w_first, NT) + mm(d_z, w_z, NT)
    d_norm_gain = jnp.sum(d_normed * normed.astype(f32), axis=0) / norm_gain
    d_skip = jnp.sum(d_conv_x[n_taps + 1].reshape(own_heads, head), axis=1)
    packed = jnp.concatenate(
        [
            d_conv_x[: n_taps + 1].reshape(-1),
            jnp.stack(w_sums).reshape(-1),
            d_gain,
            d_heads[0, :own_heads],
            d_heads[1, :own_heads],
            d_skip,
            d_norm_gain,
        ]
    )
    lines = jnp.concatenate([x_lines, small_lines], axis=-1)
    packed = added_over(packed, reversed(bits_of(groups)[1:]))
    lines, packed = lax.optimization_barrier((lines, packed))
    shares = shared_rows(lines)
    parts, result = lax.optimization_barrier((after(parts, lines), result))
    d_norm = after(d_normed.astype(bf16), parts)
    d_norm = lax.psum_scatter(d_norm, "seq", scatter_dimension=0, tiled=True).astype(f32)

    def own_rows(part):
        out = turned(part.reshape(size, in_rows, -1))
        return out.transpose(1, 0, 2).astype(f32)

    out_part = unfolded(parts[None, z_rows:], n_width)
    d_out_weight = lax.ppermute(out_part, ("dp", "seq"), back).astype(f32)
    in_z = own_rows(parts[:z_rows])
    shares, in_z, d_out_weight = lax.optimization_barrier((shares, in_z, d_out_weight))
    packed = gathered(added_over(after(packed, shares), bits_of(groups)[:1])[None])
    first_part = sum(share.astype(f32) for share in shares)
    in_first = own_rows(first_part.astype(bf16))
    d_in_weight = jnp.concatenate(
        [
            in_z.reshape(in_rows, n_inner),
            in_first[:, :, :own_inner].reshape(in_rows, n_inner),
            in_first[:, :, n_first - own_bc :].reshape(in_rows, 2 * n_state),
            in_first[:, :, own_inner : own_inner + own_heads].reshape(in_rows, n_heads),
        ],
        axis=1,
    )

    lifted = d_norm * norm_gain
    d_flat = inv * lifted - flat * (
        inv * inv * inv * jnp.mean(lifted * flat, axis=-1, keepdims=True)
    )
    d_hidden = (cot_own.astype(f32) + d_flat).reshape(n_seqs, block, n_width)

    at = 0

    def take(count):
        nonlocal at
        at += count
        return packed[:, at - count : at]

    got_x = take((n_taps + 1) * own_inner).reshape(size, n_taps + 1, own_inner)
    got_bc = take((n_taps + 1) * own_bc).reshape(size, n_taps + 1, own_bc)
    got_x = got_x.transpose(1, 0, 2).reshape(n_taps + 1, n_inner)
    got_bc = got_bc.transpose(1, 0, 2).reshape(n_taps + 1, 2 * n_state)
    conv_all = jnp.concatenate([got_x, got_bc], axis=1)
    d_gate_gain = take(own_inner).reshape(n_inner)
    d_step_bias = take(own_heads).reshape(n_heads)
    d_log_rate = take(own_heads).reshape(n_heads)
    d_skip_gain = take(own_heads).reshape(n_heads)
    d_norm_all = jnp.sum(take(n_width), axis=0)
    return (
        result,
        d_hidden,
        d_norm_all,
        d_in_weight,
        conv_all[:n_taps],
        conv_all[n_taps],
        d_step_bias,
        d_log_rate,
        d_skip_gain,
        d_gate_gain,
        d_out_weight,
    )


def solution(mesh):
    tokens = P("dp", "seq", None)
    rows = P(("dp", "seq"), None)
    return jax.shard_map(
        shards,
        mesh=mesh,
        in_specs=(tokens, P("dp", "seq"), tokens, P(), rows, P(), P(), P(), P(), P(), P(), rows),
        out_specs=(tokens, tokens, P(), rows, P(), P(), P(), P(), P(), P(), rows),
        check_vma=False,
    )
```

```python
import functools

import jax
import jax.numpy as jnp
from jax import lax
from jax.experimental import pallas as pl
from jax.experimental.layout import Layout, with_layout_constraint
from jax.experimental.pallas import tpu as pltpu
from jax.sharding import PartitionSpec as P

epsilon = 1e-05
highest = lax.Precision.HIGHEST
f32 = jnp.float32
bf16 = jnp.bfloat16
LANES = 128
HALO = 16
NEG = -1e30


def mm(a, b, dims, out=f32):
    return lax.dot_general(a, b, (dims, ((), ())), preferred_element_type=out)


NN = ((1,), (0,))
NT = ((1,), (1,))
TN = ((0,), (0,))


def exact(a, b, dims):
    return lax.dot_general(a, b, (dims, ((), ())), precision=highest, preferred_element_type=f32)


def softplus(v):
    return jnp.maximum(v, 0.0) + jnp.log1p(jnp.exp(-jnp.abs(v)))


def sigmoid(v):
    return 1.0 / (1.0 + jnp.exp(-v))


def lane_iota(shape):
    return lax.broadcasted_iota(jnp.int32, shape, len(shape) - 1)


def spread(columns, first, second, wide):
    rows = columns.shape[0]
    left = jnp.broadcast_to(columns[:, first : first + 1], (rows, LANES))
    right = jnp.broadcast_to(columns[:, second : second + 1], (rows, LANES))
    return jnp.where(wide, left, right)


def step_parts(raw, rate, q):
    row = lax.broadcasted_iota(jnp.int32, (q, q), 0)
    col = lax.broadcasted_iota(jnp.int32, (q, q), 1)
    tri = jnp.where(row >= col, 1.0, 0.0).astype(f32)
    step = softplus(raw)
    decay = -step * rate
    total = exact(tri, decay, NN)
    return step, decay, total, tri, row >= col


def convolve(ext, docs_ext, own, weights, bias, lanes, q, taps):
    running = bias + weights[0:1, lanes] * ext[pl.ds(HALO, q), lanes]
    for lag in range(1, taps):
        same = jnp.where(docs_ext[pl.ds(HALO - lag, q), :] == own, 1.0, 0.0)
        running = running + weights[lag : lag + 1, lanes] * ext[pl.ds(HALO - lag, q), lanes] * same
    return running


def scan_forward(
    q, taps, pairs, head,
    x_ref, small_ref, bct_ref, dcol_ref, drow_ref, w_ref, b_ref, sb_ref, rate_ref, skip_ref,
    y_ref, states_ref,
    state, ext, docs_ext, xs, xt, last_doc,
):
    c = pl.program_id(0)
    n = bct_ref.shape[0] // 2

    @pl.when(c == 0)
    def _():
        state[...] = jnp.zeros_like(state)
        ext[pl.ds(0, HALO), :] = jnp.zeros((HALO, ext.shape[1]), f32)
        docs_ext[pl.ds(0, HALO), :] = jnp.full((HALO, LANES), -1.0, f32)
        last_doc[...] = jnp.full(last_doc.shape, -1.0, f32)

    own = dcol_ref[...]
    ext[pl.ds(HALO, q), :] = x_ref[...].astype(f32)
    docs_ext[pl.ds(HALO, q), :] = own
    step, _, cum, _, causal = step_parts(small_ref[...] + sb_ref[...], rate_ref[...], q)
    step_t = step.T
    cum_t = cum.T
    end = cum[q - 1 : q, :]
    id_in = last_doc[0:1, :]
    final = own[q - 1 : q, :]
    linked = jnp.where(final == id_in, 1.0, 0.0)
    fade = linked * jnp.exp(end)
    entering = jnp.where(own == id_in, 1.0, 0.0) * jnp.exp(cum)
    to_end = jnp.where(own == final, 1.0, 0.0) * jnp.exp(end - cum) * step
    same_doc = jnp.broadcast_to(own[:, 0:1], (q, q)) == jnp.broadcast_to(drow_ref[0:1, :], (q, q))
    hide = jnp.where(jnp.logical_and(causal, same_doc), 0.0, NEG)
    bt = bct_ref[0:n, :]
    ct = bct_ref[n : 2 * n, :]
    scores = mm(ct, bt, TN)
    states_ref[0] = state[...]
    old = state[...].astype(bf16)
    wide = lane_iota((q, LANES)) < head
    wide_row = lane_iota((1, LANES)) < head
    for k in range(pairs):
        lanes = slice(k * LANES, (k + 1) * LANES)
        h0, h1 = 2 * k, 2 * k + 1
        conv = convolve(ext, docs_ext, own, w_ref, b_ref[:, lanes], lanes, q, taps)
        x = conv * sigmoid(conv)
        xd = x * spread(step, h0, h1, wide)
        xt[:, lanes] = (x * spread(to_end, h0, h1, wide)).astype(bf16)
        mats = []
        for h in (h0, h1):
            gap = cum[:, h : h + 1] - cum_t[h : h + 1, :] + hide
            mats.append((jnp.exp(gap) * scores).astype(bf16))
        out = mm(mats[0], jnp.where(wide, xd, 0.0).astype(bf16), NN)
        out = out + mm(mats[1], jnp.where(wide, 0.0, xd).astype(bf16), NN)
        out = out + mm(ct, old[:, lanes], TN) * spread(entering, h0, h1, wide)
        y_ref[:, lanes] = out + skip_ref[:, lanes] * x
    update = mm(bt, xt[...], NN)
    for k in range(pairs):
        lanes = slice(k * LANES, (k + 1) * LANES)
        state[:, lanes] = state[:, lanes] * spread(fade, 2 * k, 2 * k + 1, wide_row) + update[:, lanes]
    ext[pl.ds(0, HALO), :] = ext[pl.ds(q, HALO), :]
    docs_ext[pl.ds(0, HALO), :] = docs_ext[pl.ds(q, HALO), :]
    last_doc[...] = jnp.broadcast_to(final, last_doc.shape)


def scan_backward(
    q, taps, pairs, head, chunks,
    x_ref, xp_ref, small_ref, bct_ref, dcol_ref, dcolp_ref, drow_ref, w_ref, b_ref, sb_ref, rate_ref,
    skip_ref, dy_ref, states_ref,
    dx_ref, dsmall_ref, dbct_ref, dconv_ref, dhead_ref,
    dstate, ext, docs_ext, dcv, docs_after, dye, xt, col_t,
):
    step_at = pl.program_id(0)
    c = chunks - 1 - step_at
    n = bct_ref.shape[0] // 2
    width = x_ref.shape[1]

    @pl.when(step_at == 0)
    def _():
        dstate[...] = jnp.zeros_like(dstate)
        dcv[pl.ds(q, HALO), :] = jnp.zeros((HALO, width), f32)
        docs_after[pl.ds(q, HALO), :] = jnp.full((HALO, LANES), -1.0, f32)
        dconv_ref[...] = jnp.zeros_like(dconv_ref)
        dhead_ref[...] = jnp.zeros_like(dhead_ref)
        col_t[...] = jnp.zeros_like(col_t)

    first = c == 0
    own = dcol_ref[...]
    before = jnp.where(first, -1.0, dcolp_ref[...])
    ext[pl.ds(0, HALO), :] = xp_ref[...].astype(f32)
    ext[pl.ds(HALO, q), :] = x_ref[...].astype(f32)
    docs_ext[pl.ds(0, HALO), :] = before
    docs_ext[pl.ds(HALO, q), :] = own
    docs_after[pl.ds(0, q), :] = own
    raw = small_ref[...] + sb_ref[...]
    rate = rate_ref[...]
    step, decay, cum, tri, causal = step_parts(raw, rate, q)
    step_t = step.T
    cum_t = cum.T
    end = cum[q - 1 : q, :]
    id_in = before[HALO - 1 : HALO, :]
    final = own[q - 1 : q, :]
    linked = jnp.where(final == id_in, 1.0, 0.0)
    fade = linked * jnp.exp(end)
    entering = jnp.where(own == id_in, 1.0, 0.0) * jnp.exp(cum)
    tail = jnp.where(own == final, 1.0, 0.0) * jnp.exp(end - cum)
    to_end = tail * step
    same_doc = jnp.broadcast_to(own[:, 0:1], (q, q)) == jnp.broadcast_to(drow_ref[0:1, :], (q, q))
    hide = jnp.where(jnp.logical_and(causal, same_doc), 0.0, NEG)
    bt = bct_ref[0:n, :]
    ct = bct_ref[n : 2 * n, :]
    scores = mm(ct, bt, TN)
    old = states_ref[0].astype(bf16)
    after = dstate[...].astype(bf16)
    wide = lane_iota((q, LANES)) < head
    wide_row = lane_iota((1, LANES)) < head
    lane = lane_iota((q, LANES))
    d_scores = jnp.zeros((q, q), f32)
    rows = jnp.zeros((q, LANES), f32)
    d_enter = jnp.zeros((q, LANES), f32)
    d_toend = jnp.zeros((q, LANES), f32)
    d_fade = jnp.zeros((8, LANES), f32)
    part = lax.broadcasted_iota(jnp.int32, (LANES, LANES), 0) // head
    to = lane_iota((LANES, LANES))
    for k in range(pairs):
        lanes = slice(k * LANES, (k + 1) * LANES)
        h0, h1 = 2 * k, 2 * k + 1
        pick = jnp.where(part + 2 * k == to, 1.0, 0.0)
        conv = convolve(ext, docs_ext, own, w_ref, b_ref[:, lanes], lanes, q, taps)
        sig = sigmoid(conv)
        x = conv * sig
        xb = x.astype(bf16)
        dy = dy_ref[:, lanes]
        halves = (jnp.where(wide, dy, 0.0).astype(bf16), jnp.where(wide, 0.0, dy).astype(bf16))
        dxd = jnp.zeros((q, LANES), f32)
        for h, half in ((h0, halves[0]), (h1, halves[1])):
            inner = mm(half, xb, NT)
            keep = jnp.exp(cum[:, h : h + 1] - cum_t[h : h + 1, :] + hide)
            grown = keep * inner
            mat = keep * scores
            dt = step_t[h : h + 1, :]
            g = grown * scores
            d_scores = d_scores + grown * dt
            rows = jnp.where(lane == h, jnp.sum(g * dt, axis=1, keepdims=True), rows)
            col_t[h : h + 1, :] = jnp.sum(g, axis=0, keepdims=True)
            dxd = dxd + mm(mat.astype(bf16), half, TN)
        v = mm(bt, after[:, lanes], TN)
        u = mm(ct, old[:, lanes], TN)
        enter_k = spread(entering, h0, h1, wide)
        end_k = spread(to_end, h0, h1, wide)
        d_enter = d_enter + exact(dy * u, pick, NN)
        d_toend = d_toend + exact(x * v, pick, NN)
        hh = jnp.sum(dstate[:, lanes] * states_ref[0, :, lanes], axis=0, keepdims=True)
        d_fade = d_fade + exact(jnp.broadcast_to(hh, (8, LANES)), pick, NN)
        dye[:, lanes] = (dy * enter_k).astype(bf16)
        xt[:, lanes] = (x * end_k).astype(bf16)
        dx = dxd * spread(step, h0, h1, wide) + end_k * v + skip_ref[:, lanes] * dy
        dconv = dx * (sig * (1.0 + conv * (1.0 - sig)))
        dcv[pl.ds(0, q), lanes] = dconv
        sums = [jnp.sum(dconv * ext[pl.ds(HALO, q), lanes], axis=0, keepdims=True)]
        dxin = w_ref[0:1, lanes] * dconv
        for lag in range(1, taps):
            same = jnp.where(docs_ext[pl.ds(HALO - lag, q), :] == own, 1.0, 0.0)
            sums.append(jnp.sum(dconv * same * ext[pl.ds(HALO - lag, q), lanes], axis=0, keepdims=True))
            follow = jnp.where(docs_after[pl.ds(lag, q), :] == own, 1.0, 0.0)
            dxin = dxin + w_ref[lag : lag + 1, lanes] * dcv[pl.ds(lag, q), lanes] * follow
        sums.append(jnp.sum(dconv, axis=0, keepdims=True))
        sums.append(jnp.sum(dy * x, axis=0, keepdims=True))
        dx_ref[:, lanes] = dxin.astype(bf16)
        for i, s in enumerate(sums):
            dconv_ref[i : i + 1, lanes] = dconv_ref[i : i + 1, lanes] + s
    dsb = d_scores.astype(bf16)
    dbct_ref[0:n, :] = mm(ct, dsb, NN) + mm(after, xt[...], NT)
    dbct_ref[n : 2 * n, :] = mm(bt, dsb, NT) + mm(old, dye[...], NT)
    new = mm(ct, dye[...], NN)
    for k in range(pairs):
        lanes = slice(k * LANES, (k + 1) * LANES)
        dstate[:, lanes] = dstate[:, lanes] * spread(fade, 2 * k, 2 * k + 1, wide_row) + new[:, lanes]
    cols = col_t[...].T
    pulled = d_toend * to_end
    at_end = jnp.sum(pulled, axis=0, keepdims=True) + fade * d_fade[0:1, :]
    d_cum = rows - step * cols + d_enter * entering - pulled
    last_row = lax.broadcasted_iota(jnp.int32, (q, LANES), 0) == q - 1
    d_cum = d_cum + jnp.where(last_row, at_end, 0.0)
    d_decay = exact(tri, d_cum, TN)
    d_step = cols + d_toend * tail - rate * d_decay
    d_raw = d_step * sigmoid(raw)
    dsmall_ref[...] = d_raw
    dhead_ref[0:1, :] = dhead_ref[0:1, :] + jnp.sum(d_raw, axis=0, keepdims=True)
    dhead_ref[1:2, :] = dhead_ref[1:2, :] + jnp.sum(d_decay * decay, axis=0, keepdims=True)
    dcv[pl.ds(q, HALO), :] = dcv[pl.ds(0, HALO), :]
    docs_after[pl.ds(q, HALO), :] = docs_after[pl.ds(0, HALO), :]


def whole(array):
    return pl.BlockSpec(array.shape, lambda c: (0,) * array.ndim)


def run_forward(q, x_in, small, bct, dcol, drow, conv_w, conv_b, sb, rate, skip, head):
    tokens, width = x_in.shape
    n = bct.shape[0] // 2
    chunks = tokens // q
    pairs = width // LANES
    taps = conv_w.shape[0]
    return pl.pallas_call(
        functools.partial(scan_forward, q, taps, pairs, head),
        grid=(chunks,),
        in_specs=[
            pl.BlockSpec((q, width), lambda c: (c, 0)),
            pl.BlockSpec((q, LANES), lambda c: (c, 0)),
            pl.BlockSpec((2 * n, q), lambda c: (0, c)),
            pl.BlockSpec((q, LANES), lambda c: (c, 0)),
            pl.BlockSpec((8, q), lambda c: (0, c)),
            whole(conv_w), whole(conv_b), whole(sb), whole(rate), whole(skip),
        ],
        out_specs=[
            pl.BlockSpec((q, width), lambda c: (c, 0)),
            pl.BlockSpec((1, n, width), lambda c: (c, 0, 0)),
        ],
        out_shape=[
            jax.ShapeDtypeStruct((tokens, width), f32),
            jax.ShapeDtypeStruct((chunks, n, width), f32),
        ],
        scratch_shapes=[
            pltpu.VMEM((n, width), f32),
            pltpu.VMEM((HALO + q, width), f32),
            pltpu.VMEM((HALO + q, LANES), f32),
            pltpu.VMEM((8, LANES), f32),
            pltpu.VMEM((q, width), bf16),
            pltpu.VMEM((8, LANES), f32),
        ],
        name="scan_forward",
    )(x_in, small, bct, dcol, drow, conv_w, conv_b, sb, rate, skip)


def run_backward(q, x_in, small, bct, dcol, drow, conv_w, conv_b, sb, rate, skip, dy, states, head):
    tokens, width = x_in.shape
    n = bct.shape[0] // 2
    chunks = tokens // q
    pairs = width // LANES
    taps = conv_w.shape[0]
    per = q // HALO

    def at(c):
        return chunks - 1 - c

    def prior(c):
        return jnp.maximum((chunks - 1 - c) * per - 1, 0)

    return pl.pallas_call(
        functools.partial(scan_backward, q, taps, pairs, head, chunks),
        grid=(chunks,),
        in_specs=[
            pl.BlockSpec((q, width), lambda c: (at(c), 0)),
            pl.BlockSpec((HALO, width), lambda c: (prior(c), 0)),
            pl.BlockSpec((q, LANES), lambda c: (at(c), 0)),
            pl.BlockSpec((2 * n, q), lambda c: (0, at(c))),
            pl.BlockSpec((q, LANES), lambda c: (at(c), 0)),
            pl.BlockSpec((HALO, LANES), lambda c: (prior(c), 0)),
            pl.BlockSpec((8, q), lambda c: (0, at(c))),
            whole(conv_w), whole(conv_b), whole(sb), whole(rate), whole(skip),
            pl.BlockSpec((q, width), lambda c: (at(c), 0)),
            pl.BlockSpec((1, n, width), lambda c: (at(c), 0, 0)),
        ],
        out_specs=[
            pl.BlockSpec((q, width), lambda c: (at(c), 0)),
            pl.BlockSpec((q, LANES), lambda c: (at(c), 0)),
            pl.BlockSpec((2 * n, q), lambda c: (0, at(c))),
            pl.BlockSpec((8, width), lambda c: (0, 0)),
            pl.BlockSpec((8, LANES), lambda c: (0, 0)),
        ],
        out_shape=[
            jax.ShapeDtypeStruct((tokens, width), bf16),
            jax.ShapeDtypeStruct((tokens, LANES), f32),
            jax.ShapeDtypeStruct((2 * n, tokens), f32),
            jax.ShapeDtypeStruct((8, width), f32),
            jax.ShapeDtypeStruct((8, LANES), f32),
        ],
        scratch_shapes=[
            pltpu.VMEM((n, width), f32),
            pltpu.VMEM((HALO + q, width), f32),
            pltpu.VMEM((HALO + q, LANES), f32),
            pltpu.VMEM((q + HALO, width), f32),
            pltpu.VMEM((q + HALO, LANES), f32),
            pltpu.VMEM((q, width), bf16),
            pltpu.VMEM((q, width), bf16),
            pltpu.VMEM((LANES, q), f32),
        ],
        name="scan_backward",
    )(x_in, x_in, small, bct, dcol, dcol, drow, conv_w, conv_b, sb, rate, skip, dy, states)


def gate_forward(
    groups, z_rows, tall,
    normed_ref, cot_ref, joined_ref, y_ref, gain_ref, z_ref, dgn_ref, sums_ref, wz, wo,
):
    parts, held, width = wo.shape

    @pl.when(pl.program_id(0) == 0)
    def _():
        for g in range(groups):
            wz[pl.ds(g * z_rows, z_rows), :] = joined_ref[g, pl.ds(0, z_rows), :]
            for k in range(parts):
                wo[k, pl.ds(g * tall, tall), :] = joined_ref[g, pl.ds(z_rows + k * tall, tall), :]

    z = mm(normed_ref[...], wz[...], NN)
    d_gn = mm(cot_ref[:, 0:width], wo[0], NT)
    for k in range(1, parts):
        d_gn = d_gn + mm(cot_ref[:, k * width : (k + 1) * width], wo[k], NT)
    z_ref[...] = z
    dgn_ref[...] = d_gn
    gated = y_ref[...] * (z * sigmoid(z))
    square = jnp.sum(gated * gated, axis=1, keepdims=True)
    cross = jnp.sum(d_gn * gain_ref[...] * gated, axis=1, keepdims=True)
    lane = lane_iota((square.shape[0], LANES))
    sums_ref[...] = jnp.where(lane == 0, square, jnp.where(lane == 1, cross, 0.0)).T[0:8, :]


def gate_backward(
    blocks, tile, z_rows, tall, channels,
    normed_ref, cot_ref, y_ref, z_ref, dgn_ref, sums_ref, gain_ref,
    gate_ref, dz_ref, dy_ref, dgain_ref, terms_ref,
):
    step = pl.program_id(0)
    rows, width = y_ref.shape
    parts = normed_ref.shape[1] // width

    @pl.when(step == 0)
    def _():
        dgain_ref[...] = jnp.zeros_like(dgain_ref)

    @pl.when(step < blocks)
    def _():
        own = pl.ds(pl.multiple_of(step * rows, rows), rows)
        columns = jnp.concatenate([sums_ref[...], jnp.zeros((LANES - 8, rows), f32)], axis=0).T
        inv = lax.rsqrt(columns[:, 0:1] / channels + epsilon)
        slope = inv * inv * inv * (columns[:, 1:2] / channels)
        for k in range(width // LANES):
            lanes = slice(k * LANES, (k + 1) * LANES)
            y, z, d_gn, gain = y_ref[:, lanes], z_ref[:, lanes], dgn_ref[:, lanes], gain_ref[:, lanes]
            sig = sigmoid(z)
            act = z * sig
            gated = y * act
            scaled = gated * inv
            gate_ref[own, lanes] = (scaled * gain).astype(bf16)
            dgain_ref[0:1, lanes] = dgain_ref[0:1, lanes] + jnp.sum(d_gn * scaled, axis=0, keepdims=True)
            d_gated = inv * (d_gn * gain) - gated * slope
            dz_ref[own, lanes] = (d_gated * y * (sig * (1.0 + z * (1.0 - sig)))).astype(bf16)
            dy_ref[:, lanes] = d_gated * act

    def store(term, at, within, base):
        if within >= tile:
            start = pl.multiple_of(base + at * tile, 16)
            terms_ref[0, pl.ds(start, tile), :] = term
        else:
            for n in range(tile // within):
                piece = term[n * within : (n + 1) * within]
                terms_ref[at * (tile // within) + n, pl.ds(base, within), :] = piece

    @pl.when(step >= blocks)
    def _():
        i = step - blocks
        lanes = pl.ds(pl.multiple_of(i * tile, LANES), tile)
        store(mm(normed_ref[:, lanes], dz_ref[...], TN).astype(bf16), i, z_rows, 0)
        j = i // parts
        lanes = pl.ds(pl.multiple_of(j * tile, LANES), tile)
        left = gate_ref[:, lanes]
        for k in range(parts):

            @pl.when(i % parts == k)
            def _():
                right = cot_ref[:, k * width : (k + 1) * width]
                store(mm(left, right, TN).astype(bf16), j, tall, z_rows + k * tall)


def run_gate_forward(joined, z_rows, normed, cot, y, gain):
    groups, deep, width = joined.shape
    tokens, n_width = normed.shape
    parts = n_width // width
    tall = (deep - z_rows) // parts
    rows = min(256, tokens)

    def tokens_of(columns):
        return pl.BlockSpec((rows, columns), lambda c: (c, 0))

    return pl.pallas_call(
        functools.partial(gate_forward, groups, z_rows, tall),
        grid=(tokens // rows,),
        in_specs=[tokens_of(n_width), tokens_of(n_width), whole(joined), tokens_of(width), whole(gain)],
        out_specs=[
            tokens_of(width), tokens_of(width), pl.BlockSpec((8, rows), lambda c: (0, c)),
            pl.BlockSpec((groups * z_rows, width), lambda c: (0, 0)),
            pl.BlockSpec((parts, groups * tall, width), lambda c: (0, 0, 0)),
        ],
        out_shape=[
            jax.ShapeDtypeStruct((tokens, width), f32),
            jax.ShapeDtypeStruct((tokens, width), f32),
            jax.ShapeDtypeStruct((8, tokens), f32),
            jax.ShapeDtypeStruct((groups * z_rows, width), bf16),
            jax.ShapeDtypeStruct((parts, groups * tall, width), bf16),
        ],
        name="gate_forward",
    )(normed, cot, joined, y, gain)


def run_gate_backward(groups, z_rows, tall, channels, normed, cot, y, z, d_gn, sums, gain):
    tokens, n_width = normed.shape
    width = y.shape[1]
    parts = n_width // width
    rows = min(256, tokens)
    blocks = tokens // rows
    tile = 3 * LANES
    deep = z_rows + parts * tall

    def tokens_of(columns):
        return pl.BlockSpec((rows, columns), lambda c: (jnp.minimum(c, blocks - 1), 0))

    return pl.pallas_call(
        functools.partial(gate_backward, blocks, tile, z_rows, tall, channels),
        grid=(blocks + n_width // tile,),
        in_specs=[
            whole(normed), whole(cot), tokens_of(width), tokens_of(width), tokens_of(width),
            pl.BlockSpec((8, rows), lambda c: (0, jnp.minimum(c, blocks - 1))), whole(gain),
        ],
        out_specs=[
            pl.BlockSpec((tokens, width), lambda c: (0, 0)),
            pl.BlockSpec((tokens, width), lambda c: (0, 0)),
            tokens_of(width),
            pl.BlockSpec((8, width), lambda c: (0, 0)),
            pl.BlockSpec((groups, deep, width), lambda c: (0, 0, 0)),
        ],
        out_shape=[
            jax.ShapeDtypeStruct((tokens, width), bf16),
            jax.ShapeDtypeStruct((tokens, width), bf16),
            jax.ShapeDtypeStruct((tokens, width), f32),
            jax.ShapeDtypeStruct((8, width), f32),
            jax.ShapeDtypeStruct((groups, deep, width), bf16),
        ],
        name="gate_backward",
    )(normed, cot, y, z, d_gn, sums, gain)


def swapped(block, bit):
    size = lax.axis_size("seq")
    return lax.ppermute(block, "seq", [(i, i ^ bit) for i in range(size)])


def bits_of(size):
    bits, bit = [], 1
    while bit < size:
        bits.append(bit)
        bit *= 2
    return bits


def joined_by(held, bit):
    other = swapped(held, bit)
    upper = (lax.axis_index("seq") & bit) != 0
    both = jnp.where(upper, jnp.stack([other, held], axis=1), jnp.stack([held, other], axis=1))
    return both.reshape((-1,) + both.shape[2:])


def opened(block):
    bits = bits_of(lax.axis_size("seq"))
    return joined_by(block[None], bits[-1]) if bits else block[None]


def gathered(block, held=None):
    held = opened(block) if held is None else held
    for bit in reversed(bits_of(lax.axis_size("seq"))[:-1]):
        held = joined_by(held, bit)
    return held.reshape((-1,) + held.shape[2:])


def scattered(parts, between=lambda held: held):
    index = lax.axis_index("seq")
    size = lax.axis_size("seq")
    rest = parts.shape[1:]
    lead = parts.shape[0]
    held = parts.reshape((size, lead // size) + rest)
    for bit in bits_of(size):
        half = held.reshape((held.shape[0] // 2, 2) + held.shape[1:])
        upper = (index & bit) != 0
        mine = jnp.where(upper, half[:, 1], half[:, 0])
        theirs = jnp.where(upper, half[:, 0], half[:, 1]).astype(bf16)
        held = between(mine.astype(f32) + swapped(theirs, bit).astype(f32))
    return held[0]


def added_over(block, bits):
    for bit in bits:
        block = block + crossed(block, bit)
    return block


def moved_by(block, step):
    count = lax.axis_size("dp")
    route = [(i, i + 2 * step) for i in range(count) if 0 <= i + 2 * step < count]
    return lax.ppermute(block, "dp", route)


def crossed(block, bits):
    return lax.ppermute(block, "dp", [(i, i ^ bits) for i in range(lax.axis_size("dp"))])


def gathered_rows(block, waits):
    count = lax.axis_size("dp")
    length = count // 2
    if not is_small(count):
        return lax.all_gather(block, "dp", axis=0, tiled=True), block
    at = lax.axis_index("dp")
    place, side = at // 2, at % 2
    rows = block.shape[0]
    whole_rows = jnp.zeros((count * rows, block.shape[1]), block.dtype)

    def put(into, piece, pair, half):
        return lax.dynamic_update_slice(into, piece, ((pair * 2 + half) * rows, 0))

    whole_rows = put(whole_rows, block, place, side)
    other = crossed(block, 1)
    whole_rows = put(whole_rows, other, place, 1 - side)
    up, down, ready = block, block, []
    for hop in range(1, length):
        up, down = after((moved_by(up, 1), moved_by(down, -1)), (other, waits[hop - 1 : hop]))
        ready.append((down, up))
        piece, pair = None, None
        for spot in range(length):
            near = min(spot, length - 1 - spot)
            if hop <= 2 * near:
                away, from_below = (hop + 1) // 2, hop % 2 == 0
            else:
                away, from_below = hop - near, spot > length - 1 - spot
            chosen = ready[away - 1][1 if from_below else 0]
            source = spot - away if from_below else spot + away
            here = place == spot
            piece = chosen if piece is None else jnp.where(here, chosen, piece)
            pair = source if pair is None else jnp.where(here, source, pair)
        whole_rows = put(whole_rows, piece, pair, side)
        other = crossed(piece, 1)
        whole_rows = put(whole_rows, other, pair, 1 - side)
    return whole_rows, ready[min(1, length - 2)]


def is_small(count):
    return count <= 8 and count & (count - 1) == 0


def halved_rows(term):
    count = lax.axis_size("dp")
    if not is_small(count):
        return term
    at = lax.axis_index("dp")
    pairs = term.reshape(count // 2, 2, -1, term.shape[1])

    def side(which):
        return lax.dynamic_index_in_dim(pairs, which, 1, keepdims=False)

    came = crossed(side((at & 1) ^ 1), 1)
    return (side(at & 1).astype(f32) + came.astype(f32)).astype(bf16)


def shared_rows(lines):
    count = lax.axis_size("dp")
    if not is_small(count):
        return [lax.psum_scatter(lines, "dp", scatter_dimension=0, tiled=True)]
    at = lax.axis_index("dp")

    def part(owner):
        return lax.dynamic_index_in_dim(lines, owner // 2, 0, keepdims=False)

    return [part(at)] + [crossed(part(at ^ bits), bits) for bits in range(2, count, 2)]


def after(value, other):
    return lax.optimization_barrier((value, other))[0]


def turned(blocks):
    size = lax.axis_size("seq")
    index = lax.axis_index("seq")
    if size & (size - 1):
        return lax.all_to_all(blocks, "seq", 0, 0, tiled=True)
    out = blocks
    for bits in range(1, size):
        piece = lax.dynamic_slice_in_dim(blocks, index ^ bits, 1, 0)
        piece = lax.ppermute(piece, "seq", [(i, i ^ bits) for i in range(size)])
        out = lax.dynamic_update_slice_in_dim(out, piece, index ^ bits, 0)
    return out


def folded(rows, lead, width):
    cut = rows.reshape(lead, rows.shape[0] // lead, rows.shape[1] // width, width)
    cut = cut.transpose(0, 2, 1, 3).reshape(lead, -1, width)
    return cut[0] if lead == 1 else cut


def unfolded(pieces, width):
    lead, stacked, narrow = pieces.shape
    cut = pieces.reshape(lead, width // narrow, stacked * narrow // width, narrow)
    return cut.transpose(0, 2, 1, 3).reshape(-1, width)


def exchanged(parts):
    size = lax.axis_size("seq")
    index = lax.axis_index("seq")
    held = parts.reshape((size, -1) + parts.shape[1:])

    def part(owner):
        return lax.dynamic_index_in_dim(held, owner, 0, keepdims=False)

    came = [
        lax.ppermute(part(index ^ bits).astype(bf16), "seq", [(i, i ^ bits) for i in range(size)])
        for bits in range(1, size)
    ]
    return sum([piece.astype(f32) for piece in came], part(index))


def by_rows(array):
    return with_layout_constraint(array, Layout(major_to_minor=(0, 1)))


def padded(rows, width):
    return jnp.pad(rows, ((0, 0), (0, width - rows.shape[1])))


def shards(
    hidden, segments, cotangent, norm_gain, in_weight, conv_weight, conv_bias, step_bias, log_rate,
    skip_gain, gate_gain, out_weight,
):
    n_seqs, block, n_width = hidden.shape
    size = lax.axis_size("seq")
    groups = lax.axis_size("dp")
    index = lax.axis_index("seq")
    tokens = size * block
    n_inner = gate_gain.shape[0]
    n_heads = step_bias.shape[0]
    n_taps = conv_weight.shape[0]
    n_mixed = conv_bias.shape[0]
    n_state = (n_mixed - n_inner) // 2
    head = n_inner // n_heads
    own_inner = n_inner // size
    own_heads = n_heads // size
    own_bc = 2 * n_state // size
    q = min(128, block)
    in_rows = in_weight.shape[0]

    in_low = in_weight.astype(bf16)
    runs = 2 if groups % 2 == 0 else 1

    def dealt(columns):
        cut = columns.reshape(columns.shape[0], runs, size, -1)
        return cut.transpose(0, 2, 1, 3).reshape(columns.shape[0], size, -1)

    def undealt(columns):
        cut = columns.reshape(columns.shape[0], size, runs, -1)
        return cut.transpose(0, 2, 1, 3).reshape(columns.shape[0], -1)

    def own_columns(columns):
        wide = columns.shape[1] // runs
        narrow = wide // size
        starts = [run * wide + index * narrow for run in range(runs)]
        cut = [lax.dynamic_slice_in_dim(columns, start, narrow, 1) for start in starts]
        return jnp.concatenate(cut, axis=1)

    z_cols = dealt(in_low[:, :n_inner])
    x_cols = dealt(in_low[:, n_inner : 2 * n_inner])
    bc_cols = in_low[:, 2 * n_inner : n_inner + n_mixed].reshape(in_rows, size, own_bc)
    dt_cols = dealt(in_low[:, n_inner + n_mixed :])
    gap = jnp.zeros((in_rows, size, LANES - own_heads - own_bc), bf16)
    laid = jnp.concatenate([x_cols, dt_cols, gap, bc_cols, z_cols], axis=2).transpose(1, 0, 2)
    mine = lax.all_to_all(laid, "seq", 0, 0, tiled=True)
    flat = hidden.reshape(block, n_width).astype(f32)
    inv = lax.rsqrt(jnp.mean(flat * flat, axis=-1, keepdims=True) + epsilon)
    unit = flat * inv
    normed_own = (unit * norm_gain).astype(bf16)
    docs = gathered(segments).reshape(tokens).astype(f32)
    half = groups // runs
    order = []
    for f in range(groups * size):
        run, owner, spot = f // (half * size), f // half % size, f % half
        order.append((f, (run * half + spot) * size + owner))
    back = [(b, a) for a, b in order]
    out_moved = lax.ppermute(out_weight.astype(bf16), ("dp", "seq"), order)
    channels = [conv_weight[:, :n_inner], conv_bias[None, :n_inner], gate_gain[None]]
    channels = own_columns(jnp.concatenate(channels, axis=0))
    conv_x, bias_x, gain = channels[:n_taps], channels[n_taps : n_taps + 1], channels[n_taps + 1 :]
    heads = own_columns(jnp.stack([step_bias, jnp.exp(log_rate), skip_gain]))
    sb, rate = padded(heads[0:1], LANES), padded(heads[1:2], LANES)
    skip = jnp.repeat(heads[2:3], head, axis=1)
    dcol = jnp.broadcast_to(docs[:, None], (tokens, LANES))
    drow = jnp.broadcast_to(docs[None, :], (8, tokens))
    early = (docs, out_moved, conv_x, bias_x, gain, sb, rate, skip, dcol, drow)
    mine, normed_own = lax.optimization_barrier((after(mine, early), normed_own))
    mine = mine.reshape(size * in_rows, -1)
    n_first = own_inner + LANES
    cot_own = cotangent.reshape(block, n_width)
    normed_held = opened(normed_own)
    cot_held = opened(after(cot_own, mine))
    w_first, hopped = gathered_rows(mine[:, :n_first], [normed_held, cot_held])
    z_block = jnp.concatenate([mine[:, n_first:], folded(out_moved, 1, own_inner)], axis=0)

    normed = gathered(normed_own, normed_held)
    joined = lax.all_gather(after(z_block, hopped), "dp", axis=0, tiled=True).reshape(groups, -1, own_inner)
    z_rows = size * in_rows
    cot = gathered(cot_own, cot_held)

    def own_part(vector, parts):
        return lax.dynamic_slice_in_dim(vector, index * parts, parts, vector.ndim - 1)

    w_x, w_small = w_first[:, :own_inner], w_first[:, own_inner:]
    small = mm(normed, w_small, NN)
    x_in = mm(normed, w_x, NN).astype(bf16)
    conv_bc = own_part(conv_weight[:, n_inner:], own_bc)
    bias_bc = own_part(conv_bias[None, n_inner:], own_bc)

    head_lanes = jnp.arange(LANES) < own_heads
    bc_in = small[:, LANES - own_bc :].astype(bf16).astype(f32)
    small_dt = jnp.where(head_lanes, small, 0.0)

    def earlier(rows, lag):
        return jnp.pad(rows, ((lag, 0), (0, 0)))[:tokens]

    def later(rows, lag):
        return jnp.pad(rows, ((0, lag), (0, 0)))[lag:]

    same = [None] + [
        jnp.where(jnp.pad(docs, (lag, 0), constant_values=-1.0)[:tokens] == docs, 1.0, 0.0)[:, None]
        for lag in range(1, n_taps)
    ]
    bc_conv = bias_bc + conv_bc[0:1] * bc_in
    for lag in range(1, n_taps):
        bc_conv = bc_conv + conv_bc[lag : lag + 1] * earlier(bc_in, lag) * same[lag]
    bc_sig = jax.nn.sigmoid(bc_conv)
    bct = gathered(by_rows((bc_conv * bc_sig).astype(bf16).T))

    y, states = run_forward(
        q, x_in, small_dt, bct, dcol, drow, conv_x, bias_x, sb, rate, skip, head
    )

    out_rows = own_inner // groups
    tiled = z_rows % 16 == 0 and out_rows % 16 == 0
    if tiled:
        lead, deep, tall, gate_in = groups, z_rows, out_rows, joined
    else:
        lead, deep, tall = 1, groups * z_rows, own_inner
        w_out = unfolded(joined[:, z_rows:], n_width)
        gate_in = [joined[:, :z_rows].reshape(-1, own_inner), folded(w_out, 1, own_inner)]
        gate_in = jnp.concatenate(gate_in, axis=0)[None]
    z, d_gn, sums, w_z, w_out = run_gate_forward(gate_in, deep, normed, cot, y, gain)
    w_out = jnp.concatenate(list(w_out), axis=1)
    sums = lax.psum(sums[:2], "seq")
    sums = jnp.pad(sums, ((0, 6), (0, 0)))
    gate_low, d_z, d_y, d_gain, terms = run_gate_backward(
        lead, deep, tall, n_inner, normed, cot, y, z, d_gn, sums, gain
    )
    d_gain = d_gain[0]
    if not tiled:
        z_term = terms[0, :deep].reshape(groups, z_rows, own_inner)
        out_term = terms[0, deep:].reshape(n_width // own_inner, groups, out_rows, own_inner)
        out_term = out_term.transpose(1, 0, 2, 3).reshape(groups, -1, own_inner)
        terms = jnp.concatenate([z_term, out_term], axis=1)
    terms = terms.reshape(-1, own_inner)
    parts = lax.psum_scatter(terms, "dp", scatter_dimension=0, tiled=True)

    d_x, d_dt, d_bct, d_conv_x, d_heads = run_backward(
        q, x_in, small_dt, bct, dcol, drow, conv_x, bias_x, sb, rate, skip, d_y, states, head
    )
    x_term = mm(normed, d_x, TN).astype(bf16)
    x_term, d_bct = lax.optimization_barrier((x_term, d_bct))
    x_lines = halved_rows(x_term)
    d_bc = by_rows(exchanged(d_bct)).T
    d_bcc = d_bc * (bc_sig * (1.0 + bc_conv * (1.0 - bc_sig)))
    d_bc_in = conv_bc[0:1] * d_bcc
    w_sums = [jnp.sum(d_bcc * bc_in, axis=0)]
    for lag in range(1, n_taps):
        held = d_bcc * same[lag]
        d_bc_in = d_bc_in + conv_bc[lag : lag + 1] * later(held, lag)
        w_sums.append(jnp.sum(held * earlier(bc_in, lag), axis=0))
    w_sums.append(jnp.sum(d_bcc, axis=0))
    d_small = jnp.concatenate([d_dt[:, : LANES - own_bc], d_bc_in], axis=1).astype(bf16)
    d_first = jnp.concatenate([d_x, d_small], axis=1)
    small_lines = halved_rows(mm(normed, d_small, TN).astype(bf16))
    branch = scattered(mm(after(gate_low, d_bc), w_out, NN).astype(bf16))
    result = (flat + branch).reshape(n_seqs, block, n_width).astype(bf16)
    d_normed = mm(d_first, w_first, NT) + mm(d_z, w_z, NT)
    d_norm_gain = jnp.sum(d_normed * normed.astype(f32), axis=0) / norm_gain
    d_skip = jnp.sum(d_conv_x[n_taps + 1].reshape(own_heads, head), axis=1)
    packed = jnp.concatenate(
        [
            d_conv_x[: n_taps + 1].reshape(-1),
            jnp.stack(w_sums).reshape(-1),
            d_gain,
            d_heads[0, :own_heads],
            d_heads[1, :own_heads],
            d_skip,
            d_norm_gain,
        ]
    )
    lines = jnp.concatenate([x_lines, small_lines], axis=-1)
    packed = added_over(packed, reversed(bits_of(groups)[1:]))
    lines, packed = lax.optimization_barrier((lines, packed))
    shares = shared_rows(lines)
    packed = gathered(added_over(packed, bits_of(groups)[:1])[None])
    parts, result = lax.optimization_barrier((after(parts, lines), result))
    d_norm = after(d_normed.astype(bf16), parts)
    d_norm = lax.psum_scatter(d_norm, "seq", scatter_dimension=0, tiled=True).astype(f32)

    def own_rows(part):
        out = turned(part.reshape(size, in_rows, -1))
        return out.transpose(1, 0, 2).astype(f32)

    out_part = unfolded(parts[None, z_rows:], n_width)
    d_out_weight = lax.ppermute(out_part, ("dp", "seq"), back).astype(f32)
    in_z = own_rows(parts[:z_rows])
    shares, in_z, d_out_weight = lax.optimization_barrier((shares, in_z, d_out_weight))
    first_part = sum(share.astype(f32) for share in shares)
    in_first = own_rows(first_part.astype(bf16))
    d_in_weight = jnp.concatenate(
        [
            undealt(in_z),
            undealt(in_first[:, :, :own_inner]),
            in_first[:, :, n_first - own_bc :].reshape(in_rows, 2 * n_state),
            undealt(in_first[:, :, own_inner : own_inner + own_heads]),
        ],
        axis=1,
    )

    lifted = d_norm * norm_gain
    d_flat = inv * lifted - flat * (
        inv * inv * inv * jnp.mean(lifted * flat, axis=-1, keepdims=True)
    )
    d_hidden = (cot_own.astype(f32) + d_flat).reshape(n_seqs, block, n_width)

    at = 0

    def take(count):
        nonlocal at
        at += count
        return packed[:, at - count : at]

    got_x = take((n_taps + 1) * own_inner).reshape(size, n_taps + 1, own_inner)
    got_bc = take((n_taps + 1) * own_bc).reshape(size, n_taps + 1, own_bc)
    got_x = undealt(got_x.transpose(1, 0, 2))
    got_bc = got_bc.transpose(1, 0, 2).reshape(n_taps + 1, 2 * n_state)
    conv_all = jnp.concatenate([got_x, got_bc], axis=1)
    d_gate_gain = undealt(take(own_inner)[None])[0]
    d_step_bias = undealt(take(own_heads)[None])[0]
    d_log_rate = undealt(take(own_heads)[None])[0]
    d_skip_gain = undealt(take(own_heads)[None])[0]
    d_norm_all = jnp.sum(take(n_width), axis=0)
    return (
        result,
        d_hidden,
        d_norm_all,
        d_in_weight,
        conv_all[:n_taps],
        conv_all[n_taps],
        d_step_bias,
        d_log_rate,
        d_skip_gain,
        d_gate_gain,
        d_out_weight,
    )


def solution(mesh):
    tokens = P("dp", "seq", None)
    rows = P(("dp", "seq"), None)
    return jax.shard_map(
        shards,
        mesh=mesh,
        in_specs=(tokens, P("dp", "seq"), tokens, P(), rows, P(), P(), P(), P(), P(), P(), rows),
        out_specs=(tokens, tokens, P(), rows, P(), P(), P(), P(), P(), P(), rows),
        check_vma=False,
    )
```

```python
import functools

import jax
import jax.numpy as jnp
from jax import lax
from jax.experimental import pallas as pl
from jax.experimental.layout import Layout, with_layout_constraint
from jax.experimental.pallas import tpu as pltpu
from jax.sharding import PartitionSpec as P

epsilon = 1e-05
highest = lax.Precision.HIGHEST
f32 = jnp.float32
bf16 = jnp.bfloat16
LANES = 128
HALO = 16
NEG = -1e30


def mm(a, b, dims, out=f32):
    return lax.dot_general(a, b, (dims, ((), ())), preferred_element_type=out)


NN = ((1,), (0,))
NT = ((1,), (1,))
TN = ((0,), (0,))


def exact(a, b, dims):
    return lax.dot_general(a, b, (dims, ((), ())), precision=highest, preferred_element_type=f32)


def softplus(v):
    return jnp.maximum(v, 0.0) + jnp.log1p(jnp.exp(-jnp.abs(v)))


def sigmoid(v):
    return 1.0 / (1.0 + jnp.exp(-v))


def lane_iota(shape):
    return lax.broadcasted_iota(jnp.int32, shape, len(shape) - 1)


def spread(columns, first, second, wide):
    rows = columns.shape[0]
    left = jnp.broadcast_to(columns[:, first : first + 1], (rows, LANES))
    right = jnp.broadcast_to(columns[:, second : second + 1], (rows, LANES))
    return jnp.where(wide, left, right)


def step_parts(raw, rate, q):
    row = lax.broadcasted_iota(jnp.int32, (q, q), 0)
    col = lax.broadcasted_iota(jnp.int32, (q, q), 1)
    tri = jnp.where(row >= col, 1.0, 0.0).astype(f32)
    step = softplus(raw)
    decay = -step * rate
    total = exact(tri, decay, NN)
    return step, decay, total, tri, row >= col


def convolve(ext, docs_ext, own, weights, bias, lanes, q, taps):
    running = bias + weights[0:1, lanes] * ext[pl.ds(HALO, q), lanes]
    for lag in range(1, taps):
        same = jnp.where(docs_ext[pl.ds(HALO - lag, q), :] == own, 1.0, 0.0)
        running = running + weights[lag : lag + 1, lanes] * ext[pl.ds(HALO - lag, q), lanes] * same
    return running


def scan_forward(
    q, taps, pairs, head,
    x_ref, small_ref, bct_ref, dcol_ref, drow_ref, w_ref, b_ref, sb_ref, rate_ref, skip_ref,
    y_ref, states_ref,
    state, ext, docs_ext, xs, xt, last_doc,
):
    c = pl.program_id(0)
    n = bct_ref.shape[0] // 2

    @pl.when(c == 0)
    def _():
        state[...] = jnp.zeros_like(state)
        ext[pl.ds(0, HALO), :] = jnp.zeros((HALO, ext.shape[1]), f32)
        docs_ext[pl.ds(0, HALO), :] = jnp.full((HALO, LANES), -1.0, f32)
        last_doc[...] = jnp.full(last_doc.shape, -1.0, f32)

    own = dcol_ref[...]
    ext[pl.ds(HALO, q), :] = x_ref[...].astype(f32)
    docs_ext[pl.ds(HALO, q), :] = own
    step, _, cum, _, causal = step_parts(small_ref[...] + sb_ref[...], rate_ref[...], q)
    step_t = step.T
    cum_t = cum.T
    end = cum[q - 1 : q, :]
    id_in = last_doc[0:1, :]
    final = own[q - 1 : q, :]
    linked = jnp.where(final == id_in, 1.0, 0.0)
    fade = linked * jnp.exp(end)
    entering = jnp.where(own == id_in, 1.0, 0.0) * jnp.exp(cum)
    to_end = jnp.where(own == final, 1.0, 0.0) * jnp.exp(end - cum) * step
    same_doc = jnp.broadcast_to(own[:, 0:1], (q, q)) == jnp.broadcast_to(drow_ref[0:1, :], (q, q))
    hide = jnp.where(jnp.logical_and(causal, same_doc), 0.0, NEG)
    bt = bct_ref[0:n, :]
    ct = bct_ref[n : 2 * n, :]
    scores = mm(ct, bt, TN)
    states_ref[0] = state[...]
    old = state[...].astype(bf16)
    wide = lane_iota((q, LANES)) < head
    wide_row = lane_iota((1, LANES)) < head
    for k in range(pairs):
        lanes = slice(k * LANES, (k + 1) * LANES)
        h0, h1 = 2 * k, 2 * k + 1
        conv = convolve(ext, docs_ext, own, w_ref, b_ref[:, lanes], lanes, q, taps)
        x = conv * sigmoid(conv)
        xd = x * spread(step, h0, h1, wide)
        xt[:, lanes] = (x * spread(to_end, h0, h1, wide)).astype(bf16)
        mats = []
        for h in (h0, h1):
            gap = cum[:, h : h + 1] - cum_t[h : h + 1, :] + hide
            mats.append((jnp.exp(gap) * scores).astype(bf16))
        out = mm(mats[0], jnp.where(wide, xd, 0.0).astype(bf16), NN)
        out = out + mm(mats[1], jnp.where(wide, 0.0, xd).astype(bf16), NN)
        out = out + mm(ct, old[:, lanes], TN) * spread(entering, h0, h1, wide)
        y_ref[:, lanes] = out + skip_ref[:, lanes] * x
    update = mm(bt, xt[...], NN)
    for k in range(pairs):
        lanes = slice(k * LANES, (k + 1) * LANES)
        state[:, lanes] = state[:, lanes] * spread(fade, 2 * k, 2 * k + 1, wide_row) + update[:, lanes]
    ext[pl.ds(0, HALO), :] = ext[pl.ds(q, HALO), :]
    docs_ext[pl.ds(0, HALO), :] = docs_ext[pl.ds(q, HALO), :]
    last_doc[...] = jnp.broadcast_to(final, last_doc.shape)


def scan_backward(
    q, taps, pairs, head, chunks,
    x_ref, xp_ref, small_ref, bct_ref, dcol_ref, dcolp_ref, drow_ref, w_ref, b_ref, sb_ref, rate_ref,
    skip_ref, dy_ref, states_ref,
    dx_ref, dsmall_ref, dbct_ref, dconv_ref, dhead_ref,
    dstate, ext, docs_ext, dcv, docs_after, dye, xt, col_t,
):
    step_at = pl.program_id(0)
    c = chunks - 1 - step_at
    n = bct_ref.shape[0] // 2
    width = x_ref.shape[1]

    @pl.when(step_at == 0)
    def _():
        dstate[...] = jnp.zeros_like(dstate)
        dcv[pl.ds(q, HALO), :] = jnp.zeros((HALO, width), f32)
        docs_after[pl.ds(q, HALO), :] = jnp.full((HALO, LANES), -1.0, f32)
        dconv_ref[...] = jnp.zeros_like(dconv_ref)
        dhead_ref[...] = jnp.zeros_like(dhead_ref)
        col_t[...] = jnp.zeros_like(col_t)

    first = c == 0
    own = dcol_ref[...]
    before = jnp.where(first, -1.0, dcolp_ref[...])
    ext[pl.ds(0, HALO), :] = xp_ref[...].astype(f32)
    ext[pl.ds(HALO, q), :] = x_ref[...].astype(f32)
    docs_ext[pl.ds(0, HALO), :] = before
    docs_ext[pl.ds(HALO, q), :] = own
    docs_after[pl.ds(0, q), :] = own
    raw = small_ref[...] + sb_ref[...]
    rate = rate_ref[...]
    step, decay, cum, tri, causal = step_parts(raw, rate, q)
    step_t = step.T
    cum_t = cum.T
    end = cum[q - 1 : q, :]
    id_in = before[HALO - 1 : HALO, :]
    final = own[q - 1 : q, :]
    linked = jnp.where(final == id_in, 1.0, 0.0)
    fade = linked * jnp.exp(end)
    entering = jnp.where(own == id_in, 1.0, 0.0) * jnp.exp(cum)
    tail = jnp.where(own == final, 1.0, 0.0) * jnp.exp(end - cum)
    to_end = tail * step
    same_doc = jnp.broadcast_to(own[:, 0:1], (q, q)) == jnp.broadcast_to(drow_ref[0:1, :], (q, q))
    hide = jnp.where(jnp.logical_and(causal, same_doc), 0.0, NEG)
    bt = bct_ref[0:n, :]
    ct = bct_ref[n : 2 * n, :]
    scores = mm(ct, bt, TN)
    old = states_ref[0].astype(bf16)
    after = dstate[...].astype(bf16)
    wide = lane_iota((q, LANES)) < head
    wide_row = lane_iota((1, LANES)) < head
    lane = lane_iota((q, LANES))
    d_scores = jnp.zeros((q, q), f32)
    rows = jnp.zeros((q, LANES), f32)
    d_enter = jnp.zeros((q, LANES), f32)
    d_toend = jnp.zeros((q, LANES), f32)
    d_fade = jnp.zeros((8, LANES), f32)
    part = lax.broadcasted_iota(jnp.int32, (LANES, LANES), 0) // head
    to = lane_iota((LANES, LANES))
    for k in range(pairs):
        lanes = slice(k * LANES, (k + 1) * LANES)
        h0, h1 = 2 * k, 2 * k + 1
        pick = jnp.where(part + 2 * k == to, 1.0, 0.0)
        conv = convolve(ext, docs_ext, own, w_ref, b_ref[:, lanes], lanes, q, taps)
        sig = sigmoid(conv)
        x = conv * sig
        xb = x.astype(bf16)
        dy = dy_ref[:, lanes]
        halves = (jnp.where(wide, dy, 0.0).astype(bf16), jnp.where(wide, 0.0, dy).astype(bf16))
        dxd = jnp.zeros((q, LANES), f32)
        for h, half in ((h0, halves[0]), (h1, halves[1])):
            inner = mm(half, xb, NT)
            keep = jnp.exp(cum[:, h : h + 1] - cum_t[h : h + 1, :] + hide)
            grown = keep * inner
            mat = keep * scores
            dt = step_t[h : h + 1, :]
            g = grown * scores
            d_scores = d_scores + grown * dt
            rows = jnp.where(lane == h, jnp.sum(g * dt, axis=1, keepdims=True), rows)
            col_t[h : h + 1, :] = jnp.sum(g, axis=0, keepdims=True)
            dxd = dxd + mm(mat.astype(bf16), half, TN)
        v = mm(bt, after[:, lanes], TN)
        u = mm(ct, old[:, lanes], TN)
        enter_k = spread(entering, h0, h1, wide)
        end_k = spread(to_end, h0, h1, wide)
        d_enter = d_enter + exact(dy * u, pick, NN)
        d_toend = d_toend + exact(x * v, pick, NN)
        hh = jnp.sum(dstate[:, lanes] * states_ref[0, :, lanes], axis=0, keepdims=True)
        d_fade = d_fade + exact(jnp.broadcast_to(hh, (8, LANES)), pick, NN)
        dye[:, lanes] = (dy * enter_k).astype(bf16)
        xt[:, lanes] = (x * end_k).astype(bf16)
        dx = dxd * spread(step, h0, h1, wide) + end_k * v + skip_ref[:, lanes] * dy
        dconv = dx * (sig * (1.0 + conv * (1.0 - sig)))
        dcv[pl.ds(0, q), lanes] = dconv
        sums = [jnp.sum(dconv * ext[pl.ds(HALO, q), lanes], axis=0, keepdims=True)]
        dxin = w_ref[0:1, lanes] * dconv
        for lag in range(1, taps):
            same = jnp.where(docs_ext[pl.ds(HALO - lag, q), :] == own, 1.0, 0.0)
            sums.append(jnp.sum(dconv * same * ext[pl.ds(HALO - lag, q), lanes], axis=0, keepdims=True))
            follow = jnp.where(docs_after[pl.ds(lag, q), :] == own, 1.0, 0.0)
            dxin = dxin + w_ref[lag : lag + 1, lanes] * dcv[pl.ds(lag, q), lanes] * follow
        sums.append(jnp.sum(dconv, axis=0, keepdims=True))
        sums.append(jnp.sum(dy * x, axis=0, keepdims=True))
        dx_ref[:, lanes] = dxin.astype(bf16)
        for i, s in enumerate(sums):
            dconv_ref[i : i + 1, lanes] = dconv_ref[i : i + 1, lanes] + s
    dsb = d_scores.astype(bf16)
    dbct_ref[0:n, :] = mm(ct, dsb, NN) + mm(after, xt[...], NT)
    dbct_ref[n : 2 * n, :] = mm(bt, dsb, NT) + mm(old, dye[...], NT)
    new = mm(ct, dye[...], NN)
    for k in range(pairs):
        lanes = slice(k * LANES, (k + 1) * LANES)
        dstate[:, lanes] = dstate[:, lanes] * spread(fade, 2 * k, 2 * k + 1, wide_row) + new[:, lanes]
    cols = col_t[...].T
    pulled = d_toend * to_end
    at_end = jnp.sum(pulled, axis=0, keepdims=True) + fade * d_fade[0:1, :]
    d_cum = rows - step * cols + d_enter * entering - pulled
    last_row = lax.broadcasted_iota(jnp.int32, (q, LANES), 0) == q - 1
    d_cum = d_cum + jnp.where(last_row, at_end, 0.0)
    d_decay = exact(tri, d_cum, TN)
    d_step = cols + d_toend * tail - rate * d_decay
    d_raw = d_step * sigmoid(raw)
    dsmall_ref[...] = d_raw
    dhead_ref[0:1, :] = dhead_ref[0:1, :] + jnp.sum(d_raw, axis=0, keepdims=True)
    dhead_ref[1:2, :] = dhead_ref[1:2, :] + jnp.sum(d_decay * decay, axis=0, keepdims=True)
    dcv[pl.ds(q, HALO), :] = dcv[pl.ds(0, HALO), :]
    docs_after[pl.ds(q, HALO), :] = docs_after[pl.ds(0, HALO), :]


def whole(array):
    return pl.BlockSpec(array.shape, lambda c: (0,) * array.ndim)


def run_forward(q, x_in, small, bct, dcol, drow, conv_w, conv_b, sb, rate, skip, head):
    tokens, width = x_in.shape
    n = bct.shape[0] // 2
    chunks = tokens // q
    pairs = width // LANES
    taps = conv_w.shape[0]
    return pl.pallas_call(
        functools.partial(scan_forward, q, taps, pairs, head),
        grid=(chunks,),
        in_specs=[
            pl.BlockSpec((q, width), lambda c: (c, 0)),
            pl.BlockSpec((q, LANES), lambda c: (c, 0)),
            pl.BlockSpec((2 * n, q), lambda c: (0, c)),
            pl.BlockSpec((q, LANES), lambda c: (c, 0)),
            pl.BlockSpec((8, q), lambda c: (0, c)),
            whole(conv_w), whole(conv_b), whole(sb), whole(rate), whole(skip),
        ],
        out_specs=[
            pl.BlockSpec((q, width), lambda c: (c, 0)),
            pl.BlockSpec((1, n, width), lambda c: (c, 0, 0)),
        ],
        out_shape=[
            jax.ShapeDtypeStruct((tokens, width), f32),
            jax.ShapeDtypeStruct((chunks, n, width), f32),
        ],
        scratch_shapes=[
            pltpu.VMEM((n, width), f32),
            pltpu.VMEM((HALO + q, width), f32),
            pltpu.VMEM((HALO + q, LANES), f32),
            pltpu.VMEM((8, LANES), f32),
            pltpu.VMEM((q, width), bf16),
            pltpu.VMEM((8, LANES), f32),
        ],
        name="scan_forward",
    )(x_in, small, bct, dcol, drow, conv_w, conv_b, sb, rate, skip)


def run_backward(q, x_in, small, bct, dcol, drow, conv_w, conv_b, sb, rate, skip, dy, states, head):
    tokens, width = x_in.shape
    n = bct.shape[0] // 2
    chunks = tokens // q
    pairs = width // LANES
    taps = conv_w.shape[0]
    per = q // HALO

    def at(c):
        return chunks - 1 - c

    def prior(c):
        return jnp.maximum((chunks - 1 - c) * per - 1, 0)

    return pl.pallas_call(
        functools.partial(scan_backward, q, taps, pairs, head, chunks),
        grid=(chunks,),
        in_specs=[
            pl.BlockSpec((q, width), lambda c: (at(c), 0)),
            pl.BlockSpec((HALO, width), lambda c: (prior(c), 0)),
            pl.BlockSpec((q, LANES), lambda c: (at(c), 0)),
            pl.BlockSpec((2 * n, q), lambda c: (0, at(c))),
            pl.BlockSpec((q, LANES), lambda c: (at(c), 0)),
            pl.BlockSpec((HALO, LANES), lambda c: (prior(c), 0)),
            pl.BlockSpec((8, q), lambda c: (0, at(c))),
            whole(conv_w), whole(conv_b), whole(sb), whole(rate), whole(skip),
            pl.BlockSpec((q, width), lambda c: (at(c), 0)),
            pl.BlockSpec((1, n, width), lambda c: (at(c), 0, 0)),
        ],
        out_specs=[
            pl.BlockSpec((q, width), lambda c: (at(c), 0)),
            pl.BlockSpec((q, LANES), lambda c: (at(c), 0)),
            pl.BlockSpec((2 * n, q), lambda c: (0, at(c))),
            pl.BlockSpec((8, width), lambda c: (0, 0)),
            pl.BlockSpec((8, LANES), lambda c: (0, 0)),
        ],
        out_shape=[
            jax.ShapeDtypeStruct((tokens, width), bf16),
            jax.ShapeDtypeStruct((tokens, LANES), f32),
            jax.ShapeDtypeStruct((2 * n, tokens), f32),
            jax.ShapeDtypeStruct((8, width), f32),
            jax.ShapeDtypeStruct((8, LANES), f32),
        ],
        scratch_shapes=[
            pltpu.VMEM((n, width), f32),
            pltpu.VMEM((HALO + q, width), f32),
            pltpu.VMEM((HALO + q, LANES), f32),
            pltpu.VMEM((q + HALO, width), f32),
            pltpu.VMEM((q + HALO, LANES), f32),
            pltpu.VMEM((q, width), bf16),
            pltpu.VMEM((q, width), bf16),
            pltpu.VMEM((LANES, q), f32),
        ],
        name="scan_backward",
    )(x_in, x_in, small, bct, dcol, dcol, drow, conv_w, conv_b, sb, rate, skip, dy, states)


def gate_forward(
    groups, z_rows, tall,
    normed_ref, cot_ref, joined_ref, y_ref, gain_ref, z_ref, dgn_ref, sums_ref, wz, wo,
):
    parts, held, width = wo.shape

    @pl.when(pl.program_id(0) == 0)
    def _():
        for g in range(groups):
            wz[pl.ds(g * z_rows, z_rows), :] = joined_ref[g, pl.ds(0, z_rows), :]
            for k in range(parts):
                wo[k, pl.ds(g * tall, tall), :] = joined_ref[g, pl.ds(z_rows + k * tall, tall), :]

    z = mm(normed_ref[...], wz[...], NN)
    d_gn = mm(cot_ref[:, 0:width], wo[0], NT)
    for k in range(1, parts):
        d_gn = d_gn + mm(cot_ref[:, k * width : (k + 1) * width], wo[k], NT)
    z_ref[...] = z
    dgn_ref[...] = d_gn
    gated = y_ref[...] * (z * sigmoid(z))
    square = jnp.sum(gated * gated, axis=1, keepdims=True)
    cross = jnp.sum(d_gn * gain_ref[...] * gated, axis=1, keepdims=True)
    lane = lane_iota((square.shape[0], LANES))
    sums_ref[...] = jnp.where(lane == 0, square, jnp.where(lane == 1, cross, 0.0)).T[0:8, :]


def gate_backward(
    blocks, tile, z_rows, tall, channels,
    normed_ref, cot_ref, y_ref, z_ref, dgn_ref, sums_ref, gain_ref,
    gate_ref, dz_ref, dy_ref, dgain_ref, terms_ref,
):
    step = pl.program_id(0)
    rows, width = y_ref.shape
    parts = normed_ref.shape[1] // width

    @pl.when(step == 0)
    def _():
        dgain_ref[...] = jnp.zeros_like(dgain_ref)

    @pl.when(step < blocks)
    def _():
        own = pl.ds(pl.multiple_of(step * rows, rows), rows)
        columns = jnp.concatenate([sums_ref[...], jnp.zeros((LANES - 8, rows), f32)], axis=0).T
        inv = lax.rsqrt(columns[:, 0:1] / channels + epsilon)
        slope = inv * inv * inv * (columns[:, 1:2] / channels)
        for k in range(width // LANES):
            lanes = slice(k * LANES, (k + 1) * LANES)
            y, z, d_gn, gain = y_ref[:, lanes], z_ref[:, lanes], dgn_ref[:, lanes], gain_ref[:, lanes]
            sig = sigmoid(z)
            act = z * sig
            gated = y * act
            scaled = gated * inv
            gate_ref[own, lanes] = (scaled * gain).astype(bf16)
            dgain_ref[0:1, lanes] = dgain_ref[0:1, lanes] + jnp.sum(d_gn * scaled, axis=0, keepdims=True)
            d_gated = inv * (d_gn * gain) - gated * slope
            dz_ref[own, lanes] = (d_gated * y * (sig * (1.0 + z * (1.0 - sig)))).astype(bf16)
            dy_ref[:, lanes] = d_gated * act

    def store(term, at, within, base):
        if within >= tile:
            start = pl.multiple_of(base + at * tile, 16)
            terms_ref[0, pl.ds(start, tile), :] = term
        else:
            for n in range(tile // within):
                piece = term[n * within : (n + 1) * within]
                terms_ref[at * (tile // within) + n, pl.ds(base, within), :] = piece

    @pl.when(step >= blocks)
    def _():
        i = step - blocks
        lanes = pl.ds(pl.multiple_of(i * tile, LANES), tile)
        store(mm(normed_ref[:, lanes], dz_ref[...], TN).astype(bf16), i, z_rows, 0)
        j = i // parts
        lanes = pl.ds(pl.multiple_of(j * tile, LANES), tile)
        left = gate_ref[:, lanes]
        for k in range(parts):

            @pl.when(i % parts == k)
            def _():
                right = cot_ref[:, k * width : (k + 1) * width]
                store(mm(left, right, TN).astype(bf16), j, tall, z_rows + k * tall)


def run_gate_forward(joined, z_rows, normed, cot, y, gain):
    groups, deep, width = joined.shape
    tokens, n_width = normed.shape
    parts = n_width // width
    tall = (deep - z_rows) // parts
    rows = min(256, tokens)

    def tokens_of(columns):
        return pl.BlockSpec((rows, columns), lambda c: (c, 0))

    return pl.pallas_call(
        functools.partial(gate_forward, groups, z_rows, tall),
        grid=(tokens // rows,),
        in_specs=[tokens_of(n_width), tokens_of(n_width), whole(joined), tokens_of(width), whole(gain)],
        out_specs=[
            tokens_of(width), tokens_of(width), pl.BlockSpec((8, rows), lambda c: (0, c)),
            pl.BlockSpec((groups * z_rows, width), lambda c: (0, 0)),
            pl.BlockSpec((parts, groups * tall, width), lambda c: (0, 0, 0)),
        ],
        out_shape=[
            jax.ShapeDtypeStruct((tokens, width), f32),
            jax.ShapeDtypeStruct((tokens, width), f32),
            jax.ShapeDtypeStruct((8, tokens), f32),
            jax.ShapeDtypeStruct((groups * z_rows, width), bf16),
            jax.ShapeDtypeStruct((parts, groups * tall, width), bf16),
        ],
        name="gate_forward",
    )(normed, cot, joined, y, gain)


def run_gate_backward(groups, z_rows, tall, channels, normed, cot, y, z, d_gn, sums, gain):
    tokens, n_width = normed.shape
    width = y.shape[1]
    parts = n_width // width
    rows = min(256, tokens)
    blocks = tokens // rows
    tile = 3 * LANES
    deep = z_rows + parts * tall

    def tokens_of(columns):
        return pl.BlockSpec((rows, columns), lambda c: (jnp.minimum(c, blocks - 1), 0))

    return pl.pallas_call(
        functools.partial(gate_backward, blocks, tile, z_rows, tall, channels),
        grid=(blocks + n_width // tile,),
        in_specs=[
            whole(normed), whole(cot), tokens_of(width), tokens_of(width), tokens_of(width),
            pl.BlockSpec((8, rows), lambda c: (0, jnp.minimum(c, blocks - 1))), whole(gain),
        ],
        out_specs=[
            pl.BlockSpec((tokens, width), lambda c: (0, 0)),
            pl.BlockSpec((tokens, width), lambda c: (0, 0)),
            tokens_of(width),
            pl.BlockSpec((8, width), lambda c: (0, 0)),
            pl.BlockSpec((groups, deep, width), lambda c: (0, 0, 0)),
        ],
        out_shape=[
            jax.ShapeDtypeStruct((tokens, width), bf16),
            jax.ShapeDtypeStruct((tokens, width), bf16),
            jax.ShapeDtypeStruct((tokens, width), f32),
            jax.ShapeDtypeStruct((8, width), f32),
            jax.ShapeDtypeStruct((groups, deep, width), bf16),
        ],
        name="gate_backward",
    )(normed, cot, y, z, d_gn, sums, gain)


def swapped(block, bit):
    size = lax.axis_size("seq")
    return lax.ppermute(block, "seq", [(i, i ^ bit) for i in range(size)])


def bits_of(size):
    bits, bit = [], 1
    while bit < size:
        bits.append(bit)
        bit *= 2
    return bits


def joined_by(held, bit):
    other = swapped(held, bit)
    upper = (lax.axis_index("seq") & bit) != 0
    both = jnp.where(upper, jnp.stack([other, held], axis=1), jnp.stack([held, other], axis=1))
    return both.reshape((-1,) + both.shape[2:])


def opened(block):
    bits = bits_of(lax.axis_size("seq"))
    return joined_by(block[None], bits[-1]) if bits else block[None]


def gathered(block, held=None):
    held = opened(block) if held is None else held
    for bit in reversed(bits_of(lax.axis_size("seq"))[:-1]):
        held = joined_by(held, bit)
    return held.reshape((-1,) + held.shape[2:])


def scattered(parts, between=lambda held: held):
    index = lax.axis_index("seq")
    size = lax.axis_size("seq")
    rest = parts.shape[1:]
    lead = parts.shape[0]
    held = parts.reshape((size, lead // size) + rest)
    for bit in bits_of(size):
        half = held.reshape((held.shape[0] // 2, 2) + held.shape[1:])
        upper = (index & bit) != 0
        mine = jnp.where(upper, half[:, 1], half[:, 0])
        theirs = jnp.where(upper, half[:, 0], half[:, 1]).astype(bf16)
        held = between(mine.astype(f32) + swapped(theirs, bit).astype(f32))
    return held[0]


def added_over(block, bits):
    for bit in bits:
        block = block + crossed(block, bit)
    return block


def moved_by(block, step):
    count = lax.axis_size("dp")
    route = [(i, i + 2 * step) for i in range(count) if 0 <= i + 2 * step < count]
    return lax.ppermute(block, "dp", route)


def crossed(block, bits):
    return lax.ppermute(block, "dp", [(i, i ^ bits) for i in range(lax.axis_size("dp"))])


def gathered_rows(block, waits, whole_rows):
    count = lax.axis_size("dp")
    length = count // 2
    if not is_small(count):
        return lax.all_gather(block, "dp", axis=0, tiled=True), block
    at = lax.axis_index("dp")
    place, side = at // 2, at % 2
    rows = block.shape[0]

    def put(into, piece, pair, half):
        return lax.dynamic_update_slice(into, piece, ((pair * 2 + half) * rows, 0))

    whole_rows = put(whole_rows, block, place, side)
    other = crossed(block, 1)
    whole_rows = put(whole_rows, other, place, 1 - side)
    up, down, ready = block, block, []
    for hop in range(1, length):
        up, down = after((moved_by(up, 1), moved_by(down, -1)), (other, waits[hop - 1 : hop]))
        ready.append((down, up))
        piece, pair = None, None
        for spot in range(length):
            near = min(spot, length - 1 - spot)
            if hop <= 2 * near:
                away, from_below = (hop + 1) // 2, hop % 2 == 0
            else:
                away, from_below = hop - near, spot > length - 1 - spot
            chosen = ready[away - 1][1 if from_below else 0]
            source = spot - away if from_below else spot + away
            here = place == spot
            piece = chosen if piece is None else jnp.where(here, chosen, piece)
            pair = source if pair is None else jnp.where(here, source, pair)
        whole_rows = put(whole_rows, piece, pair, side)
        other = crossed(piece, 1)
        whole_rows = put(whole_rows, other, pair, 1 - side)
    return whole_rows, ready[min(1, length - 2)]


def is_small(count):
    return count <= 8 and count & (count - 1) == 0


def halved_rows(term):
    count = lax.axis_size("dp")
    if not is_small(count):
        return term
    at = lax.axis_index("dp")
    pairs = term.reshape(count // 2, 2, -1, term.shape[1])

    def side(which):
        return lax.dynamic_index_in_dim(pairs, which, 1, keepdims=False)

    came = crossed(side((at & 1) ^ 1), 1)
    return (side(at & 1).astype(f32) + came.astype(f32)).astype(bf16)


def shared_rows(lines):
    count = lax.axis_size("dp")
    if not is_small(count):
        return [lax.psum_scatter(lines, "dp", scatter_dimension=0, tiled=True)]
    at = lax.axis_index("dp")

    def part(owner):
        return lax.dynamic_index_in_dim(lines, owner // 2, 0, keepdims=False)

    return [part(at)] + [crossed(part(at ^ bits), bits) for bits in range(2, count, 2)]


def after(value, other):
    return lax.optimization_barrier((value, other))[0]


def turned(blocks):
    size = lax.axis_size("seq")
    index = lax.axis_index("seq")
    if size & (size - 1):
        return lax.all_to_all(blocks, "seq", 0, 0, tiled=True)
    out = blocks
    for bits in range(1, size):
        piece = lax.dynamic_slice_in_dim(blocks, index ^ bits, 1, 0)
        piece = lax.ppermute(piece, "seq", [(i, i ^ bits) for i in range(size)])
        out = lax.dynamic_update_slice_in_dim(out, piece, index ^ bits, 0)
    return out


def folded(rows, lead, width):
    cut = rows.reshape(lead, rows.shape[0] // lead, rows.shape[1] // width, width)
    cut = cut.transpose(0, 2, 1, 3).reshape(lead, -1, width)
    return cut[0] if lead == 1 else cut


def unfolded(pieces, width):
    lead, stacked, narrow = pieces.shape
    cut = pieces.reshape(lead, width // narrow, stacked * narrow // width, narrow)
    return cut.transpose(0, 2, 1, 3).reshape(-1, width)


def exchanged(parts):
    size = lax.axis_size("seq")
    index = lax.axis_index("seq")
    held = parts.reshape((size, -1) + parts.shape[1:])

    def part(owner):
        return lax.dynamic_index_in_dim(held, owner, 0, keepdims=False)

    came = [
        lax.ppermute(part(index ^ bits).astype(bf16), "seq", [(i, i ^ bits) for i in range(size)])
        for bits in range(1, size)
    ]
    return sum([piece.astype(f32) for piece in came], part(index))


def by_rows(array):
    return with_layout_constraint(array, Layout(major_to_minor=(0, 1)))


def padded(rows, width):
    return jnp.pad(rows, ((0, 0), (0, width - rows.shape[1])))


def shards(
    hidden, segments, cotangent, norm_gain, in_weight, conv_weight, conv_bias, step_bias, log_rate,
    skip_gain, gate_gain, out_weight,
):
    n_seqs, block, n_width = hidden.shape
    size = lax.axis_size("seq")
    groups = lax.axis_size("dp")
    index = lax.axis_index("seq")
    tokens = size * block
    n_inner = gate_gain.shape[0]
    n_heads = step_bias.shape[0]
    n_taps = conv_weight.shape[0]
    n_mixed = conv_bias.shape[0]
    n_state = (n_mixed - n_inner) // 2
    head = n_inner // n_heads
    own_inner = n_inner // size
    own_heads = n_heads // size
    own_bc = 2 * n_state // size
    q = min(128, block)
    in_rows = in_weight.shape[0]

    in_low = in_weight.astype(bf16)
    runs = 2 if groups % 2 == 0 else 1

    def dealt(columns):
        cut = columns.reshape(columns.shape[0], runs, size, -1)
        return cut.transpose(0, 2, 1, 3).reshape(columns.shape[0], size, -1)

    def undealt(columns):
        cut = columns.reshape(columns.shape[0], size, runs, -1)
        return cut.transpose(0, 2, 1, 3).reshape(columns.shape[0], -1)

    def own_columns(columns):
        wide = columns.shape[1] // runs
        narrow = wide // size
        starts = [run * wide + index * narrow for run in range(runs)]
        cut = [lax.dynamic_slice_in_dim(columns, start, narrow, 1) for start in starts]
        return jnp.concatenate(cut, axis=1)

    z_cols = dealt(in_low[:, :n_inner])
    x_cols = dealt(in_low[:, n_inner : 2 * n_inner])
    bc_cols = in_low[:, 2 * n_inner : n_inner + n_mixed].reshape(in_rows, size, own_bc)
    dt_cols = dealt(in_low[:, n_inner + n_mixed :])
    gap = jnp.zeros((in_rows, size, LANES - own_heads - own_bc), bf16)
    laid = jnp.concatenate([x_cols, dt_cols, gap, bc_cols, z_cols], axis=2).transpose(1, 0, 2)
    mine = lax.all_to_all(laid, "seq", 0, 0, tiled=True)
    flat = hidden.reshape(block, n_width).astype(f32)
    inv = lax.rsqrt(jnp.mean(flat * flat, axis=-1, keepdims=True) + epsilon)
    unit = flat * inv
    normed_own = (unit * norm_gain).astype(bf16)
    docs = gathered(segments).reshape(tokens).astype(f32)
    half = groups // runs
    order = []
    for f in range(groups * size):
        run, owner, spot = f // (half * size), f // half % size, f % half
        order.append((f, (run * half + spot) * size + owner))
    back = [(b, a) for a, b in order]
    out_moved = lax.ppermute(out_weight.astype(bf16), ("dp", "seq"), order)
    channels = [conv_weight[:, :n_inner], conv_bias[None, :n_inner], gate_gain[None]]
    channels = own_columns(jnp.concatenate(channels, axis=0))
    conv_x, bias_x, gain = channels[:n_taps], channels[n_taps : n_taps + 1], channels[n_taps + 1 :]
    heads = own_columns(jnp.stack([step_bias, jnp.exp(log_rate), skip_gain]))
    sb, rate = padded(heads[0:1], LANES), padded(heads[1:2], LANES)
    skip = jnp.repeat(heads[2:3], head, axis=1)
    dcol = jnp.broadcast_to(docs[:, None], (tokens, LANES))
    drow = jnp.broadcast_to(docs[None, :], (8, tokens))
    early = (docs, out_moved, conv_x, bias_x, gain, sb, rate, skip, dcol, drow)
    n_first = own_inner + LANES
    cleared = jnp.zeros((groups * size * in_rows, n_first), bf16)
    mine, normed_own, cleared = lax.optimization_barrier((after(mine, early), normed_own, cleared))
    mine = mine.reshape(size * in_rows, -1)
    n_first = own_inner + LANES
    cot_own = cotangent.reshape(block, n_width)
    normed_held = opened(normed_own)
    cot_held = opened(after(cot_own, mine))
    w_first, hopped = gathered_rows(mine[:, :n_first], [normed_held, cot_held], cleared)
    z_block = jnp.concatenate([mine[:, n_first:], folded(out_moved, 1, own_inner)], axis=0)

    normed = gathered(normed_own, normed_held)
    joined = lax.all_gather(after(z_block, hopped), "dp", axis=0, tiled=True).reshape(groups, -1, own_inner)
    z_rows = size * in_rows
    cot = gathered(cot_own, cot_held)

    def own_part(vector, parts):
        return lax.dynamic_slice_in_dim(vector, index * parts, parts, vector.ndim - 1)

    w_x, w_small = w_first[:, :own_inner], w_first[:, own_inner:]
    small = mm(normed, w_small, NN)
    x_in = mm(normed, w_x, NN).astype(bf16)
    conv_bc = own_part(conv_weight[:, n_inner:], own_bc)
    bias_bc = own_part(conv_bias[None, n_inner:], own_bc)

    head_lanes = jnp.arange(LANES) < own_heads
    bc_in = small[:, LANES - own_bc :].astype(bf16).astype(f32)
    small_dt = jnp.where(head_lanes, small, 0.0)

    def earlier(rows, lag):
        return jnp.pad(rows, ((lag, 0), (0, 0)))[:tokens]

    def later(rows, lag):
        return jnp.pad(rows, ((0, lag), (0, 0)))[lag:]

    same = [None] + [
        jnp.where(jnp.pad(docs, (lag, 0), constant_values=-1.0)[:tokens] == docs, 1.0, 0.0)[:, None]
        for lag in range(1, n_taps)
    ]
    bc_conv = bias_bc + conv_bc[0:1] * bc_in
    for lag in range(1, n_taps):
        bc_conv = bc_conv + conv_bc[lag : lag + 1] * earlier(bc_in, lag) * same[lag]
    bc_sig = jax.nn.sigmoid(bc_conv)
    bct = gathered(by_rows((bc_conv * bc_sig).astype(bf16).T))

    y, states = run_forward(
        q, x_in, small_dt, bct, dcol, drow, conv_x, bias_x, sb, rate, skip, head
    )

    out_rows = own_inner // groups
    tiled = z_rows % 16 == 0 and out_rows % 16 == 0
    if tiled:
        lead, deep, tall, gate_in = groups, z_rows, out_rows, joined
    else:
        lead, deep, tall = 1, groups * z_rows, own_inner
        w_out = unfolded(joined[:, z_rows:], n_width)
        gate_in = [joined[:, :z_rows].reshape(-1, own_inner), folded(w_out, 1, own_inner)]
        gate_in = jnp.concatenate(gate_in, axis=0)[None]
    z, d_gn, sums, w_z, w_out = run_gate_forward(gate_in, deep, normed, cot, y, gain)
    w_out = jnp.concatenate(list(w_out), axis=1)
    sums = lax.psum(sums[:2], "seq")
    sums = jnp.pad(sums, ((0, 6), (0, 0)))
    gate_low, d_z, d_y, d_gain, terms = run_gate_backward(
        lead, deep, tall, n_inner, normed, cot, y, z, d_gn, sums, gain
    )
    d_gain = d_gain[0]
    if not tiled:
        z_term = terms[0, :deep].reshape(groups, z_rows, own_inner)
        out_term = terms[0, deep:].reshape(n_width // own_inner, groups, out_rows, own_inner)
        out_term = out_term.transpose(1, 0, 2, 3).reshape(groups, -1, own_inner)
        terms = jnp.concatenate([z_term, out_term], axis=1)
    terms = terms.reshape(-1, own_inner)
    parts = lax.psum_scatter(terms, "dp", scatter_dimension=0, tiled=True)

    d_x, d_dt, d_bct, d_conv_x, d_heads = run_backward(
        q, x_in, small_dt, bct, dcol, drow, conv_x, bias_x, sb, rate, skip, d_y, states, head
    )
    x_term = mm(normed, d_x, TN).astype(bf16)
    x_term, d_bct = lax.optimization_barrier((x_term, d_bct))
    x_lines = halved_rows(x_term)
    d_bc = by_rows(exchanged(d_bct)).T
    d_bcc = d_bc * (bc_sig * (1.0 + bc_conv * (1.0 - bc_sig)))
    d_bc_in = conv_bc[0:1] * d_bcc
    w_sums = [jnp.sum(d_bcc * bc_in, axis=0)]
    for lag in range(1, n_taps):
        held = d_bcc * same[lag]
        d_bc_in = d_bc_in + conv_bc[lag : lag + 1] * later(held, lag)
        w_sums.append(jnp.sum(held * earlier(bc_in, lag), axis=0))
    w_sums.append(jnp.sum(d_bcc, axis=0))
    d_small = jnp.concatenate([d_dt[:, : LANES - own_bc], d_bc_in], axis=1).astype(bf16)
    d_first = jnp.concatenate([d_x, d_small], axis=1)
    small_lines = halved_rows(mm(normed, d_small, TN).astype(bf16))
    branch = scattered(mm(after(gate_low, d_bc), w_out, NN).astype(bf16))
    result = (flat + branch).reshape(n_seqs, block, n_width).astype(bf16)
    d_normed = mm(d_first, w_first, NT) + mm(d_z, w_z, NT)
    d_norm_gain = jnp.sum(d_normed * normed.astype(f32), axis=0) / norm_gain
    d_skip = jnp.sum(d_conv_x[n_taps + 1].reshape(own_heads, head), axis=1)
    packed = jnp.concatenate(
        [
            d_conv_x[: n_taps + 1].reshape(-1),
            jnp.stack(w_sums).reshape(-1),
            d_gain,
            d_heads[0, :own_heads],
            d_heads[1, :own_heads],
            d_skip,
            d_norm_gain,
        ]
    )
    lines = jnp.concatenate([x_lines, small_lines], axis=-1)
    packed = added_over(packed, reversed(bits_of(groups)[1:]))
    lines, packed = lax.optimization_barrier((lines, packed))
    shares = shared_rows(lines)
    packed = gathered(added_over(packed, bits_of(groups)[:1])[None])
    parts, result = lax.optimization_barrier((after(parts, lines), result))
    d_norm = after(d_normed.astype(bf16), parts)
    d_norm = lax.psum_scatter(d_norm, "seq", scatter_dimension=0, tiled=True).astype(f32)

    def own_rows(part):
        return turned(part.reshape(size, in_rows, -1))

    def placed(rows, cuts=runs):
        wide = rows.shape[2] // cuts
        spots = [(run * wide, owner) for run in range(cuts) for owner in range(size)]
        pieces = [rows[owner, :, at : at + wide] for at, owner in spots]
        return jnp.concatenate(pieces, axis=1).astype(f32)

    out_part = unfolded(parts[None, z_rows:], n_width)
    d_out_weight = lax.ppermute(out_part, ("dp", "seq"), back).astype(f32)
    in_z = placed(own_rows(parts[:z_rows]))
    shares, in_z, d_out_weight = lax.optimization_barrier((shares, in_z, d_out_weight))
    first_part = sum(share.astype(f32) for share in shares)
    in_first = own_rows(first_part.astype(bf16))
    lifted = d_norm * norm_gain
    d_flat = inv * lifted - flat * (
        inv * inv * inv * jnp.mean(lifted * flat, axis=-1, keepdims=True)
    )
    d_hidden = (cot_own.astype(f32) + d_flat).reshape(n_seqs, block, n_width)
    in_first, d_hidden = lax.optimization_barrier((in_first, d_hidden))
    d_in_weight = jnp.concatenate(
        [
            in_z,
            placed(in_first[:, :, :own_inner]),
            placed(in_first[:, :, n_first - own_bc :], 1),
            placed(in_first[:, :, own_inner : own_inner + own_heads]),
        ],
        axis=1,
    )

    at = 0

    def take(count):
        nonlocal at
        at += count
        return packed[:, at - count : at]

    got_x = take((n_taps + 1) * own_inner).reshape(size, n_taps + 1, own_inner)
    got_bc = take((n_taps + 1) * own_bc).reshape(size, n_taps + 1, own_bc)
    got_x = undealt(got_x.transpose(1, 0, 2))
    got_bc = got_bc.transpose(1, 0, 2).reshape(n_taps + 1, 2 * n_state)
    conv_all = jnp.concatenate([got_x, got_bc], axis=1)
    d_gate_gain = undealt(take(own_inner)[None])[0]
    d_step_bias = undealt(take(own_heads)[None])[0]
    d_log_rate = undealt(take(own_heads)[None])[0]
    d_skip_gain = undealt(take(own_heads)[None])[0]
    d_norm_all = jnp.sum(take(n_width), axis=0)
    return (
        result,
        d_hidden,
        d_norm_all,
        d_in_weight,
        conv_all[:n_taps],
        conv_all[n_taps],
        d_step_bias,
        d_log_rate,
        d_skip_gain,
        d_gate_gain,
        d_out_weight,
    )


def solution(mesh):
    tokens = P("dp", "seq", None)
    rows = P(("dp", "seq"), None)
    return jax.shard_map(
        shards,
        mesh=mesh,
        in_specs=(tokens, P("dp", "seq"), tokens, P(), rows, P(), P(), P(), P(), P(), P(), rows),
        out_specs=(tokens, tokens, P(), rows, P(), P(), P(), P(), P(), P(), rows),
        check_vma=False,
    )
```

```python
import functools

import jax
import jax.numpy as jnp
from jax import lax
from jax.experimental import pallas as pl
from jax.experimental.layout import Layout, with_layout_constraint
from jax.experimental.pallas import tpu as pltpu
from jax.sharding import PartitionSpec as P

epsilon = 1e-05
highest = lax.Precision.HIGHEST
f32 = jnp.float32
bf16 = jnp.bfloat16
LANES = 128
HALO = 16
NEG = -1e30


def mm(a, b, dims, out=f32):
    return lax.dot_general(a, b, (dims, ((), ())), preferred_element_type=out)


NN = ((1,), (0,))
NT = ((1,), (1,))
TN = ((0,), (0,))


def exact(a, b, dims):
    return lax.dot_general(a, b, (dims, ((), ())), precision=highest, preferred_element_type=f32)


def softplus(v):
    return jnp.maximum(v, 0.0) + jnp.log1p(jnp.exp(-jnp.abs(v)))


def sigmoid(v):
    return 1.0 / (1.0 + jnp.exp(-v))


def lane_iota(shape):
    return lax.broadcasted_iota(jnp.int32, shape, len(shape) - 1)


def spread(columns, first, second, wide):
    rows = columns.shape[0]
    left = jnp.broadcast_to(columns[:, first : first + 1], (rows, LANES))
    right = jnp.broadcast_to(columns[:, second : second + 1], (rows, LANES))
    return jnp.where(wide, left, right)


def step_parts(raw, rate, q):
    row = lax.broadcasted_iota(jnp.int32, (q, q), 0)
    col = lax.broadcasted_iota(jnp.int32, (q, q), 1)
    tri = jnp.where(row >= col, 1.0, 0.0).astype(f32)
    step = softplus(raw)
    decay = -step * rate
    total = exact(tri, decay, NN)
    return step, decay, total, tri, row >= col


def convolve(ext, docs_ext, own, weights, bias, lanes, q, taps):
    running = bias + weights[0:1, lanes] * ext[pl.ds(HALO, q), lanes]
    for lag in range(1, taps):
        same = jnp.where(docs_ext[pl.ds(HALO - lag, q), :] == own, 1.0, 0.0)
        running = running + weights[lag : lag + 1, lanes] * ext[pl.ds(HALO - lag, q), lanes] * same
    return running


def scan_forward(
    q, taps, pairs, head,
    x_ref, small_ref, bct_ref, dcol_ref, drow_ref, w_ref, b_ref, sb_ref, rate_ref, skip_ref,
    y_ref, states_ref,
    state, ext, docs_ext, xs, xt, last_doc,
):
    c = pl.program_id(0)
    n = bct_ref.shape[0] // 2

    @pl.when(c == 0)
    def _():
        state[...] = jnp.zeros_like(state)
        ext[pl.ds(0, HALO), :] = jnp.zeros((HALO, ext.shape[1]), f32)
        docs_ext[pl.ds(0, HALO), :] = jnp.full((HALO, LANES), -1.0, f32)
        last_doc[...] = jnp.full(last_doc.shape, -1.0, f32)

    own = dcol_ref[...]
    ext[pl.ds(HALO, q), :] = x_ref[...].astype(f32)
    docs_ext[pl.ds(HALO, q), :] = own
    step, _, cum, _, causal = step_parts(small_ref[...] + sb_ref[...], rate_ref[...], q)
    step_t = step.T
    cum_t = cum.T
    end = cum[q - 1 : q, :]
    id_in = last_doc[0:1, :]
    final = own[q - 1 : q, :]
    linked = jnp.where(final == id_in, 1.0, 0.0)
    fade = linked * jnp.exp(end)
    entering = jnp.where(own == id_in, 1.0, 0.0) * jnp.exp(cum)
    to_end = jnp.where(own == final, 1.0, 0.0) * jnp.exp(end - cum) * step
    same_doc = jnp.broadcast_to(own[:, 0:1], (q, q)) == jnp.broadcast_to(drow_ref[0:1, :], (q, q))
    hide = jnp.where(jnp.logical_and(causal, same_doc), 0.0, NEG)
    bt = bct_ref[0:n, :]
    ct = bct_ref[n : 2 * n, :]
    scores = mm(ct, bt, TN)
    states_ref[0] = state[...]
    old = state[...].astype(bf16)
    wide = lane_iota((q, LANES)) < head
    wide_row = lane_iota((1, LANES)) < head
    for k in range(pairs):
        lanes = slice(k * LANES, (k + 1) * LANES)
        h0, h1 = 2 * k, 2 * k + 1
        conv = convolve(ext, docs_ext, own, w_ref, b_ref[:, lanes], lanes, q, taps)
        x = conv * sigmoid(conv)
        xd = x * spread(step, h0, h1, wide)
        xt[:, lanes] = (x * spread(to_end, h0, h1, wide)).astype(bf16)
        mats = []
        for h in (h0, h1):
            gap = cum[:, h : h + 1] - cum_t[h : h + 1, :] + hide
            mats.append((jnp.exp(gap) * scores).astype(bf16))
        out = mm(mats[0], jnp.where(wide, xd, 0.0).astype(bf16), NN)
        out = out + mm(mats[1], jnp.where(wide, 0.0, xd).astype(bf16), NN)
        out = out + mm(ct, old[:, lanes], TN) * spread(entering, h0, h1, wide)
        y_ref[:, lanes] = out + skip_ref[:, lanes] * x
    update = mm(bt, xt[...], NN)
    for k in range(pairs):
        lanes = slice(k * LANES, (k + 1) * LANES)
        state[:, lanes] = state[:, lanes] * spread(fade, 2 * k, 2 * k + 1, wide_row) + update[:, lanes]
    ext[pl.ds(0, HALO), :] = ext[pl.ds(q, HALO), :]
    docs_ext[pl.ds(0, HALO), :] = docs_ext[pl.ds(q, HALO), :]
    last_doc[...] = jnp.broadcast_to(final, last_doc.shape)


def scan_backward(
    q, taps, pairs, head, chunks,
    x_ref, xp_ref, small_ref, bct_ref, dcol_ref, dcolp_ref, drow_ref, w_ref, b_ref, sb_ref, rate_ref,
    skip_ref, dy_ref, states_ref,
    dx_ref, dsmall_ref, dbct_ref, dconv_ref, dhead_ref,
    dstate, ext, docs_ext, dcv, docs_after, dye, xt, col_t,
):
    step_at = pl.program_id(0)
    c = chunks - 1 - step_at
    n = bct_ref.shape[0] // 2
    width = x_ref.shape[1]

    @pl.when(step_at == 0)
    def _():
        dstate[...] = jnp.zeros_like(dstate)
        dcv[pl.ds(q, HALO), :] = jnp.zeros((HALO, width), f32)
        docs_after[pl.ds(q, HALO), :] = jnp.full((HALO, LANES), -1.0, f32)
        dconv_ref[...] = jnp.zeros_like(dconv_ref)
        dhead_ref[...] = jnp.zeros_like(dhead_ref)
        col_t[...] = jnp.zeros_like(col_t)

    first = c == 0
    own = dcol_ref[...]
    before = jnp.where(first, -1.0, dcolp_ref[...])
    ext[pl.ds(0, HALO), :] = xp_ref[...].astype(f32)
    ext[pl.ds(HALO, q), :] = x_ref[...].astype(f32)
    docs_ext[pl.ds(0, HALO), :] = before
    docs_ext[pl.ds(HALO, q), :] = own
    docs_after[pl.ds(0, q), :] = own
    raw = small_ref[...] + sb_ref[...]
    rate = rate_ref[...]
    step, decay, cum, tri, causal = step_parts(raw, rate, q)
    step_t = step.T
    cum_t = cum.T
    end = cum[q - 1 : q, :]
    id_in = before[HALO - 1 : HALO, :]
    final = own[q - 1 : q, :]
    linked = jnp.where(final == id_in, 1.0, 0.0)
    fade = linked * jnp.exp(end)
    entering = jnp.where(own == id_in, 1.0, 0.0) * jnp.exp(cum)
    tail = jnp.where(own == final, 1.0, 0.0) * jnp.exp(end - cum)
    to_end = tail * step
    same_doc = jnp.broadcast_to(own[:, 0:1], (q, q)) == jnp.broadcast_to(drow_ref[0:1, :], (q, q))
    hide = jnp.where(jnp.logical_and(causal, same_doc), 0.0, NEG)
    bt = bct_ref[0:n, :]
    ct = bct_ref[n : 2 * n, :]
    scores = mm(ct, bt, TN)
    old = states_ref[0].astype(bf16)
    after = dstate[...].astype(bf16)
    wide = lane_iota((q, LANES)) < head
    wide_row = lane_iota((1, LANES)) < head
    lane = lane_iota((q, LANES))
    d_scores = jnp.zeros((q, q), f32)
    rows = jnp.zeros((q, LANES), f32)
    d_enter = jnp.zeros((q, LANES), f32)
    d_toend = jnp.zeros((q, LANES), f32)
    d_fade = jnp.zeros((8, LANES), f32)
    part = lax.broadcasted_iota(jnp.int32, (LANES, LANES), 0) // head
    to = lane_iota((LANES, LANES))
    for k in range(pairs):
        lanes = slice(k * LANES, (k + 1) * LANES)
        h0, h1 = 2 * k, 2 * k + 1
        pick = jnp.where(part + 2 * k == to, 1.0, 0.0)
        conv = convolve(ext, docs_ext, own, w_ref, b_ref[:, lanes], lanes, q, taps)
        sig = sigmoid(conv)
        x = conv * sig
        xb = x.astype(bf16)
        dy = dy_ref[:, lanes]
        halves = (jnp.where(wide, dy, 0.0).astype(bf16), jnp.where(wide, 0.0, dy).astype(bf16))
        dxd = jnp.zeros((q, LANES), f32)
        for h, half in ((h0, halves[0]), (h1, halves[1])):
            inner = mm(half, xb, NT)
            keep = jnp.exp(cum[:, h : h + 1] - cum_t[h : h + 1, :] + hide)
            grown = keep * inner
            mat = keep * scores
            dt = step_t[h : h + 1, :]
            g = grown * scores
            d_scores = d_scores + grown * dt
            rows = jnp.where(lane == h, jnp.sum(g * dt, axis=1, keepdims=True), rows)
            col_t[h : h + 1, :] = jnp.sum(g, axis=0, keepdims=True)
            dxd = dxd + mm(mat.astype(bf16), half, TN)
        v = mm(bt, after[:, lanes], TN)
        u = mm(ct, old[:, lanes], TN)
        enter_k = spread(entering, h0, h1, wide)
        end_k = spread(to_end, h0, h1, wide)
        d_enter = d_enter + exact(dy * u, pick, NN)
        d_toend = d_toend + exact(x * v, pick, NN)
        hh = jnp.sum(dstate[:, lanes] * states_ref[0, :, lanes], axis=0, keepdims=True)
        d_fade = d_fade + exact(jnp.broadcast_to(hh, (8, LANES)), pick, NN)
        dye[:, lanes] = (dy * enter_k).astype(bf16)
        xt[:, lanes] = (x * end_k).astype(bf16)
        dx = dxd * spread(step, h0, h1, wide) + end_k * v + skip_ref[:, lanes] * dy
        dconv = dx * (sig * (1.0 + conv * (1.0 - sig)))
        dcv[pl.ds(0, q), lanes] = dconv
        sums = [jnp.sum(dconv * ext[pl.ds(HALO, q), lanes], axis=0, keepdims=True)]
        dxin = w_ref[0:1, lanes] * dconv
        for lag in range(1, taps):
            same = jnp.where(docs_ext[pl.ds(HALO - lag, q), :] == own, 1.0, 0.0)
            sums.append(jnp.sum(dconv * same * ext[pl.ds(HALO - lag, q), lanes], axis=0, keepdims=True))
            follow = jnp.where(docs_after[pl.ds(lag, q), :] == own, 1.0, 0.0)
            dxin = dxin + w_ref[lag : lag + 1, lanes] * dcv[pl.ds(lag, q), lanes] * follow
        sums.append(jnp.sum(dconv, axis=0, keepdims=True))
        sums.append(jnp.sum(dy * x, axis=0, keepdims=True))
        dx_ref[:, lanes] = dxin.astype(bf16)
        for i, s in enumerate(sums):
            dconv_ref[i : i + 1, lanes] = dconv_ref[i : i + 1, lanes] + s
    dsb = d_scores.astype(bf16)
    dbct_ref[0:n, :] = mm(ct, dsb, NN) + mm(after, xt[...], NT)
    dbct_ref[n : 2 * n, :] = mm(bt, dsb, NT) + mm(old, dye[...], NT)
    new = mm(ct, dye[...], NN)
    for k in range(pairs):
        lanes = slice(k * LANES, (k + 1) * LANES)
        dstate[:, lanes] = dstate[:, lanes] * spread(fade, 2 * k, 2 * k + 1, wide_row) + new[:, lanes]
    cols = col_t[...].T
    pulled = d_toend * to_end
    at_end = jnp.sum(pulled, axis=0, keepdims=True) + fade * d_fade[0:1, :]
    d_cum = rows - step * cols + d_enter * entering - pulled
    last_row = lax.broadcasted_iota(jnp.int32, (q, LANES), 0) == q - 1
    d_cum = d_cum + jnp.where(last_row, at_end, 0.0)
    d_decay = exact(tri, d_cum, TN)
    d_step = cols + d_toend * tail - rate * d_decay
    d_raw = d_step * sigmoid(raw)
    dsmall_ref[...] = d_raw
    dhead_ref[0:1, :] = dhead_ref[0:1, :] + jnp.sum(d_raw, axis=0, keepdims=True)
    dhead_ref[1:2, :] = dhead_ref[1:2, :] + jnp.sum(d_decay * decay, axis=0, keepdims=True)
    dcv[pl.ds(q, HALO), :] = dcv[pl.ds(0, HALO), :]
    docs_after[pl.ds(q, HALO), :] = docs_after[pl.ds(0, HALO), :]


def whole(array):
    return pl.BlockSpec(array.shape, lambda c: (0,) * array.ndim)


def run_forward(q, x_in, small, bct, dcol, drow, conv_w, conv_b, sb, rate, skip, head):
    tokens, width = x_in.shape
    n = bct.shape[0] // 2
    chunks = tokens // q
    pairs = width // LANES
    taps = conv_w.shape[0]
    return pl.pallas_call(
        functools.partial(scan_forward, q, taps, pairs, head),
        grid=(chunks,),
        in_specs=[
            pl.BlockSpec((q, width), lambda c: (c, 0)),
            pl.BlockSpec((q, LANES), lambda c: (c, 0)),
            pl.BlockSpec((2 * n, q), lambda c: (0, c)),
            pl.BlockSpec((q, LANES), lambda c: (c, 0)),
            pl.BlockSpec((8, q), lambda c: (0, c)),
            whole(conv_w), whole(conv_b), whole(sb), whole(rate), whole(skip),
        ],
        out_specs=[
            pl.BlockSpec((q, width), lambda c: (c, 0)),
            pl.BlockSpec((1, n, width), lambda c: (c, 0, 0)),
        ],
        out_shape=[
            jax.ShapeDtypeStruct((tokens, width), f32),
            jax.ShapeDtypeStruct((chunks, n, width), f32),
        ],
        scratch_shapes=[
            pltpu.VMEM((n, width), f32),
            pltpu.VMEM((HALO + q, width), f32),
            pltpu.VMEM((HALO + q, LANES), f32),
            pltpu.VMEM((8, LANES), f32),
            pltpu.VMEM((q, width), bf16),
            pltpu.VMEM((8, LANES), f32),
        ],
        name="scan_forward",
    )(x_in, small, bct, dcol, drow, conv_w, conv_b, sb, rate, skip)


def run_backward(q, x_in, small, bct, dcol, drow, conv_w, conv_b, sb, rate, skip, dy, states, head):
    tokens, width = x_in.shape
    n = bct.shape[0] // 2
    chunks = tokens // q
    pairs = width // LANES
    taps = conv_w.shape[0]
    per = q // HALO

    def at(c):
        return chunks - 1 - c

    def prior(c):
        return jnp.maximum((chunks - 1 - c) * per - 1, 0)

    return pl.pallas_call(
        functools.partial(scan_backward, q, taps, pairs, head, chunks),
        grid=(chunks,),
        in_specs=[
            pl.BlockSpec((q, width), lambda c: (at(c), 0)),
            pl.BlockSpec((HALO, width), lambda c: (prior(c), 0)),
            pl.BlockSpec((q, LANES), lambda c: (at(c), 0)),
            pl.BlockSpec((2 * n, q), lambda c: (0, at(c))),
            pl.BlockSpec((q, LANES), lambda c: (at(c), 0)),
            pl.BlockSpec((HALO, LANES), lambda c: (prior(c), 0)),
            pl.BlockSpec((8, q), lambda c: (0, at(c))),
            whole(conv_w), whole(conv_b), whole(sb), whole(rate), whole(skip),
            pl.BlockSpec((q, width), lambda c: (at(c), 0)),
            pl.BlockSpec((1, n, width), lambda c: (at(c), 0, 0)),
        ],
        out_specs=[
            pl.BlockSpec((q, width), lambda c: (at(c), 0)),
            pl.BlockSpec((q, LANES), lambda c: (at(c), 0)),
            pl.BlockSpec((2 * n, q), lambda c: (0, at(c))),
            pl.BlockSpec((8, width), lambda c: (0, 0)),
            pl.BlockSpec((8, LANES), lambda c: (0, 0)),
        ],
        out_shape=[
            jax.ShapeDtypeStruct((tokens, width), bf16),
            jax.ShapeDtypeStruct((tokens, LANES), f32),
            jax.ShapeDtypeStruct((2 * n, tokens), f32),
            jax.ShapeDtypeStruct((8, width), f32),
            jax.ShapeDtypeStruct((8, LANES), f32),
        ],
        scratch_shapes=[
            pltpu.VMEM((n, width), f32),
            pltpu.VMEM((HALO + q, width), f32),
            pltpu.VMEM((HALO + q, LANES), f32),
            pltpu.VMEM((q + HALO, width), f32),
            pltpu.VMEM((q + HALO, LANES), f32),
            pltpu.VMEM((q, width), bf16),
            pltpu.VMEM((q, width), bf16),
            pltpu.VMEM((LANES, q), f32),
        ],
        name="scan_backward",
    )(x_in, x_in, small, bct, dcol, dcol, drow, conv_w, conv_b, sb, rate, skip, dy, states)


def gate_forward(
    groups, z_rows, tall,
    normed_ref, cot_ref, joined_ref, y_ref, gain_ref, z_ref, dgn_ref, sums_ref, wz, wo,
):
    parts, held, width = wo.shape

    @pl.when(pl.program_id(0) == 0)
    def _():
        for g in range(groups):
            wz[pl.ds(g * z_rows, z_rows), :] = joined_ref[g, pl.ds(0, z_rows), :]
            for k in range(parts):
                wo[k, pl.ds(g * tall, tall), :] = joined_ref[g, pl.ds(z_rows + k * tall, tall), :]

    z = mm(normed_ref[...], wz[...], NN)
    d_gn = mm(cot_ref[:, 0:width], wo[0], NT)
    for k in range(1, parts):
        d_gn = d_gn + mm(cot_ref[:, k * width : (k + 1) * width], wo[k], NT)
    z_ref[...] = z
    dgn_ref[...] = d_gn
    gated = y_ref[...] * (z * sigmoid(z))
    square = jnp.sum(gated * gated, axis=1, keepdims=True)
    cross = jnp.sum(d_gn * gain_ref[...] * gated, axis=1, keepdims=True)
    lane = lane_iota((square.shape[0], LANES))
    sums_ref[...] = jnp.where(lane == 0, square, jnp.where(lane == 1, cross, 0.0)).T[0:8, :]


def gate_backward(
    blocks, tile, z_rows, tall, channels,
    normed_ref, cot_ref, y_ref, z_ref, dgn_ref, sums_ref, gain_ref,
    gate_ref, dz_ref, dy_ref, dgain_ref, terms_ref,
):
    step = pl.program_id(0)
    rows, width = y_ref.shape
    parts = normed_ref.shape[1] // width

    @pl.when(step == 0)
    def _():
        dgain_ref[...] = jnp.zeros_like(dgain_ref)

    @pl.when(step < blocks)
    def _():
        own = pl.ds(pl.multiple_of(step * rows, rows), rows)
        columns = jnp.concatenate([sums_ref[...], jnp.zeros((LANES - 8, rows), f32)], axis=0).T
        inv = lax.rsqrt(columns[:, 0:1] / channels + epsilon)
        slope = inv * inv * inv * (columns[:, 1:2] / channels)
        for k in range(width // LANES):
            lanes = slice(k * LANES, (k + 1) * LANES)
            y, z, d_gn, gain = y_ref[:, lanes], z_ref[:, lanes], dgn_ref[:, lanes], gain_ref[:, lanes]
            sig = sigmoid(z)
            act = z * sig
            gated = y * act
            scaled = gated * inv
            gate_ref[own, lanes] = (scaled * gain).astype(bf16)
            dgain_ref[0:1, lanes] = dgain_ref[0:1, lanes] + jnp.sum(d_gn * scaled, axis=0, keepdims=True)
            d_gated = inv * (d_gn * gain) - gated * slope
            dz_ref[own, lanes] = (d_gated * y * (sig * (1.0 + z * (1.0 - sig)))).astype(bf16)
            dy_ref[:, lanes] = d_gated * act

    def store(term, at, within, base):
        if within >= tile:
            start = pl.multiple_of(base + at * tile, 16)
            terms_ref[0, pl.ds(start, tile), :] = term
        else:
            for n in range(tile // within):
                piece = term[n * within : (n + 1) * within]
                terms_ref[at * (tile // within) + n, pl.ds(base, within), :] = piece

    @pl.when(step >= blocks)
    def _():
        i = step - blocks
        lanes = pl.ds(pl.multiple_of(i * tile, LANES), tile)
        store(mm(normed_ref[:, lanes], dz_ref[...], TN).astype(bf16), i, z_rows, 0)
        j = i // parts
        lanes = pl.ds(pl.multiple_of(j * tile, LANES), tile)
        left = gate_ref[:, lanes]
        for k in range(parts):

            @pl.when(i % parts == k)
            def _():
                right = cot_ref[:, k * width : (k + 1) * width]
                store(mm(left, right, TN).astype(bf16), j, tall, z_rows + k * tall)


def run_gate_forward(joined, z_rows, normed, cot, y, gain):
    groups, deep, width = joined.shape
    tokens, n_width = normed.shape
    parts = n_width // width
    tall = (deep - z_rows) // parts
    rows = min(256, tokens)

    def tokens_of(columns):
        return pl.BlockSpec((rows, columns), lambda c: (c, 0))

    return pl.pallas_call(
        functools.partial(gate_forward, groups, z_rows, tall),
        grid=(tokens // rows,),
        in_specs=[tokens_of(n_width), tokens_of(n_width), whole(joined), tokens_of(width), whole(gain)],
        out_specs=[
            tokens_of(width), tokens_of(width), pl.BlockSpec((8, rows), lambda c: (0, c)),
            pl.BlockSpec((groups * z_rows, width), lambda c: (0, 0)),
            pl.BlockSpec((parts, groups * tall, width), lambda c: (0, 0, 0)),
        ],
        out_shape=[
            jax.ShapeDtypeStruct((tokens, width), f32),
            jax.ShapeDtypeStruct((tokens, width), f32),
            jax.ShapeDtypeStruct((8, tokens), f32),
            jax.ShapeDtypeStruct((groups * z_rows, width), bf16),
            jax.ShapeDtypeStruct((parts, groups * tall, width), bf16),
        ],
        name="gate_forward",
    )(normed, cot, joined, y, gain)


def run_gate_backward(groups, z_rows, tall, channels, normed, cot, y, z, d_gn, sums, gain):
    tokens, n_width = normed.shape
    width = y.shape[1]
    parts = n_width // width
    rows = min(256, tokens)
    blocks = tokens // rows
    tile = 3 * LANES
    deep = z_rows + parts * tall

    def tokens_of(columns):
        return pl.BlockSpec((rows, columns), lambda c: (jnp.minimum(c, blocks - 1), 0))

    return pl.pallas_call(
        functools.partial(gate_backward, blocks, tile, z_rows, tall, channels),
        grid=(blocks + n_width // tile,),
        in_specs=[
            whole(normed), whole(cot), tokens_of(width), tokens_of(width), tokens_of(width),
            pl.BlockSpec((8, rows), lambda c: (0, jnp.minimum(c, blocks - 1))), whole(gain),
        ],
        out_specs=[
            pl.BlockSpec((tokens, width), lambda c: (0, 0)),
            pl.BlockSpec((tokens, width), lambda c: (0, 0)),
            tokens_of(width),
            pl.BlockSpec((8, width), lambda c: (0, 0)),
            pl.BlockSpec((groups, deep, width), lambda c: (0, 0, 0)),
        ],
        out_shape=[
            jax.ShapeDtypeStruct((tokens, width), bf16),
            jax.ShapeDtypeStruct((tokens, width), bf16),
            jax.ShapeDtypeStruct((tokens, width), f32),
            jax.ShapeDtypeStruct((8, width), f32),
            jax.ShapeDtypeStruct((groups, deep, width), bf16),
        ],
        name="gate_backward",
    )(normed, cot, y, z, d_gn, sums, gain)


def swapped(block, bit):
    size = lax.axis_size("seq")
    return lax.ppermute(block, "seq", [(i, i ^ bit) for i in range(size)])


def bits_of(size):
    bits, bit = [], 1
    while bit < size:
        bits.append(bit)
        bit *= 2
    return bits


def joined_by(held, bit):
    other = swapped(held, bit)
    upper = (lax.axis_index("seq") & bit) != 0
    both = jnp.where(upper, jnp.stack([other, held], axis=1), jnp.stack([held, other], axis=1))
    return both.reshape((-1,) + both.shape[2:])


def opened(block):
    bits = bits_of(lax.axis_size("seq"))
    return joined_by(block[None], bits[-1]) if bits else block[None]


def gathered(block, held=None):
    held = opened(block) if held is None else held
    for bit in reversed(bits_of(lax.axis_size("seq"))[:-1]):
        held = joined_by(held, bit)
    return held.reshape((-1,) + held.shape[2:])


def scattered(parts, between=lambda held: held):
    index = lax.axis_index("seq")
    size = lax.axis_size("seq")
    rest = parts.shape[1:]
    lead = parts.shape[0]
    held = parts.reshape((size, lead // size) + rest)
    for bit in bits_of(size):
        half = held.reshape((held.shape[0] // 2, 2) + held.shape[1:])
        upper = (index & bit) != 0
        mine = jnp.where(upper, half[:, 1], half[:, 0])
        theirs = jnp.where(upper, half[:, 0], half[:, 1]).astype(bf16)
        held = between(mine.astype(f32) + swapped(theirs, bit).astype(f32))
    return held[0]


def added_over(block, bits):
    for bit in bits:
        block = block + crossed(block, bit)
    return block


def moved_by(block, step):
    count = lax.axis_size("dp")
    route = [(i, i + 2 * step) for i in range(count) if 0 <= i + 2 * step < count]
    return lax.ppermute(block, "dp", route)


def crossed(block, bits):
    return lax.ppermute(block, "dp", [(i, i ^ bits) for i in range(lax.axis_size("dp"))])


def gathered_rows(block, waits, whole_rows):
    count = lax.axis_size("dp")
    length = count // 2
    if not is_small(count):
        return lax.all_gather(block, "dp", axis=0, tiled=True), block
    at = lax.axis_index("dp")
    place, side = at // 2, at % 2
    rows = block.shape[0]

    def put(into, piece, pair, half):
        return lax.dynamic_update_slice(into, piece, ((pair * 2 + half) * rows, 0))

    whole_rows = put(whole_rows, block, place, side)
    other = crossed(block, 1)
    whole_rows = put(whole_rows, other, place, 1 - side)
    up, down, ready = block, block, []
    for hop in range(1, length):
        up, down = after((moved_by(up, 1), moved_by(down, -1)), (other, waits[hop - 1 : hop]))
        ready.append((down, up))
        piece, pair = None, None
        for spot in range(length):
            near = min(spot, length - 1 - spot)
            if hop <= 2 * near:
                away, from_below = (hop + 1) // 2, hop % 2 == 0
            else:
                away, from_below = hop - near, spot > length - 1 - spot
            chosen = ready[away - 1][1 if from_below else 0]
            source = spot - away if from_below else spot + away
            here = place == spot
            piece = chosen if piece is None else jnp.where(here, chosen, piece)
            pair = source if pair is None else jnp.where(here, source, pair)
        whole_rows = put(whole_rows, piece, pair, side)
        other = crossed(piece, 1)
        whole_rows = put(whole_rows, other, pair, 1 - side)
    return whole_rows, ready[min(1, length - 2)]


def is_small(count):
    return count <= 8 and count & (count - 1) == 0


def halved_rows(term):
    count = lax.axis_size("dp")
    if not is_small(count):
        return term
    at = lax.axis_index("dp")
    pairs = term.reshape(count // 2, 2, -1, term.shape[1])

    def side(which):
        return lax.dynamic_index_in_dim(pairs, which, 1, keepdims=False)

    came = crossed(side((at & 1) ^ 1), 1)
    return (side(at & 1).astype(f32) + came.astype(f32)).astype(bf16)


def shared_rows(lines):
    count = lax.axis_size("dp")
    if not is_small(count):
        return [lax.psum_scatter(lines, "dp", scatter_dimension=0, tiled=True)]
    at = lax.axis_index("dp")

    def part(owner):
        return lax.dynamic_index_in_dim(lines, owner // 2, 0, keepdims=False)

    return [part(at)] + [crossed(part(at ^ bits), bits) for bits in range(2, count, 2)]


def after(value, other):
    return lax.optimization_barrier((value, other))[0]


def turned(blocks):
    size = lax.axis_size("seq")
    index = lax.axis_index("seq")
    if size & (size - 1):
        return lax.all_to_all(blocks, "seq", 0, 0, tiled=True)
    out = blocks
    for bits in range(1, size):
        piece = lax.dynamic_slice_in_dim(blocks, index ^ bits, 1, 0)
        piece = lax.ppermute(piece, "seq", [(i, i ^ bits) for i in range(size)])
        out = lax.dynamic_update_slice_in_dim(out, piece, index ^ bits, 0)
    return out


def folded(rows, lead, width):
    cut = rows.reshape(lead, rows.shape[0] // lead, rows.shape[1] // width, width)
    cut = cut.transpose(0, 2, 1, 3).reshape(lead, -1, width)
    return cut[0] if lead == 1 else cut


def unfolded(pieces, width):
    lead, stacked, narrow = pieces.shape
    cut = pieces.reshape(lead, width // narrow, stacked * narrow // width, narrow)
    return cut.transpose(0, 2, 1, 3).reshape(-1, width)


def exchanged(parts):
    size = lax.axis_size("seq")
    index = lax.axis_index("seq")
    held = parts.reshape((size, -1) + parts.shape[1:])

    def part(owner):
        return lax.dynamic_index_in_dim(held, owner, 0, keepdims=False)

    came = [
        lax.ppermute(part(index ^ bits).astype(bf16), "seq", [(i, i ^ bits) for i in range(size)])
        for bits in range(1, size)
    ]
    return sum([piece.astype(f32) for piece in came], part(index))


def by_rows(array):
    return with_layout_constraint(array, Layout(major_to_minor=(0, 1)))


def padded(rows, width):
    return jnp.pad(rows, ((0, 0), (0, width - rows.shape[1])))


def shards(
    hidden, segments, cotangent, norm_gain, in_weight, conv_weight, conv_bias, step_bias, log_rate,
    skip_gain, gate_gain, out_weight,
):
    n_seqs, block, n_width = hidden.shape
    size = lax.axis_size("seq")
    groups = lax.axis_size("dp")
    index = lax.axis_index("seq")
    tokens = size * block
    n_inner = gate_gain.shape[0]
    n_heads = step_bias.shape[0]
    n_taps = conv_weight.shape[0]
    n_mixed = conv_bias.shape[0]
    n_state = (n_mixed - n_inner) // 2
    head = n_inner // n_heads
    own_inner = n_inner // size
    own_heads = n_heads // size
    own_bc = 2 * n_state // size
    q = min(128, block)
    in_rows = in_weight.shape[0]

    in_low = in_weight.astype(bf16)
    runs = 2 if groups % 2 == 0 else 1

    def dealt(columns):
        cut = columns.reshape(columns.shape[0], runs, size, -1)
        return cut.transpose(0, 2, 1, 3).reshape(columns.shape[0], size, -1)

    def undealt(columns):
        cut = columns.reshape(columns.shape[0], size, runs, -1)
        return cut.transpose(0, 2, 1, 3).reshape(columns.shape[0], -1)

    def own_columns(columns):
        wide = columns.shape[1] // runs
        narrow = wide // size
        starts = [run * wide + index * narrow for run in range(runs)]
        cut = [lax.dynamic_slice_in_dim(columns, start, narrow, 1) for start in starts]
        return jnp.concatenate(cut, axis=1)

    z_cols = dealt(in_low[:, :n_inner])
    x_cols = dealt(in_low[:, n_inner : 2 * n_inner])
    bc_cols = in_low[:, 2 * n_inner : n_inner + n_mixed].reshape(in_rows, size, own_bc)
    dt_cols = dealt(in_low[:, n_inner + n_mixed :])
    gap = jnp.zeros((in_rows, size, LANES - own_heads - own_bc), bf16)
    laid = jnp.concatenate([x_cols, dt_cols, gap, bc_cols, z_cols], axis=2).transpose(1, 0, 2)
    mine = lax.all_to_all(laid, "seq", 0, 0, tiled=True)
    flat = hidden.reshape(block, n_width).astype(f32)
    inv = lax.rsqrt(jnp.mean(flat * flat, axis=-1, keepdims=True) + epsilon)
    unit = flat * inv
    normed_own = (unit * norm_gain).astype(bf16)
    docs = gathered(segments).reshape(tokens).astype(f32)
    half = groups // runs
    order = []
    for f in range(groups * size):
        run, owner, spot = f // (half * size), f // half % size, f % half
        order.append((f, (run * half + spot) * size + owner))
    back = [(b, a) for a, b in order]
    out_moved = lax.ppermute(out_weight.astype(bf16), ("dp", "seq"), order)
    channels = [conv_weight[:, :n_inner], conv_bias[None, :n_inner], gate_gain[None]]
    channels = own_columns(jnp.concatenate(channels, axis=0))
    conv_x, bias_x, gain = channels[:n_taps], channels[n_taps : n_taps + 1], channels[n_taps + 1 :]
    heads = own_columns(jnp.stack([step_bias, jnp.exp(log_rate), skip_gain]))
    sb, rate = padded(heads[0:1], LANES), padded(heads[1:2], LANES)
    skip = jnp.repeat(heads[2:3], head, axis=1)
    dcol = jnp.broadcast_to(docs[:, None], (tokens, LANES))
    drow = jnp.broadcast_to(docs[None, :], (8, tokens))
    early = (docs, out_moved, conv_x, bias_x, gain, sb, rate, skip, dcol, drow)
    n_first = own_inner + LANES
    cleared = jnp.zeros((groups * size * in_rows, n_first), bf16)
    mine, normed_own, cleared = lax.optimization_barrier((after(mine, early), normed_own, cleared))
    mine = mine.reshape(size * in_rows, -1)
    n_first = own_inner + LANES
    cot_own = cotangent.reshape(block, n_width)
    normed_held = opened(normed_own)
    cot_held = opened(after(cot_own, mine))
    w_first, hopped = gathered_rows(mine[:, :n_first], [normed_held, cot_held], cleared)
    z_block = jnp.concatenate([mine[:, n_first:], folded(out_moved, 1, own_inner)], axis=0)

    normed = gathered(normed_own, normed_held)
    joined = lax.all_gather(after(z_block, hopped), "dp", axis=0, tiled=True).reshape(groups, -1, own_inner)
    z_rows = size * in_rows
    cot = gathered(cot_own, cot_held)

    def own_part(vector, parts):
        return lax.dynamic_slice_in_dim(vector, index * parts, parts, vector.ndim - 1)

    w_x, w_small = w_first[:, :own_inner], w_first[:, own_inner:]
    small = mm(normed, w_small, NN)
    x_in = mm(normed, w_x, NN).astype(bf16)
    conv_bc = own_part(conv_weight[:, n_inner:], own_bc)
    bias_bc = own_part(conv_bias[None, n_inner:], own_bc)

    head_lanes = jnp.arange(LANES) < own_heads
    bc_in = small[:, LANES - own_bc :].astype(bf16).astype(f32)
    small_dt = jnp.where(head_lanes, small, 0.0)

    def earlier(rows, lag):
        return jnp.pad(rows, ((lag, 0), (0, 0)))[:tokens]

    def later(rows, lag):
        return jnp.pad(rows, ((0, lag), (0, 0)))[lag:]

    same = [None] + [
        jnp.where(jnp.pad(docs, (lag, 0), constant_values=-1.0)[:tokens] == docs, 1.0, 0.0)[:, None]
        for lag in range(1, n_taps)
    ]
    bc_conv = bias_bc + conv_bc[0:1] * bc_in
    for lag in range(1, n_taps):
        bc_conv = bc_conv + conv_bc[lag : lag + 1] * earlier(bc_in, lag) * same[lag]
    bc_sig = jax.nn.sigmoid(bc_conv)
    bct = gathered(by_rows((bc_conv * bc_sig).astype(bf16).T))

    y, states = run_forward(
        q, x_in, small_dt, bct, dcol, drow, conv_x, bias_x, sb, rate, skip, head
    )

    out_rows = own_inner // groups
    tiled = z_rows % 16 == 0 and out_rows % 16 == 0
    if tiled:
        lead, deep, tall, gate_in = groups, z_rows, out_rows, joined
    else:
        lead, deep, tall = 1, groups * z_rows, own_inner
        w_out = unfolded(joined[:, z_rows:], n_width)
        gate_in = [joined[:, :z_rows].reshape(-1, own_inner), folded(w_out, 1, own_inner)]
        gate_in = jnp.concatenate(gate_in, axis=0)[None]
    z, d_gn, sums, w_z, w_out = run_gate_forward(gate_in, deep, normed, cot, y, gain)
    w_out = jnp.concatenate(list(w_out), axis=1)
    sums = lax.psum(sums[:2], "seq")
    sums = jnp.pad(sums, ((0, 6), (0, 0)))
    gate_low, d_z, d_y, d_gain, terms = run_gate_backward(
        lead, deep, tall, n_inner, normed, cot, y, z, d_gn, sums, gain
    )
    d_gain = d_gain[0]
    if not tiled:
        z_term = terms[0, :deep].reshape(groups, z_rows, own_inner)
        out_term = terms[0, deep:].reshape(n_width // own_inner, groups, out_rows, own_inner)
        out_term = out_term.transpose(1, 0, 2, 3).reshape(groups, -1, own_inner)
        terms = jnp.concatenate([z_term, out_term], axis=1)
    terms = terms.reshape(-1, own_inner)
    parts = lax.psum_scatter(terms, "dp", scatter_dimension=0, tiled=True)

    d_x, d_dt, d_bct, d_conv_x, d_heads = run_backward(
        q, x_in, small_dt, bct, dcol, drow, conv_x, bias_x, sb, rate, skip, d_y, states, head
    )
    x_term = mm(normed, d_x, TN).astype(bf16)
    x_term, d_bct = lax.optimization_barrier((x_term, d_bct))
    x_lines = halved_rows(x_term)
    d_bc = by_rows(exchanged(d_bct)).T
    d_bcc = d_bc * (bc_sig * (1.0 + bc_conv * (1.0 - bc_sig)))
    d_bc_in = conv_bc[0:1] * d_bcc
    w_sums = [jnp.sum(d_bcc * bc_in, axis=0)]
    for lag in range(1, n_taps):
        held = d_bcc * same[lag]
        d_bc_in = d_bc_in + conv_bc[lag : lag + 1] * later(held, lag)
        w_sums.append(jnp.sum(held * earlier(bc_in, lag), axis=0))
    w_sums.append(jnp.sum(d_bcc, axis=0))
    d_small = jnp.concatenate([d_dt[:, : LANES - own_bc], d_bc_in], axis=1).astype(bf16)
    d_first = jnp.concatenate([d_x, d_small], axis=1)
    small_lines = halved_rows(mm(normed, d_small, TN).astype(bf16))
    branch = scattered(mm(after(gate_low, d_bc), w_out, NN).astype(bf16))
    result = (flat + branch).reshape(n_seqs, block, n_width).astype(bf16)
    d_normed = mm(d_first, w_first, NT) + mm(d_z, w_z, NT)
    d_norm_gain = jnp.sum(d_normed * normed.astype(f32), axis=0) / norm_gain
    d_skip = jnp.sum(d_conv_x[n_taps + 1].reshape(own_heads, head), axis=1)
    packed = jnp.concatenate(
        [
            d_conv_x[: n_taps + 1].reshape(-1),
            jnp.stack(w_sums).reshape(-1),
            d_gain,
            d_heads[0, :own_heads],
            d_heads[1, :own_heads],
            d_skip,
            d_norm_gain,
        ]
    )
    lines = jnp.concatenate([x_lines, small_lines], axis=-1)
    packed = added_over(packed, reversed(bits_of(groups)[1:]))
    packed, result = lax.optimization_barrier((packed, result))
    lines, packed = lax.optimization_barrier((lines, packed))
    shares = shared_rows(lines)
    packed = gathered(added_over(packed, bits_of(groups)[:1])[None])
    parts = after(parts, lines)
    d_norm = after(d_normed.astype(bf16), parts)
    d_norm = lax.psum_scatter(d_norm, "seq", scatter_dimension=0, tiled=True).astype(f32)

    def own_rows(part):
        return turned(part.reshape(size, in_rows, -1))

    def placed(rows, cuts=runs):
        wide = rows.shape[2] // cuts
        spots = [(run * wide, owner) for run in range(cuts) for owner in range(size)]
        pieces = [rows[owner, :, at : at + wide] for at, owner in spots]
        return jnp.concatenate(pieces, axis=1).astype(f32)

    out_part = unfolded(parts[None, z_rows:], n_width)
    d_out_weight = lax.ppermute(out_part, ("dp", "seq"), back).astype(f32)
    in_z = placed(own_rows(parts[:z_rows]))
    shares, in_z, d_out_weight = lax.optimization_barrier((shares, in_z, d_out_weight))
    first_part = sum(share.astype(f32) for share in shares)
    in_first = own_rows(first_part.astype(bf16))
    lifted = d_norm * norm_gain
    d_flat = inv * lifted - flat * (
        inv * inv * inv * jnp.mean(lifted * flat, axis=-1, keepdims=True)
    )
    d_hidden = (cot_own.astype(f32) + d_flat).reshape(n_seqs, block, n_width)
    in_first, d_hidden = lax.optimization_barrier((in_first, d_hidden))
    d_in_weight = jnp.concatenate(
        [
            in_z,
            placed(in_first[:, :, :own_inner]),
            placed(in_first[:, :, n_first - own_bc :], 1),
            placed(in_first[:, :, own_inner : own_inner + own_heads]),
        ],
        axis=1,
    )

    at = 0

    def take(count):
        nonlocal at
        at += count
        return packed[:, at - count : at]

    got_x = take((n_taps + 1) * own_inner).reshape(size, n_taps + 1, own_inner)
    got_bc = take((n_taps + 1) * own_bc).reshape(size, n_taps + 1, own_bc)
    got_x = undealt(got_x.transpose(1, 0, 2))
    got_bc = got_bc.transpose(1, 0, 2).reshape(n_taps + 1, 2 * n_state)
    conv_all = jnp.concatenate([got_x, got_bc], axis=1)
    d_gate_gain = undealt(take(own_inner)[None])[0]
    d_step_bias = undealt(take(own_heads)[None])[0]
    d_log_rate = undealt(take(own_heads)[None])[0]
    d_skip_gain = undealt(take(own_heads)[None])[0]
    d_norm_all = jnp.sum(take(n_width), axis=0)
    return (
        result,
        d_hidden,
        d_norm_all,
        d_in_weight,
        conv_all[:n_taps],
        conv_all[n_taps],
        d_step_bias,
        d_log_rate,
        d_skip_gain,
        d_gate_gain,
        d_out_weight,
    )


def solution(mesh):
    tokens = P("dp", "seq", None)
    rows = P(("dp", "seq"), None)
    return jax.shard_map(
        shards,
        mesh=mesh,
        in_specs=(tokens, P("dp", "seq"), tokens, P(), rows, P(), P(), P(), P(), P(), P(), rows),
        out_specs=(tokens, tokens, P(), rows, P(), P(), P(), P(), P(), P(), rows),
        check_vma=False,
    )
```

```python
import functools

import jax
import jax.numpy as jnp
from jax import lax
from jax.experimental import pallas as pl
from jax.experimental.layout import Layout, with_layout_constraint
from jax.experimental.pallas import tpu as pltpu
from jax.sharding import PartitionSpec as P

epsilon = 1e-05
highest = lax.Precision.HIGHEST
f32 = jnp.float32
bf16 = jnp.bfloat16
LANES = 128
HALO = 16
NEG = -1e30


def mm(a, b, dims, out=f32):
    return lax.dot_general(a, b, (dims, ((), ())), preferred_element_type=out)


NN = ((1,), (0,))
NT = ((1,), (1,))
TN = ((0,), (0,))


def exact(a, b, dims):
    return lax.dot_general(a, b, (dims, ((), ())), precision=highest, preferred_element_type=f32)


def softplus(v):
    return jnp.maximum(v, 0.0) + jnp.log1p(jnp.exp(-jnp.abs(v)))


def sigmoid(v):
    return 1.0 / (1.0 + jnp.exp(-v))


def lane_iota(shape):
    return lax.broadcasted_iota(jnp.int32, shape, len(shape) - 1)


def spread(columns, first, second, wide):
    rows = columns.shape[0]
    left = jnp.broadcast_to(columns[:, first : first + 1], (rows, LANES))
    right = jnp.broadcast_to(columns[:, second : second + 1], (rows, LANES))
    return jnp.where(wide, left, right)


def step_parts(raw, rate, q):
    row = lax.broadcasted_iota(jnp.int32, (q, q), 0)
    col = lax.broadcasted_iota(jnp.int32, (q, q), 1)
    tri = jnp.where(row >= col, 1.0, 0.0).astype(f32)
    step = softplus(raw)
    decay = -step * rate
    total = exact(tri, decay, NN)
    return step, decay, total, tri, row >= col


def convolve(ext, docs_ext, own, weights, bias, lanes, q, taps):
    running = bias + weights[0:1, lanes] * ext[pl.ds(HALO, q), lanes]
    for lag in range(1, taps):
        same = jnp.where(docs_ext[pl.ds(HALO - lag, q), :] == own, 1.0, 0.0)
        running = running + weights[lag : lag + 1, lanes] * ext[pl.ds(HALO - lag, q), lanes] * same
    return running


def scan_forward(
    q, taps, pairs, head,
    x_ref, small_ref, bct_ref, dcol_ref, drow_ref, w_ref, b_ref, sb_ref, rate_ref, skip_ref,
    y_ref, states_ref,
    state, ext, docs_ext, xs, xt, last_doc,
):
    c = pl.program_id(0)
    n = bct_ref.shape[0] // 2

    @pl.when(c == 0)
    def _():
        state[...] = jnp.zeros_like(state)
        ext[pl.ds(0, HALO), :] = jnp.zeros((HALO, ext.shape[1]), f32)
        docs_ext[pl.ds(0, HALO), :] = jnp.full((HALO, LANES), -1.0, f32)
        last_doc[...] = jnp.full(last_doc.shape, -1.0, f32)

    own = dcol_ref[...]
    ext[pl.ds(HALO, q), :] = x_ref[...].astype(f32)
    docs_ext[pl.ds(HALO, q), :] = own
    step, _, cum, _, causal = step_parts(small_ref[...] + sb_ref[...], rate_ref[...], q)
    step_t = step.T
    cum_t = cum.T
    end = cum[q - 1 : q, :]
    id_in = last_doc[0:1, :]
    final = own[q - 1 : q, :]
    linked = jnp.where(final == id_in, 1.0, 0.0)
    fade = linked * jnp.exp(end)
    entering = jnp.where(own == id_in, 1.0, 0.0) * jnp.exp(cum)
    to_end = jnp.where(own == final, 1.0, 0.0) * jnp.exp(end - cum) * step
    same_doc = jnp.broadcast_to(own[:, 0:1], (q, q)) == jnp.broadcast_to(drow_ref[0:1, :], (q, q))
    hide = jnp.where(jnp.logical_and(causal, same_doc), 0.0, NEG)
    bt = bct_ref[0:n, :]
    ct = bct_ref[n : 2 * n, :]
    scores = mm(ct, bt, TN)
    states_ref[0] = state[...]
    old = state[...].astype(bf16)
    wide = lane_iota((q, LANES)) < head
    wide_row = lane_iota((1, LANES)) < head
    for k in range(pairs):
        lanes = slice(k * LANES, (k + 1) * LANES)
        h0, h1 = 2 * k, 2 * k + 1
        conv = convolve(ext, docs_ext, own, w_ref, b_ref[:, lanes], lanes, q, taps)
        x = conv * sigmoid(conv)
        xd = x * spread(step, h0, h1, wide)
        xt[:, lanes] = (x * spread(to_end, h0, h1, wide)).astype(bf16)
        mats = []
        for h in (h0, h1):
            gap = cum[:, h : h + 1] - cum_t[h : h + 1, :] + hide
            mats.append((jnp.exp(gap) * scores).astype(bf16))
        out = mm(mats[0], jnp.where(wide, xd, 0.0).astype(bf16), NN)
        out = out + mm(mats[1], jnp.where(wide, 0.0, xd).astype(bf16), NN)
        out = out + mm(ct, old[:, lanes], TN) * spread(entering, h0, h1, wide)
        y_ref[:, lanes] = out + skip_ref[:, lanes] * x
    update = mm(bt, xt[...], NN)
    for k in range(pairs):
        lanes = slice(k * LANES, (k + 1) * LANES)
        state[:, lanes] = state[:, lanes] * spread(fade, 2 * k, 2 * k + 1, wide_row) + update[:, lanes]
    ext[pl.ds(0, HALO), :] = ext[pl.ds(q, HALO), :]
    docs_ext[pl.ds(0, HALO), :] = docs_ext[pl.ds(q, HALO), :]
    last_doc[...] = jnp.broadcast_to(final, last_doc.shape)


def scan_backward(
    q, taps, pairs, head, chunks,
    x_ref, xp_ref, small_ref, bct_ref, dcol_ref, dcolp_ref, drow_ref, w_ref, b_ref, sb_ref, rate_ref,
    skip_ref, dy_ref, states_ref,
    dx_ref, dsmall_ref, dbct_ref, dconv_ref, dhead_ref,
    dstate, ext, docs_ext, dcv, docs_after, dye, xt, col_t,
):
    step_at = pl.program_id(0)
    c = chunks - 1 - step_at
    n = bct_ref.shape[0] // 2
    width = x_ref.shape[1]

    @pl.when(step_at == 0)
    def _():
        dstate[...] = jnp.zeros_like(dstate)
        dcv[pl.ds(q, HALO), :] = jnp.zeros((HALO, width), f32)
        docs_after[pl.ds(q, HALO), :] = jnp.full((HALO, LANES), -1.0, f32)
        dconv_ref[...] = jnp.zeros_like(dconv_ref)
        dhead_ref[...] = jnp.zeros_like(dhead_ref)
        col_t[...] = jnp.zeros_like(col_t)

    first = c == 0
    own = dcol_ref[...]
    before = jnp.where(first, -1.0, dcolp_ref[...])
    ext[pl.ds(0, HALO), :] = xp_ref[...].astype(f32)
    ext[pl.ds(HALO, q), :] = x_ref[...].astype(f32)
    docs_ext[pl.ds(0, HALO), :] = before
    docs_ext[pl.ds(HALO, q), :] = own
    docs_after[pl.ds(0, q), :] = own
    raw = small_ref[...] + sb_ref[...]
    rate = rate_ref[...]
    step, decay, cum, tri, causal = step_parts(raw, rate, q)
    step_t = step.T
    cum_t = cum.T
    end = cum[q - 1 : q, :]
    id_in = before[HALO - 1 : HALO, :]
    final = own[q - 1 : q, :]
    linked = jnp.where(final == id_in, 1.0, 0.0)
    fade = linked * jnp.exp(end)
    entering = jnp.where(own == id_in, 1.0, 0.0) * jnp.exp(cum)
    tail = jnp.where(own == final, 1.0, 0.0) * jnp.exp(end - cum)
    to_end = tail * step
    same_doc = jnp.broadcast_to(own[:, 0:1], (q, q)) == jnp.broadcast_to(drow_ref[0:1, :], (q, q))
    hide = jnp.where(jnp.logical_and(causal, same_doc), 0.0, NEG)
    bt = bct_ref[0:n, :]
    ct = bct_ref[n : 2 * n, :]
    scores = mm(ct, bt, TN)
    old = states_ref[0].astype(bf16)
    after = dstate[...].astype(bf16)
    wide = lane_iota((q, LANES)) < head
    wide_row = lane_iota((1, LANES)) < head
    lane = lane_iota((q, LANES))
    d_scores = jnp.zeros((q, q), f32)
    rows = jnp.zeros((q, LANES), f32)
    d_enter = jnp.zeros((q, LANES), f32)
    d_toend = jnp.zeros((q, LANES), f32)
    d_fade = jnp.zeros((8, LANES), f32)
    part = lax.broadcasted_iota(jnp.int32, (LANES, LANES), 0) // head
    to = lane_iota((LANES, LANES))
    for k in range(pairs):
        lanes = slice(k * LANES, (k + 1) * LANES)
        h0, h1 = 2 * k, 2 * k + 1
        pick = jnp.where(part + 2 * k == to, 1.0, 0.0)
        conv = convolve(ext, docs_ext, own, w_ref, b_ref[:, lanes], lanes, q, taps)
        sig = sigmoid(conv)
        x = conv * sig
        xb = x.astype(bf16)
        dy = dy_ref[:, lanes]
        halves = (jnp.where(wide, dy, 0.0).astype(bf16), jnp.where(wide, 0.0, dy).astype(bf16))
        dxd = jnp.zeros((q, LANES), f32)
        for h, half in ((h0, halves[0]), (h1, halves[1])):
            inner = mm(half, xb, NT)
            keep = jnp.exp(cum[:, h : h + 1] - cum_t[h : h + 1, :] + hide)
            grown = keep * inner
            mat = keep * scores
            dt = step_t[h : h + 1, :]
            g = grown * scores
            d_scores = d_scores + grown * dt
            rows = jnp.where(lane == h, jnp.sum(g * dt, axis=1, keepdims=True), rows)
            col_t[h : h + 1, :] = jnp.sum(g, axis=0, keepdims=True)
            dxd = dxd + mm(mat.astype(bf16), half, TN)
        v = mm(bt, after[:, lanes], TN)
        u = mm(ct, old[:, lanes], TN)
        enter_k = spread(entering, h0, h1, wide)
        end_k = spread(to_end, h0, h1, wide)
        d_enter = d_enter + exact(dy * u, pick, NN)
        d_toend = d_toend + exact(x * v, pick, NN)
        hh = jnp.sum(dstate[:, lanes] * states_ref[0, :, lanes], axis=0, keepdims=True)
        d_fade = d_fade + exact(jnp.broadcast_to(hh, (8, LANES)), pick, NN)
        dye[:, lanes] = (dy * enter_k).astype(bf16)
        xt[:, lanes] = (x * end_k).astype(bf16)
        dx = dxd * spread(step, h0, h1, wide) + end_k * v + skip_ref[:, lanes] * dy
        dconv = dx * (sig * (1.0 + conv * (1.0 - sig)))
        dcv[pl.ds(0, q), lanes] = dconv
        sums = [jnp.sum(dconv * ext[pl.ds(HALO, q), lanes], axis=0, keepdims=True)]
        dxin = w_ref[0:1, lanes] * dconv
        for lag in range(1, taps):
            same = jnp.where(docs_ext[pl.ds(HALO - lag, q), :] == own, 1.0, 0.0)
            sums.append(jnp.sum(dconv * same * ext[pl.ds(HALO - lag, q), lanes], axis=0, keepdims=True))
            follow = jnp.where(docs_after[pl.ds(lag, q), :] == own, 1.0, 0.0)
            dxin = dxin + w_ref[lag : lag + 1, lanes] * dcv[pl.ds(lag, q), lanes] * follow
        sums.append(jnp.sum(dconv, axis=0, keepdims=True))
        sums.append(jnp.sum(dy * x, axis=0, keepdims=True))
        dx_ref[:, lanes] = dxin.astype(bf16)
        for i, s in enumerate(sums):
            dconv_ref[i : i + 1, lanes] = dconv_ref[i : i + 1, lanes] + s
    dsb = d_scores.astype(bf16)
    dbct_ref[0:n, :] = mm(ct, dsb, NN) + mm(after, xt[...], NT)
    dbct_ref[n : 2 * n, :] = mm(bt, dsb, NT) + mm(old, dye[...], NT)
    new = mm(ct, dye[...], NN)
    for k in range(pairs):
        lanes = slice(k * LANES, (k + 1) * LANES)
        dstate[:, lanes] = dstate[:, lanes] * spread(fade, 2 * k, 2 * k + 1, wide_row) + new[:, lanes]
    cols = col_t[...].T
    pulled = d_toend * to_end
    at_end = jnp.sum(pulled, axis=0, keepdims=True) + fade * d_fade[0:1, :]
    d_cum = rows - step * cols + d_enter * entering - pulled
    last_row = lax.broadcasted_iota(jnp.int32, (q, LANES), 0) == q - 1
    d_cum = d_cum + jnp.where(last_row, at_end, 0.0)
    d_decay = exact(tri, d_cum, TN)
    d_step = cols + d_toend * tail - rate * d_decay
    d_raw = d_step * sigmoid(raw)
    dsmall_ref[...] = d_raw
    dhead_ref[0:1, :] = dhead_ref[0:1, :] + jnp.sum(d_raw, axis=0, keepdims=True)
    dhead_ref[1:2, :] = dhead_ref[1:2, :] + jnp.sum(d_decay * decay, axis=0, keepdims=True)
    dcv[pl.ds(q, HALO), :] = dcv[pl.ds(0, HALO), :]
    docs_after[pl.ds(q, HALO), :] = docs_after[pl.ds(0, HALO), :]


def whole(array):
    return pl.BlockSpec(array.shape, lambda c: (0,) * array.ndim)


def run_forward(q, x_in, small, bct, dcol, drow, conv_w, conv_b, sb, rate, skip, head):
    tokens, width = x_in.shape
    n = bct.shape[0] // 2
    chunks = tokens // q
    pairs = width // LANES
    taps = conv_w.shape[0]
    return pl.pallas_call(
        functools.partial(scan_forward, q, taps, pairs, head),
        grid=(chunks,),
        in_specs=[
            pl.BlockSpec((q, width), lambda c: (c, 0)),
            pl.BlockSpec((q, LANES), lambda c: (c, 0)),
            pl.BlockSpec((2 * n, q), lambda c: (0, c)),
            pl.BlockSpec((q, LANES), lambda c: (c, 0)),
            pl.BlockSpec((8, q), lambda c: (0, c)),
            whole(conv_w), whole(conv_b), whole(sb), whole(rate), whole(skip),
        ],
        out_specs=[
            pl.BlockSpec((q, width), lambda c: (c, 0)),
            pl.BlockSpec((1, n, width), lambda c: (c, 0, 0)),
        ],
        out_shape=[
            jax.ShapeDtypeStruct((tokens, width), f32),
            jax.ShapeDtypeStruct((chunks, n, width), f32),
        ],
        scratch_shapes=[
            pltpu.VMEM((n, width), f32),
            pltpu.VMEM((HALO + q, width), f32),
            pltpu.VMEM((HALO + q, LANES), f32),
            pltpu.VMEM((8, LANES), f32),
            pltpu.VMEM((q, width), bf16),
            pltpu.VMEM((8, LANES), f32),
        ],
        name="scan_forward",
    )(x_in, small, bct, dcol, drow, conv_w, conv_b, sb, rate, skip)


def run_backward(q, x_in, small, bct, dcol, drow, conv_w, conv_b, sb, rate, skip, dy, states, head):
    tokens, width = x_in.shape
    n = bct.shape[0] // 2
    chunks = tokens // q
    pairs = width // LANES
    taps = conv_w.shape[0]
    per = q // HALO

    def at(c):
        return chunks - 1 - c

    def prior(c):
        return jnp.maximum((chunks - 1 - c) * per - 1, 0)

    return pl.pallas_call(
        functools.partial(scan_backward, q, taps, pairs, head, chunks),
        grid=(chunks,),
        in_specs=[
            pl.BlockSpec((q, width), lambda c: (at(c), 0)),
            pl.BlockSpec((HALO, width), lambda c: (prior(c), 0)),
            pl.BlockSpec((q, LANES), lambda c: (at(c), 0)),
            pl.BlockSpec((2 * n, q), lambda c: (0, at(c))),
            pl.BlockSpec((q, LANES), lambda c: (at(c), 0)),
            pl.BlockSpec((HALO, LANES), lambda c: (prior(c), 0)),
            pl.BlockSpec((8, q), lambda c: (0, at(c))),
            whole(conv_w), whole(conv_b), whole(sb), whole(rate), whole(skip),
            pl.BlockSpec((q, width), lambda c: (at(c), 0)),
            pl.BlockSpec((1, n, width), lambda c: (at(c), 0, 0)),
        ],
        out_specs=[
            pl.BlockSpec((q, width), lambda c: (at(c), 0)),
            pl.BlockSpec((q, LANES), lambda c: (at(c), 0)),
            pl.BlockSpec((2 * n, q), lambda c: (0, at(c))),
            pl.BlockSpec((8, width), lambda c: (0, 0)),
            pl.BlockSpec((8, LANES), lambda c: (0, 0)),
        ],
        out_shape=[
            jax.ShapeDtypeStruct((tokens, width), bf16),
            jax.ShapeDtypeStruct((tokens, LANES), f32),
            jax.ShapeDtypeStruct((2 * n, tokens), f32),
            jax.ShapeDtypeStruct((8, width), f32),
            jax.ShapeDtypeStruct((8, LANES), f32),
        ],
        scratch_shapes=[
            pltpu.VMEM((n, width), f32),
            pltpu.VMEM((HALO + q, width), f32),
            pltpu.VMEM((HALO + q, LANES), f32),
            pltpu.VMEM((q + HALO, width), f32),
            pltpu.VMEM((q + HALO, LANES), f32),
            pltpu.VMEM((q, width), bf16),
            pltpu.VMEM((q, width), bf16),
            pltpu.VMEM((LANES, q), f32),
        ],
        name="scan_backward",
    )(x_in, x_in, small, bct, dcol, dcol, drow, conv_w, conv_b, sb, rate, skip, dy, states)


def gate_forward(
    groups, z_rows, tall,
    normed_ref, cot_ref, joined_ref, y_ref, gain_ref, z_ref, dgn_ref, sums_ref, wz, wo,
):
    parts, held, width = wo.shape

    @pl.when(pl.program_id(0) == 0)
    def _():
        for g in range(groups):
            wz[pl.ds(g * z_rows, z_rows), :] = joined_ref[g, pl.ds(0, z_rows), :]
            for k in range(parts):
                wo[k, pl.ds(g * tall, tall), :] = joined_ref[g, pl.ds(z_rows + k * tall, tall), :]

    z = mm(normed_ref[...], wz[...], NN)
    d_gn = mm(cot_ref[:, 0:width], wo[0], NT)
    for k in range(1, parts):
        d_gn = d_gn + mm(cot_ref[:, k * width : (k + 1) * width], wo[k], NT)
    z_ref[...] = z
    dgn_ref[...] = d_gn
    gated = y_ref[...] * (z * sigmoid(z))
    square = jnp.sum(gated * gated, axis=1, keepdims=True)
    cross = jnp.sum(d_gn * gain_ref[...] * gated, axis=1, keepdims=True)
    lane = lane_iota((square.shape[0], LANES))
    sums_ref[...] = jnp.where(lane == 0, square, jnp.where(lane == 1, cross, 0.0)).T[0:8, :]


def gate_backward(
    blocks, tile, z_rows, tall, channels,
    normed_ref, cot_ref, y_ref, z_ref, dgn_ref, sums_ref, gain_ref,
    gate_ref, dz_ref, dy_ref, dgain_ref, terms_ref,
):
    step = pl.program_id(0)
    rows, width = y_ref.shape
    parts = normed_ref.shape[1] // width

    @pl.when(step == 0)
    def _():
        dgain_ref[...] = jnp.zeros_like(dgain_ref)

    @pl.when(step < blocks)
    def _():
        own = pl.ds(pl.multiple_of(step * rows, rows), rows)
        columns = jnp.concatenate([sums_ref[...], jnp.zeros((LANES - 8, rows), f32)], axis=0).T
        inv = lax.rsqrt(columns[:, 0:1] / channels + epsilon)
        slope = inv * inv * inv * (columns[:, 1:2] / channels)
        for k in range(width // LANES):
            lanes = slice(k * LANES, (k + 1) * LANES)
            y, z, d_gn, gain = y_ref[:, lanes], z_ref[:, lanes], dgn_ref[:, lanes], gain_ref[:, lanes]
            sig = sigmoid(z)
            act = z * sig
            gated = y * act
            scaled = gated * inv
            gate_ref[own, lanes] = (scaled * gain).astype(bf16)
            dgain_ref[0:1, lanes] = dgain_ref[0:1, lanes] + jnp.sum(d_gn * scaled, axis=0, keepdims=True)
            d_gated = inv * (d_gn * gain) - gated * slope
            dz_ref[own, lanes] = (d_gated * y * (sig * (1.0 + z * (1.0 - sig)))).astype(bf16)
            dy_ref[:, lanes] = d_gated * act

    def store(term, at, within, base):
        if within >= tile:
            start = pl.multiple_of(base + at * tile, 16)
            terms_ref[0, pl.ds(start, tile), :] = term
        else:
            for n in range(tile // within):
                piece = term[n * within : (n + 1) * within]
                terms_ref[at * (tile // within) + n, pl.ds(base, within), :] = piece

    @pl.when(step >= blocks)
    def _():
        i = step - blocks
        lanes = pl.ds(pl.multiple_of(i * tile, LANES), tile)
        store(mm(normed_ref[:, lanes], dz_ref[...], TN).astype(bf16), i, z_rows, 0)
        j = i // parts
        lanes = pl.ds(pl.multiple_of(j * tile, LANES), tile)
        left = gate_ref[:, lanes]
        for k in range(parts):

            @pl.when(i % parts == k)
            def _():
                right = cot_ref[:, k * width : (k + 1) * width]
                store(mm(left, right, TN).astype(bf16), j, tall, z_rows + k * tall)


def run_gate_forward(joined, z_rows, normed, cot, y, gain):
    groups, deep, width = joined.shape
    tokens, n_width = normed.shape
    parts = n_width // width
    tall = (deep - z_rows) // parts
    rows = min(256, tokens)

    def tokens_of(columns):
        return pl.BlockSpec((rows, columns), lambda c: (c, 0))

    return pl.pallas_call(
        functools.partial(gate_forward, groups, z_rows, tall),
        grid=(tokens // rows,),
        in_specs=[tokens_of(n_width), tokens_of(n_width), whole(joined), tokens_of(width), whole(gain)],
        out_specs=[
            tokens_of(width), tokens_of(width), pl.BlockSpec((8, rows), lambda c: (0, c)),
            pl.BlockSpec((groups * z_rows, width), lambda c: (0, 0)),
            pl.BlockSpec((parts, groups * tall, width), lambda c: (0, 0, 0)),
        ],
        out_shape=[
            jax.ShapeDtypeStruct((tokens, width), f32),
            jax.ShapeDtypeStruct((tokens, width), f32),
            jax.ShapeDtypeStruct((8, tokens), f32),
            jax.ShapeDtypeStruct((groups * z_rows, width), bf16),
            jax.ShapeDtypeStruct((parts, groups * tall, width), bf16),
        ],
        name="gate_forward",
    )(normed, cot, joined, y, gain)


def run_gate_backward(groups, z_rows, tall, channels, normed, cot, y, z, d_gn, sums, gain):
    tokens, n_width = normed.shape
    width = y.shape[1]
    parts = n_width // width
    rows = min(256, tokens)
    blocks = tokens // rows
    tile = 3 * LANES
    deep = z_rows + parts * tall

    def tokens_of(columns):
        return pl.BlockSpec((rows, columns), lambda c: (jnp.minimum(c, blocks - 1), 0))

    return pl.pallas_call(
        functools.partial(gate_backward, blocks, tile, z_rows, tall, channels),
        grid=(blocks + n_width // tile,),
        in_specs=[
            whole(normed), whole(cot), tokens_of(width), tokens_of(width), tokens_of(width),
            pl.BlockSpec((8, rows), lambda c: (0, jnp.minimum(c, blocks - 1))), whole(gain),
        ],
        out_specs=[
            pl.BlockSpec((tokens, width), lambda c: (0, 0)),
            pl.BlockSpec((tokens, width), lambda c: (0, 0)),
            tokens_of(width),
            pl.BlockSpec((8, width), lambda c: (0, 0)),
            pl.BlockSpec((groups, deep, width), lambda c: (0, 0, 0)),
        ],
        out_shape=[
            jax.ShapeDtypeStruct((tokens, width), bf16),
            jax.ShapeDtypeStruct((tokens, width), bf16),
            jax.ShapeDtypeStruct((tokens, width), f32),
            jax.ShapeDtypeStruct((8, width), f32),
            jax.ShapeDtypeStruct((groups, deep, width), bf16),
        ],
        name="gate_backward",
    )(normed, cot, y, z, d_gn, sums, gain)


def swapped(block, bit):
    size = lax.axis_size("seq")
    return lax.ppermute(block, "seq", [(i, i ^ bit) for i in range(size)])


def bits_of(size):
    bits, bit = [], 1
    while bit < size:
        bits.append(bit)
        bit *= 2
    return bits


def joined_by(held, bit):
    other = swapped(held, bit)
    upper = (lax.axis_index("seq") & bit) != 0
    both = jnp.where(upper, jnp.stack([other, held], axis=1), jnp.stack([held, other], axis=1))
    return both.reshape((-1,) + both.shape[2:])


def opened(block):
    bits = bits_of(lax.axis_size("seq"))
    return joined_by(block[None], bits[-1]) if bits else block[None]


def gathered(block, held=None):
    held = opened(block) if held is None else held
    for bit in reversed(bits_of(lax.axis_size("seq"))[:-1]):
        held = joined_by(held, bit)
    return held.reshape((-1,) + held.shape[2:])


def scattered(parts, between=lambda held: held):
    index = lax.axis_index("seq")
    size = lax.axis_size("seq")
    rest = parts.shape[1:]
    lead = parts.shape[0]
    held = parts.reshape((size, lead // size) + rest)
    for bit in bits_of(size):
        half = held.reshape((held.shape[0] // 2, 2) + held.shape[1:])
        upper = (index & bit) != 0
        mine = jnp.where(upper, half[:, 1], half[:, 0])
        theirs = jnp.where(upper, half[:, 0], half[:, 1]).astype(bf16)
        held = between(mine.astype(f32) + swapped(theirs, bit).astype(f32))
    return held[0]


def added_over(block, bits):
    for bit in bits:
        block = block + crossed(block, bit)
    return block


def moved_by(block, step):
    count = lax.axis_size("dp")
    route = [(i, i + 2 * step) for i in range(count) if 0 <= i + 2 * step < count]
    return lax.ppermute(block, "dp", route)


def crossed(block, bits):
    return lax.ppermute(block, "dp", [(i, i ^ bits) for i in range(lax.axis_size("dp"))])


def gathered_rows(block, waits, whole_rows):
    count = lax.axis_size("dp")
    length = count // 2
    if not is_small(count):
        return lax.all_gather(block, "dp", axis=0, tiled=True), block
    at = lax.axis_index("dp")
    place, side = at // 2, at % 2
    rows = block.shape[0]

    def put(into, piece, pair, half):
        return lax.dynamic_update_slice(into, piece, ((pair * 2 + half) * rows, 0))

    whole_rows = put(whole_rows, block, place, side)
    other = crossed(block, 1)
    whole_rows = put(whole_rows, other, place, 1 - side)
    up, down, ready = block, block, []
    for hop in range(1, length):
        up, down = after((moved_by(up, 1), moved_by(down, -1)), (other, waits[hop - 1 : hop]))
        ready.append((down, up))
        piece, pair = None, None
        for spot in range(length):
            near = min(spot, length - 1 - spot)
            if hop <= 2 * near:
                away, from_below = (hop + 1) // 2, hop % 2 == 0
            else:
                away, from_below = hop - near, spot > length - 1 - spot
            chosen = ready[away - 1][1 if from_below else 0]
            source = spot - away if from_below else spot + away
            here = place == spot
            piece = chosen if piece is None else jnp.where(here, chosen, piece)
            pair = source if pair is None else jnp.where(here, source, pair)
        whole_rows = put(whole_rows, piece, pair, side)
        other = crossed(piece, 1)
        whole_rows = put(whole_rows, other, pair, 1 - side)
    return whole_rows, ready[min(1, length - 2)]


def is_small(count):
    return count <= 8 and count & (count - 1) == 0


def halved_rows(term):
    count = lax.axis_size("dp")
    if not is_small(count):
        return term
    at = lax.axis_index("dp")
    pairs = term.reshape(count // 2, 2, -1, term.shape[1])

    def side(which):
        return lax.dynamic_index_in_dim(pairs, which, 1, keepdims=False)

    came = crossed(side((at & 1) ^ 1), 1)
    return (side(at & 1).astype(f32) + came.astype(f32)).astype(bf16)


def shared_rows(lines):
    count = lax.axis_size("dp")
    if not is_small(count):
        return [lax.psum_scatter(lines, "dp", scatter_dimension=0, tiled=True)]
    at = lax.axis_index("dp")

    def part(owner):
        return lax.dynamic_index_in_dim(lines, owner // 2, 0, keepdims=False)

    return [part(at)] + [crossed(part(at ^ bits), bits) for bits in range(2, count, 2)]


def after(value, other):
    return lax.optimization_barrier((value, other))[0]


def turned(blocks, together=False):
    size = lax.axis_size("seq")
    index = lax.axis_index("seq")
    if size & (size - 1):
        return lax.all_to_all(blocks, "seq", 0, 0, tiled=True)
    pieces = []
    for bits in range(1, size):
        piece = lax.dynamic_slice_in_dim(blocks, index ^ bits, 1, 0)
        pieces.append(lax.ppermute(piece, "seq", [(i, i ^ bits) for i in range(size)]))
    out = blocks
    for bits, piece in enumerate(lax.optimization_barrier(pieces) if together else pieces, 1):
        out = lax.dynamic_update_slice_in_dim(out, piece, index ^ bits, 0)
    return out


def folded(rows, lead, width):
    cut = rows.reshape(lead, rows.shape[0] // lead, rows.shape[1] // width, width)
    cut = cut.transpose(0, 2, 1, 3).reshape(lead, -1, width)
    return cut[0] if lead == 1 else cut


def unfolded(pieces, width):
    lead, stacked, narrow = pieces.shape
    cut = pieces.reshape(lead, width // narrow, stacked * narrow // width, narrow)
    return cut.transpose(0, 2, 1, 3).reshape(-1, width)


def exchanged(parts):
    size = lax.axis_size("seq")
    index = lax.axis_index("seq")
    held = parts.reshape((size, -1) + parts.shape[1:])

    def part(owner):
        return lax.dynamic_index_in_dim(held, owner, 0, keepdims=False)

    came = [
        lax.ppermute(part(index ^ bits).astype(bf16), "seq", [(i, i ^ bits) for i in range(size)])
        for bits in range(1, size)
    ]
    return sum([piece.astype(f32) for piece in came], part(index))


def by_rows(array):
    return with_layout_constraint(array, Layout(major_to_minor=(0, 1)))


def padded(rows, width):
    return jnp.pad(rows, ((0, 0), (0, width - rows.shape[1])))


def shards(
    hidden, segments, cotangent, norm_gain, in_weight, conv_weight, conv_bias, step_bias, log_rate,
    skip_gain, gate_gain, out_weight,
):
    n_seqs, block, n_width = hidden.shape
    size = lax.axis_size("seq")
    groups = lax.axis_size("dp")
    index = lax.axis_index("seq")
    tokens = size * block
    n_inner = gate_gain.shape[0]
    n_heads = step_bias.shape[0]
    n_taps = conv_weight.shape[0]
    n_mixed = conv_bias.shape[0]
    n_state = (n_mixed - n_inner) // 2
    head = n_inner // n_heads
    own_inner = n_inner // size
    own_heads = n_heads // size
    own_bc = 2 * n_state // size
    q = min(128, block)
    in_rows = in_weight.shape[0]

    in_low = in_weight.astype(bf16)
    runs = 2 if groups % 2 == 0 else 1

    def dealt(columns):
        cut = columns.reshape(columns.shape[0], runs, size, -1)
        return cut.transpose(0, 2, 1, 3).reshape(columns.shape[0], size, -1)

    def undealt(columns):
        cut = columns.reshape(columns.shape[0], size, runs, -1)
        return cut.transpose(0, 2, 1, 3).reshape(columns.shape[0], -1)

    def own_columns(columns):
        wide = columns.shape[1] // runs
        narrow = wide // size
        starts = [run * wide + index * narrow for run in range(runs)]
        cut = [lax.dynamic_slice_in_dim(columns, start, narrow, 1) for start in starts]
        return jnp.concatenate(cut, axis=1)

    z_cols = dealt(in_low[:, :n_inner])
    x_cols = dealt(in_low[:, n_inner : 2 * n_inner])
    bc_cols = in_low[:, 2 * n_inner : n_inner + n_mixed].reshape(in_rows, size, own_bc)
    dt_cols = dealt(in_low[:, n_inner + n_mixed :])
    gap = jnp.zeros((in_rows, size, LANES - own_heads - own_bc), bf16)
    laid = jnp.concatenate([x_cols, dt_cols, gap, bc_cols, z_cols], axis=2).transpose(1, 0, 2)
    mine = lax.all_to_all(laid, "seq", 0, 0, tiled=True)
    flat = hidden.reshape(block, n_width).astype(f32)
    inv = lax.rsqrt(jnp.mean(flat * flat, axis=-1, keepdims=True) + epsilon)
    unit = flat * inv
    normed_own = (unit * norm_gain).astype(bf16)
    docs = gathered(segments).reshape(tokens).astype(f32)
    half = groups // runs
    order = []
    for f in range(groups * size):
        run, owner, spot = f // (half * size), f // half % size, f % half
        order.append((f, (run * half + spot) * size + owner))
    back = [(b, a) for a, b in order]
    out_moved = lax.ppermute(out_weight.astype(bf16), ("dp", "seq"), order)
    channels = [conv_weight[:, :n_inner], conv_bias[None, :n_inner], gate_gain[None]]
    channels = own_columns(jnp.concatenate(channels, axis=0))
    conv_x, bias_x, gain = channels[:n_taps], channels[n_taps : n_taps + 1], channels[n_taps + 1 :]
    heads = own_columns(jnp.stack([step_bias, jnp.exp(log_rate), skip_gain]))
    sb, rate = padded(heads[0:1], LANES), padded(heads[1:2], LANES)
    skip = jnp.repeat(heads[2:3], head, axis=1)
    dcol = jnp.broadcast_to(docs[:, None], (tokens, LANES))
    drow = jnp.broadcast_to(docs[None, :], (8, tokens))
    early = (docs, out_moved, conv_x, bias_x, gain, sb, rate, skip, dcol, drow)
    n_first = own_inner + LANES
    cleared = jnp.zeros((groups * size * in_rows, n_first), bf16)
    mine, normed_own, cleared = lax.optimization_barrier((after(mine, early), normed_own, cleared))
    mine = mine.reshape(size * in_rows, -1)
    n_first = own_inner + LANES
    cot_own = cotangent.reshape(block, n_width)
    normed_held = opened(normed_own)
    cot_held = opened(after(cot_own, mine))
    w_first, hopped = gathered_rows(mine[:, :n_first], [normed_held, cot_held], cleared)
    z_block = jnp.concatenate([mine[:, n_first:], folded(out_moved, 1, own_inner)], axis=0)

    normed = gathered(normed_own, normed_held)
    joined = lax.all_gather(after(z_block, hopped), "dp", axis=0, tiled=True).reshape(groups, -1, own_inner)
    z_rows = size * in_rows
    cot = gathered(cot_own, cot_held)

    def own_part(vector, parts):
        return lax.dynamic_slice_in_dim(vector, index * parts, parts, vector.ndim - 1)

    w_x, w_small = w_first[:, :own_inner], w_first[:, own_inner:]
    small = mm(normed, w_small, NN)
    x_in = mm(normed, w_x, NN).astype(bf16)
    conv_bc = own_part(conv_weight[:, n_inner:], own_bc)
    bias_bc = own_part(conv_bias[None, n_inner:], own_bc)

    head_lanes = jnp.arange(LANES) < own_heads
    bc_in = small[:, LANES - own_bc :].astype(bf16).astype(f32)
    small_dt = jnp.where(head_lanes, small, 0.0)

    def earlier(rows, lag):
        return jnp.pad(rows, ((lag, 0), (0, 0)))[:tokens]

    def later(rows, lag):
        return jnp.pad(rows, ((0, lag), (0, 0)))[lag:]

    same = [None] + [
        jnp.where(jnp.pad(docs, (lag, 0), constant_values=-1.0)[:tokens] == docs, 1.0, 0.0)[:, None]
        for lag in range(1, n_taps)
    ]
    bc_conv = bias_bc + conv_bc[0:1] * bc_in
    for lag in range(1, n_taps):
        bc_conv = bc_conv + conv_bc[lag : lag + 1] * earlier(bc_in, lag) * same[lag]
    bc_sig = jax.nn.sigmoid(bc_conv)
    bct = gathered(by_rows((bc_conv * bc_sig).astype(bf16).T))

    y, states = run_forward(
        q, x_in, small_dt, bct, dcol, drow, conv_x, bias_x, sb, rate, skip, head
    )

    out_rows = own_inner // groups
    tiled = z_rows % 16 == 0 and out_rows % 16 == 0
    if tiled:
        lead, deep, tall, gate_in = groups, z_rows, out_rows, joined
    else:
        lead, deep, tall = 1, groups * z_rows, own_inner
        w_out = unfolded(joined[:, z_rows:], n_width)
        gate_in = [joined[:, :z_rows].reshape(-1, own_inner), folded(w_out, 1, own_inner)]
        gate_in = jnp.concatenate(gate_in, axis=0)[None]
    z, d_gn, sums, w_z, w_out = run_gate_forward(gate_in, deep, normed, cot, y, gain)
    w_out = jnp.concatenate(list(w_out), axis=1)
    sums = lax.psum(sums[:2], "seq")
    sums = jnp.pad(sums, ((0, 6), (0, 0)))
    gate_low, d_z, d_y, d_gain, terms = run_gate_backward(
        lead, deep, tall, n_inner, normed, cot, y, z, d_gn, sums, gain
    )
    d_gain = d_gain[0]
    if not tiled:
        z_term = terms[0, :deep].reshape(groups, z_rows, own_inner)
        out_term = terms[0, deep:].reshape(n_width // own_inner, groups, out_rows, own_inner)
        out_term = out_term.transpose(1, 0, 2, 3).reshape(groups, -1, own_inner)
        terms = jnp.concatenate([z_term, out_term], axis=1)
    terms = terms.reshape(-1, own_inner)
    parts = lax.psum_scatter(terms, "dp", scatter_dimension=0, tiled=True)

    d_x, d_dt, d_bct, d_conv_x, d_heads = run_backward(
        q, x_in, small_dt, bct, dcol, drow, conv_x, bias_x, sb, rate, skip, d_y, states, head
    )
    x_term = mm(normed, d_x, TN).astype(bf16)
    x_term, d_bct = lax.optimization_barrier((x_term, d_bct))
    x_lines = halved_rows(x_term)
    d_bc = by_rows(exchanged(d_bct)).T
    d_bcc = d_bc * (bc_sig * (1.0 + bc_conv * (1.0 - bc_sig)))
    d_bc_in = conv_bc[0:1] * d_bcc
    w_sums = [jnp.sum(d_bcc * bc_in, axis=0)]
    for lag in range(1, n_taps):
        held = d_bcc * same[lag]
        d_bc_in = d_bc_in + conv_bc[lag : lag + 1] * later(held, lag)
        w_sums.append(jnp.sum(held * earlier(bc_in, lag), axis=0))
    w_sums.append(jnp.sum(d_bcc, axis=0))
    d_small = jnp.concatenate([d_dt[:, : LANES - own_bc], d_bc_in], axis=1).astype(bf16)
    d_first = jnp.concatenate([d_x, d_small], axis=1)
    small_lines = halved_rows(mm(normed, d_small, TN).astype(bf16))
    branch = scattered(mm(after(gate_low, d_bc), w_out, NN).astype(bf16))
    result = (flat + branch).reshape(n_seqs, block, n_width).astype(bf16)
    d_normed = mm(d_first, w_first, NT) + mm(d_z, w_z, NT)
    d_norm_gain = jnp.sum(d_normed * normed.astype(f32), axis=0) / norm_gain
    d_skip = jnp.sum(d_conv_x[n_taps + 1].reshape(own_heads, head), axis=1)
    packed = jnp.concatenate(
        [
            d_conv_x[: n_taps + 1].reshape(-1),
            jnp.stack(w_sums).reshape(-1),
            d_gain,
            d_heads[0, :own_heads],
            d_heads[1, :own_heads],
            d_skip,
            d_norm_gain,
        ]
    )
    lines = jnp.concatenate([x_lines, small_lines], axis=-1)
    packed = added_over(packed, reversed(bits_of(groups)[1:]))
    lines, packed = lax.optimization_barrier((lines, packed))
    shares = shared_rows(lines)
    packed = gathered(added_over(packed, bits_of(groups)[:1])[None])
    parts, result = lax.optimization_barrier((after(parts, lines), result))
    d_norm = after(d_normed.astype(bf16), parts)
    d_norm = lax.psum_scatter(d_norm, "seq", scatter_dimension=0, tiled=True).astype(f32)

    def own_rows(part, together=False):
        return turned(part.reshape(size, in_rows, -1), together)

    def placed(rows, cuts=runs):
        wide = rows.shape[2] // cuts
        spots = [(run * wide, owner) for run in range(cuts) for owner in range(size)]
        pieces = [rows[owner, :, at : at + wide] for at, owner in spots]
        return jnp.concatenate(pieces, axis=1).astype(f32)

    out_part = unfolded(parts[None, z_rows:], n_width)
    d_out_weight = lax.ppermute(out_part, ("dp", "seq"), back).astype(f32)
    in_z = placed(own_rows(parts[:z_rows]))
    shares, in_z, d_out_weight = lax.optimization_barrier((shares, in_z, d_out_weight))
    first_part = sum(share.astype(f32) for share in shares)
    in_first = own_rows(first_part.astype(bf16), True)
    lifted = d_norm * norm_gain
    d_flat = inv * lifted - flat * (
        inv * inv * inv * jnp.mean(lifted * flat, axis=-1, keepdims=True)
    )
    d_hidden = (cot_own.astype(f32) + d_flat).reshape(n_seqs, block, n_width)
    in_first, d_hidden = lax.optimization_barrier((in_first, d_hidden))
    d_in_weight = jnp.concatenate(
        [
            in_z,
            placed(in_first[:, :, :own_inner]),
            placed(in_first[:, :, n_first - own_bc :], 1),
            placed(in_first[:, :, own_inner : own_inner + own_heads]),
        ],
        axis=1,
    )

    at = 0

    def take(count):
        nonlocal at
        at += count
        return packed[:, at - count : at]

    got_x = take((n_taps + 1) * own_inner).reshape(size, n_taps + 1, own_inner)
    got_bc = take((n_taps + 1) * own_bc).reshape(size, n_taps + 1, own_bc)
    got_x = undealt(got_x.transpose(1, 0, 2))
    got_bc = got_bc.transpose(1, 0, 2).reshape(n_taps + 1, 2 * n_state)
    conv_all = jnp.concatenate([got_x, got_bc], axis=1)
    d_gate_gain = undealt(take(own_inner)[None])[0]
    d_step_bias = undealt(take(own_heads)[None])[0]
    d_log_rate = undealt(take(own_heads)[None])[0]
    d_skip_gain = undealt(take(own_heads)[None])[0]
    d_norm_all = jnp.sum(take(n_width), axis=0)
    return (
        result,
        d_hidden,
        d_norm_all,
        d_in_weight,
        conv_all[:n_taps],
        conv_all[n_taps],
        d_step_bias,
        d_log_rate,
        d_skip_gain,
        d_gate_gain,
        d_out_weight,
    )


def solution(mesh):
    tokens = P("dp", "seq", None)
    rows = P(("dp", "seq"), None)
    return jax.shard_map(
        shards,
        mesh=mesh,
        in_specs=(tokens, P("dp", "seq"), tokens, P(), rows, P(), P(), P(), P(), P(), P(), rows),
        out_specs=(tokens, tokens, P(), rows, P(), P(), P(), P(), P(), P(), rows),
        check_vma=False,
    )
```
